32 devices in a mesh: gx: 4 (over y, x), gy: 8 (over z, core).
Axes of the slice: x: 2, y: 2, z: 4, core: 2. Of those that a mesh axis runs over, the one named last changes fastest.
Arguments:
- load_vector: float32 [112, 50176], P('gx', 'gy'), may hold values from -6 to 6
- initial_guess: float32 [112, 50176], P('gx', 'gy'), may hold values from -3 to 3
Outputs:
- smoothed: float32 [112, 50176], P('gx', 'gy')
- level_three: float32 [48, 9216], P('gx', 'gy')
- coarse_err: float32 [16, 1024], P('gx', 'gy')
The draws below stay inside these ranges and needn't reach their ends.
All inputs are finite; a program needn't handle non-finite values.
Results may differ from the reference program's by a relative error of at most 0.0003.
Values sent between devices are 32-bit elements; how exact they have to be, the bound alone decides.
No kernel may reach another device: no remote copies, remote signals or barrier semaphores. Data moves between devices by JAX's collectives and lax.ppermute only.
A program may use at most 192 MiB of HBM per device.

```python
import math
import jax
import jax.numpy as jnp
import numpy as np
from jax import lax

EXD = 4
EZ = 32
JAC = 4
NEX = 16
NEY = 32
NODX = 112
NODY = 224
NODZ = 224
N_GX = 4


def steps_of(own_key, shape, split, least, top_value):
    factor_of, own = 1.0, jax.random.fold_in(own_key, 6)
    for dim, parts in split:
        draws = jnp.exp(jax.random.uniform(jax.random.fold_in(own, dim), (parts,), jnp.float32, least / len(split), top_value / len(split)))
        factor_of = factor_of * jnp.repeat(draws, shape[dim] // parts).reshape([-1 if axis == dim else 1 for axis in range(len(shape))])
    return factor_of


def centred(rng, dims, scale, reach, pieces=(), kind=jnp.bfloat16):
    values = scale * jax.random.normal(rng, dims, jnp.float32)
    if pieces:
        values = values * steps_of(rng, dims, pieces, -0.22, 0.18)
    return jnp.clip(values, -reach, reach).astype(kind)


def setup_inputs(seed: int = 0) -> dict:
    key_of = jax.random.split(jax.random.key(seed), 3)
    load_vector = centred(key_of[0], (NODX, NODY * NODZ), 1.0, 6.0, ((0, 4), (1, 8)), jnp.float32)
    initial_guess = centred(key_of[1], (NODX, NODY * NODZ), 0.5, 3.0, ((0, 4), (1, 8)), jnp.float32)
    return dict(load_vector=load_vector, initial_guess=initial_guess)


highest = lax.Precision.HIGHEST
points_seven = (-1.0, -0.8717401485096066, -0.5917001814331423, -0.2092992179024789, 0.2092992179024789, 0.5917001814331423, 0.8717401485096066, 1.0)
points_three = (-1.0, -0.4472135954999579, 0.4472135954999579, 1.0)
points_one = (-1.0, 1.0)
damping = 2.0 / 3.0

def legendre_at(degree, location):
    previous, current = (1.0, location)
    for level_idx in range(1, degree):
        previous, current = (current, ((2 * level_idx + 1) * location * current - level_idx * previous) / (level_idx + 1))
    return current

def quadrature_weights():
    return np.array([2.0 / (56.0 * legendre_at(7, x) * legendre_at(7, x)) for x in points_seven])

def derivative_matrix():
    points = np.array(points_seven)
    products = np.array([np.prod([points[i] - points[k] for k in range(8) if k != i]) for i in range(8)])
    result = np.zeros((8, 8))
    for i in range(8):
        for j in range(8):
            if i != j:
                result[i, j] = products[i] / (products[j] * (points[i] - points[j]))
        result[i, i] = np.sum([1.0 / (points[i] - points[k]) for k in range(8) if k != i])
    return result

def element_stiffness():
    derivative = derivative_matrix()
    return derivative.T @ (quadrature_weights()[:, None] * derivative)

def assemble_line(elements):
    stiffness = element_stiffness()
    weights = quadrature_weights()
    extent = 7 * elements + 1
    global_stiff = np.zeros((extent, extent))
    lumped = np.zeros(extent)
    for m in range(elements):
        global_stiff[7 * m:7 * m + 8, 7 * m:7 * m + 8] += stiffness
        lumped[7 * m:7 * m + 8] += weights
    return (global_stiff, lumped)

def jacobi_eigen(matrix):
    rotated_mat = matrix.copy()
    extent = matrix.shape[0]
    vectors = np.eye(extent)
    for sweep_idx in range(12):
        for p in range(extent - 1):
            for q in range(p + 1, extent):
                angle_rot = 0.5 * math.atan2(2.0 * float(rotated_mat[p, q]), float(rotated_mat[q, q] - rotated_mat[p, p]))
                rotation = np.eye(extent)
                rotation[p, p] = math.cos(angle_rot)
                rotation[q, q] = math.cos(angle_rot)
                rotation[p, q] = math.sin(angle_rot)
                rotation[q, p] = -math.sin(angle_rot)
                rotated_mat = rotation.T @ rotated_mat @ rotation
                vectors = vectors @ rotation
    return (np.array([rotated_mat[i, i] for i in range(extent)]), vectors)

def patch_basis():
    global_stiff, lumped = assemble_line(2)
    inv_root = 1.0 / np.sqrt(lumped[1:14])
    eigvals, vectors = jacobi_eigen(inv_root[:, None] * global_stiff[1:14, 1:14] * inv_root[None, :])
    return (eigvals, inv_root[:, None] * vectors)

def interp_matrix(coarse_pts):
    result = np.ones((8, len(coarse_pts)))
    for a in range(8):
        for c in range(len(coarse_pts)):
            for k in range(len(coarse_pts)):
                if k != c:
                    result[a, c] *= (points_seven[a] - coarse_pts[k]) / (coarse_pts[c] - coarse_pts[k])
    return result

def restriction_rows(coarse_pts):
    shared = np.ones(8)
    shared[0] = 0.5
    shared[7] = 0.5
    return (interp_matrix(coarse_pts) * shared[:, None]).T

def line_map(values, axis_pos, matrix, stride):
    rotated = jnp.moveaxis(values, axis_pos, -1)
    front_shape = rotated.shape[:-1]
    elements = rotated.shape[-1] // 7
    padded = jnp.concatenate([rotated, jnp.zeros(front_shape + (1,), jnp.float32)], -1)
    leading = padded[..., :7 * elements].reshape(front_shape + (elements, 7))
    closing = padded[..., 7::7][..., None]
    element_view = jnp.concatenate([leading, closing], -1)
    result = jnp.einsum('...ma,ca->...mc', element_view, jnp.asarray(matrix, jnp.float32), precision=highest)
    summed = jnp.concatenate([result[..., :stride].reshape(front_shape + (elements * stride,)), jnp.zeros(front_shape + (1,), jnp.float32)], -1)
    summed = summed.at[..., stride::stride].add(result[..., stride])
    return jnp.moveaxis(summed[..., :elements * stride], -1, axis_pos)

def operator_global(values, mass_x, mass_y, mass_z):
    stiffness = element_stiffness()
    term_x = line_map(values, 0, stiffness, 7) * (mass_y[:, None] * mass_z[None, :])[None, :, :]
    term_y = line_map(values, 1, stiffness, 7) * (mass_x[:, None] * mass_z[None, :])[:, None, :]
    term_z = line_map(values, 2, stiffness, 7) * (mass_x[:, None] * mass_y[None, :])[:, :, None]
    return term_x + term_y + term_z

def windows_along(values, axis_pos, elements):
    rotated = jnp.moveaxis(values, axis_pos, -1)
    front_shape = rotated.shape[:-1]
    leading = rotated[..., :7 * elements].reshape(front_shape + (elements, 7))
    trailing = rotated[..., 7:7 * elements + 7].reshape(front_shape + (elements, 7))[..., :6]
    return jnp.moveaxis(jnp.concatenate([leading, trailing], -1), (-2, -1), (axis_pos, axis_pos + 1))

def unwindows_along(blocks, axis_pos, elements):
    rotated = jnp.moveaxis(blocks, (axis_pos, axis_pos + 1), (-2, -1))
    front_shape = rotated.shape[:-2]
    leading = rotated[..., :7].reshape(front_shape + (7 * elements,))
    trailing = jnp.concatenate([rotated[..., 7:], jnp.zeros(front_shape + (elements, 1), jnp.float32)], -1).reshape(front_shape + (7 * elements,))
    zero_pad = jnp.zeros(front_shape + (7,), jnp.float32)
    summed = jnp.concatenate([leading, zero_pad], -1) + jnp.concatenate([zero_pad, trailing], -1)
    return jnp.moveaxis(summed, -1, axis_pos)

def schwarz_global(residual):
    eigvals, eigbasis = patch_basis()
    inverse = jnp.asarray(1.0 / (eigvals[:, None, None] + eigvals[None, :, None] + eigvals[None, None, :]), jnp.float32)
    basis_mat = jnp.asarray(eigbasis, jnp.float32)
    padded_x = jnp.pad(residual, ((6, 7), (0, 0), (0, 0)))
    active_y = (jnp.arange(NEY, dtype=jnp.int32) >= 1).astype(jnp.float32)
    active_z = (jnp.arange(EZ, dtype=jnp.int32) >= 1).astype(jnp.float32)

    def slab(accum, slab_idx):
        offset = slab_idx * (7 * EXD)
        segment = lax.dynamic_slice_in_dim(padded_x, offset, 7 * EXD + 7, 0)
        blocks = windows_along(segment, 0, EXD)
        blocks = windows_along(jnp.pad(blocks, ((0, 0), (0, 0), (6, 7), (0, 0))), 2, NEY)
        blocks = windows_along(jnp.pad(blocks, ((0, 0), (0, 0), (0, 0), (0, 0), (6, 7))), 4, EZ)
        spectral = jnp.einsum('vawekf,ab,ec,fd->vbwckd', blocks, basis_mat, basis_mat, basis_mat, precision=highest)
        active_x = (slab_idx * EXD + jnp.arange(EXD, dtype=jnp.int32) >= 1).astype(jnp.float32)
        spectral = spectral * inverse[None, :, None, :, None, :] * active_x[:, None, None, None, None, None] * active_y[None, None, :, None, None, None] * active_z[None, None, None, None, :, None]
        returned = jnp.einsum('vbwckd,ab,ec,fd->vawekf', spectral, basis_mat, basis_mat, basis_mat, precision=highest)
        returned = unwindows_along(returned, 4, EZ)[:, :, :, :, 6:6 + NODZ]
        returned = unwindows_along(returned, 2, NEY)[:, :, 6:6 + NODY, :]
        returned = unwindows_along(returned, 0, EXD)
        current = lax.dynamic_slice_in_dim(accum, offset, 7 * EXD + 7, 0)
        return (lax.dynamic_update_slice_in_dim(accum, current + returned, offset, 0), None)
    accum, unused_out = lax.scan(slab, jnp.zeros((NODX + 13, NODY, NODZ), jnp.float32), jnp.arange(N_GX, dtype=jnp.int32))
    return accum[6:6 + NODX]

def coarse_sweeps(level_one, mask_one):
    coarse_err = jnp.zeros_like(level_one)
    for sweep_idx in range(JAC):
        padded = jnp.pad(coarse_err, 1)
        neighbours = padded[2:, 1:-1, 1:-1] + padded[:-2, 1:-1, 1:-1] + padded[1:-1, 2:, 1:-1] + padded[1:-1, :-2, 1:-1] + padded[1:-1, 1:-1, 2:] + padded[1:-1, 1:-1, :-2]
        applied = 12.0 * coarse_err - 2.0 * neighbours
        coarse_err = (coarse_err + damping / 12.0 * (level_one - applied)) * mask_one
    return coarse_err

def grid_mask(extent_x, extent_y, extent_z):
    line_x = (jnp.arange(extent_x, dtype=jnp.int32) >= 1).astype(jnp.float32)
    line_y = (jnp.arange(extent_y, dtype=jnp.int32) >= 1).astype(jnp.float32)
    line_z = (jnp.arange(extent_z, dtype=jnp.int32) >= 1).astype(jnp.float32)
    return line_x[:, None, None] * line_y[None, :, None] * line_z[None, None, :]

def reference(load_vector, initial_guess):
    load_grid = load_vector.reshape(NODX, NODY, NODZ)
    guess_grid = initial_guess.reshape(NODX, NODY, NODZ)
    masked = grid_mask(NODX, NODY, NODZ)
    mass_x = jnp.asarray(assemble_line(NEX)[1][:NODX], jnp.float32)
    mass_y = jnp.asarray(assemble_line(NEY)[1][:NODY], jnp.float32)
    mass_z = jnp.asarray(assemble_line(EZ)[1][:NODZ], jnp.float32)
    start_field = guess_grid * masked
    force_field = load_grid * masked
    residual = (force_field - operator_global(start_field, mass_x, mass_y, mass_z)) * masked
    correction = schwarz_global(residual)
    weight_x = jnp.asarray(np.where(np.arange(NODX) % 7 == 0, 1.0, 0.5), jnp.float32)
    weight_y = jnp.asarray(np.where(np.arange(NODY) % 7 == 0, 1.0, 0.5), jnp.float32)
    weight_z = jnp.asarray(np.where(np.arange(NODZ) % 7 == 0, 1.0, 0.5), jnp.float32)
    node_weight = weight_x[:, None, None] * weight_y[None, :, None] * weight_z[None, None, :]
    smoothed = (start_field + node_weight * correction) * masked
    resid_after = (force_field - operator_global(smoothed, mass_x, mass_y, mass_z)) * masked
    rows_three = restriction_rows(points_three)
    level_three = line_map(line_map(line_map(resid_after, 0, rows_three, 3), 1, rows_three, 3), 2, rows_three, 3)
    level_three = level_three * grid_mask(3 * NEX, 3 * NEY, 3 * EZ)
    rows_one = restriction_rows(points_one)
    level_one = line_map(line_map(line_map(resid_after, 0, rows_one, 1), 1, rows_one, 1), 2, rows_one, 1)
    mask_one = grid_mask(NEX, NEY, EZ)
    level_one = level_one * mask_one
    coarse_err = coarse_sweeps(level_one, mask_one)
    return (smoothed.reshape(NODX, NODY * NODZ), level_three.reshape(3 * NEX, 9 * NEY * EZ), coarse_err.reshape(NEX, NEY * EZ))
```

```python
import math

import jax
import jax.numpy as jnp
import numpy as np
from jax import lax
from jax.experimental import pallas as pl
from jax.experimental.pallas import tpu as pltpu
from jax.sharding import PartitionSpec as P

EZ = 32
JAC = 4


points_seven = (
    -1.0,
    -0.8717401485096066,
    -0.5917001814331423,
    -0.2092992179024789,
    0.2092992179024789,
    0.5917001814331423,
    0.8717401485096066,
    1.0,
)
points_three = (-1.0, -0.4472135954999579, 0.4472135954999579, 1.0)
points_one = (-1.0, 1.0)
damping = 2.0 / 3.0


def shifted(array, axis, by):
    devices = lax.axis_size(axis)
    pairs = [(i, i + by) for i in range(devices) if 0 <= i + by < devices]
    return lax.ppermute(array, axis, pairs)


def legendre_at(degree, location):
    previous, current = (1.0, location)
    for level_idx in range(1, degree):
        previous, current = (
            current,
            ((2 * level_idx + 1) * location * current - level_idx * previous) / (level_idx + 1),
        )
    return current


def quadrature_weights():
    return np.array([2.0 / (56.0 * legendre_at(7, x) * legendre_at(7, x)) for x in points_seven])


def derivative_matrix():
    points = np.array(points_seven)
    products = np.array(
        [np.prod([points[i] - points[k] for k in range(8) if k != i]) for i in range(8)]
    )
    result = np.zeros((8, 8))
    for i in range(8):
        for j in range(8):
            if i != j:
                result[i, j] = products[i] / (products[j] * (points[i] - points[j]))
        result[i, i] = np.sum([1.0 / (points[i] - points[k]) for k in range(8) if k != i])
    return result


def element_stiffness():
    derivative = derivative_matrix()
    return derivative.T @ (quadrature_weights()[:, None] * derivative)


def assemble_line(elements):
    stiffness = element_stiffness()
    weights = quadrature_weights()
    extent = 7 * elements + 1
    global_stiff = np.zeros((extent, extent))
    lumped = np.zeros(extent)
    for m in range(elements):
        global_stiff[7 * m : 7 * m + 8, 7 * m : 7 * m + 8] += stiffness
        lumped[7 * m : 7 * m + 8] += weights
    return (global_stiff, lumped)


def jacobi_eigen(matrix):
    rotated_mat = matrix.copy()
    extent = matrix.shape[0]
    vectors = np.eye(extent)
    for sweep_idx in range(12):
        for p in range(extent - 1):
            for q in range(p + 1, extent):
                angle_rot = 0.5 * math.atan2(
                    2.0 * float(rotated_mat[p, q]), float(rotated_mat[q, q] - rotated_mat[p, p])
                )
                rotation = np.eye(extent)
                rotation[p, p] = math.cos(angle_rot)
                rotation[q, q] = math.cos(angle_rot)
                rotation[p, q] = math.sin(angle_rot)
                rotation[q, p] = -math.sin(angle_rot)
                rotated_mat = rotation.T @ rotated_mat @ rotation
                vectors = vectors @ rotation
    return (np.array([rotated_mat[i, i] for i in range(extent)]), vectors)


def patch_basis():
    global_stiff, lumped = assemble_line(2)
    inv_root = 1.0 / np.sqrt(lumped[1:14])
    eigvals, vectors = jacobi_eigen(
        inv_root[:, None] * global_stiff[1:14, 1:14] * inv_root[None, :]
    )
    return (eigvals, inv_root[:, None] * vectors)


def interp_matrix(coarse_pts):
    result = np.ones((8, len(coarse_pts)))
    for a in range(8):
        for c in range(len(coarse_pts)):
            for k in range(len(coarse_pts)):
                if k != c:
                    result[a, c] *= (points_seven[a] - coarse_pts[k]) / (
                        coarse_pts[c] - coarse_pts[k]
                    )
    return result


def restriction_rows(coarse_pts):
    shared = np.ones(8)
    shared[0] = 0.5
    shared[7] = 0.5
    return (interp_matrix(coarse_pts) * shared[:, None]).T


def restriction_line(elements, coarse_pts):
    degree = len(coarse_pts) - 1
    rows_mat = restriction_rows(coarse_pts)
    result = np.zeros((degree * elements + 1, 7 * elements + 1))
    for m in range(elements):
        result[degree * m : degree * m + degree + 1, 7 * m : 7 * m + 8] += rows_mat
    return result


def patch_matrix(eigbasis, vertices, extent):
    result = np.zeros((13 * vertices, extent))
    for b in range(13):
        for v in range(vertices):
            for a in range(13):
                node_idx = 7 * v + a
                result[b * vertices + v, node_idx] = eigbasis[a, b]
    return result


high = lax.Precision.HIGH
LANES = 128
f32 = jnp.float32


def up_to(length, multiple):
    return -(-length // multiple) * multiple


def placed(matrix, shape, row=0, col=0):
    result = np.zeros(shape, np.float32)
    result[row : row + matrix.shape[0], col : col + matrix.shape[1]] = matrix
    return result


def mm(left, right):
    return lax.dot_general(
        left, right, (((1,), (0,)), ((), ())), precision=high, preferred_element_type=f32
    )


class Sizes:
    def __init__(self, x_nodes, y_nodes, z_nodes):
        self.x_nodes, self.y_nodes, self.z_nodes = (x_nodes, y_nodes, z_nodes)
        self.x_elems, self.y_elems, self.z_elems = (x_nodes // 7, y_nodes // 7, z_nodes // 7)
        self.rows = up_to(x_nodes + 9, 8)
        self.lanes = up_to(z_nodes, LANES)
        self.modes_x = up_to(13 * self.x_elems, 8)
        self.modes_z = up_to(13 * self.z_elems, LANES)
        self.coarse_x = 3 * self.x_elems + 4
        self.coarse_y = 3 * self.y_elems + 4
        self.coarse_z = 3 * self.z_elems
        self.coarse_rows = up_to(self.coarse_x, 8)
        self.coarse_lanes = up_to(self.coarse_z, LANES)


def line_tables(elements):
    nodes = 7 * elements
    stiff, lumped = assemble_line(elements + 2)
    restrict = restriction_line(elements + 3, points_three)[3 : 3 * elements + 7, 7 : nodes + 15]
    columns = np.arange(-6, nodes)
    weight = np.where(columns % 7 == 0, 1.0, 0.5)
    mass_part = restrict[:, 1:-1] * (lumped[1 : nodes + 7] * weight)[None, :]
    stiff_part = restrict @ (stiff[: nodes + 8, 1 : nodes + 7] * weight[None, :])
    return dict(
        stiff=stiff[1 : nodes + 7, : nodes + 8],
        mass=lumped[1 : nodes + 7],
        own=restrict[:, 7:-1],
        mass_part=mass_part,
        stiff_part=stiff_part,
    )


def linear_from_cubic(first, last, first_three, last_three):
    result = np.zeros((last - first + 1, last_three - first_three + 1))
    for m in range(first, last + 1):
        for offset, factor in (
            (0, 1.0),
            (1, (1.0 - points_three[1]) / 2.0),
            (2, (1.0 - points_three[2]) / 2.0),
            (-2, (1.0 + points_three[1]) / 2.0),
            (-1, (1.0 + points_three[2]) / 2.0),
        ):
            node = 3 * m + offset - first_three
            if 0 <= node < result.shape[1]:
                result[m - first, node] = factor
    return result


def patch_constants(s):
    line_x = line_tables(s.x_elems)
    stiff_z, lumped_z = assemble_line(s.z_elems)
    stiff_z, lumped_z = (stiff_z[: s.z_nodes, : s.z_nodes], lumped_z[: s.z_nodes])
    weight_z = np.where(np.arange(s.z_nodes) % 7 == 0, 1.0, 0.5)
    restrict_z = restriction_line(s.z_elems, points_three)[: s.coarse_z, : s.z_nodes]
    eigvals, eigbasis = patch_basis()
    square = (s.rows, s.rows)
    mass_z = np.zeros(s.lanes)
    mass_z[: s.z_nodes] = lumped_z
    mass_x = np.zeros(s.rows)
    mass_x[2 : s.x_nodes + 8] = line_x["mass"]
    spread = np.ones((s.rows, s.lanes))
    fwd_x = placed(
        patch_matrix(eigbasis, s.x_elems, s.x_nodes + 6), (s.modes_x, s.rows), col=2
    )
    fwd_z = patch_matrix(eigbasis, s.z_elems, s.z_nodes + 6)[:, 6:]
    vertex_z = np.arange(13 * s.z_elems) % s.z_elems
    fwd_z = np.where((vertex_z >= 1)[:, None], fwd_z, 0.0)
    inverse = 1.0 / (eigvals[:, None, None] + eigvals[None, :, None] + eigvals[None, None, :])
    factor = np.zeros((13, s.modes_x, s.modes_z), np.float32)
    factor[:, : 13 * s.x_elems, : 13 * s.z_elems] = np.repeat(
        np.repeat(inverse, s.x_elems, 1), s.z_elems, 2
    )
    coarse_of_z = np.zeros((s.lanes, 2 * s.coarse_lanes), np.float32)
    coarse_of_z[: s.z_nodes, : s.coarse_z] = (restrict_z * (lumped_z * weight_z)[None, :]).T
    coarse_of_z[: s.z_nodes, s.coarse_lanes : s.coarse_lanes + s.coarse_z] = (
        restrict_z @ (stiff_z * weight_z[None, :])
    ).T
    coarse_of_x = np.zeros((2 * s.coarse_rows, s.rows), np.float32)
    coarse_of_x[: s.coarse_x, 2 : s.x_nodes + 8] = line_x["mass_part"]
    coarse_of_x[s.coarse_rows : s.coarse_rows + s.coarse_x, 2 : s.x_nodes + 8] = line_x[
        "stiff_part"
    ]
    own_x = placed(line_x["own"], (s.coarse_rows, s.rows), col=8)
    own_z = placed(restrict_z.T, (s.lanes, s.coarse_lanes))
    one_z = placed(
        linear_from_cubic(0, s.z_elems - 1, 0, s.coarse_z - 1).T, (s.coarse_lanes, LANES)
    )
    one_x = placed(
        linear_from_cubic(-1, s.x_elems, -3, 3 * s.x_elems), (8, s.coarse_rows)
    )
    return [
        placed(line_x["stiff"], square, row=2, col=1),
        placed(stiff_z, (s.lanes, s.lanes)),
        spread * mass_x[:, None],
        spread * mass_z[None, :],
        mass_x[:, None] * mass_z[None, :],
        fwd_x,
        fwd_x.T,
        placed(fwd_z.T, (s.lanes, s.modes_z)),
        placed(fwd_z, (s.modes_z, s.lanes)),
        factor,
        coarse_of_z,
        coarse_of_x,
        own_z,
        own_x,
        one_z,
        one_x,
    ]


def line_of_planes(coefficients, planes):
    total = None
    for coefficient, plane in zip(coefficients, planes):
        if coefficient != 0.0:
            part = plane() * float(coefficient)
            total = part if total is None else total + part
    return total


def patch_kernel(s):
    rows, lanes, nz = (s.rows, s.lanes, s.z_nodes)
    ey, ny = (s.y_elems, s.y_nodes)
    line_y = line_tables(ey)
    _, eigbasis = patch_basis()
    stiffness = element_stiffness()
    mass_y = line_y["mass"]
    one_y = linear_from_cubic(-1, ey, -3, 3 * ey)

    def kernel(
        guess, load, below, above,
        k_x, k_z, m_x, m_z, m_xz, w_x, w_xt, w_z, w_zt, factor, q_z, q_x, r_z, r_x, o_z, o_x,
        edge_out, own_out, three_out, one_out, down_out, up_out,
        u, r, xf, xb, c, cz, rz, hx, ex, rx,
    ):
        gx = lax.axis_index("gx")
        gy = lax.axis_index("gy")
        lane = lax.broadcasted_iota(jnp.int32, (rows, lanes), 1)
        row = lax.broadcasted_iota(jnp.int32, (rows, lanes), 0)
        live = ((lane >= 1) & (lane < nz) & ((row != 8) | (gx > 0))).astype(f32)
        live_y = (gy > 0).astype(f32)
        for j in range(7):
            u[j] = below[:, nz * j : nz * j + lanes] * live
        for j in range(ny):
            mask = live if j else live * live_y
            u[7 + j] = guess[:, nz * j : nz * j + lanes] * mask
        u[ny + 7] = above[...] * live
        inside = ((lane < nz)).astype(f32)
        for j in range(6):
            r[j] = below[:, nz * (7 + j) : nz * (7 + j) + lanes] * inside
        for j in range(ny):
            r[6 + j] = load[:, nz * j : nz * j + lanes] * inside
        r[ny + 6] = jnp.zeros((rows, lanes), f32)

        def direct(chunk, carry):
            base = chunk * 7
            planes = u[pl.ds(base + 1, 7)]
            z_term = mm(planes.reshape(7 * rows, lanes), k_z[...]).reshape(7, rows, lanes)
            for i in range(7):
                x_term = mm(k_x[...], planes[i])
                both = x_term * m_z[...] + z_term[i] * m_x[...]
                r[base + i] = r[base + i] - float(mass_y[i]) * both
            return carry

        lax.fori_loop(0, ey + 1, direct, 0)

        def along_y(tile, carry):
            at = pl.ds(pl.multiple_of(tile * 8, 8), 8)
            scale = m_xz[at, :]
            corner = None
            for e in range(ey + 1):
                nodes = [u[7 * e + i, at, :] for i in range(8)]
                plus = [nodes[i] + nodes[7 - i] for i in range(4)]
                minus = [nodes[i] - nodes[7 - i] for i in range(4)]
                out = [None] * 8
                for i in range(4):
                    even = sum(
                        plus[k] * float(0.5 * (stiffness[i, k] + stiffness[i, 7 - k]))
                        for k in range(4)
                    )
                    odd = sum(
                        minus[k] * float(0.5 * (stiffness[i, k] - stiffness[i, 7 - k]))
                        for k in range(4)
                    )
                    out[i], out[7 - i] = (even + odd, even - odd)
                if e:
                    out[0] = out[0] + corner
                corner = out[7]
                for i in range(0 if e else 1, 7):
                    plane = 7 * e + i - 1
                    r[plane, at, :] = r[plane, at, :] - out[i] * scale
            active = (gy > 0).astype(f32)
            for v in range(ey):
                first = [r[7 * v + a, at, :] for a in range(13)]
                if v == 0:
                    first = [value * active for value in first]
                even = [first[6]] + [first[6 + a] + first[6 - a] for a in range(1, 7)]
                odd = [first[6 + a] - first[6 - a] for a in range(1, 7)]
                for b in range(13):
                    if symmetric(eigbasis[:, b]):
                        xf[b, v, at, :] = sum(
                            even[a] * float(eigbasis[6 + a, b]) for a in range(7)
                        )
                    else:
                        xf[b, v, at, :] = sum(
                            odd[a] * float(eigbasis[7 + a, b]) for a in range(6)
                        )
            return carry

        lax.fori_loop(0, rows // 8, along_y, 0)
        mode = lax.broadcasted_iota(jnp.int32, (s.modes_x, rows), 0)
        forward_x = w_x[...] * ((mode % s.x_elems != 0) | (gx > 0)).astype(f32)

        def spectral(b, carry):
            parts = [mm(forward_x, xf[b, v]) for v in range(ey)]
            modes = mm(jnp.concatenate(parts, 0), w_z[...])
            scaled = modes.reshape(ey, s.modes_x, s.modes_z) * factor[b][None]
            back = mm(scaled.reshape(ey * s.modes_x, s.modes_z), w_zt[...])
            for v in range(ey):
                xb[b, v] = mm(w_xt[...], back[v * s.modes_x : (v + 1) * s.modes_x])
            return carry

        lax.fori_loop(0, 13, spectral, 0)

        def back_y(tile, carry):
            at = pl.ds(pl.multiple_of(tile * 8, 8), 8)
            tail = None
            for v in range(ey):
                modes = [xb[b, v, at, :] for b in range(13)]
                out = [None] * 13
                for a in range(7):
                    even = sum(
                        modes[b] * float(eigbasis[6 + a, b])
                        for b in range(13)
                        if symmetric(eigbasis[:, b])
                    )
                    if a == 0:
                        out[6] = even
                        continue
                    odd = sum(
                        modes[b] * float(eigbasis[6 + a, b])
                        for b in range(13)
                        if not symmetric(eigbasis[:, b])
                    )
                    out[6 + a], out[6 - a] = (even + odd, even - odd)
                if v:
                    out[:6] = [value + other for value, other in zip(out[:6], tail)]
                tail = out[7:]
                for a in range(13 if v == ey - 1 else 7):
                    c[7 * v + a, at, :] = out[a]
            return carry

        lax.fori_loop(0, rows // 8, back_y, 0)

        for j in range(6):
            down_out[:, lanes * j : lanes * (j + 1)] = c[j]
        edge_out[...] = c[6:, 0:8, :]
        own_out[...] = c[6:, 8:, :]

        half = s.coarse_lanes
        rows_c = s.coarse_rows
        cz[...] = mm(c[...].reshape((ny + 6) * rows, lanes), q_z[...]).reshape(
            ny + 6, rows, 2 * half
        )
        rz[...] = mm(r[6 : ny + 6].reshape(ny * rows, lanes), r_z[...]).reshape(ny, rows, half)
        for y in range(ny + 6):
            plane = mm(q_x[...], cz[y])
            hx[y] = plane[:rows_c, :half]
            ex[y] = plane[rows_c:, :half] + plane[:rows_c, half:]
        for y in range(ny):
            rx[y] = mm(r_x[...], rz[y])
        for j in range(s.coarse_y):
            total = line_of_planes(
                np.concatenate(
                    [line_y["own"][j], -line_y["stiff_part"][j], -line_y["mass_part"][j]]
                ),
                [lambda y=y: rx[y] for y in range(ny)]
                + [lambda y=y: hx[y] for y in range(ny + 6)]
                + [lambda y=y: ex[y] for y in range(ny + 6)],
            )
            three_out[j] = total
        one_all = mm(
            three_out[...].reshape(s.coarse_y * rows_c, half), o_z[...]
        ).reshape(s.coarse_y, rows_c, LANES)
        for m in range(ey + 2):
            mixed = line_of_planes(
                one_y[m], [lambda j=j: one_all[j] for j in range(s.coarse_y)]
            )
            one_out[m] = mm(o_x[...], mixed)
        base = 6 * lanes
        for j in range(4):
            at = base + half * j
            if j < 3:
                down_out[0:rows_c, at : at + half] = three_out[j]
            else:
                down_out[0:rows_c, at : at + half] = jnp.zeros((rows_c, half), f32)
            down_out[rows_c : rows_c + 8, at : at + LANES] = one_out[j]
            down_out[rows_c + 8 :, at : at + half] = jnp.zeros((rows - rows_c - 8, half), f32)
            up_at = half * j
            if j == 0:
                up_out[0:rows_c, up_at : up_at + half] = three_out[s.coarse_y - 1]
            else:
                up_out[0:rows_c, up_at : up_at + half] = jnp.zeros((rows_c, half), f32)
            up_out[rows_c : rows_c + 8, up_at : up_at + LANES] = one_out[ey - 2 + j]

    return kernel


def symmetric(vector):
    return abs(vector[0] - vector[-1]) < abs(vector[0] + vector[-1])


def join_kernel(s):
    lanes, half, rows_c = (s.lanes, s.coarse_lanes, s.coarse_rows)
    ey, ny = (s.y_elems, s.y_nodes)

    def kernel(edge, three, one, down, up, down_out, up_out, three_out, one_out):
        for y in range(ny):
            plane = edge[y]
            if y >= ny - 6:
                j = y - (ny - 6)
                plane = plane + down[0:8, lanes * j : lanes * (j + 1)]
            down_out[:, lanes * y : lanes * (y + 1)] = plane
        base = 6 * lanes
        tiles = ny * lanes
        for j in range(max(3 * ey, ey + 6)):
            at = tiles + half * j
            down_out[:, at : at + half] = jnp.zeros((8, half), f32)
            up_out[:, half * j : half * (j + 1)] = jnp.zeros((8, half), f32)
        for j in range(3 * ey):
            plane = three[3 + j]
            if j >= 3 * ey - 3:
                k = j - (3 * ey - 3)
                plane = plane + down[0:rows_c, base + half * k : base + half * (k + 1)]
            if j == 0:
                plane = plane + up[0:rows_c, 0:half]
            three_out[j] = plane
            at = tiles + half * j
            down_out[0:3, at : at + half] = plane[0:3]
            up_out[0:1, half * j : half * (j + 1)] = plane[s.coarse_x - 1 : s.coarse_x]
        for j in range(ey + 6):
            y = j - 3
            plane = None
            if -1 <= y <= ey:
                plane = one[y + 1]
            if y <= 0:
                k = y + 3
                part = up[rows_c : rows_c + 8, half * k : half * k + LANES]
                plane = part if plane is None else plane + part
            if y >= ey - 1:
                k = y - (ey - 1)
                at = base + half * k
                part = down[rows_c : rows_c + 8, at : at + LANES]
                plane = part if plane is None else plane + part
            one_out[j] = plane
            at = tiles + half * j
            down_out[4:8, at : at + LANES] = plane[0:4]
            up_out[4:8, half * j : half * j + LANES] = plane[s.x_elems - 2 : s.x_elems + 2]

    return kernel


def finish_kernel(s, x_total, y_total):
    lanes, half, rows_c, nz = (s.lanes, s.coarse_lanes, s.coarse_rows, s.z_nodes)
    ex, ey, nx, ny = (s.x_elems, s.y_elems, s.x_nodes, s.y_nodes)
    one_rows = up_to(ex + 6, 8)

    def kernel(
        guess, weight, own, down, right, left, three, one,
        smooth_out, three_out, coarse_out, corr, fine, level,
    ):
        gx = lax.axis_index("gx")
        gy = lax.axis_index("gy")
        lane = lax.broadcasted_iota(jnp.int32, (nx, nz), 1)
        row = lax.broadcasted_iota(jnp.int32, (nx, nz), 0)
        live = ((lane >= 1) & ((row >= 1) | (gx > 0))).astype(f32)
        live_y = (gy > 0).astype(f32)
        for y in range(ny):
            corr[...] = own[y]
            if y >= ny - 6:
                j = y - (ny - 6)
                corr[...] += down[8:, lanes * j : lanes * (j + 1)]
            corr[nx - 6 : nx, :] += right[2:8, lanes * y : lanes * (y + 1)]
            mask = live if y else live * live_y
            factor = weight[...] * (1.0 if y % 7 == 0 else 0.5)
            smooth_out[:, nz * y : nz * (y + 1)] = (
                guess[:, nz * y : nz * (y + 1)] + factor * corr[0:nx, 0:nz]
            ) * mask
        tiles = ny * lanes
        nzc = s.coarse_z
        lane = lax.broadcasted_iota(jnp.int32, (3 * ex, nzc), 1)
        row = lax.broadcasted_iota(jnp.int32, (3 * ex, nzc), 0)
        live = ((lane >= 1) & ((row >= 1) | (gx > 0))).astype(f32)
        for j in range(3 * ey):
            fine[...] = three[j]
            at = tiles + half * j
            fine[3 * ex : 3 * ex + 3, :] += right[0:3, at : at + half]
            fine[3:4, :] += left[0:1, half * j : half * (j + 1)]
            mask = live if j else live * live_y
            three_out[:, nzc * j : nzc * (j + 1)] = fine[3 : 3 * ex + 3, 0:nzc] * mask
        level[...] = jnp.zeros((ey + 6, one_rows, LANES), f32)
        for j in range(ey + 6):
            level[j, 2 : ex + 4, :] = one[j, 0 : ex + 2, :]
            at = tiles + half * j
            level[j, 0:4, :] += left[4:8, half * j : half * j + LANES]
            level[j, ex + 2 : ex + 6, :] += right[4:8, at : at + LANES]
        shape = (one_rows, LANES)
        lane = lax.broadcasted_iota(jnp.int32, shape, 1)
        row = lax.broadcasted_iota(jnp.int32, shape, 0)
        global_x = gx * ex + row - 3
        plane_mask = (
            (lane >= 1) & (lane < s.z_elems) & (row < ex + 6)
            & (global_x >= 1) & (global_x < x_total)
        )
        masks = []
        for j in range(ey + 6):
            global_y = gy * ey + (j - 3)
            inside = (global_y >= 1) & (global_y < y_total)
            masks.append((plane_mask & inside).astype(f32))
        levels = [level[j] for j in range(ey + 6)]
        error = [damping / 12.0 * a * m for a, m in zip(levels, masks)]
        zero = jnp.zeros(shape, f32)
        for sweep in range(1, JAC):
            lower = [zero] + error[:-1]
            upper = error[1:] + [zero]
            fresh = []
            for j in range(ey + 6):
                here = error[j]
                neighbours = (
                    lower[j]
                    + upper[j]
                    + pltpu.roll(here, 1, 0)
                    + pltpu.roll(here, one_rows - 1, 0)
                    + pltpu.roll(here, 1, 1)
                    + pltpu.roll(here, LANES - 1, 1)
                )
                applied = 12.0 * here - 2.0 * neighbours
                fresh.append((here + damping / 12.0 * (levels[j] - applied)) * masks[j])
            error = fresh
        nze = s.z_elems
        for j in range(ey):
            coarse_out[:, nze * j : nze * (j + 1)] = error[3 + j][3 : 3 + ex, 0:nze]

    return kernel


def local(load_vector, initial_guess):
    z_nodes = 7 * EZ
    x_nodes = load_vector.shape[0]
    y_nodes = load_vector.shape[1] // z_nodes
    s = Sizes(x_nodes, y_nodes, z_nodes)
    rows, lanes, half = (s.rows, s.lanes, s.coarse_lanes)
    ny, ey = (s.y_nodes, s.y_elems)
    width = y_nodes * z_nodes
    sent_up = jnp.concatenate([initial_guess[x_nodes - 7 :], load_vector[x_nodes - 6 :]], 0)
    from_below = shifted(sent_up, "gx", 1)
    from_above = shifted(initial_guess[:1], "gx", -1)
    tail = up_to((ny - 1) * z_nodes + lanes, LANES) - width

    def framed(pieces, first):
        used = first + sum(piece.shape[0] for piece in pieces)
        parts = (
            [jnp.zeros((first, width), f32)] + pieces + [jnp.zeros((rows - used, width), f32)]
        )
        return jnp.pad(jnp.concatenate(parts, 0), ((0, 0), (0, tail)))

    guess_ext = framed([from_below[:7], initial_guess, from_above], 1)
    load_ext = framed([from_below[7:], load_vector], 2)
    message = jnp.concatenate(
        [guess_ext[:, (ny - 7) * z_nodes : width], load_ext[:, (ny - 6) * z_nodes : width]], 1
    )
    message = jnp.pad(message, ((0, 0), (0, up_to(12 * z_nodes + lanes, LANES) - 13 * z_nodes)))
    y_below = shifted(message, "gy", 1)
    y_above = shifted(guess_ext[:, :lanes], "gy", -1)
    constants = [jnp.asarray(value, f32) for value in patch_constants(s)]
    shape = lambda *dims: jax.ShapeDtypeStruct(dims, f32)
    params = pltpu.CompilerParams(vmem_limit_bytes=56 * 2**20)
    edge, own, three, one, down, up = pl.pallas_call(
        patch_kernel(s),
        out_shape=(
            shape(ny, 8, lanes),
            shape(ny, rows - 8, lanes),
            shape(s.coarse_y, s.coarse_rows, half),
            shape(ey + 2, 8, LANES),
            shape(rows, 6 * lanes + 4 * half),
            shape(s.coarse_rows + 8, 4 * half),
        ),
        scratch_shapes=[
            pltpu.VMEM((ny + 8, rows, lanes), f32),
            pltpu.VMEM((ny + 7, rows, lanes), f32),
            pltpu.VMEM((13, ey, rows, lanes), f32),
            pltpu.VMEM((13, ey, rows, lanes), f32),
            pltpu.VMEM((ny + 6, rows, lanes), f32),
            pltpu.VMEM((ny + 6, rows, 2 * half), f32),
            pltpu.VMEM((ny, rows, half), f32),
            pltpu.VMEM((ny + 6, s.coarse_rows, half), f32),
            pltpu.VMEM((ny + 6, s.coarse_rows, half), f32),
            pltpu.VMEM((ny, s.coarse_rows, half), f32),
        ],
        compiler_params=params,
        name="patches",
    )(guess_ext, load_ext, y_below, y_above, *constants)
    down = shifted(down, "gy", -1)
    up = shifted(up, "gy", 1)
    tiles = max(3 * ey, ey + 6)
    right, left, three, one = pl.pallas_call(
        join_kernel(s),
        out_shape=(
            shape(8, ny * lanes + tiles * half),
            shape(8, tiles * half),
            shape(3 * ey, s.coarse_rows, half),
            shape(ey + 6, 8, LANES),
        ),
        compiler_params=params,
        name="join",
    )(edge, three, one, down, up)
    right = shifted(right, "gx", -1)
    left = shifted(left, "gx", 1)
    weight = np.where(np.arange(x_nodes) % 7 == 0, 1.0, 0.5)[:, None] * np.where(
        np.arange(z_nodes) % 7 == 0, 1.0, 0.5
    )
    return pl.pallas_call(
        finish_kernel(
            s, s.x_elems * lax.axis_size("gx"), ey * lax.axis_size("gy")
        ),
        out_shape=(
            shape(x_nodes, width),
            shape(3 * s.x_elems, 3 * ey * s.coarse_z),
            shape(s.x_elems, ey * s.z_elems),
        ),
        scratch_shapes=[
            pltpu.VMEM((rows - 8, lanes), f32),
            pltpu.VMEM((s.coarse_rows, half), f32),
            pltpu.VMEM((ey + 6, up_to(s.x_elems + 6, 8), LANES), f32),
        ],
        compiler_params=params,
        name="finish",
    )(initial_guess, jnp.asarray(weight, f32), own, down, right, left, three, one)


def solution(mesh):
    in_specs = (P("gx", "gy"), P("gx", "gy"))
    out_specs = (P("gx", "gy"), P("gx", "gy"), P("gx", "gy"))
    return jax.shard_map(local, mesh=mesh, in_specs=in_specs, out_specs=out_specs, check_vma=False)
```

```python
import math

import jax
import jax.numpy as jnp
import numpy as np
from jax import lax
from jax.experimental import pallas as pl
from jax.experimental.pallas import tpu as pltpu
from jax.sharding import PartitionSpec as P

EZ = 32
JAC = 4


points_seven = (
    -1.0,
    -0.8717401485096066,
    -0.5917001814331423,
    -0.2092992179024789,
    0.2092992179024789,
    0.5917001814331423,
    0.8717401485096066,
    1.0,
)
points_three = (-1.0, -0.4472135954999579, 0.4472135954999579, 1.0)
points_one = (-1.0, 1.0)
damping = 2.0 / 3.0


def shifted(array, axis, by):
    devices = lax.axis_size(axis)
    pairs = [(i, i + by) for i in range(devices) if 0 <= i + by < devices]
    return lax.ppermute(array, axis, pairs)


def legendre_at(degree, location):
    previous, current = (1.0, location)
    for level_idx in range(1, degree):
        previous, current = (
            current,
            ((2 * level_idx + 1) * location * current - level_idx * previous) / (level_idx + 1),
        )
    return current


def quadrature_weights():
    return np.array([2.0 / (56.0 * legendre_at(7, x) * legendre_at(7, x)) for x in points_seven])


def derivative_matrix():
    points = np.array(points_seven)
    products = np.array(
        [np.prod([points[i] - points[k] for k in range(8) if k != i]) for i in range(8)]
    )
    result = np.zeros((8, 8))
    for i in range(8):
        for j in range(8):
            if i != j:
                result[i, j] = products[i] / (products[j] * (points[i] - points[j]))
        result[i, i] = np.sum([1.0 / (points[i] - points[k]) for k in range(8) if k != i])
    return result


def element_stiffness():
    derivative = derivative_matrix()
    return derivative.T @ (quadrature_weights()[:, None] * derivative)


def assemble_line(elements):
    stiffness = element_stiffness()
    weights = quadrature_weights()
    extent = 7 * elements + 1
    global_stiff = np.zeros((extent, extent))
    lumped = np.zeros(extent)
    for m in range(elements):
        global_stiff[7 * m : 7 * m + 8, 7 * m : 7 * m + 8] += stiffness
        lumped[7 * m : 7 * m + 8] += weights
    return (global_stiff, lumped)


def jacobi_eigen(matrix):
    rotated_mat = matrix.copy()
    extent = matrix.shape[0]
    vectors = np.eye(extent)
    for sweep_idx in range(12):
        for p in range(extent - 1):
            for q in range(p + 1, extent):
                angle_rot = 0.5 * math.atan2(
                    2.0 * float(rotated_mat[p, q]), float(rotated_mat[q, q] - rotated_mat[p, p])
                )
                rotation = np.eye(extent)
                rotation[p, p] = math.cos(angle_rot)
                rotation[q, q] = math.cos(angle_rot)
                rotation[p, q] = math.sin(angle_rot)
                rotation[q, p] = -math.sin(angle_rot)
                rotated_mat = rotation.T @ rotated_mat @ rotation
                vectors = vectors @ rotation
    return (np.array([rotated_mat[i, i] for i in range(extent)]), vectors)


def patch_basis():
    global_stiff, lumped = assemble_line(2)
    inv_root = 1.0 / np.sqrt(lumped[1:14])
    eigvals, vectors = jacobi_eigen(
        inv_root[:, None] * global_stiff[1:14, 1:14] * inv_root[None, :]
    )
    return (eigvals, inv_root[:, None] * vectors)


def interp_matrix(coarse_pts):
    result = np.ones((8, len(coarse_pts)))
    for a in range(8):
        for c in range(len(coarse_pts)):
            for k in range(len(coarse_pts)):
                if k != c:
                    result[a, c] *= (points_seven[a] - coarse_pts[k]) / (
                        coarse_pts[c] - coarse_pts[k]
                    )
    return result


def restriction_rows(coarse_pts):
    shared = np.ones(8)
    shared[0] = 0.5
    shared[7] = 0.5
    return (interp_matrix(coarse_pts) * shared[:, None]).T


def restriction_line(elements, coarse_pts):
    degree = len(coarse_pts) - 1
    rows_mat = restriction_rows(coarse_pts)
    result = np.zeros((degree * elements + 1, 7 * elements + 1))
    for m in range(elements):
        result[degree * m : degree * m + degree + 1, 7 * m : 7 * m + 8] += rows_mat
    return result


def patch_matrix(eigbasis, vertices, extent):
    result = np.zeros((13 * vertices, extent))
    for b in range(13):
        for v in range(vertices):
            for a in range(13):
                node_idx = 7 * v + a
                result[b * vertices + v, node_idx] = eigbasis[a, b]
    return result


high = lax.Precision.HIGH
LANES = 128
f32 = jnp.float32


def up_to(length, multiple):
    return -(-length // multiple) * multiple


def placed(matrix, shape, row=0, col=0):
    result = np.zeros(shape, np.float32)
    result[row : row + matrix.shape[0], col : col + matrix.shape[1]] = matrix
    return result


def mm(left, right):
    return lax.dot_general(
        left, right, (((1,), (0,)), ((), ())), precision=high, preferred_element_type=f32
    )


class Sizes:
    def __init__(self, x_nodes, y_nodes, z_nodes):
        self.x_nodes, self.y_nodes, self.z_nodes = (x_nodes, y_nodes, z_nodes)
        self.x_elems, self.y_elems, self.z_elems = (x_nodes // 7, y_nodes // 7, z_nodes // 7)
        self.rows = up_to(x_nodes + 9, 8)
        self.lanes = up_to(z_nodes, LANES)
        self.modes_x = up_to(13 * self.x_elems, 8)
        self.modes_z = up_to(13 * self.z_elems, LANES)
        self.coarse_x = 3 * self.x_elems + 4
        self.coarse_y = 3 * self.y_elems + 4
        self.coarse_z = 3 * self.z_elems
        self.coarse_rows = up_to(self.coarse_x, 8)
        self.coarse_lanes = up_to(self.coarse_z, LANES)


def line_tables(elements):
    nodes = 7 * elements
    stiff, lumped = assemble_line(elements + 2)
    restrict = restriction_line(elements + 3, points_three)[3 : 3 * elements + 7, 7 : nodes + 15]
    columns = np.arange(-6, nodes)
    weight = np.where(columns % 7 == 0, 1.0, 0.5)
    mass_part = restrict[:, 1:-1] * (lumped[1 : nodes + 7] * weight)[None, :]
    stiff_part = restrict @ (stiff[: nodes + 8, 1 : nodes + 7] * weight[None, :])
    return dict(
        stiff=stiff[1 : nodes + 7, : nodes + 8],
        mass=lumped[1 : nodes + 7],
        own=restrict[:, 7:-1],
        mass_part=mass_part,
        stiff_part=stiff_part,
    )


def linear_from_cubic(first, last, first_three, last_three):
    result = np.zeros((last - first + 1, last_three - first_three + 1))
    for m in range(first, last + 1):
        for offset, factor in (
            (0, 1.0),
            (1, (1.0 - points_three[1]) / 2.0),
            (2, (1.0 - points_three[2]) / 2.0),
            (-2, (1.0 + points_three[1]) / 2.0),
            (-1, (1.0 + points_three[2]) / 2.0),
        ):
            node = 3 * m + offset - first_three
            if 0 <= node < result.shape[1]:
                result[m - first, node] = factor
    return result


def patch_constants(s):
    line_x = line_tables(s.x_elems)
    stiff_z, lumped_z = assemble_line(s.z_elems)
    stiff_z, lumped_z = (stiff_z[: s.z_nodes, : s.z_nodes], lumped_z[: s.z_nodes])
    weight_z = np.where(np.arange(s.z_nodes) % 7 == 0, 1.0, 0.5)
    restrict_z = restriction_line(s.z_elems, points_three)[: s.coarse_z, : s.z_nodes]
    eigvals, eigbasis = patch_basis()
    square = (s.rows, s.rows)
    mass_z = np.zeros(s.lanes)
    mass_z[: s.z_nodes] = lumped_z
    mass_x = np.zeros(s.rows)
    mass_x[2 : s.x_nodes + 8] = line_x["mass"]
    spread = np.ones((s.rows, s.lanes))
    fwd_x = placed(
        patch_matrix(eigbasis, s.x_elems, s.x_nodes + 6), (s.modes_x, s.rows), col=2
    )
    fwd_z = patch_matrix(eigbasis, s.z_elems, s.z_nodes + 6)[:, 6:]
    vertex_z = np.arange(13 * s.z_elems) % s.z_elems
    fwd_z = np.where((vertex_z >= 1)[:, None], fwd_z, 0.0)
    inverse = 1.0 / (eigvals[:, None, None] + eigvals[None, :, None] + eigvals[None, None, :])
    factor = np.zeros((13, s.modes_x, s.modes_z), np.float32)
    factor[:, : 13 * s.x_elems, : 13 * s.z_elems] = np.repeat(
        np.repeat(inverse, s.x_elems, 1), s.z_elems, 2
    )
    coarse_of_z = np.zeros((s.lanes, 2 * s.coarse_lanes), np.float32)
    coarse_of_z[: s.z_nodes, : s.coarse_z] = (restrict_z * (lumped_z * weight_z)[None, :]).T
    coarse_of_z[: s.z_nodes, s.coarse_lanes : s.coarse_lanes + s.coarse_z] = (
        restrict_z @ (stiff_z * weight_z[None, :])
    ).T
    coarse_of_x = np.zeros((2 * s.coarse_rows, s.rows), np.float32)
    coarse_of_x[: s.coarse_x, 2 : s.x_nodes + 8] = line_x["mass_part"]
    coarse_of_x[s.coarse_rows : s.coarse_rows + s.coarse_x, 2 : s.x_nodes + 8] = line_x[
        "stiff_part"
    ]
    own_x = placed(line_x["own"], (s.coarse_rows, s.rows), col=8)
    own_z = placed(restrict_z.T, (s.lanes, s.coarse_lanes))
    one_z = placed(
        linear_from_cubic(0, s.z_elems - 1, 0, s.coarse_z - 1).T, (s.coarse_lanes, LANES)
    )
    one_x = placed(
        linear_from_cubic(-1, s.x_elems, -3, 3 * s.x_elems), (8, s.coarse_rows)
    )
    return [
        placed(line_x["stiff"], square, row=2, col=1),
        placed(stiff_z, (s.lanes, s.lanes)),
        spread * mass_x[:, None],
        spread * mass_z[None, :],
        mass_x[:, None] * mass_z[None, :],
        fwd_x,
        fwd_x.T,
        placed(fwd_z.T, (s.lanes, s.modes_z)),
        placed(fwd_z, (s.modes_z, s.lanes)),
        factor,
        coarse_of_z,
        coarse_of_x,
        own_z,
        own_x,
        one_z,
        one_x,
    ]


def line_of_planes(coefficients, planes):
    total = None
    for coefficient, plane in zip(coefficients, planes):
        if coefficient != 0.0:
            part = plane() * float(coefficient)
            total = part if total is None else total + part
    return total


def patch_kernel(s):
    rows, lanes, nz = (s.rows, s.lanes, s.z_nodes)
    ey, ny = (s.y_elems, s.y_nodes)
    line_y = line_tables(ey)
    _, eigbasis = patch_basis()
    stiffness = element_stiffness()
    mass_y = line_y["mass"]
    one_y = linear_from_cubic(-1, ey, -3, 3 * ey)

    def kernel(
        guess, load, below, above,
        k_x, k_z, m_x, m_z, m_xz, w_x, w_xt, w_z, w_zt, factor, q_z, q_x, r_z, r_x, o_z, o_x,
        edge_out, own_out, three_out, one_out, down_out, up_out,
        u, r, xf, xb, c, cz, rz, hx, ex, rx,
    ):
        gx = lax.axis_index("gx")
        gy = lax.axis_index("gy")
        lane = lax.broadcasted_iota(jnp.int32, (rows, lanes), 1)
        row = lax.broadcasted_iota(jnp.int32, (rows, lanes), 0)
        live = ((lane >= 1) & (lane < nz) & ((row != 8) | (gx > 0))).astype(f32)
        live_y = (gy > 0).astype(f32)
        for j in range(7):
            u[j] = below[:, nz * j : nz * j + lanes] * live
        for j in range(ny):
            mask = live if j else live * live_y
            u[7 + j] = guess[:, nz * j : nz * j + lanes] * mask
        u[ny + 7] = above[...] * live
        inside = ((lane < nz)).astype(f32)
        for j in range(6):
            r[j] = below[:, nz * (7 + j) : nz * (7 + j) + lanes] * inside
        for j in range(ny):
            r[6 + j] = load[:, nz * j : nz * j + lanes] * inside
        r[ny + 6] = jnp.zeros((rows, lanes), f32)

        def direct(chunk, carry):
            base = chunk * 7
            planes = u[pl.ds(base + 1, 7)]
            z_term = mm(planes.reshape(7 * rows, lanes), k_z[...]).reshape(7, rows, lanes)
            for i in range(7):
                x_term = mm(k_x[...], planes[i])
                both = x_term * m_z[...] + z_term[i] * m_x[...]
                r[base + i] = r[base + i] - float(mass_y[i]) * both
            return carry

        lax.fori_loop(0, ey + 1, direct, 0)

        def along_y(tile, carry):
            at = pl.ds(pl.multiple_of(tile * 8, 8), 8)
            scale = m_xz[at, :]
            corner = None
            for e in range(ey + 1):
                nodes = [u[7 * e + i, at, :] for i in range(8)]
                plus = [nodes[i] + nodes[7 - i] for i in range(4)]
                minus = [nodes[i] - nodes[7 - i] for i in range(4)]
                out = [None] * 8
                for i in range(4):
                    even = sum(
                        plus[k] * float(0.5 * (stiffness[i, k] + stiffness[i, 7 - k]))
                        for k in range(4)
                    )
                    odd = sum(
                        minus[k] * float(0.5 * (stiffness[i, k] - stiffness[i, 7 - k]))
                        for k in range(4)
                    )
                    out[i], out[7 - i] = (even + odd, even - odd)
                if e:
                    out[0] = out[0] + corner
                corner = out[7]
                for i in range(0 if e else 1, 7):
                    plane = 7 * e + i - 1
                    r[plane, at, :] = r[plane, at, :] - out[i] * scale
            active = (gy > 0).astype(f32)
            for v in range(ey):
                first = [r[7 * v + a, at, :] for a in range(13)]
                if v == 0:
                    first = [value * active for value in first]
                even = [first[6]] + [first[6 + a] + first[6 - a] for a in range(1, 7)]
                odd = [first[6 + a] - first[6 - a] for a in range(1, 7)]
                for b in range(13):
                    if symmetric(eigbasis[:, b]):
                        xf[b, v, at, :] = sum(
                            even[a] * float(eigbasis[6 + a, b]) for a in range(7)
                        )
                    else:
                        xf[b, v, at, :] = sum(
                            odd[a] * float(eigbasis[7 + a, b]) for a in range(6)
                        )
            return carry

        lax.fori_loop(0, rows // 8, along_y, 0)
        mode = lax.broadcasted_iota(jnp.int32, (s.modes_x, rows), 0)
        forward_x = w_x[...] * ((mode % s.x_elems != 0) | (gx > 0)).astype(f32)

        def spectral(b, carry):
            parts = [mm(forward_x, xf[b, v]) for v in range(ey)]
            modes = mm(jnp.concatenate(parts, 0), w_z[...])
            scaled = modes.reshape(ey, s.modes_x, s.modes_z) * factor[b][None]
            back = mm(scaled.reshape(ey * s.modes_x, s.modes_z), w_zt[...])
            for v in range(ey):
                xb[b, v] = mm(w_xt[...], back[v * s.modes_x : (v + 1) * s.modes_x])
            return carry

        lax.fori_loop(0, 13, spectral, 0)

        def back_y(tile, carry):
            at = pl.ds(pl.multiple_of(tile * 8, 8), 8)
            tail = None
            for v in range(ey):
                modes = [xb[b, v, at, :] for b in range(13)]
                out = [None] * 13
                for a in range(7):
                    even = sum(
                        modes[b] * float(eigbasis[6 + a, b])
                        for b in range(13)
                        if symmetric(eigbasis[:, b])
                    )
                    if a == 0:
                        out[6] = even
                        continue
                    odd = sum(
                        modes[b] * float(eigbasis[6 + a, b])
                        for b in range(13)
                        if not symmetric(eigbasis[:, b])
                    )
                    out[6 + a], out[6 - a] = (even + odd, even - odd)
                if v:
                    out[:6] = [value + other for value, other in zip(out[:6], tail)]
                tail = out[7:]
                for a in range(13 if v == ey - 1 else 7):
                    c[7 * v + a, at, :] = out[a]
            return carry

        lax.fori_loop(0, rows // 8, back_y, 0)

        for j in range(6):
            down_out[:, lanes * j : lanes * (j + 1)] = c[j]
        edge_out[...] = c[6:, 0:8, :]
        own_out[...] = c[6:, 8:, :]

        half = s.coarse_lanes
        rows_c = s.coarse_rows
        cz[...] = mm(c[...].reshape((ny + 6) * rows, lanes), q_z[...]).reshape(
            ny + 6, rows, 2 * half
        )
        rz[...] = mm(r[6 : ny + 6].reshape(ny * rows, lanes), r_z[...]).reshape(ny, rows, half)
        for y in range(ny + 6):
            plane = mm(q_x[...], cz[y])
            hx[y] = plane[:rows_c, :half]
            ex[y] = plane[rows_c:, :half] + plane[:rows_c, half:]
        for y in range(ny):
            rx[y] = mm(r_x[...], rz[y])
        for j in range(s.coarse_y):
            total = line_of_planes(
                np.concatenate(
                    [line_y["own"][j], -line_y["stiff_part"][j], -line_y["mass_part"][j]]
                ),
                [lambda y=y: rx[y] for y in range(ny)]
                + [lambda y=y: hx[y] for y in range(ny + 6)]
                + [lambda y=y: ex[y] for y in range(ny + 6)],
            )
            three_out[j] = total
        one_all = mm(
            three_out[...].reshape(s.coarse_y * rows_c, half), o_z[...]
        ).reshape(s.coarse_y, rows_c, LANES)
        for m in range(ey + 2):
            mixed = line_of_planes(
                one_y[m], [lambda j=j: one_all[j] for j in range(s.coarse_y)]
            )
            one_out[m] = mm(o_x[...], mixed)
        base = 6 * lanes
        for j in range(4):
            at = base + half * j
            if j < 3:
                down_out[0:rows_c, at : at + half] = three_out[j]
            else:
                down_out[0:rows_c, at : at + half] = jnp.zeros((rows_c, half), f32)
            down_out[rows_c : rows_c + 8, at : at + LANES] = one_out[j]
            down_out[rows_c + 8 :, at : at + half] = jnp.zeros((rows - rows_c - 8, half), f32)
            up_at = half * j
            if j == 0:
                up_out[0:rows_c, up_at : up_at + half] = three_out[s.coarse_y - 1]
            else:
                up_out[0:rows_c, up_at : up_at + half] = jnp.zeros((rows_c, half), f32)
            up_out[rows_c : rows_c + 8, up_at : up_at + LANES] = one_out[ey - 2 + j]

    return kernel


def symmetric(vector):
    return abs(vector[0] - vector[-1]) < abs(vector[0] + vector[-1])


def join_kernel(s):
    lanes, half, rows_c = (s.lanes, s.coarse_lanes, s.coarse_rows)
    ey, ny = (s.y_elems, s.y_nodes)

    def kernel(edge, three, one, down, up, down_out, up_out, three_out, one_out):
        for y in range(ny):
            plane = edge[y]
            if y >= ny - 6:
                j = y - (ny - 6)
                plane = plane + down[0:8, lanes * j : lanes * (j + 1)]
            down_out[:, lanes * y : lanes * (y + 1)] = plane
        base = 6 * lanes
        tiles = ny * lanes
        for j in range(max(3 * ey, ey + 6)):
            at = tiles + half * j
            down_out[:, at : at + half] = jnp.zeros((8, half), f32)
            up_out[:, half * j : half * (j + 1)] = jnp.zeros((8, half), f32)
        for j in range(3 * ey):
            plane = three[3 + j]
            if j >= 3 * ey - 3:
                k = j - (3 * ey - 3)
                plane = plane + down[0:rows_c, base + half * k : base + half * (k + 1)]
            if j == 0:
                plane = plane + up[0:rows_c, 0:half]
            three_out[j] = plane
            at = tiles + half * j
            down_out[0:3, at : at + half] = plane[0:3]
            up_out[0:1, half * j : half * (j + 1)] = plane[s.coarse_x - 1 : s.coarse_x]
        for j in range(ey + 6):
            y = j - 3
            plane = None
            if -1 <= y <= ey:
                plane = one[y + 1]
            if y <= 0:
                k = y + 3
                part = up[rows_c : rows_c + 8, half * k : half * k + LANES]
                plane = part if plane is None else plane + part
            if y >= ey - 1:
                k = y - (ey - 1)
                at = base + half * k
                part = down[rows_c : rows_c + 8, at : at + LANES]
                plane = part if plane is None else plane + part
            one_out[j] = plane
            at = tiles + half * j
            down_out[4:8, at : at + LANES] = plane[0:4]
            up_out[4:8, half * j : half * j + LANES] = plane[s.x_elems - 2 : s.x_elems + 2]

    return kernel


def finish_kernel(s, x_total, y_total):
    lanes, half, rows_c, nz = (s.lanes, s.coarse_lanes, s.coarse_rows, s.z_nodes)
    ex, ey, nx, ny = (s.x_elems, s.y_elems, s.x_nodes, s.y_nodes)
    one_rows = up_to(ex + 6, 8)

    def kernel(
        guess, weight, own, down, right, left, three, one,
        smooth_out, three_out, coarse_out, corr, fine, level,
    ):
        gx = lax.axis_index("gx")
        gy = lax.axis_index("gy")
        lane = lax.broadcasted_iota(jnp.int32, (nx, nz), 1)
        row = lax.broadcasted_iota(jnp.int32, (nx, nz), 0)
        live = ((lane >= 1) & ((row >= 1) | (gx > 0))).astype(f32)
        live_y = (gy > 0).astype(f32)
        for y in range(ny):
            corr[...] = own[y]
            if y >= ny - 6:
                j = y - (ny - 6)
                corr[...] += down[8:, lanes * j : lanes * (j + 1)]
            corr[nx - 6 : nx, :] += right[2:8, lanes * y : lanes * (y + 1)]
            mask = live if y else live * live_y
            factor = weight[...] * (1.0 if y % 7 == 0 else 0.5)
            smooth_out[:, nz * y : nz * (y + 1)] = (
                guess[:, nz * y : nz * (y + 1)] + factor * corr[0:nx, 0:nz]
            ) * mask
        tiles = ny * lanes
        nzc = s.coarse_z
        lane = lax.broadcasted_iota(jnp.int32, (3 * ex, nzc), 1)
        row = lax.broadcasted_iota(jnp.int32, (3 * ex, nzc), 0)
        live = ((lane >= 1) & ((row >= 1) | (gx > 0))).astype(f32)
        for j in range(3 * ey):
            fine[...] = three[j]
            at = tiles + half * j
            fine[3 * ex : 3 * ex + 3, :] += right[0:3, at : at + half]
            fine[3:4, :] += left[0:1, half * j : half * (j + 1)]
            mask = live if j else live * live_y
            three_out[:, nzc * j : nzc * (j + 1)] = fine[3 : 3 * ex + 3, 0:nzc] * mask
        level[...] = jnp.zeros((ey + 6, one_rows, LANES), f32)
        for j in range(ey + 6):
            level[j, 2 : ex + 4, :] = one[j, 0 : ex + 2, :]
            at = tiles + half * j
            level[j, 0:4, :] += left[4:8, half * j : half * j + LANES]
            level[j, ex + 2 : ex + 6, :] += right[4:8, at : at + LANES]
        shape = (one_rows, LANES)
        lane = lax.broadcasted_iota(jnp.int32, shape, 1)
        row = lax.broadcasted_iota(jnp.int32, shape, 0)
        global_x = gx * ex + row - 3
        plane_mask = (
            (lane >= 1) & (lane < s.z_elems) & (row < ex + 6)
            & (global_x >= 1) & (global_x < x_total)
        )
        masks = []
        for j in range(ey + 6):
            global_y = gy * ey + (j - 3)
            inside = (global_y >= 1) & (global_y < y_total)
            masks.append((plane_mask & inside).astype(f32))
        levels = [level[j] for j in range(ey + 6)]
        error = [damping / 12.0 * a * m for a, m in zip(levels, masks)]
        zero = jnp.zeros(shape, f32)
        for sweep in range(1, JAC):
            lower = [zero] + error[:-1]
            upper = error[1:] + [zero]
            fresh = []
            for j in range(ey + 6):
                here = error[j]
                neighbours = (
                    lower[j]
                    + upper[j]
                    + pltpu.roll(here, 1, 0)
                    + pltpu.roll(here, one_rows - 1, 0)
                    + pltpu.roll(here, 1, 1)
                    + pltpu.roll(here, LANES - 1, 1)
                )
                applied = 12.0 * here - 2.0 * neighbours
                fresh.append((here + damping / 12.0 * (levels[j] - applied)) * masks[j])
            error = fresh
        nze = s.z_elems
        for j in range(ey):
            coarse_out[:, nze * j : nze * (j + 1)] = error[3 + j][3 : 3 + ex, 0:nze]

    return kernel


def local(load_vector, initial_guess):
    z_nodes = 7 * EZ
    x_nodes = load_vector.shape[0]
    y_nodes = load_vector.shape[1] // z_nodes
    s = Sizes(x_nodes, y_nodes, z_nodes)
    rows, lanes, half = (s.rows, s.lanes, s.coarse_lanes)
    ny, ey = (s.y_nodes, s.y_elems)
    width = y_nodes * z_nodes
    sent_up = jnp.concatenate([initial_guess[x_nodes - 7 :], load_vector[x_nodes - 6 :]], 0)
    from_below = shifted(sent_up, "gx", 1)
    from_above = shifted(initial_guess[:1], "gx", -1)
    tail = up_to((ny - 1) * z_nodes + lanes, LANES) - width

    def framed(pieces, first):
        used = first + sum(piece.shape[0] for piece in pieces)
        parts = (
            [jnp.zeros((first, width), f32)] + pieces + [jnp.zeros((rows - used, width), f32)]
        )
        return jnp.pad(jnp.concatenate(parts, 0), ((0, 0), (0, tail)))

    guess_ext = framed([from_below[:7], initial_guess, from_above], 1)
    load_ext = framed([from_below[7:], load_vector], 2)
    message = jnp.concatenate(
        [guess_ext[:, (ny - 7) * z_nodes : width], load_ext[:, (ny - 6) * z_nodes : width]], 1
    )
    message = jnp.pad(message, ((0, 0), (0, up_to(12 * z_nodes + lanes, LANES) - 13 * z_nodes)))
    y_below = shifted(message, "gy", 1)
    y_above = shifted(guess_ext[:, :lanes], "gy", -1)
    constants = [jnp.asarray(value, f32) for value in patch_constants(s)]
    shape = lambda *dims: jax.ShapeDtypeStruct(dims, f32)
    params = pltpu.CompilerParams(vmem_limit_bytes=36 * 2**20)
    vmem = lambda count: [pl.BlockSpec(memory_space=pltpu.VMEM)] * count
    edge, own, three, one, down, up = pl.pallas_call(
        patch_kernel(s),
        out_shape=(
            shape(ny, 8, lanes),
            shape(ny, rows - 8, lanes),
            shape(s.coarse_y, s.coarse_rows, half),
            shape(ey + 2, 8, LANES),
            shape(rows, 6 * lanes + 4 * half),
            shape(s.coarse_rows + 8, 4 * half),
        ),
        in_specs=vmem(4 + len(constants)),
        out_specs=tuple(vmem(6)),
        scratch_shapes=[
            pltpu.VMEM((ny + 8, rows, lanes), f32),
            pltpu.VMEM((ny + 7, rows, lanes), f32),
            pltpu.VMEM((13, ey, rows, lanes), f32),
            pltpu.VMEM((13, ey, rows, lanes), f32),
            pltpu.VMEM((ny + 6, rows, lanes), f32),
            pltpu.VMEM((ny + 6, rows, 2 * half), f32),
            pltpu.VMEM((ny, rows, half), f32),
            pltpu.VMEM((ny + 6, s.coarse_rows, half), f32),
            pltpu.VMEM((ny + 6, s.coarse_rows, half), f32),
            pltpu.VMEM((ny, s.coarse_rows, half), f32),
        ],
        compiler_params=params,
        name="patches",
    )(guess_ext, load_ext, y_below, y_above, *constants)
    down = shifted(down, "gy", -1)
    up = shifted(up, "gy", 1)
    tiles = max(3 * ey, ey + 6)
    right, left, three, one = pl.pallas_call(
        join_kernel(s),
        out_shape=(
            shape(8, ny * lanes + tiles * half),
            shape(8, tiles * half),
            shape(3 * ey, s.coarse_rows, half),
            shape(ey + 6, 8, LANES),
        ),
        in_specs=vmem(5),
        out_specs=tuple(vmem(4)),
        compiler_params=params,
        name="join",
    )(edge, three, one, down, up)
    right = shifted(right, "gx", -1)
    left = shifted(left, "gx", 1)
    weight = np.where(np.arange(x_nodes) % 7 == 0, 1.0, 0.5)[:, None] * np.where(
        np.arange(z_nodes) % 7 == 0, 1.0, 0.5
    )
    return pl.pallas_call(
        finish_kernel(
            s, s.x_elems * lax.axis_size("gx"), ey * lax.axis_size("gy")
        ),
        out_shape=(
            shape(x_nodes, width),
            shape(3 * s.x_elems, 3 * ey * s.coarse_z),
            shape(s.x_elems, ey * s.z_elems),
        ),
        in_specs=vmem(8),
        out_specs=tuple(vmem(3)),
        scratch_shapes=[
            pltpu.VMEM((rows - 8, lanes), f32),
            pltpu.VMEM((s.coarse_rows, half), f32),
            pltpu.VMEM((ey + 6, up_to(s.x_elems + 6, 8), LANES), f32),
        ],
        compiler_params=params,
        name="finish",
    )(initial_guess, jnp.asarray(weight, f32), own, down, right, left, three, one)


def solution(mesh):
    in_specs = (P("gx", "gy"), P("gx", "gy"))
    out_specs = (P("gx", "gy"), P("gx", "gy"), P("gx", "gy"))
    return jax.shard_map(local, mesh=mesh, in_specs=in_specs, out_specs=out_specs, check_vma=False)
```

```python
import math

import jax
import jax.numpy as jnp
import numpy as np
from jax import lax
from jax.experimental import pallas as pl
from jax.experimental.pallas import tpu as pltpu
from jax.sharding import PartitionSpec as P

EZ = 32
JAC = 4


points_seven = (
    -1.0,
    -0.8717401485096066,
    -0.5917001814331423,
    -0.2092992179024789,
    0.2092992179024789,
    0.5917001814331423,
    0.8717401485096066,
    1.0,
)
points_three = (-1.0, -0.4472135954999579, 0.4472135954999579, 1.0)
points_one = (-1.0, 1.0)
damping = 2.0 / 3.0


def shifted(array, axis, by):
    devices = lax.axis_size(axis)
    pairs = [(i, i + by) for i in range(devices) if 0 <= i + by < devices]
    return lax.ppermute(array, axis, pairs)


def legendre_at(degree, location):
    previous, current = (1.0, location)
    for level_idx in range(1, degree):
        previous, current = (
            current,
            ((2 * level_idx + 1) * location * current - level_idx * previous) / (level_idx + 1),
        )
    return current


def quadrature_weights():
    return np.array([2.0 / (56.0 * legendre_at(7, x) * legendre_at(7, x)) for x in points_seven])


def derivative_matrix():
    points = np.array(points_seven)
    products = np.array(
        [np.prod([points[i] - points[k] for k in range(8) if k != i]) for i in range(8)]
    )
    result = np.zeros((8, 8))
    for i in range(8):
        for j in range(8):
            if i != j:
                result[i, j] = products[i] / (products[j] * (points[i] - points[j]))
        result[i, i] = np.sum([1.0 / (points[i] - points[k]) for k in range(8) if k != i])
    return result


def element_stiffness():
    derivative = derivative_matrix()
    return derivative.T @ (quadrature_weights()[:, None] * derivative)


def assemble_line(elements):
    stiffness = element_stiffness()
    weights = quadrature_weights()
    extent = 7 * elements + 1
    global_stiff = np.zeros((extent, extent))
    lumped = np.zeros(extent)
    for m in range(elements):
        global_stiff[7 * m : 7 * m + 8, 7 * m : 7 * m + 8] += stiffness
        lumped[7 * m : 7 * m + 8] += weights
    return (global_stiff, lumped)


def jacobi_eigen(matrix):
    rotated_mat = matrix.copy()
    extent = matrix.shape[0]
    vectors = np.eye(extent)
    for sweep_idx in range(12):
        for p in range(extent - 1):
            for q in range(p + 1, extent):
                angle_rot = 0.5 * math.atan2(
                    2.0 * float(rotated_mat[p, q]), float(rotated_mat[q, q] - rotated_mat[p, p])
                )
                rotation = np.eye(extent)
                rotation[p, p] = math.cos(angle_rot)
                rotation[q, q] = math.cos(angle_rot)
                rotation[p, q] = math.sin(angle_rot)
                rotation[q, p] = -math.sin(angle_rot)
                rotated_mat = rotation.T @ rotated_mat @ rotation
                vectors = vectors @ rotation
    return (np.array([rotated_mat[i, i] for i in range(extent)]), vectors)


def patch_basis():
    global_stiff, lumped = assemble_line(2)
    inv_root = 1.0 / np.sqrt(lumped[1:14])
    eigvals, vectors = jacobi_eigen(
        inv_root[:, None] * global_stiff[1:14, 1:14] * inv_root[None, :]
    )
    return (eigvals, inv_root[:, None] * vectors)


def interp_matrix(coarse_pts):
    result = np.ones((8, len(coarse_pts)))
    for a in range(8):
        for c in range(len(coarse_pts)):
            for k in range(len(coarse_pts)):
                if k != c:
                    result[a, c] *= (points_seven[a] - coarse_pts[k]) / (
                        coarse_pts[c] - coarse_pts[k]
                    )
    return result


def restriction_rows(coarse_pts):
    shared = np.ones(8)
    shared[0] = 0.5
    shared[7] = 0.5
    return (interp_matrix(coarse_pts) * shared[:, None]).T


def restriction_line(elements, coarse_pts):
    degree = len(coarse_pts) - 1
    rows_mat = restriction_rows(coarse_pts)
    result = np.zeros((degree * elements + 1, 7 * elements + 1))
    for m in range(elements):
        result[degree * m : degree * m + degree + 1, 7 * m : 7 * m + 8] += rows_mat
    return result


def patch_matrix(eigbasis, vertices, extent):
    result = np.zeros((13 * vertices, extent))
    for b in range(13):
        for v in range(vertices):
            for a in range(13):
                node_idx = 7 * v + a
                result[b * vertices + v, node_idx] = eigbasis[a, b]
    return result


high = lax.Precision.HIGH
LANES = 128
f32 = jnp.float32


def up_to(length, multiple):
    return -(-length // multiple) * multiple


def placed(matrix, shape, row=0, col=0):
    result = np.zeros(shape, np.float32)
    result[row : row + matrix.shape[0], col : col + matrix.shape[1]] = matrix
    return result


def mm(left, right):
    return lax.dot_general(
        left, right, (((1,), (0,)), ((), ())), precision=high, preferred_element_type=f32
    )


class Sizes:
    def __init__(self, x_nodes, y_nodes, z_nodes):
        self.x_nodes, self.y_nodes, self.z_nodes = (x_nodes, y_nodes, z_nodes)
        self.x_elems, self.y_elems, self.z_elems = (x_nodes // 7, y_nodes // 7, z_nodes // 7)
        self.own_rows = up_to(x_nodes + 1, 8)
        self.rows = up_to(x_nodes + 8, 8)
        self.half_z = self.z_elems // 2
        self.lanes = 2 * LANES
        self.modes_x = up_to(13 * self.x_elems, 8)
        self.modes_z = up_to(13 * self.half_z, LANES)
        self.coarse_x = 3 * self.x_elems + 4
        self.coarse_y = 3 * self.y_elems + 4
        self.coarse_z = 3 * self.z_elems
        self.coarse_rows = up_to(self.coarse_x, 8)
        self.coarse_lanes = up_to(self.coarse_z, LANES)
        split = 7 * self.half_z
        self.split = split
        self.node_of_lane = np.full(self.lanes, -1)
        self.node_of_lane[6 : 6 + split] = np.arange(split)
        self.node_of_lane[LANES : LANES + split + 6] = np.arange(split - 6, 2 * split)
        self.first_copy = self.node_of_lane >= 0
        self.first_copy[LANES : LANES + 6] = False


def line_tables(elements):
    nodes = 7 * elements
    stiff, lumped = assemble_line(elements + 2)
    restrict = restriction_line(elements + 3, points_three)[3 : 3 * elements + 7, 7 : nodes + 15]
    columns = np.arange(-6, nodes)
    weight = np.where(columns % 7 == 0, 1.0, 0.5)
    mass_part = restrict[:, 1:-1] * (lumped[1 : nodes + 7] * weight)[None, :]
    stiff_part = restrict @ (stiff[: nodes + 8, 1 : nodes + 7] * weight[None, :])
    return dict(
        own_stiff=stiff[7 : nodes + 8, 7 : nodes + 7],
        mass=lumped[1 : nodes + 7],
        own=restrict[:, 7:-1],
        mass_part=mass_part,
        stiff_part=stiff_part,
    )


def rows_by_node(s, matrix, every_copy):
    used = s.node_of_lane >= 0 if every_copy else s.first_copy
    return np.where(used[:, None], matrix[np.maximum(s.node_of_lane, 0)], 0.0)


def two_parts(matrix):
    high_part = matrix.astype(np.float32).astype(jnp.bfloat16)
    low_part = (matrix - high_part.astype(np.float64)).astype(jnp.bfloat16)
    return high_part, low_part


def residual_constants(s):
    line_x = line_tables(s.x_elems)
    stiff_z, lumped_z = assemble_line(s.z_elems)
    stiff_z, lumped_z = (stiff_z[: s.z_nodes, : s.z_nodes], lumped_z[: s.z_nodes])
    mass_x = np.zeros(s.own_rows)
    mass_x[: s.x_nodes] = line_x["mass"][6:]
    mass_z = rows_by_node(s, lumped_z[:, None], True)[:, 0]
    spread = np.ones((s.own_rows, s.lanes))
    stiff = rows_by_node(s, stiff_z, False)
    stiff = rows_by_node(s, stiff.T, True).T
    wide = placed(line_x["own_stiff"], (s.own_rows, s.lanes))
    return np.concatenate(
        [
            stiff,
            spread * mass_x[:, None],
            spread * mass_z[None, :],
            mass_x[:, None] * mass_z[None, :],
            wide,
        ]
    )


def coupling_constants(s):
    stiffness = element_stiffness()
    lumped_z = assemble_line(s.z_elems)[1][: s.z_nodes]
    mass_z = rows_by_node(s, lumped_z[:, None], True)[:, 0]
    below, above = (np.zeros(s.rows), np.zeros(s.rows))
    below[2:8] = stiffness[1:7, 7]
    above[8 + s.x_nodes - 7 : 8 + s.x_nodes] = stiffness[:7, 7]
    return [below[:, None] * mass_z[None, :], above[:, None] * mass_z[None, :]]


def patch_constants(s):
    line_x = line_tables(s.x_elems)
    stiff_z, lumped_z = assemble_line(s.z_elems)
    stiff_z, lumped_z = (stiff_z[: s.z_nodes, : s.z_nodes], lumped_z[: s.z_nodes])
    weight_z = np.where(np.arange(s.z_nodes) % 7 == 0, 1.0, 0.5)
    restrict_z = restriction_line(s.z_elems, points_three)[: s.coarse_z, : s.z_nodes]
    eigvals, eigbasis = patch_basis()
    mass_z = rows_by_node(s, lumped_z[:, None], True)[:, 0]
    mass_x = np.zeros(s.rows)
    mass_x[2 : s.x_nodes + 8] = line_x["mass"]
    fwd_x = placed(
        patch_matrix(eigbasis, s.x_elems, s.x_nodes + 6), (s.modes_x, s.rows), col=2
    )
    high_x, low_x = two_parts(fwd_x.astype(np.float64))
    fwd_z = np.zeros((LANES, s.modes_z))
    fwd_z[:, : 13 * s.half_z] = patch_matrix(eigbasis, s.half_z, LANES).T
    high_z, low_z = two_parts(fwd_z)
    sums = np.ones((s.modes_x, s.modes_z))
    sums[: 13 * s.x_elems, : 13 * s.half_z] = (
        np.repeat(eigvals, s.x_elems)[:, None] + np.repeat(eigvals, s.half_z)[None, :]
    )
    coarse_of_z = np.zeros((s.z_nodes, 2 * s.coarse_lanes))
    coarse_of_z[:, : s.coarse_z] = (restrict_z * (lumped_z * weight_z)[None, :]).T
    coarse_of_z[:, s.coarse_lanes : s.coarse_lanes + s.coarse_z] = (
        restrict_z @ (stiff_z * weight_z[None, :])
    ).T
    coarse_of_x = np.zeros((2 * s.coarse_rows, s.rows))
    coarse_of_x[: s.coarse_x, 2 : s.x_nodes + 8] = line_x["mass_part"]
    coarse_of_x[s.coarse_rows : s.coarse_rows + s.coarse_x, 2 : s.x_nodes + 8] = line_x[
        "stiff_part"
    ]
    own_z = np.zeros((s.z_nodes, s.coarse_lanes))
    own_z[:, : s.coarse_z] = restrict_z.T
    one_z = placed(
        linear_from_cubic(0, s.z_elems - 1, 0, s.coarse_z - 1).T, (s.coarse_lanes, LANES)
    )
    one_x = placed(linear_from_cubic(-1, s.x_elems, -3, 3 * s.x_elems), (8, s.coarse_rows))
    singles = [
        mass_x[:, None] * mass_z[None, :],
        sums,
        rows_by_node(s, coarse_of_z, True),
        coarse_of_x,
        rows_by_node(s, own_z, False),
        placed(line_x["own"], (s.coarse_rows, s.rows), col=8),
        one_z,
        one_x,
    ]
    halves = [
        np.concatenate([high_x, high_x, low_x], 1),
        np.concatenate([high_x.T, high_x.T, low_x.T], 1),
        np.concatenate([high_z, high_z], 0),
        low_z,
        np.concatenate([high_z.T, low_z.T], 1),
        high_z.T,
    ]
    return (
        [jnp.asarray(eigvals, f32)]
        + [jnp.asarray(value, f32) for value in singles]
        + [jnp.asarray(value, jnp.bfloat16) for value in halves]
    )


def halves_of(value):
    high_part = value.astype(jnp.bfloat16)
    return high_part, (value - high_part.astype(f32)).astype(jnp.bfloat16)


def stacked_rows(value):
    high_part = value.astype(jnp.bfloat16).astype(f32)
    return jnp.concatenate([high_part, value - high_part, high_part], 0).astype(jnp.bfloat16)


def dot(left, right):
    return lax.dot_general(left, right, (((1,), (0,)), ((), ())), preferred_element_type=f32)


def linear_from_cubic(first, last, first_three, last_three):
    result = np.zeros((last - first + 1, last_three - first_three + 1))
    for m in range(first, last + 1):
        for offset, factor in (
            (0, 1.0),
            (1, (1.0 - points_three[1]) / 2.0),
            (2, (1.0 - points_three[2]) / 2.0),
            (-2, (1.0 + points_three[1]) / 2.0),
            (-1, (1.0 + points_three[2]) / 2.0),
        ):
            node = 3 * m + offset - first_three
            if 0 <= node < result.shape[1]:
                result[m - first, node] = factor
    return result


def line_of_planes(coefficients, planes):
    total = None
    for coefficient, plane in zip(coefficients, planes):
        if coefficient != 0.0:
            part = plane() * float(coefficient)
            total = part if total is None else total + part
    return total


def symmetric(vector):
    return abs(vector[0] - vector[-1]) < abs(vector[0] + vector[-1])


def lane_window(ref, start, width):
    if start < 0:
        return pltpu.roll(ref[:, 0:LANES], -start, 1)
    if start + LANES > width:
        return pltpu.roll(ref[:, width - LANES : width], width - start, 1)
    return ref[:, start : start + LANES]


def lane_mask(s, shape, first):
    lane = lax.broadcasted_iota(jnp.int32, shape, 1)
    return ((lane >= 6 + first) & (lane < 6 + s.split)) | (
        (lane >= LANES) & (lane < LANES + s.split + 6)
    )


def put_line(s, ref, index, plane):
    at = s.z_nodes * index
    rows = plane.shape[0]
    ref[0:rows, at : at + s.split] = plane[:, 6 : 6 + s.split]
    ref[0:rows, at + s.split : at + 2 * s.split] = plane[:, LANES + 6 : LANES + 6 + s.split]


def get_line(s, ref, index, width):
    at = s.z_nodes * index
    return jnp.concatenate(
        [lane_window(ref, at - 6, width), lane_window(ref, at + s.split - 6, width)], 1
    )


def residual_kernel(s):
    rows, lanes = (s.own_rows, s.lanes)
    ex, ey, nx, ny = (s.x_elems, s.y_elems, s.x_nodes, s.y_nodes)
    width = ny * s.z_nodes
    mass_y = line_tables(ey)["mass"][6:]
    stiffness = element_stiffness()

    def kernel(guess_hbm, load_hbm, table_hbm, r, edge, up_out, down_out, u, guess, load, table, sems):
        copies = [
            pltpu.make_async_copy(source, target, sems.at[index])
            for index, (source, target) in enumerate(
                [(guess_hbm, guess), (load_hbm, load), (table_hbm, table)]
            )
        ]
        for copy in copies:
            copy.start()
        k_z = table.at[0:lanes]
        m_x, m_z, m_xz, k_x_wide = [
            table.at[lanes + rows * i : lanes + rows * (i + 1)] for i in range(4)
        ]
        k_x = k_x_wide.at[:, 0:rows]
        gx = lax.axis_index("gx")
        gy = lax.axis_index("gy")
        shape = (nx, lanes)
        row = lax.broadcasted_iota(jnp.int32, shape, 0)
        live = (lane_mask(s, shape, 1) & ((row != 0) | (gx > 0))).astype(f32)
        live_y = (gy > 0).astype(f32)
        inside = lane_mask(s, shape, 0).astype(f32)
        pad = jnp.zeros((rows - nx, lanes), f32)
        copies[0].wait()
        for y in range(ny):
            mask = live if y else live * live_y
            u[y, 0:nx] = get_line(s, guess, y, width) * mask
            u[y, nx:] = pad
        copies[1].wait()
        for y in range(ny):
            r[y, 0:nx] = get_line(s, load, y, width) * inside
            r[y, nx:] = pad
        u[ny] = jnp.zeros((rows, lanes), f32)
        r[ny] = jnp.zeros((rows, lanes), f32)

        copies[2].wait()

        def direct(chunk, carry):
            base = chunk * 7
            planes = u[pl.ds(base, 7)]
            z_term = mm(planes.reshape(7 * rows, lanes), k_z[...]).reshape(7, rows, lanes)
            for i in range(7):
                x_term = mm(k_x[...], planes[i])
                both = x_term * m_z[...] + z_term[i] * m_x[...]
                r[base + i] = r[base + i] - float(mass_y[i]) * both
            return carry

        lax.fori_loop(0, ey, direct, 0)

        def along_y(tile, carry):
            at = pl.ds(pl.multiple_of(tile * 8, 8), 8)
            scale = m_xz[at, :]
            corner = None
            for e in range(ey):
                nodes = [u[7 * e + i, at, :] for i in range(8)]
                plus = [nodes[i] + nodes[7 - i] for i in range(4)]
                minus = [nodes[i] - nodes[7 - i] for i in range(4)]
                out = [None] * 8
                for i in range(4):
                    even = sum(
                        plus[k] * float(0.5 * (stiffness[i, k] + stiffness[i, 7 - k]))
                        for k in range(4)
                    )
                    odd = sum(
                        minus[k] * float(0.5 * (stiffness[i, k] - stiffness[i, 7 - k]))
                        for k in range(4)
                    )
                    out[i], out[7 - i] = (even + odd, even - odd)
                if e:
                    out[0] = out[0] + corner
                else:
                    out[0] = out[0] + nodes[0] * float(stiffness[7, 7])
                corner = out[7]
                for i in range(8 if e == ey - 1 else 7):
                    plane = 7 * e + i
                    r[plane, at, :] = r[plane, at, :] - out[i] * scale
            return carry

        lax.fori_loop(0, rows // 8, along_y, 0)
        for y in range(ny + 1):
            put_line(s, up_out, y, r[y, nx - 6 : nx + 1, :])
        up_out[7:8, :] = jnp.zeros((1, up_out.shape[1]), f32)
        put_line(s, up_out, ny + 1, u[0, nx - 6 : nx, :])
        up_out[6:7, (ny + 1) * s.z_nodes :] = jnp.zeros(
            (1, up_out.shape[1] - (ny + 1) * s.z_nodes), f32
        )
        for y in range(ny):
            down_out[y : y + 1, :] = u[y, 0:1, :]
        down_out[ny:, :] = jnp.zeros((down_out.shape[0] - ny, lanes), f32)
        edge[...] = u[0]

    return kernel


def joined_x_kernel(s):
    rows, lanes = (s.rows, s.lanes)
    nx, ny = (s.x_nodes, s.y_nodes)
    mass_y = line_tables(s.y_elems)["mass"][6:]

    def kernel(r_own, edge, u_first, below, above, c_below, c_above, r, line, up_out):
        width = below.shape[1]
        shape = (8, lanes)
        row = lax.broadcasted_iota(jnp.int32, shape, 0)
        inside = lane_mask(s, shape, 0)
        keep = (inside & (row < 6)).astype(f32)
        only = (inside & (row == 6)).astype(f32)
        zero = jnp.zeros((rows - 8 - nx, lanes), f32) if rows - 8 - nx else None
        for y in range(ny + 2):
            got = get_line(s, below, y, width)
            place = line if y == ny + 1 else r.at[y]
            own = edge[0:nx] if y == ny + 1 else r_own[y, 0:nx, :]
            place[0:2, :] = jnp.zeros((2, lanes), f32)
            place[2:8, :] = (got * keep)[0:6]
            place[8 : 8 + nx, :] = own
            if zero is not None:
                place[8 + nx :, :] = zero
            if y < ny:
                place[8:9, :] += (got * only)[6:7]
                both = (
                    c_below[...] * u_first[y : y + 1, :] + c_above[...] * above[y : y + 1, :]
                ) * float(mass_y[y])
                place[...] = place[...] - both
        for j in range(7):
            put_line(s, up_out, j, r[ny - 6 + j])
        up_out[:, 7 * s.z_nodes :] = jnp.zeros((rows, up_out.shape[1] - 7 * s.z_nodes), f32)

    return kernel


def patch_kernel(s):
    rows, lanes = (s.rows, s.lanes)
    ey, ny = (s.y_elems, s.y_nodes)
    line_y = line_tables(ey)
    _, eigbasis = patch_basis()
    stiffness = element_stiffness()
    one_y = linear_from_cubic(-1, ey, -3, 3 * ey)
    evens = [b for b in range(13) if symmetric(eigbasis[:, b])]
    odds = [b for b in range(13) if b not in evens]

    def kernel(
        r_own, line, below, above,
        lam, m_xz, sums, q_z, q_x, r_z, r_x, o_z, o_x, f_x, b_x, f_z, f_z_low, b_z, b_z_high,
        edge_out, own_out, three_out, one_out, down_out, up_out,
        r, xf, xb, c, cz, rz, hx, ex, rx, live,
    ):
        gx = lax.axis_index("gx")
        gy = lax.axis_index("gy")
        inside = lane_mask(s, (rows, lanes), 0).astype(f32)
        width = below.shape[1]
        lower = line[...] * m_xz[...]
        upper = above[...] * m_xz[...]
        for j in range(7):
            got = get_line(s, below, j, width) * inside
            if j < 6:
                r[j] = got - lower * float(stiffness[1 + j, 7])
            else:
                r[6] = r_own[0] + got
        for y in range(1, ny):
            plane = r_own[y]
            if y >= ny - 7:
                plane = plane - upper * float(stiffness[y - (ny - 7), 7])
            r[6 + y] = plane
        shape = (s.modes_x, s.modes_z)
        mode = lax.broadcasted_iota(jnp.int32, shape, 0)
        vertex = lax.broadcasted_iota(jnp.int32, shape, 1) % s.half_z
        live_x = (mode % s.x_elems != 0) | (gx > 0)
        live[0] = (live_x & (vertex != 0)).astype(f32)
        live[1] = live_x.astype(f32)
        active = (gy > 0).astype(f32)

        def along_y(tile, carry):
            at = pl.ds(pl.multiple_of(tile * 8, 8), 8)
            for v in range(ey):
                first = [r[7 * v + a, at, :] for a in range(13)]
                if v == 0:
                    first = [value * active for value in first]
                even = [first[6]] + [first[6 + a] + first[6 - a] for a in range(1, 7)]
                odd = [first[6 + a] - first[6 - a] for a in range(1, 7)]
                for b in range(13):
                    if b in evens:
                        xf[b, v, at, :] = sum(
                            even[a] * float(eigbasis[6 + a, b]) for a in range(7)
                        )
                    else:
                        xf[b, v, at, :] = sum(
                            odd[a] * float(eigbasis[7 + a, b]) for a in range(6)
                        )
            return carry

        lax.fori_loop(0, rows // 8, along_y, 0)

        def spectral(b, carry):
            planes = [dot(f_x[...], stacked_rows(xf[b, v])) for v in range(ey)]
            modes = jnp.concatenate(
                [plane[:, :LANES] for plane in planes] + [plane[:, LANES:] for plane in planes], 0
            )
            high_part, low_part = halves_of(modes)
            modes = dot(jnp.concatenate([high_part, low_part], 1), f_z[...]) + dot(
                high_part, f_z_low[...]
            )
            factor = 1.0 / (sums[...] + lam[b])
            modes = modes.reshape(2, ey, s.modes_x, s.modes_z)
            modes = jnp.concatenate(
                [
                    (modes[t] * (factor * live[t])[None]).reshape(ey * s.modes_x, s.modes_z)
                    for t in range(2)
                ],
                0,
            )
            high_part, low_part = halves_of(modes)
            both = dot(high_part, b_z[...])
            back = both[:, :LANES] + both[:, LANES:] + dot(low_part, b_z_high[...])
            for v in range(ey):
                first = v * s.modes_x
                second = (ey + v) * s.modes_x
                plane = jnp.concatenate(
                    [back[first : first + s.modes_x], back[second : second + s.modes_x]], 1
                )
                xb[b, v] = dot(b_x[...], stacked_rows(plane))
            return carry

        lax.fori_loop(0, 13, spectral, 0)

        def back_y(tile, carry):
            at = pl.ds(pl.multiple_of(tile * 8, 8), 8)
            tail = None
            for v in range(ey):
                modes = [xb[b, v, at, :] for b in range(13)]
                out = [None] * 13
                for a in range(7):
                    even = sum(modes[b] * float(eigbasis[6 + a, b]) for b in evens)
                    if a == 0:
                        out[6] = even
                        continue
                    odd = sum(modes[b] * float(eigbasis[6 + a, b]) for b in odds)
                    out[6 + a], out[6 - a] = (even + odd, even - odd)
                if v:
                    out[:6] = [value + other for value, other in zip(out[:6], tail)]
                tail = out[7:]
                for a in range(13 if v == ey - 1 else 7):
                    c[7 * v + a, at, :] = out[a]
            return carry

        lax.fori_loop(0, rows // 8, back_y, 0)

        for j in range(6):
            down_out[:, lanes * j : lanes * (j + 1)] = c[j]
        edge_out[...] = c[6:, 0:8, :]
        own_out[...] = c[6:, 8:, :]

        half = s.coarse_lanes
        rows_c = s.coarse_rows
        cz[...] = mm(c[...].reshape((ny + 6) * rows, lanes), q_z[...]).reshape(
            ny + 6, rows, 2 * half
        )
        rz[...] = mm(r[6 : ny + 6].reshape(ny * rows, lanes), r_z[...]).reshape(ny, rows, half)
        for y in range(ny + 6):
            plane = mm(q_x[...], cz[y])
            hx[y] = plane[:rows_c, :half]
            ex[y] = plane[rows_c:, :half] + plane[:rows_c, half:]
        for y in range(ny):
            rx[y] = mm(r_x[...], rz[y])
        for j in range(s.coarse_y):
            three_out[j] = line_of_planes(
                np.concatenate(
                    [line_y["own"][j], -line_y["stiff_part"][j], -line_y["mass_part"][j]]
                ),
                [lambda y=y: rx[y] for y in range(ny)]
                + [lambda y=y: hx[y] for y in range(ny + 6)]
                + [lambda y=y: ex[y] for y in range(ny + 6)],
            )
        one_all = mm(
            three_out[...].reshape(s.coarse_y * rows_c, half), o_z[...]
        ).reshape(s.coarse_y, rows_c, LANES)
        for m in range(ey + 2):
            mixed = line_of_planes(
                one_y[m], [lambda j=j: one_all[j] for j in range(s.coarse_y)]
            )
            one_out[m] = mm(o_x[...], mixed)
        base = 6 * lanes
        for j in range(4):
            at = base + half * j
            if j < 3:
                down_out[0:rows_c, at : at + half] = three_out[j]
            else:
                down_out[0:rows_c, at : at + half] = jnp.zeros((rows_c, half), f32)
            down_out[rows_c : rows_c + 8, at : at + LANES] = one_out[j]
            down_out[rows_c + 8 :, at : at + half] = jnp.zeros((rows - rows_c - 8, half), f32)
            up_at = half * j
            if j == 0:
                up_out[0:rows_c, up_at : up_at + half] = three_out[s.coarse_y - 1]
            else:
                up_out[0:rows_c, up_at : up_at + half] = jnp.zeros((rows_c, half), f32)
            up_out[rows_c : rows_c + 8, up_at : up_at + LANES] = one_out[ey - 2 + j]

    return kernel


def join_kernel(s):
    lanes, half, rows_c = (s.lanes, s.coarse_lanes, s.coarse_rows)
    ey, ny = (s.y_elems, s.y_nodes)

    def kernel(edge, three, one, down, up, down_out, up_out, three_out, one_out):
        for y in range(ny):
            plane = edge[y]
            if y >= ny - 6:
                j = y - (ny - 6)
                plane = plane + down[0:8, lanes * j : lanes * (j + 1)]
            down_out[6 * y : 6 * y + 6, :] = plane[2:8]
        base = 6 * lanes
        first = 6 * ny
        down_out[first:, :] = jnp.zeros((down_out.shape[0] - first, lanes), f32)
        up_out[...] = jnp.zeros(up_out.shape, f32)
        for j in range(3 * ey):
            plane = three[3 + j]
            if j >= 3 * ey - 3:
                k = j - (3 * ey - 3)
                plane = plane + down[0:rows_c, base + half * k : base + half * (k + 1)]
            if j == 0:
                plane = plane + up[0:rows_c, 0:half]
            three_out[j] = plane
            down_out[first + 3 * j : first + 3 * j + 3, 0:half] = plane[0:3]
            up_out[j : j + 1, 0:half] = plane[s.coarse_x - 1 : s.coarse_x]
        for j in range(ey + 6):
            y = j - 3
            plane = None
            if -1 <= y <= ey:
                plane = one[y + 1]
            if y <= 0:
                k = y + 3
                part = up[rows_c : rows_c + 8, half * k : half * k + LANES]
                plane = part if plane is None else plane + part
            if y >= ey - 1:
                k = y - (ey - 1)
                at = base + half * k
                part = down[rows_c : rows_c + 8, at : at + LANES]
                plane = part if plane is None else plane + part
            one_out[j] = plane
            down_out[first + 4 * j : first + 4 * j + 4, half : half + LANES] = plane[0:4]
            up_out[4 * j : 4 * j + 4, half : half + LANES] = plane[s.x_elems - 2 : s.x_elems + 2]

    return kernel


def shared_lanes(s, shape):
    lane = lax.broadcasted_iota(jnp.int32, shape, 1)
    return ((lane >= s.split) & (lane < s.split + 6)).astype(f32)


def base_kernel(s):
    lanes, nx, ny = (s.lanes, s.x_nodes, s.y_nodes)
    width = ny * s.z_nodes

    def kernel(guess, weight, own, down, out):
        gx = lax.axis_index("gx")
        gy = lax.axis_index("gy")
        shape = (nx, lanes)
        row = lax.broadcasted_iota(jnp.int32, shape, 0)
        live = (lane_mask(s, shape, 1) & ((row != 0) | (gx > 0))).astype(f32)
        live_y = (gy > 0).astype(f32)
        shared = shared_lanes(s, shape)
        for y in range(ny):
            plane = own[y, 0:nx, :]
            if y >= ny - 6:
                j = y - (ny - 6)
                plane = plane + down[8 : 8 + nx, lanes * j : lanes * (j + 1)]
            plane = plane + pltpu.roll(plane, lanes - (LANES - s.split), 1) * shared
            mask = live if y else live * live_y
            factor = weight[...] * (1.0 if y % 7 == 0 else 0.5)
            put_line(s, out, y, (get_line(s, guess, y, width) + factor * plane) * mask)

    return kernel


def finish_kernel(s, x_total, y_total):
    lanes, half, rows_c, nz = (s.lanes, s.coarse_lanes, s.coarse_rows, s.z_nodes)
    ex, ey, nx, ny = (s.x_elems, s.y_elems, s.x_nodes, s.y_nodes)
    one_rows = up_to(ex + 6, 8)
    split = s.split

    def kernel(
        base, weight, right, left, three, one,
        smooth_out, three_out, coarse_out, fine, level,
    ):
        gx = lax.axis_index("gx")
        gy = lax.axis_index("gy")
        live_y = (gy > 0).astype(f32)
        shared = shared_lanes(s, (6, lanes))
        smooth_out[...] = base[...]
        for y in range(ny):
            plane = right[6 * y : 6 * y + 6, :]
            plane = plane + pltpu.roll(plane, lanes - (LANES - split), 1) * shared
            plane = plane * weight[nx - 6 : nx, :] * (1.0 if y % 7 == 0 else 0.5)
            for t in range(2):
                at = nz * y + split * t
                lanes_at = LANES * t + 6
                smooth_out[nx - 6 : nx, at : at + split] += plane[:, lanes_at : lanes_at + split]
        first = 6 * ny
        nzc = s.coarse_z
        lane = lax.broadcasted_iota(jnp.int32, (3 * ex, nzc), 1)
        row = lax.broadcasted_iota(jnp.int32, (3 * ex, nzc), 0)
        live = ((lane >= 1) & ((row >= 1) | (gx > 0))).astype(f32)
        for j in range(3 * ey):
            fine[j] = three[j]
            fine[j, 3 * ex : 3 * ex + 3, :] += right[first + 3 * j : first + 3 * j + 3, 0:half]
            fine[j, 3:4, :] += left[j : j + 1, 0:half]
            mask = live if j else live * live_y
            three_out[:, nzc * j : nzc * (j + 1)] = fine[j, 3 : 3 * ex + 3, 0:nzc] * mask
        level[...] = jnp.zeros((ey + 6, one_rows, LANES), f32)
        for j in range(ey + 6):
            level[j, 2 : ex + 4, :] = one[j, 0 : ex + 2, :]
            level[j, 0:4, :] += left[4 * j : 4 * j + 4, half : half + LANES]
            level[j, ex + 2 : ex + 6, :] += right[
                first + 4 * j : first + 4 * j + 4, half : half + LANES
            ]
        shape = (one_rows, LANES)
        lane = lax.broadcasted_iota(jnp.int32, shape, 1)
        row = lax.broadcasted_iota(jnp.int32, shape, 0)
        global_x = gx * ex + row - 3
        plane_mask = (
            (lane >= 1) & (lane < s.z_elems) & (row < ex + 6)
            & (global_x >= 1) & (global_x < x_total)
        )
        masks = []
        for j in range(ey + 6):
            global_y = gy * ey + (j - 3)
            inside = (global_y >= 1) & (global_y < y_total)
            masks.append((plane_mask & inside).astype(f32))
        levels = [level[j] for j in range(ey + 6)]
        error = [damping / 12.0 * a * m for a, m in zip(levels, masks)]
        zero = jnp.zeros(shape, f32)
        for sweep in range(1, JAC):
            lower = [zero] + error[:-1]
            upper = error[1:] + [zero]
            fresh = []
            for j in range(ey + 6):
                here = error[j]
                neighbours = (
                    lower[j]
                    + upper[j]
                    + pltpu.roll(here, 1, 0)
                    + pltpu.roll(here, one_rows - 1, 0)
                    + pltpu.roll(here, 1, 1)
                    + pltpu.roll(here, LANES - 1, 1)
                )
                applied = 12.0 * here - 2.0 * neighbours
                fresh.append((here + damping / 12.0 * (levels[j] - applied)) * masks[j])
            error = fresh
        nze = s.z_elems
        for j in range(ey):
            coarse_out[:, nze * j : nze * (j + 1)] = error[3 + j][3 : 3 + ex, 0:nze]

    return kernel


def local(load_vector, initial_guess):
    z_nodes = 7 * EZ
    x_nodes = load_vector.shape[0]
    y_nodes = load_vector.shape[1] // z_nodes
    s = Sizes(x_nodes, y_nodes, z_nodes)
    rows, lanes, half = (s.rows, s.lanes, s.coarse_lanes)
    ny, ey = (s.y_nodes, s.y_elems)
    width = y_nodes * z_nodes
    shape = lambda *dims: jax.ShapeDtypeStruct(dims, f32)
    params = pltpu.CompilerParams(vmem_limit_bytes=36 * 2**20)
    vmem = lambda count: [pl.BlockSpec(memory_space=pltpu.VMEM)] * count

    def call(kernel, name, outputs, operands, scratch=(), spaces=None, semaphores=0):
        specs = vmem(len(operands))
        for index, space in (spaces or {}).items():
            specs[index] = pl.BlockSpec(memory_space=space)
        return pl.pallas_call(
            kernel,
            out_shape=tuple(shape(*dims) for dims in outputs),
            in_specs=specs,
            out_specs=tuple(vmem(len(outputs))),
            scratch_shapes=[pltpu.VMEM(dims, f32) for dims in scratch]
            + ([pltpu.SemaphoreType.DMA((semaphores,))] if semaphores else []),
            compiler_params=params,
            name=name,
        )(*operands)

    table = residual_constants(s)
    r_own, edge, up, u_first = call(
        residual_kernel(s),
        "residual",
        (
            (ny + 1, s.own_rows, lanes),
            (s.own_rows, lanes),
            (8, up_to((ny + 2) * z_nodes, LANES)),
            (up_to(ny, 8), lanes),
        ),
        [
            pltpu.with_memory_space_constraint(value, pltpu.HBM)
            for value in (initial_guess, load_vector, jnp.asarray(table, f32))
        ],
        [
            (ny + 1, s.own_rows, lanes),
            initial_guess.shape,
            load_vector.shape,
            table.shape,
        ],
        spaces={0: pltpu.HBM, 1: pltpu.HBM, 2: pltpu.HBM},
        semaphores=3,
    )
    below = shifted(up, "gx", 1)
    above = shifted(u_first, "gx", -1)
    r_x, line, up = call(
        joined_x_kernel(s),
        "joined_x",
        (
            (ny + 1, rows, lanes),
            (rows, lanes),
            (rows, up_to(7 * z_nodes, LANES)),
        ),
        [r_own, edge, u_first, below, above]
        + [jnp.asarray(v, f32) for v in coupling_constants(s)],
    )
    below = shifted(up, "gy", 1)
    above = shifted(line, "gy", -1)
    edge, own, three, one, down, up = call(
        patch_kernel(s),
        "patches",
        (
            (ny, 8, lanes),
            (ny, rows - 8, lanes),
            (s.coarse_y, s.coarse_rows, half),
            (ey + 2, 8, LANES),
            (rows, 6 * lanes + 4 * half),
            (s.coarse_rows + 8, 4 * half),
        ),
        [r_x, line, below, above] + patch_constants(s),
        [
            (ny + 6, rows, lanes),
            (13, ey, rows, lanes),
            (13, ey, rows, lanes),
            (ny + 6, rows, lanes),
            (ny + 6, rows, 2 * half),
            (ny, rows, half),
            (ny + 6, s.coarse_rows, half),
            (ny + 6, s.coarse_rows, half),
            (ny, s.coarse_rows, half),
            (2, s.modes_x, s.modes_z),
        ],
        spaces={4: pltpu.SMEM},
    )
    down = shifted(down, "gy", -1)
    up = shifted(up, "gy", 1)
    coarse_part = up_to(max(9 * ey, 4 * ey + 24), 8)
    right, left, three, one = call(
        join_kernel(s),
        "join",
        (
            (6 * ny + coarse_part, lanes),
            (up_to(max(3 * ey, 4 * ey + 24), 8), lanes),
            (3 * ey, s.coarse_rows, half),
            (ey + 6, 8, LANES),
        ),
        [edge, three, one, down, up],
    )
    right = shifted(right, "gx", -1)
    left = shifted(left, "gx", 1)
    weight_z = np.where(np.arange(z_nodes) % 7 == 0, 1.0, 0.5)
    weight = jnp.asarray(
        np.where(np.arange(x_nodes) % 7 == 0, 1.0, 0.5)[:, None]
        * rows_by_node(s, weight_z[:, None], True)[:, 0],
        f32,
    )
    (base,) = call(
        base_kernel(s), "base", ((x_nodes, width),), [initial_guess, weight, own, down]
    )
    return call(
        finish_kernel(s, s.x_elems * lax.axis_size("gx"), ey * lax.axis_size("gy")),
        "finish",
        (
            (x_nodes, width),
            (3 * s.x_elems, 3 * ey * s.coarse_z),
            (s.x_elems, ey * s.z_elems),
        ),
        [base, weight, right, left, three, one],
        [
            (3 * ey, s.coarse_rows, half),
            (ey + 6, up_to(s.x_elems + 6, 8), LANES),
        ],
    )


def solution(mesh):
    in_specs = (P("gx", "gy"), P("gx", "gy"))
    out_specs = (P("gx", "gy"), P("gx", "gy"), P("gx", "gy"))
    return jax.shard_map(local, mesh=mesh, in_specs=in_specs, out_specs=out_specs, check_vma=False)
```

```python
import math

import jax
import jax.numpy as jnp
import numpy as np
from jax import lax
from jax.experimental import pallas as pl
from jax.experimental.pallas import tpu as pltpu
from jax.sharding import PartitionSpec as P

EZ = 32
JAC = 4


points_seven = (
    -1.0,
    -0.8717401485096066,
    -0.5917001814331423,
    -0.2092992179024789,
    0.2092992179024789,
    0.5917001814331423,
    0.8717401485096066,
    1.0,
)
points_three = (-1.0, -0.4472135954999579, 0.4472135954999579, 1.0)
points_one = (-1.0, 1.0)
damping = 2.0 / 3.0


def shifted(array, axis, by):
    devices = lax.axis_size(axis)
    pairs = [(i, i + by) for i in range(devices) if 0 <= i + by < devices]
    return lax.ppermute(array, axis, pairs)


def legendre_at(degree, location):
    previous, current = (1.0, location)
    for level_idx in range(1, degree):
        previous, current = (
            current,
            ((2 * level_idx + 1) * location * current - level_idx * previous) / (level_idx + 1),
        )
    return current


def quadrature_weights():
    return np.array([2.0 / (56.0 * legendre_at(7, x) * legendre_at(7, x)) for x in points_seven])


def derivative_matrix():
    points = np.array(points_seven)
    products = np.array(
        [np.prod([points[i] - points[k] for k in range(8) if k != i]) for i in range(8)]
    )
    result = np.zeros((8, 8))
    for i in range(8):
        for j in range(8):
            if i != j:
                result[i, j] = products[i] / (products[j] * (points[i] - points[j]))
        result[i, i] = np.sum([1.0 / (points[i] - points[k]) for k in range(8) if k != i])
    return result


def element_stiffness():
    derivative = derivative_matrix()
    return derivative.T @ (quadrature_weights()[:, None] * derivative)


def assemble_line(elements):
    stiffness = element_stiffness()
    weights = quadrature_weights()
    extent = 7 * elements + 1
    global_stiff = np.zeros((extent, extent))
    lumped = np.zeros(extent)
    for m in range(elements):
        global_stiff[7 * m : 7 * m + 8, 7 * m : 7 * m + 8] += stiffness
        lumped[7 * m : 7 * m + 8] += weights
    return (global_stiff, lumped)


def jacobi_eigen(matrix):
    rotated_mat = matrix.copy()
    extent = matrix.shape[0]
    vectors = np.eye(extent)
    for sweep_idx in range(12):
        for p in range(extent - 1):
            for q in range(p + 1, extent):
                angle_rot = 0.5 * math.atan2(
                    2.0 * float(rotated_mat[p, q]), float(rotated_mat[q, q] - rotated_mat[p, p])
                )
                rotation = np.eye(extent)
                rotation[p, p] = math.cos(angle_rot)
                rotation[q, q] = math.cos(angle_rot)
                rotation[p, q] = math.sin(angle_rot)
                rotation[q, p] = -math.sin(angle_rot)
                rotated_mat = rotation.T @ rotated_mat @ rotation
                vectors = vectors @ rotation
    return (np.array([rotated_mat[i, i] for i in range(extent)]), vectors)


def patch_basis():
    global_stiff, lumped = assemble_line(2)
    inv_root = 1.0 / np.sqrt(lumped[1:14])
    eigvals, vectors = jacobi_eigen(
        inv_root[:, None] * global_stiff[1:14, 1:14] * inv_root[None, :]
    )
    return (eigvals, inv_root[:, None] * vectors)


def interp_matrix(coarse_pts):
    result = np.ones((8, len(coarse_pts)))
    for a in range(8):
        for c in range(len(coarse_pts)):
            for k in range(len(coarse_pts)):
                if k != c:
                    result[a, c] *= (points_seven[a] - coarse_pts[k]) / (
                        coarse_pts[c] - coarse_pts[k]
                    )
    return result


def restriction_rows(coarse_pts):
    shared = np.ones(8)
    shared[0] = 0.5
    shared[7] = 0.5
    return (interp_matrix(coarse_pts) * shared[:, None]).T


def restriction_line(elements, coarse_pts):
    degree = len(coarse_pts) - 1
    rows_mat = restriction_rows(coarse_pts)
    result = np.zeros((degree * elements + 1, 7 * elements + 1))
    for m in range(elements):
        result[degree * m : degree * m + degree + 1, 7 * m : 7 * m + 8] += rows_mat
    return result


def patch_matrix(eigbasis, vertices, extent):
    result = np.zeros((13 * vertices, extent))
    for b in range(13):
        for v in range(vertices):
            for a in range(13):
                node_idx = 7 * v + a
                result[b * vertices + v, node_idx] = eigbasis[a, b]
    return result


high = lax.Precision.HIGH
LANES = 128
GROUP = 7
f32 = jnp.float32


def up_to(length, multiple):
    return -(-length // multiple) * multiple


def placed(matrix, shape, row=0, col=0):
    result = np.zeros(shape, np.float32)
    result[row : row + matrix.shape[0], col : col + matrix.shape[1]] = matrix
    return result


def mm(left, right):
    return lax.dot_general(
        left, right, (((1,), (0,)), ((), ())), precision=high, preferred_element_type=f32
    )


class Sizes:
    def __init__(self, x_nodes, y_nodes, z_nodes):
        self.x_nodes, self.y_nodes, self.z_nodes = (x_nodes, y_nodes, z_nodes)
        self.x_elems, self.y_elems, self.z_elems = (x_nodes // 7, y_nodes // 7, z_nodes // 7)
        self.own_rows = up_to(x_nodes + 1, 8)
        self.rows = up_to(x_nodes + 8, 8)
        self.half_z = self.z_elems // 2
        self.lanes = 2 * LANES
        self.modes_x = up_to(13 * self.x_elems, 8)
        self.modes_z = up_to(13 * self.half_z, LANES)
        self.coarse_x = 3 * self.x_elems + 4
        self.coarse_y = 3 * self.y_elems + 4
        self.coarse_z = 3 * self.z_elems
        self.coarse_rows = up_to(self.coarse_x, 8)
        self.coarse_lanes = up_to(self.coarse_z, LANES)
        split = 7 * self.half_z
        self.split = split
        self.node_of_lane = np.full(self.lanes, -1)
        self.node_of_lane[6 : 6 + split] = np.arange(split)
        self.node_of_lane[LANES : LANES + split + 6] = np.arange(split - 6, 2 * split)
        self.first_copy = self.node_of_lane >= 0
        self.first_copy[LANES : LANES + 6] = False


def line_tables(elements):
    nodes = 7 * elements
    stiff, lumped = assemble_line(elements + 2)
    restrict = restriction_line(elements + 3, points_three)[3 : 3 * elements + 7, 7 : nodes + 15]
    columns = np.arange(-6, nodes)
    weight = np.where(columns % 7 == 0, 1.0, 0.5)
    mass_part = restrict[:, 1:-1] * (lumped[1 : nodes + 7] * weight)[None, :]
    stiff_part = restrict @ (stiff[: nodes + 8, 1 : nodes + 7] * weight[None, :])
    return dict(
        own_stiff=stiff[7 : nodes + 8, 7 : nodes + 7],
        mass=lumped[1 : nodes + 7],
        own=restrict[:, 7:-1],
        mass_part=mass_part,
        stiff_part=stiff_part,
    )


def rows_by_node(s, matrix, every_copy):
    used = s.node_of_lane >= 0 if every_copy else s.first_copy
    return np.where(used[:, None], matrix[np.maximum(s.node_of_lane, 0)], 0.0)


def two_parts(matrix):
    high_part = matrix.astype(np.float32).astype(jnp.bfloat16)
    low_part = (matrix - high_part.astype(np.float64)).astype(jnp.bfloat16)
    return high_part, low_part


def residual_constants(s):
    line_x = line_tables(s.x_elems)
    stiff_z, lumped_z = assemble_line(s.z_elems)
    stiff_z, lumped_z = (stiff_z[: s.z_nodes, : s.z_nodes], lumped_z[: s.z_nodes])
    mass_x = np.zeros(s.own_rows)
    mass_x[: s.x_nodes] = line_x["mass"][6:]
    mass_z = rows_by_node(s, lumped_z[:, None], True)[:, 0]
    spread = np.ones((s.own_rows, s.lanes))
    stiff = rows_by_node(s, stiff_z, False)
    stiff = rows_by_node(s, stiff.T, True).T
    wide = placed(line_x["own_stiff"], (s.own_rows, s.lanes))
    return np.concatenate(
        [
            stiff,
            spread * mass_x[:, None],
            spread * mass_z[None, :],
            mass_x[:, None] * mass_z[None, :],
            wide,
        ]
    )


def coupling_constants(s):
    stiffness = element_stiffness()
    lumped_z = assemble_line(s.z_elems)[1][: s.z_nodes]
    mass_z = rows_by_node(s, lumped_z[:, None], True)[:, 0]
    below, above = (np.zeros(s.rows), np.zeros(s.rows))
    below[2:8] = stiffness[1:7, 7]
    above[8 + s.x_nodes - 7 : 8 + s.x_nodes] = stiffness[:7, 7]
    return [below[:, None] * mass_z[None, :], above[:, None] * mass_z[None, :]]


def patch_constants(s):
    line_x = line_tables(s.x_elems)
    stiff_z, lumped_z = assemble_line(s.z_elems)
    stiff_z, lumped_z = (stiff_z[: s.z_nodes, : s.z_nodes], lumped_z[: s.z_nodes])
    weight_z = np.where(np.arange(s.z_nodes) % 7 == 0, 1.0, 0.5)
    restrict_z = restriction_line(s.z_elems, points_three)[: s.coarse_z, : s.z_nodes]
    eigvals, eigbasis = patch_basis()
    mass_z = rows_by_node(s, lumped_z[:, None], True)[:, 0]
    mass_x = np.zeros(s.rows)
    mass_x[2 : s.x_nodes + 8] = line_x["mass"]
    fwd_x = placed(
        patch_matrix(eigbasis, s.x_elems, s.x_nodes + 6), (s.modes_x, s.rows), col=2
    )
    high_x, low_x = two_parts(fwd_x.astype(np.float64))
    fwd_z = np.zeros((LANES, s.modes_z))
    fwd_z[:, : 13 * s.half_z] = patch_matrix(eigbasis, s.half_z, LANES).T
    high_z, low_z = two_parts(fwd_z)
    sums = np.ones((s.modes_x, s.modes_z))
    sums[: 13 * s.x_elems, : 13 * s.half_z] = (
        np.repeat(eigvals, s.x_elems)[:, None] + np.repeat(eigvals, s.half_z)[None, :]
    )
    coarse_of_z = np.zeros((s.z_nodes, 2 * s.coarse_lanes))
    coarse_of_z[:, : s.coarse_z] = (restrict_z * (lumped_z * weight_z)[None, :]).T
    coarse_of_z[:, s.coarse_lanes : s.coarse_lanes + s.coarse_z] = (
        restrict_z @ (stiff_z * weight_z[None, :])
    ).T
    coarse_of_x = np.zeros((2 * s.coarse_rows, s.rows))
    coarse_of_x[: s.coarse_x, 2 : s.x_nodes + 8] = line_x["mass_part"]
    coarse_of_x[s.coarse_rows : s.coarse_rows + s.coarse_x, 2 : s.x_nodes + 8] = line_x[
        "stiff_part"
    ]
    own_z = np.zeros((s.z_nodes, s.coarse_lanes))
    own_z[:, : s.coarse_z] = restrict_z.T
    one_z = placed(
        linear_from_cubic(0, s.z_elems - 1, 0, s.coarse_z - 1).T, (s.coarse_lanes, LANES)
    )
    one_x = placed(linear_from_cubic(-1, s.x_elems, -3, 3 * s.x_elems), (8, s.coarse_rows))
    singles = [
        mass_x[:, None] * mass_z[None, :],
        sums,
        rows_by_node(s, coarse_of_z, True),
        coarse_of_x,
        rows_by_node(s, own_z, False),
        placed(line_x["own"], (s.coarse_rows, s.rows), col=8),
        one_z,
        one_x,
    ]
    halves = [
        np.concatenate([high_x, high_x, low_x], 1),
        np.concatenate([high_x.T, high_x.T, low_x.T], 1),
        np.concatenate([high_z, high_z], 0),
        low_z,
        np.concatenate([high_z.T, low_z.T], 1),
        high_z.T,
    ]
    return (
        [jnp.asarray(eigvals, f32)]
        + [jnp.asarray(value, f32) for value in singles]
        + [jnp.asarray(value, jnp.bfloat16) for value in halves]
    )


def halves_of(value):
    high_part = value.astype(jnp.bfloat16)
    return high_part, (value - high_part.astype(f32)).astype(jnp.bfloat16)


def stacked_rows(value):
    high_part = value.astype(jnp.bfloat16).astype(f32)
    return jnp.concatenate([high_part, value - high_part, high_part], 0).astype(jnp.bfloat16)


def dot(left, right):
    return lax.dot_general(left, right, (((1,), (0,)), ((), ())), preferred_element_type=f32)


def linear_from_cubic(first, last, first_three, last_three):
    result = np.zeros((last - first + 1, last_three - first_three + 1))
    for m in range(first, last + 1):
        for offset, factor in (
            (0, 1.0),
            (1, (1.0 - points_three[1]) / 2.0),
            (2, (1.0 - points_three[2]) / 2.0),
            (-2, (1.0 + points_three[1]) / 2.0),
            (-1, (1.0 + points_three[2]) / 2.0),
        ):
            node = 3 * m + offset - first_three
            if 0 <= node < result.shape[1]:
                result[m - first, node] = factor
    return result


def line_of_planes(coefficients, planes):
    total = None
    for coefficient, plane in zip(coefficients, planes):
        if coefficient != 0.0:
            part = plane() * float(coefficient)
            total = part if total is None else total + part
    return total


def symmetric(vector):
    return abs(vector[0] - vector[-1]) < abs(vector[0] + vector[-1])


def lane_window(ref, start, width):
    if start < 0:
        return pltpu.roll(ref[:, 0:LANES], -start, 1)
    if start + LANES > width:
        return pltpu.roll(ref[:, width - LANES : width], width - start, 1)
    return ref[:, start : start + LANES]


def lane_mask(s, shape, first):
    lane = lax.broadcasted_iota(jnp.int32, shape, 1)
    return ((lane >= 6 + first) & (lane < 6 + s.split)) | (
        (lane >= LANES) & (lane < LANES + s.split + 6)
    )


def put_line(s, ref, index, plane):
    at = s.z_nodes * index
    rows = plane.shape[0]
    ref[0:rows, at : at + s.split] = plane[:, 6 : 6 + s.split]
    ref[0:rows, at + s.split : at + 2 * s.split] = plane[:, LANES + 6 : LANES + 6 + s.split]


def get_line(s, ref, index, width):
    at = s.z_nodes * index
    return jnp.concatenate(
        [lane_window(ref, at - 6, width), lane_window(ref, at + s.split - 6, width)], 1
    )


def residual_kernel(s):
    rows, lanes = (s.own_rows, s.lanes)
    ex, ey, nx, ny = (s.x_elems, s.y_elems, s.x_nodes, s.y_nodes)
    width = ny * s.z_nodes
    mass_y = line_tables(ey)["mass"][6:]
    stiffness = element_stiffness()

    def kernel(guess_hbm, load_hbm, table_hbm, r, edge, up_out, down_out, u, guess, load, table, sems):
        copies = [
            pltpu.make_async_copy(source, target, sems.at[index])
            for index, (source, target) in enumerate(
                [(guess_hbm, guess), (load_hbm, load), (table_hbm, table)]
            )
        ]
        for copy in copies:
            copy.start()
        k_z = table.at[0:lanes]
        m_x, m_z, m_xz, k_x_wide = [
            table.at[lanes + rows * i : lanes + rows * (i + 1)] for i in range(4)
        ]
        k_x = k_x_wide.at[:, 0:rows]
        gx = lax.axis_index("gx")
        gy = lax.axis_index("gy")
        shape = (nx, lanes)
        row = lax.broadcasted_iota(jnp.int32, shape, 0)
        live = (lane_mask(s, shape, 1) & ((row != 0) | (gx > 0))).astype(f32)
        live_y = (gy > 0).astype(f32)
        inside = lane_mask(s, shape, 0).astype(f32)
        pad = jnp.zeros((rows - nx, lanes), f32)
        copies[0].wait()
        for y in range(ny):
            mask = live if y else live * live_y
            u[y, 0:nx] = get_line(s, guess, y, width) * mask
            u[y, nx:] = pad
        copies[1].wait()
        for y in range(ny):
            r[y, 0:nx] = get_line(s, load, y, width) * inside
            r[y, nx:] = pad
        u[ny] = jnp.zeros((rows, lanes), f32)
        r[ny] = jnp.zeros((rows, lanes), f32)

        copies[2].wait()

        def direct(chunk, carry):
            base = chunk * 7
            planes = u[pl.ds(base, 7)]
            z_term = mm(planes.reshape(7 * rows, lanes), k_z[...]).reshape(7, rows, lanes)
            for i in range(7):
                x_term = mm(k_x[...], planes[i])
                both = x_term * m_z[...] + z_term[i] * m_x[...]
                r[base + i] = r[base + i] - float(mass_y[i]) * both
            return carry

        lax.fori_loop(0, ey, direct, 0)

        def along_y(tile, carry):
            at = pl.ds(pl.multiple_of(tile * 8, 8), 8)
            scale = m_xz[at, :]
            corner = None
            for e in range(ey):
                nodes = [u[7 * e + i, at, :] for i in range(8)]
                plus = [nodes[i] + nodes[7 - i] for i in range(4)]
                minus = [nodes[i] - nodes[7 - i] for i in range(4)]
                out = [None] * 8
                for i in range(4):
                    even = sum(
                        plus[k] * float(0.5 * (stiffness[i, k] + stiffness[i, 7 - k]))
                        for k in range(4)
                    )
                    odd = sum(
                        minus[k] * float(0.5 * (stiffness[i, k] - stiffness[i, 7 - k]))
                        for k in range(4)
                    )
                    out[i], out[7 - i] = (even + odd, even - odd)
                if e:
                    out[0] = out[0] + corner
                else:
                    out[0] = out[0] + nodes[0] * float(stiffness[7, 7])
                corner = out[7]
                for i in range(8 if e == ey - 1 else 7):
                    plane = 7 * e + i
                    r[plane, at, :] = r[plane, at, :] - out[i] * scale
            return carry

        lax.fori_loop(0, rows // 8, along_y, 0)
        for y in range(ny + 1):
            put_line(s, up_out, y, r[y, nx - 6 : nx + 1, :])
        up_out[7:8, :] = jnp.zeros((1, up_out.shape[1]), f32)
        put_line(s, up_out, ny + 1, u[0, nx - 6 : nx, :])
        up_out[6:7, (ny + 1) * s.z_nodes :] = jnp.zeros(
            (1, up_out.shape[1] - (ny + 1) * s.z_nodes), f32
        )
        for y in range(ny):
            down_out[y : y + 1, :] = u[y, 0:1, :]
        down_out[ny:, :] = jnp.zeros((down_out.shape[0] - ny, lanes), f32)
        edge[...] = u[0]

    return kernel


def joined_x_kernel(s):
    rows, lanes = (s.rows, s.lanes)
    nx, ny = (s.x_nodes, s.y_nodes)
    mass_y = line_tables(s.y_elems)["mass"][6:]

    def kernel(r_own, edge, u_first, below, above, c_below, c_above, r, line, up_out):
        width = below.shape[1]
        shape = (8, lanes)
        row = lax.broadcasted_iota(jnp.int32, shape, 0)
        inside = lane_mask(s, shape, 0)
        keep = (inside & (row < 6)).astype(f32)
        only = (inside & (row == 6)).astype(f32)
        zero = jnp.zeros((rows - 8 - nx, lanes), f32) if rows - 8 - nx else None
        for y in range(ny + 2):
            got = get_line(s, below, y, width)
            place = line if y == ny + 1 else r.at[y]
            own = edge[0:nx] if y == ny + 1 else r_own[y, 0:nx, :]
            place[0:2, :] = jnp.zeros((2, lanes), f32)
            place[2:8, :] = (got * keep)[0:6]
            place[8 : 8 + nx, :] = own
            if zero is not None:
                place[8 + nx :, :] = zero
            if y < ny:
                place[8:9, :] += (got * only)[6:7]
                both = (
                    c_below[...] * u_first[y : y + 1, :] + c_above[...] * above[y : y + 1, :]
                ) * float(mass_y[y])
                place[...] = place[...] - both
        for j in range(7):
            put_line(s, up_out, j, r[ny - 6 + j])
        up_out[:, 7 * s.z_nodes :] = jnp.zeros((rows, up_out.shape[1] - 7 * s.z_nodes), f32)

    return kernel


def patch_kernel(s):
    rows, lanes = (s.rows, s.lanes)
    ey, ny = (s.y_elems, s.y_nodes)
    line_y = line_tables(ey)
    _, eigbasis = patch_basis()
    stiffness = element_stiffness()
    one_y = linear_from_cubic(-1, ey, -3, 3 * ey)
    evens = [b for b in range(13) if symmetric(eigbasis[:, b])]
    odds = [b for b in range(13) if b not in evens]

    def kernel(
        r_own, line, below, above,
        lam, m_xz, sums, q_z, q_x, r_z, r_x, o_z, o_x, f_x, b_x, f_z, f_z_low, b_z, b_z_high,
        edge_out, own_out, three_out, one_out, down_out, up_out,
        r, xf, xb, c, cz, rz, hx, ex, rx, live,
    ):
        gx = lax.axis_index("gx")
        gy = lax.axis_index("gy")
        inside = lane_mask(s, (rows, lanes), 0).astype(f32)
        width = below.shape[1]
        lower = line[...] * m_xz[...]
        upper = above[...] * m_xz[...]
        for j in range(7):
            got = get_line(s, below, j, width) * inside
            if j < 6:
                r[j] = got - lower * float(stiffness[1 + j, 7])
            else:
                r[6] = r_own[0] + got
        for y in range(1, ny):
            plane = r_own[y]
            if y >= ny - 7:
                plane = plane - upper * float(stiffness[y - (ny - 7), 7])
            r[6 + y] = plane
        shape = (s.modes_x, s.modes_z)
        mode = lax.broadcasted_iota(jnp.int32, shape, 0)
        vertex = lax.broadcasted_iota(jnp.int32, shape, 1) % s.half_z
        live_x = (mode % s.x_elems != 0) | (gx > 0)
        live[0] = (live_x & (vertex != 0)).astype(f32)
        live[1] = live_x.astype(f32)
        active = (gy > 0).astype(f32)

        def along_y(tile, carry):
            at = pl.ds(pl.multiple_of(tile * 8, 8), 8)
            for v in range(ey):
                first = [r[7 * v + a, at, :] for a in range(13)]
                if v == 0:
                    first = [value * active for value in first]
                even = [first[6]] + [first[6 + a] + first[6 - a] for a in range(1, 7)]
                odd = [first[6 + a] - first[6 - a] for a in range(1, 7)]
                for b in range(13):
                    if b in evens:
                        xf[b, v, at, :] = sum(
                            even[a] * float(eigbasis[6 + a, b]) for a in range(7)
                        )
                    else:
                        xf[b, v, at, :] = sum(
                            odd[a] * float(eigbasis[7 + a, b]) for a in range(6)
                        )
            return carry

        lax.fori_loop(0, rows // 8, along_y, 0)

        def spectral(modes_of):
            pieces = []
            for b in modes_of:
                planes = [dot(f_x[...], stacked_rows(xf[b, v])) for v in range(ey)]
                pieces += [plane[:, :LANES] for plane in planes]
                pieces += [plane[:, LANES:] for plane in planes]
            high_part, low_part = halves_of(jnp.concatenate(pieces, 0))
            modes = dot(jnp.concatenate([high_part, low_part], 1), f_z[...]) + dot(
                high_part, f_z_low[...]
            )
            modes = modes.reshape(len(modes_of), 2, ey, s.modes_x, s.modes_z)
            pieces = []
            for i, b in enumerate(modes_of):
                factor = 1.0 / (sums[...] + lam[b])
                for t in range(2):
                    scaled = modes[i, t] * (factor * live[t])[None]
                    pieces.append(scaled.reshape(ey * s.modes_x, s.modes_z))
            high_part, low_part = halves_of(jnp.concatenate(pieces, 0))
            both = dot(high_part, b_z[...])
            back = both[:, :LANES] + both[:, LANES:] + dot(low_part, b_z_high[...])
            back = back.reshape(len(modes_of), 2, ey, s.modes_x, LANES)
            for i, b in enumerate(modes_of):
                for v in range(ey):
                    plane = jnp.concatenate([back[i, 0, v], back[i, 1, v]], 1)
                    xb[b, v] = dot(b_x[...], stacked_rows(plane))

        for first in range(0, 13, GROUP):
            spectral(range(first, min(13, first + GROUP)))

        def back_y(tile, carry):
            at = pl.ds(pl.multiple_of(tile * 8, 8), 8)
            tail = None
            for v in range(ey):
                modes = [xb[b, v, at, :] for b in range(13)]
                out = [None] * 13
                for a in range(7):
                    even = sum(modes[b] * float(eigbasis[6 + a, b]) for b in evens)
                    if a == 0:
                        out[6] = even
                        continue
                    odd = sum(modes[b] * float(eigbasis[6 + a, b]) for b in odds)
                    out[6 + a], out[6 - a] = (even + odd, even - odd)
                if v:
                    out[:6] = [value + other for value, other in zip(out[:6], tail)]
                tail = out[7:]
                for a in range(13 if v == ey - 1 else 7):
                    c[7 * v + a, at, :] = out[a]
            return carry

        lax.fori_loop(0, rows // 8, back_y, 0)

        for j in range(6):
            down_out[:, lanes * j : lanes * (j + 1)] = c[j]
        edge_out[...] = c[6:, 0:8, :]
        own_out[...] = c[6:, 8:, :]

        half = s.coarse_lanes
        rows_c = s.coarse_rows
        cz[...] = mm(c[...].reshape((ny + 6) * rows, lanes), q_z[...]).reshape(
            ny + 6, rows, 2 * half
        )
        rz[...] = mm(r[6 : ny + 6].reshape(ny * rows, lanes), r_z[...]).reshape(ny, rows, half)
        for y in range(ny + 6):
            plane = mm(q_x[...], cz[y])
            hx[y] = plane[:rows_c, :half]
            ex[y] = plane[rows_c:, :half] + plane[:rows_c, half:]
        for y in range(ny):
            rx[y] = mm(r_x[...], rz[y])
        for j in range(s.coarse_y):
            three_out[j] = line_of_planes(
                np.concatenate(
                    [line_y["own"][j], -line_y["stiff_part"][j], -line_y["mass_part"][j]]
                ),
                [lambda y=y: rx[y] for y in range(ny)]
                + [lambda y=y: hx[y] for y in range(ny + 6)]
                + [lambda y=y: ex[y] for y in range(ny + 6)],
            )
        one_all = mm(
            three_out[...].reshape(s.coarse_y * rows_c, half), o_z[...]
        ).reshape(s.coarse_y, rows_c, LANES)
        for m in range(ey + 2):
            mixed = line_of_planes(
                one_y[m], [lambda j=j: one_all[j] for j in range(s.coarse_y)]
            )
            one_out[m] = mm(o_x[...], mixed)
        base = 6 * lanes
        for j in range(4):
            at = base + half * j
            if j < 3:
                down_out[0:rows_c, at : at + half] = three_out[j]
            else:
                down_out[0:rows_c, at : at + half] = jnp.zeros((rows_c, half), f32)
            down_out[rows_c : rows_c + 8, at : at + LANES] = one_out[j]
            down_out[rows_c + 8 :, at : at + half] = jnp.zeros((rows - rows_c - 8, half), f32)
            up_at = half * j
            if j == 0:
                up_out[0:rows_c, up_at : up_at + half] = three_out[s.coarse_y - 1]
            else:
                up_out[0:rows_c, up_at : up_at + half] = jnp.zeros((rows_c, half), f32)
            up_out[rows_c : rows_c + 8, up_at : up_at + LANES] = one_out[ey - 2 + j]

    return kernel


def join_kernel(s):
    lanes, half, rows_c = (s.lanes, s.coarse_lanes, s.coarse_rows)
    ey, ny = (s.y_elems, s.y_nodes)

    def kernel(edge, three, one, down, up, down_out, up_out, three_out, one_out):
        for y in range(ny):
            plane = edge[y]
            if y >= ny - 6:
                j = y - (ny - 6)
                plane = plane + down[0:8, lanes * j : lanes * (j + 1)]
            down_out[6 * y : 6 * y + 6, :] = plane[2:8]
        base = 6 * lanes
        first = 6 * ny
        down_out[first:, :] = jnp.zeros((down_out.shape[0] - first, lanes), f32)
        up_out[...] = jnp.zeros(up_out.shape, f32)
        for j in range(3 * ey):
            plane = three[3 + j]
            if j >= 3 * ey - 3:
                k = j - (3 * ey - 3)
                plane = plane + down[0:rows_c, base + half * k : base + half * (k + 1)]
            if j == 0:
                plane = plane + up[0:rows_c, 0:half]
            three_out[j] = plane
            down_out[first + 3 * j : first + 3 * j + 3, 0:half] = plane[0:3]
            up_out[j : j + 1, 0:half] = plane[s.coarse_x - 1 : s.coarse_x]
        for j in range(ey + 6):
            y = j - 3
            plane = None
            if -1 <= y <= ey:
                plane = one[y + 1]
            if y <= 0:
                k = y + 3
                part = up[rows_c : rows_c + 8, half * k : half * k + LANES]
                plane = part if plane is None else plane + part
            if y >= ey - 1:
                k = y - (ey - 1)
                at = base + half * k
                part = down[rows_c : rows_c + 8, at : at + LANES]
                plane = part if plane is None else plane + part
            one_out[j] = plane
            down_out[first + 4 * j : first + 4 * j + 4, half : half + LANES] = plane[0:4]
            up_out[4 * j : 4 * j + 4, half : half + LANES] = plane[s.x_elems - 2 : s.x_elems + 2]

    return kernel


def shared_lanes(s, shape):
    lane = lax.broadcasted_iota(jnp.int32, shape, 1)
    return ((lane >= s.split) & (lane < s.split + 6)).astype(f32)


def base_kernel(s):
    lanes, nx, ny = (s.lanes, s.x_nodes, s.y_nodes)
    width = ny * s.z_nodes

    def kernel(guess, weight, own, down, out):
        gx = lax.axis_index("gx")
        gy = lax.axis_index("gy")
        shape = (nx, lanes)
        row = lax.broadcasted_iota(jnp.int32, shape, 0)
        live = (lane_mask(s, shape, 1) & ((row != 0) | (gx > 0))).astype(f32)
        live_y = (gy > 0).astype(f32)
        shared = shared_lanes(s, shape)
        for y in range(ny):
            plane = own[y, 0:nx, :]
            if y >= ny - 6:
                j = y - (ny - 6)
                plane = plane + down[8 : 8 + nx, lanes * j : lanes * (j + 1)]
            plane = plane + pltpu.roll(plane, lanes - (LANES - s.split), 1) * shared
            mask = live if y else live * live_y
            factor = weight[...] * (1.0 if y % 7 == 0 else 0.5)
            put_line(s, out, y, (get_line(s, guess, y, width) + factor * plane) * mask)

    return kernel


def finish_kernel(s, x_total, y_total):
    lanes, half, rows_c, nz = (s.lanes, s.coarse_lanes, s.coarse_rows, s.z_nodes)
    ex, ey, nx, ny = (s.x_elems, s.y_elems, s.x_nodes, s.y_nodes)
    one_rows = up_to(ex + 6, 8)
    split = s.split

    def kernel(
        base, weight, right, left, three, one,
        smooth_out, three_out, coarse_out, fine, level,
    ):
        gx = lax.axis_index("gx")
        gy = lax.axis_index("gy")
        live_y = (gy > 0).astype(f32)
        shared = shared_lanes(s, (6, lanes))
        smooth_out[...] = base[...]
        for y in range(ny):
            plane = right[6 * y : 6 * y + 6, :]
            plane = plane + pltpu.roll(plane, lanes - (LANES - split), 1) * shared
            plane = plane * weight[nx - 6 : nx, :] * (1.0 if y % 7 == 0 else 0.5)
            for t in range(2):
                at = nz * y + split * t
                lanes_at = LANES * t + 6
                smooth_out[nx - 6 : nx, at : at + split] += plane[:, lanes_at : lanes_at + split]
        first = 6 * ny
        nzc = s.coarse_z
        lane = lax.broadcasted_iota(jnp.int32, (3 * ex, nzc), 1)
        row = lax.broadcasted_iota(jnp.int32, (3 * ex, nzc), 0)
        live = ((lane >= 1) & ((row >= 1) | (gx > 0))).astype(f32)
        for j in range(3 * ey):
            fine[j] = three[j]
            fine[j, 3 * ex : 3 * ex + 3, :] += right[first + 3 * j : first + 3 * j + 3, 0:half]
            fine[j, 3:4, :] += left[j : j + 1, 0:half]
            mask = live if j else live * live_y
            three_out[:, nzc * j : nzc * (j + 1)] = fine[j, 3 : 3 * ex + 3, 0:nzc] * mask
        level[...] = jnp.zeros((ey + 6, one_rows, LANES), f32)
        for j in range(ey + 6):
            level[j, 2 : ex + 4, :] = one[j, 0 : ex + 2, :]
            level[j, 0:4, :] += left[4 * j : 4 * j + 4, half : half + LANES]
            level[j, ex + 2 : ex + 6, :] += right[
                first + 4 * j : first + 4 * j + 4, half : half + LANES
            ]
        shape = (one_rows, LANES)
        lane = lax.broadcasted_iota(jnp.int32, shape, 1)
        row = lax.broadcasted_iota(jnp.int32, shape, 0)
        global_x = gx * ex + row - 3
        plane_mask = (
            (lane >= 1) & (lane < s.z_elems) & (row < ex + 6)
            & (global_x >= 1) & (global_x < x_total)
        )
        masks = []
        for j in range(ey + 6):
            global_y = gy * ey + (j - 3)
            inside = (global_y >= 1) & (global_y < y_total)
            masks.append((plane_mask & inside).astype(f32))
        levels = [level[j] for j in range(ey + 6)]
        error = [damping / 12.0 * a * m for a, m in zip(levels, masks)]
        zero = jnp.zeros(shape, f32)
        for sweep in range(1, JAC):
            lower = [zero] + error[:-1]
            upper = error[1:] + [zero]
            fresh = []
            for j in range(ey + 6):
                here = error[j]
                neighbours = (
                    lower[j]
                    + upper[j]
                    + pltpu.roll(here, 1, 0)
                    + pltpu.roll(here, one_rows - 1, 0)
                    + pltpu.roll(here, 1, 1)
                    + pltpu.roll(here, LANES - 1, 1)
                )
                applied = 12.0 * here - 2.0 * neighbours
                fresh.append((here + damping / 12.0 * (levels[j] - applied)) * masks[j])
            error = fresh
        nze = s.z_elems
        for j in range(ey):
            coarse_out[:, nze * j : nze * (j + 1)] = error[3 + j][3 : 3 + ex, 0:nze]

    return kernel


def local(load_vector, initial_guess):
    z_nodes = 7 * EZ
    x_nodes = load_vector.shape[0]
    y_nodes = load_vector.shape[1] // z_nodes
    s = Sizes(x_nodes, y_nodes, z_nodes)
    rows, lanes, half = (s.rows, s.lanes, s.coarse_lanes)
    ny, ey = (s.y_nodes, s.y_elems)
    width = y_nodes * z_nodes
    shape = lambda *dims: jax.ShapeDtypeStruct(dims, f32)
    params = pltpu.CompilerParams(vmem_limit_bytes=36 * 2**20)
    vmem = lambda count: [pl.BlockSpec(memory_space=pltpu.VMEM)] * count

    def call(kernel, name, outputs, operands, scratch=(), spaces=None, semaphores=0):
        specs = vmem(len(operands))
        for index, space in (spaces or {}).items():
            specs[index] = pl.BlockSpec(memory_space=space)
        return pl.pallas_call(
            kernel,
            out_shape=tuple(shape(*dims) for dims in outputs),
            in_specs=specs,
            out_specs=tuple(vmem(len(outputs))),
            scratch_shapes=[pltpu.VMEM(dims, f32) for dims in scratch]
            + ([pltpu.SemaphoreType.DMA((semaphores,))] if semaphores else []),
            compiler_params=params,
            name=name,
        )(*operands)

    table = residual_constants(s)
    r_own, edge, up, u_first = call(
        residual_kernel(s),
        "residual",
        (
            (ny + 1, s.own_rows, lanes),
            (s.own_rows, lanes),
            (8, up_to((ny + 2) * z_nodes, LANES)),
            (up_to(ny, 8), lanes),
        ),
        [
            pltpu.with_memory_space_constraint(value, pltpu.HBM)
            for value in (initial_guess, load_vector, jnp.asarray(table, f32))
        ],
        [
            (ny + 1, s.own_rows, lanes),
            initial_guess.shape,
            load_vector.shape,
            table.shape,
        ],
        spaces={0: pltpu.HBM, 1: pltpu.HBM, 2: pltpu.HBM},
        semaphores=3,
    )
    below = shifted(up, "gx", 1)
    above = shifted(u_first, "gx", -1)
    r_x, line, up = call(
        joined_x_kernel(s),
        "joined_x",
        (
            (ny + 1, rows, lanes),
            (rows, lanes),
            (rows, up_to(7 * z_nodes, LANES)),
        ),
        [r_own, edge, u_first, below, above]
        + [jnp.asarray(v, f32) for v in coupling_constants(s)],
    )
    below = shifted(up, "gy", 1)
    above = shifted(line, "gy", -1)
    edge, own, three, one, down, up = call(
        patch_kernel(s),
        "patches",
        (
            (ny, 8, lanes),
            (ny, rows - 8, lanes),
            (s.coarse_y, s.coarse_rows, half),
            (ey + 2, 8, LANES),
            (rows, 6 * lanes + 4 * half),
            (s.coarse_rows + 8, 4 * half),
        ),
        [r_x, line, below, above] + patch_constants(s),
        [
            (ny + 6, rows, lanes),
            (13, ey, rows, lanes),
            (13, ey, rows, lanes),
            (ny + 6, rows, lanes),
            (ny + 6, rows, 2 * half),
            (ny, rows, half),
            (ny + 6, s.coarse_rows, half),
            (ny + 6, s.coarse_rows, half),
            (ny, s.coarse_rows, half),
            (2, s.modes_x, s.modes_z),
        ],
        spaces={4: pltpu.SMEM},
    )
    down = shifted(down, "gy", -1)
    up = shifted(up, "gy", 1)
    coarse_part = up_to(max(9 * ey, 4 * ey + 24), 8)
    right, left, three, one = call(
        join_kernel(s),
        "join",
        (
            (6 * ny + coarse_part, lanes),
            (up_to(max(3 * ey, 4 * ey + 24), 8), lanes),
            (3 * ey, s.coarse_rows, half),
            (ey + 6, 8, LANES),
        ),
        [edge, three, one, down, up],
    )
    right = shifted(right, "gx", -1)
    left = shifted(left, "gx", 1)
    weight_z = np.where(np.arange(z_nodes) % 7 == 0, 1.0, 0.5)
    weight = jnp.asarray(
        np.where(np.arange(x_nodes) % 7 == 0, 1.0, 0.5)[:, None]
        * rows_by_node(s, weight_z[:, None], True)[:, 0],
        f32,
    )
    (base,) = call(
        base_kernel(s), "base", ((x_nodes, width),), [initial_guess, weight, own, down]
    )
    return call(
        finish_kernel(s, s.x_elems * lax.axis_size("gx"), ey * lax.axis_size("gy")),
        "finish",
        (
            (x_nodes, width),
            (3 * s.x_elems, 3 * ey * s.coarse_z),
            (s.x_elems, ey * s.z_elems),
        ),
        [base, weight, right, left, three, one],
        [
            (3 * ey, s.coarse_rows, half),
            (ey + 6, up_to(s.x_elems + 6, 8), LANES),
        ],
    )


def solution(mesh):
    in_specs = (P("gx", "gy"), P("gx", "gy"))
    out_specs = (P("gx", "gy"), P("gx", "gy"), P("gx", "gy"))
    return jax.shard_map(local, mesh=mesh, in_specs=in_specs, out_specs=out_specs, check_vma=False)
```

```python
import math

import jax
import jax.numpy as jnp
import numpy as np
from jax import lax
from jax.experimental import pallas as pl
from jax.experimental.pallas import tpu as pltpu
from jax.sharding import PartitionSpec as P

EZ = 32
JAC = 4


points_seven = (
    -1.0,
    -0.8717401485096066,
    -0.5917001814331423,
    -0.2092992179024789,
    0.2092992179024789,
    0.5917001814331423,
    0.8717401485096066,
    1.0,
)
points_three = (-1.0, -0.4472135954999579, 0.4472135954999579, 1.0)
points_one = (-1.0, 1.0)
damping = 2.0 / 3.0


def shifted(array, axis, by):
    devices = lax.axis_size(axis)
    pairs = [(i, i + by) for i in range(devices) if 0 <= i + by < devices]
    return lax.ppermute(array, axis, pairs)


def legendre_at(degree, location):
    previous, current = (1.0, location)
    for level_idx in range(1, degree):
        previous, current = (
            current,
            ((2 * level_idx + 1) * location * current - level_idx * previous) / (level_idx + 1),
        )
    return current


def quadrature_weights():
    return np.array([2.0 / (56.0 * legendre_at(7, x) * legendre_at(7, x)) for x in points_seven])


def derivative_matrix():
    points = np.array(points_seven)
    products = np.array(
        [np.prod([points[i] - points[k] for k in range(8) if k != i]) for i in range(8)]
    )
    result = np.zeros((8, 8))
    for i in range(8):
        for j in range(8):
            if i != j:
                result[i, j] = products[i] / (products[j] * (points[i] - points[j]))
        result[i, i] = np.sum([1.0 / (points[i] - points[k]) for k in range(8) if k != i])
    return result


def element_stiffness():
    derivative = derivative_matrix()
    return derivative.T @ (quadrature_weights()[:, None] * derivative)


def assemble_line(elements):
    stiffness = element_stiffness()
    weights = quadrature_weights()
    extent = 7 * elements + 1
    global_stiff = np.zeros((extent, extent))
    lumped = np.zeros(extent)
    for m in range(elements):
        global_stiff[7 * m : 7 * m + 8, 7 * m : 7 * m + 8] += stiffness
        lumped[7 * m : 7 * m + 8] += weights
    return (global_stiff, lumped)


def jacobi_eigen(matrix):
    rotated_mat = matrix.copy()
    extent = matrix.shape[0]
    vectors = np.eye(extent)
    for sweep_idx in range(12):
        for p in range(extent - 1):
            for q in range(p + 1, extent):
                angle_rot = 0.5 * math.atan2(
                    2.0 * float(rotated_mat[p, q]), float(rotated_mat[q, q] - rotated_mat[p, p])
                )
                rotation = np.eye(extent)
                rotation[p, p] = math.cos(angle_rot)
                rotation[q, q] = math.cos(angle_rot)
                rotation[p, q] = math.sin(angle_rot)
                rotation[q, p] = -math.sin(angle_rot)
                rotated_mat = rotation.T @ rotated_mat @ rotation
                vectors = vectors @ rotation
    return (np.array([rotated_mat[i, i] for i in range(extent)]), vectors)


def patch_basis():
    global_stiff, lumped = assemble_line(2)
    inv_root = 1.0 / np.sqrt(lumped[1:14])
    eigvals, vectors = jacobi_eigen(
        inv_root[:, None] * global_stiff[1:14, 1:14] * inv_root[None, :]
    )
    return (eigvals, inv_root[:, None] * vectors)


def interp_matrix(coarse_pts):
    result = np.ones((8, len(coarse_pts)))
    for a in range(8):
        for c in range(len(coarse_pts)):
            for k in range(len(coarse_pts)):
                if k != c:
                    result[a, c] *= (points_seven[a] - coarse_pts[k]) / (
                        coarse_pts[c] - coarse_pts[k]
                    )
    return result


def restriction_rows(coarse_pts):
    shared = np.ones(8)
    shared[0] = 0.5
    shared[7] = 0.5
    return (interp_matrix(coarse_pts) * shared[:, None]).T


def restriction_line(elements, coarse_pts):
    degree = len(coarse_pts) - 1
    rows_mat = restriction_rows(coarse_pts)
    result = np.zeros((degree * elements + 1, 7 * elements + 1))
    for m in range(elements):
        result[degree * m : degree * m + degree + 1, 7 * m : 7 * m + 8] += rows_mat
    return result


def patch_matrix(eigbasis, vertices, extent):
    result = np.zeros((13 * vertices, extent))
    for b in range(13):
        for v in range(vertices):
            for a in range(13):
                node_idx = 7 * v + a
                result[b * vertices + v, node_idx] = eigbasis[a, b]
    return result


high = lax.Precision.HIGH
LANES = 128
GROUP = 7
f32 = jnp.float32


def up_to(length, multiple):
    return -(-length // multiple) * multiple


def placed(matrix, shape, row=0, col=0):
    result = np.zeros(shape, np.float32)
    result[row : row + matrix.shape[0], col : col + matrix.shape[1]] = matrix
    return result


def mm(left, right):
    return lax.dot_general(
        left, right, (((1,), (0,)), ((), ())), precision=high, preferred_element_type=f32
    )


class Sizes:
    def __init__(self, x_nodes, y_nodes, z_nodes):
        self.x_nodes, self.y_nodes, self.z_nodes = (x_nodes, y_nodes, z_nodes)
        self.x_elems, self.y_elems, self.z_elems = (x_nodes // 7, y_nodes // 7, z_nodes // 7)
        self.own_rows = up_to(x_nodes + 1, 8)
        self.rows = up_to(x_nodes + 8, 8)
        self.half_z = self.z_elems // 2
        self.lanes = 2 * LANES
        self.modes_x = up_to(13 * self.x_elems, 8)
        self.modes_z = up_to(13 * self.half_z, LANES)
        self.coarse_x = 3 * self.x_elems + 4
        self.coarse_y = 3 * self.y_elems + 4
        self.coarse_z = 3 * self.z_elems
        self.coarse_rows = up_to(self.coarse_x, 8)
        self.coarse_lanes = up_to(self.coarse_z, LANES)
        split = 7 * self.half_z
        self.split = split
        self.node_of_lane = np.full(self.lanes, -1)
        self.node_of_lane[6 : 6 + split] = np.arange(split)
        self.node_of_lane[LANES : LANES + split + 6] = np.arange(split - 6, 2 * split)
        self.first_copy = self.node_of_lane >= 0
        self.first_copy[LANES : LANES + 6] = False


def line_tables(elements):
    nodes = 7 * elements
    stiff, lumped = assemble_line(elements + 2)
    restrict = restriction_line(elements + 3, points_three)[3 : 3 * elements + 7, 7 : nodes + 15]
    columns = np.arange(-6, nodes)
    weight = np.where(columns % 7 == 0, 1.0, 0.5)
    mass_part = restrict[:, 1:-1] * (lumped[1 : nodes + 7] * weight)[None, :]
    stiff_part = restrict @ (stiff[: nodes + 8, 1 : nodes + 7] * weight[None, :])
    return dict(
        own_stiff=stiff[7 : nodes + 8, 7 : nodes + 7],
        mass=lumped[1 : nodes + 7],
        own=restrict[:, 7:-1],
        mass_part=mass_part,
        stiff_part=stiff_part,
    )


def rows_by_node(s, matrix, every_copy):
    used = s.node_of_lane >= 0 if every_copy else s.first_copy
    return np.where(used[:, None], matrix[np.maximum(s.node_of_lane, 0)], 0.0)


def two_parts(matrix):
    high_part = matrix.astype(np.float32).astype(jnp.bfloat16)
    low_part = (matrix - high_part.astype(np.float64)).astype(jnp.bfloat16)
    return high_part, low_part


def residual_constants(s, low):
    line_x = line_tables(s.x_elems)
    stiff_z, lumped_z = assemble_line(s.z_elems)
    stiff_z, lumped_z = (stiff_z[: s.z_nodes, : s.z_nodes], lumped_z[: s.z_nodes])
    rows = s.own_rows - low
    mass_x = np.zeros(s.own_rows)
    mass_x[: s.x_nodes] = line_x["mass"][6:]
    mass_x = mass_x[low:]
    mass_z = rows_by_node(s, lumped_z[:, None], True)[:, 0]
    spread = np.ones((rows, s.lanes))
    stiff = rows_by_node(s, stiff_z, False)
    stiff = rows_by_node(s, stiff.T, True).T
    own_x = placed(line_x["own_stiff"], (s.own_rows, s.own_rows)).astype(np.float64)
    high_x, low_x = two_parts(own_x[low:, low:])
    table = np.concatenate(
        [
            stiff,
            spread * mass_x[:, None],
            spread * mass_z[None, :],
            mass_x[:, None] * mass_z[None, :],
        ]
    )
    return [
        jnp.asarray(table, f32),
        jnp.asarray(np.concatenate([high_x, high_x, low_x], 1), jnp.bfloat16),
    ]


def coupling_constants(s):
    stiffness = element_stiffness()
    lumped_z = assemble_line(s.z_elems)[1][: s.z_nodes]
    mass_z = rows_by_node(s, lumped_z[:, None], True)[:, 0]
    below, above = (np.zeros(s.rows), np.zeros(s.rows))
    below[2:8] = stiffness[1:7, 7]
    above[8 + s.x_nodes - 7 : 8 + s.x_nodes] = stiffness[:7, 7]
    return [below[:, None] * mass_z[None, :], above[:, None] * mass_z[None, :]]


def patch_constants(s):
    line_x = line_tables(s.x_elems)
    stiff_z, lumped_z = assemble_line(s.z_elems)
    stiff_z, lumped_z = (stiff_z[: s.z_nodes, : s.z_nodes], lumped_z[: s.z_nodes])
    weight_z = np.where(np.arange(s.z_nodes) % 7 == 0, 1.0, 0.5)
    restrict_z = restriction_line(s.z_elems, points_three)[: s.coarse_z, : s.z_nodes]
    eigvals, eigbasis = patch_basis()
    mass_z = rows_by_node(s, lumped_z[:, None], True)[:, 0]
    mass_x = np.zeros(s.rows)
    mass_x[2 : s.x_nodes + 8] = line_x["mass"]
    fwd_x = placed(
        patch_matrix(eigbasis, s.x_elems, s.x_nodes + 6), (s.modes_x, s.rows), col=2
    )
    high_x, low_x = two_parts(fwd_x.astype(np.float64))
    fwd_z = np.zeros((LANES, s.modes_z))
    fwd_z[:, : 13 * s.half_z] = patch_matrix(eigbasis, s.half_z, LANES).T
    high_z, low_z = two_parts(fwd_z)
    sums = np.ones((s.modes_x, s.modes_z))
    sums[: 13 * s.x_elems, : 13 * s.half_z] = (
        np.repeat(eigvals, s.x_elems)[:, None] + np.repeat(eigvals, s.half_z)[None, :]
    )
    coarse_of_z = np.zeros((s.z_nodes, 2 * s.coarse_lanes))
    coarse_of_z[:, : s.coarse_z] = (restrict_z * (lumped_z * weight_z)[None, :]).T
    coarse_of_z[:, s.coarse_lanes : s.coarse_lanes + s.coarse_z] = (
        restrict_z @ (stiff_z * weight_z[None, :])
    ).T
    coarse_of_x = np.zeros((2 * s.coarse_rows, s.rows))
    coarse_of_x[: s.coarse_x, 2 : s.x_nodes + 8] = line_x["mass_part"]
    coarse_of_x[s.coarse_rows : s.coarse_rows + s.coarse_x, 2 : s.x_nodes + 8] = line_x[
        "stiff_part"
    ]
    own_z = np.zeros((s.z_nodes, s.coarse_lanes))
    own_z[:, : s.coarse_z] = restrict_z.T
    one_z = placed(
        linear_from_cubic(0, s.z_elems - 1, 0, s.coarse_z - 1).T,
        (s.coarse_lanes, LANES),
        col=s.coarse_z,
    )
    one_x = placed(linear_from_cubic(-1, s.x_elems, -3, 3 * s.x_elems), (8, s.coarse_rows))
    singles = [
        mass_x[:, None] * mass_z[None, :],
        sums,
        rows_by_node(s, coarse_of_z, True),
        rows_by_node(s, own_z, False),
        one_z,
        one_x,
    ]
    own_x = placed(line_x["own"], (s.coarse_rows, s.rows), col=8).astype(np.float64)
    high_q, low_q = two_parts(coarse_of_x)
    high_r, low_r = two_parts(own_x)
    halves = [
        np.concatenate([high_q, high_q, low_q], 1),
        np.concatenate([high_r, high_r, low_r], 1),
        np.concatenate([high_x, high_x, low_x], 1),
        np.concatenate([high_x.T, high_x.T, low_x.T], 1),
        np.concatenate([high_z, high_z], 0),
        low_z,
        np.concatenate([high_z.T, low_z.T], 1),
        high_z.T,
    ]
    return (
        [jnp.asarray(eigvals, f32)]
        + [jnp.asarray(value, f32) for value in singles]
        + [jnp.asarray(value, jnp.bfloat16) for value in halves]
    )


def halves_of(value):
    high_part = value.astype(jnp.bfloat16)
    return high_part, (value - high_part.astype(f32)).astype(jnp.bfloat16)


def stacked_rows(value):
    high_part = value.astype(jnp.bfloat16).astype(f32)
    return jnp.concatenate([high_part, value - high_part, high_part], 0).astype(jnp.bfloat16)


def dot(left, right):
    return lax.dot_general(left, right, (((1,), (0,)), ((), ())), preferred_element_type=f32)


def linear_from_cubic(first, last, first_three, last_three):
    result = np.zeros((last - first + 1, last_three - first_three + 1))
    for m in range(first, last + 1):
        for offset, factor in (
            (0, 1.0),
            (1, (1.0 - points_three[1]) / 2.0),
            (2, (1.0 - points_three[2]) / 2.0),
            (-2, (1.0 + points_three[1]) / 2.0),
            (-1, (1.0 + points_three[2]) / 2.0),
        ):
            node = 3 * m + offset - first_three
            if 0 <= node < result.shape[1]:
                result[m - first, node] = factor
    return result


def line_of_planes(coefficients, planes):
    total = None
    for coefficient, plane in zip(coefficients, planes):
        if coefficient != 0.0:
            part = plane() * float(coefficient)
            total = part if total is None else total + part
    return total


def symmetric(vector):
    return abs(vector[0] - vector[-1]) < abs(vector[0] + vector[-1])


def lane_window(ref, start, width):
    if start < 0:
        return pltpu.roll(ref[:, 0:LANES], -start, 1)
    if start + LANES > width:
        return pltpu.roll(ref[:, width - LANES : width], width - start, 1)
    return ref[:, start : start + LANES]


def lane_mask(s, shape, first):
    lane = lax.broadcasted_iota(jnp.int32, shape, 1)
    return ((lane >= 6 + first) & (lane < 6 + s.split)) | (
        (lane >= LANES) & (lane < LANES + s.split + 6)
    )


def put_line(s, ref, index, plane):
    at = s.z_nodes * index
    rows = plane.shape[0]
    ref[0:rows, at : at + s.split] = plane[:, 6 : 6 + s.split]
    ref[0:rows, at + s.split : at + 2 * s.split] = plane[:, LANES + 6 : LANES + 6 + s.split]


def get_line(s, ref, index, width):
    at = s.z_nodes * index
    return jnp.concatenate(
        [lane_window(ref, at - 6, width), lane_window(ref, at + s.split - 6, width)], 1
    )


def own_residual(s, low, first_copies, u, r, guess, load, table, k_x):
    lanes = s.lanes
    rows = s.own_rows - low
    ey, ny = (s.y_elems, s.y_nodes)
    nx = s.x_nodes - low
    width = ny * s.z_nodes
    mass_y = line_tables(ey)["mass"][6:]
    stiffness = element_stiffness()
    gx = lax.axis_index("gx")
    gy = lax.axis_index("gy")
    shape = (nx, lanes)
    row = lax.broadcasted_iota(jnp.int32, shape, 0) + low
    live = (lane_mask(s, shape, 1) & ((row != 0) | (gx > 0))).astype(f32)
    live_y = (gy > 0).astype(f32)
    inside = lane_mask(s, shape, 0).astype(f32)
    pad = jnp.zeros((rows - nx, lanes), f32)
    first_copies[0].wait()
    for y in range(ny):
        mask = live if y else live * live_y
        u[y, 0:nx] = get_line(s, guess, y, width) * mask
        u[y, nx:] = pad
    first_copies[1].wait()
    for y in range(ny):
        r[y, 0:nx] = get_line(s, load, y, width) * inside
        r[y, nx:] = pad
    u[ny] = jnp.zeros((rows, lanes), f32)
    r[ny] = jnp.zeros((rows, lanes), f32)
    for copy in first_copies[2:]:
        copy.wait()
    m_x, m_z, m_xz = [
        table.at[lanes + rows * i : lanes + rows * (i + 1)] for i in range(3)
    ]
    z_term = mm(u[0:ny].reshape(ny * rows, lanes), table[0:lanes]).reshape(ny, rows, lanes)
    for y in range(ny):
        x_term = dot(k_x[...], stacked_rows(u[y]))
        both = x_term * m_z[...] + z_term[y] * m_x[...]
        r[y] = r[y] - float(mass_y[y]) * both

    def along_y(tile, carry):
        at = pl.ds(pl.multiple_of(tile * 8, 8), 8)
        scale = m_xz[at, :]
        corner = None
        for e in range(ey):
            nodes = [u[7 * e + i, at, :] for i in range(8)]
            plus = [nodes[i] + nodes[7 - i] for i in range(4)]
            minus = [nodes[i] - nodes[7 - i] for i in range(4)]
            out = [None] * 8
            for i in range(4):
                even = sum(
                    plus[k] * float(0.5 * (stiffness[i, k] + stiffness[i, 7 - k]))
                    for k in range(4)
                )
                odd = sum(
                    minus[k] * float(0.5 * (stiffness[i, k] - stiffness[i, 7 - k]))
                    for k in range(4)
                )
                out[i], out[7 - i] = (even + odd, even - odd)
            if e:
                out[0] = out[0] + corner
            else:
                out[0] = out[0] + nodes[0] * float(stiffness[7, 7])
            corner = out[7]
            for i in range(8 if e == ey - 1 else 7):
                plane = 7 * e + i
                r[plane, at, :] = r[plane, at, :] - out[i] * scale
        return carry

    lax.fori_loop(0, rows // 8, along_y, 0)


def started(sources, targets, sems):
    copies = [
        pltpu.make_async_copy(source, target, sems.at[index])
        for index, (source, target) in enumerate(zip(sources, targets))
    ]
    for copy in copies:
        copy.start()
    return copies


def send_kernel(s):
    low = (s.x_nodes - 7) // 8 * 8
    lanes, nx, ny = (s.lanes, s.x_nodes, s.y_nodes)
    width = ny * s.z_nodes

    def kernel(
        guess_hbm, load_hbm, table_hbm, k_x_hbm,
        up_out, down_out,
        u, r, guess, load, table, k_x, top, sems,
    ):
        sources = [guess_hbm.at[low:nx], load_hbm.at[low:nx], table_hbm, k_x_hbm]
        sources += [guess_hbm.at[0:8]]
        copies = started(sources, [guess, load, table, k_x, top], sems)
        own_residual(s, low, copies[:4], u, r, guess, load, table, k_x)
        up_out[6:8, :] = jnp.zeros((2, up_out.shape[1]), f32)
        for y in range(ny + 1):
            put_line(s, up_out, y, r[y, nx - 6 - low : nx + 1 - low, :])
        put_line(s, up_out, ny + 1, u[0, nx - 6 - low : nx - low, :])
        copies[4].wait()
        gx = lax.axis_index("gx")
        gy = lax.axis_index("gy")
        live = lane_mask(s, (1, lanes), 1).astype(f32) * (gx > 0).astype(f32)
        live_y = (gy > 0).astype(f32)
        for y in range(ny):
            mask = live if y else live * live_y
            down_out[y : y + 1, :] = get_line(s, top, y, width)[0:1] * mask
        down_out[ny:, :] = jnp.zeros((down_out.shape[0] - ny, lanes), f32)

    return kernel


def residual_kernel(s):
    def kernel(
        guess_hbm, load_hbm, table_hbm, k_x_hbm,
        r, edge,
        u, guess, load, table, k_x, sems,
    ):
        sources = [guess_hbm, load_hbm, table_hbm, k_x_hbm]
        copies = started(sources, [guess, load, table, k_x], sems)
        own_residual(s, 0, copies, u, r, guess, load, table, k_x)
        edge[...] = u[0]

    return kernel


def joined_x_kernel(s):
    rows, lanes = (s.rows, s.lanes)
    nx, ny = (s.x_nodes, s.y_nodes)
    mass_y = line_tables(s.y_elems)["mass"][6:]

    def kernel(r_own, edge, u_first, below, above, c_below, c_above, r, line, up_out):
        width = below.shape[1]
        shape = (8, lanes)
        row = lax.broadcasted_iota(jnp.int32, shape, 0)
        inside = lane_mask(s, shape, 0)
        keep = (inside & (row < 6)).astype(f32)
        only = (inside & (row == 6)).astype(f32)
        zero = jnp.zeros((rows - 8 - nx, lanes), f32) if rows - 8 - nx else None
        for y in range(ny + 2):
            got = get_line(s, below, y, width)
            place = line if y == ny + 1 else r.at[y]
            own = edge[0:nx] if y == ny + 1 else r_own[y, 0:nx, :]
            place[0:2, :] = jnp.zeros((2, lanes), f32)
            place[2:8, :] = (got * keep)[0:6]
            place[8 : 8 + nx, :] = own
            if zero is not None:
                place[8 + nx :, :] = zero
            if y < ny:
                place[8:9, :] += (got * only)[6:7]
                both = (
                    c_below[...] * u_first[y : y + 1, :] + c_above[...] * above[y : y + 1, :]
                ) * float(mass_y[y])
                place[...] = place[...] - both
        for j in range(7):
            put_line(s, up_out, j, r[ny - 6 + j])
        up_out[:, 7 * s.z_nodes :] = jnp.zeros((rows, up_out.shape[1] - 7 * s.z_nodes), f32)

    return kernel


def patch_kernel(s):
    rows, lanes = (s.rows, s.lanes)
    ey, ny = (s.y_elems, s.y_nodes)
    line_y = line_tables(ey)
    _, eigbasis = patch_basis()
    stiffness = element_stiffness()
    one_y = linear_from_cubic(-1, ey, -3, 3 * ey)
    evens = [b for b in range(13) if symmetric(eigbasis[:, b])]
    odds = [b for b in range(13) if b not in evens]

    def kernel(
        r_own, line, below, above,
        lam, m_xz, sums, q_z, r_z, o_z, o_x, q_x, r_x, f_x, b_x, f_z, f_z_low, b_z, b_z_high,
        edge_out, own_out, three_out, one_out, down_out, up_out,
        r, xf, xb, c, cz, rz, hx, ex, rx, live,
    ):
        gx = lax.axis_index("gx")
        gy = lax.axis_index("gy")
        inside = lane_mask(s, (rows, lanes), 0).astype(f32)
        width = below.shape[1]
        lower = line[...] * m_xz[...]
        upper = above[...] * m_xz[...]
        for j in range(7):
            got = get_line(s, below, j, width) * inside
            if j < 6:
                r[j] = got - lower * float(stiffness[1 + j, 7])
            else:
                r[6] = r_own[0] + got
        for y in range(1, ny):
            plane = r_own[y]
            if y >= ny - 7:
                plane = plane - upper * float(stiffness[y - (ny - 7), 7])
            r[6 + y] = plane
        shape = (s.modes_x, s.modes_z)
        mode = lax.broadcasted_iota(jnp.int32, shape, 0)
        vertex = lax.broadcasted_iota(jnp.int32, shape, 1) % s.half_z
        live_x = (mode % s.x_elems != 0) | (gx > 0)
        live[0] = (live_x & (vertex != 0)).astype(f32)
        live[1] = live_x.astype(f32)
        active = (gy > 0).astype(f32)

        def along_y(tile, carry):
            at = pl.ds(pl.multiple_of(tile * 8, 8), 8)
            for v in range(ey):
                first = [r[7 * v + a, at, :] for a in range(13)]
                if v == 0:
                    first = [value * active for value in first]
                even = [first[6]] + [first[6 + a] + first[6 - a] for a in range(1, 7)]
                odd = [first[6 + a] - first[6 - a] for a in range(1, 7)]
                for b in range(13):
                    if b in evens:
                        xf[b, v, at, :] = sum(
                            even[a] * float(eigbasis[6 + a, b]) for a in range(7)
                        )
                    else:
                        xf[b, v, at, :] = sum(
                            odd[a] * float(eigbasis[7 + a, b]) for a in range(6)
                        )
            return carry

        lax.fori_loop(0, rows // 8, along_y, 0)

        def spectral(modes_of):
            pieces = []
            for b in modes_of:
                planes = [dot(f_x[...], stacked_rows(xf[b, v])) for v in range(ey)]
                pieces += [plane[:, :LANES] for plane in planes]
                pieces += [plane[:, LANES:] for plane in planes]
            high_part, low_part = halves_of(jnp.concatenate(pieces, 0))
            modes = dot(jnp.concatenate([high_part, low_part], 1), f_z[...]) + dot(
                high_part, f_z_low[...]
            )
            modes = modes.reshape(len(modes_of), 2, ey, s.modes_x, s.modes_z)
            pieces = []
            for i, b in enumerate(modes_of):
                factor = 1.0 / (sums[...] + lam[b])
                for t in range(2):
                    scaled = modes[i, t] * (factor * live[t])[None]
                    pieces.append(scaled.reshape(ey * s.modes_x, s.modes_z))
            high_part, low_part = halves_of(jnp.concatenate(pieces, 0))
            both = dot(high_part, b_z[...])
            back = both[:, :LANES] + both[:, LANES:] + dot(low_part, b_z_high[...])
            back = back.reshape(len(modes_of), 2, ey, s.modes_x, LANES)
            for i, b in enumerate(modes_of):
                for v in range(ey):
                    plane = jnp.concatenate([back[i, 0, v], back[i, 1, v]], 1)
                    xb[b, v] = dot(b_x[...], stacked_rows(plane))

        for first in range(0, 13, GROUP):
            spectral(range(first, min(13, first + GROUP)))

        def back_y(tile, carry):
            at = pl.ds(pl.multiple_of(tile * 8, 8), 8)
            tail = None
            for v in range(ey):
                modes = [xb[b, v, at, :] for b in range(13)]
                out = [None] * 13
                for a in range(7):
                    even = sum(modes[b] * float(eigbasis[6 + a, b]) for b in evens)
                    if a == 0:
                        out[6] = even
                        continue
                    odd = sum(modes[b] * float(eigbasis[6 + a, b]) for b in odds)
                    out[6 + a], out[6 - a] = (even + odd, even - odd)
                if v:
                    out[:6] = [value + other for value, other in zip(out[:6], tail)]
                tail = out[7:]
                for a in range(13 if v == ey - 1 else 7):
                    c[7 * v + a, at, :] = out[a]
            return carry

        lax.fori_loop(0, rows // 8, back_y, 0)

        for j in range(6):
            down_out[:, lanes * j : lanes * (j + 1)] = c[j]
        edge_out[...] = c[6:, 0:8, :]
        own_out[...] = c[6:, 8:, :]

        half = s.coarse_lanes
        rows_c = s.coarse_rows
        cz[...] = mm(c[...].reshape((ny + 6) * rows, lanes), q_z[...]).reshape(
            ny + 6, rows, 2 * half
        )
        rz[...] = mm(r[6 : ny + 6].reshape(ny * rows, lanes), r_z[...]).reshape(ny, rows, half)
        for y in range(ny + 6):
            plane = dot(q_x[...], stacked_rows(cz[y]))
            hx[y] = plane[:rows_c, :half]
            ex[y] = plane[rows_c:, :half] + plane[:rows_c, half:]
        for y in range(ny):
            rx[y] = dot(r_x[...], stacked_rows(rz[y]))
        for j in range(s.coarse_y):
            three_out[j] = line_of_planes(
                np.concatenate(
                    [line_y["own"][j], -line_y["stiff_part"][j], -line_y["mass_part"][j]]
                ),
                [lambda y=y: rx[y] for y in range(ny)]
                + [lambda y=y: hx[y] for y in range(ny + 6)]
                + [lambda y=y: ex[y] for y in range(ny + 6)],
            )
        one_all = mm(
            three_out[...].reshape(s.coarse_y * rows_c, half), o_z[...]
        ).reshape(s.coarse_y, rows_c, LANES)
        for m in range(ey + 2):
            mixed = line_of_planes(
                one_y[m], [lambda j=j: one_all[j] for j in range(s.coarse_y)]
            )
            one_out[m] = mm(o_x[...], mixed)
        base = 6 * lanes
        down_out[:, base:] = jnp.zeros((rows, 2 * half), f32)
        up_out[...] = jnp.zeros(up_out.shape, f32)
        up_out[:, 0:half] = three_out[s.coarse_y - 1]
        for j in range(4):
            first, at = (rows_c * (j % 2), base + half * (j // 2))
            if j < 3:
                down_out[first : first + rows_c, at : at + half] = three_out[j]
            down_out[first : first + 8, at : at + half] += one_out[j]
            up_out[0:8, half * j : half * (j + 1)] += one_out[ey - 2 + j]

    return kernel


def coarse_place(s, index):
    high_rows = coarse_height(s)
    return index % high_rows, LANES * (index // high_rows)


def coarse_height(s):
    return up_to(-(-max(9 * s.y_elems, 4 * s.y_elems + 24) // 2), 24)


def join_kernel(s):
    lanes, half, rows_c = (s.lanes, s.coarse_lanes, s.coarse_rows)
    ey, ny = (s.y_elems, s.y_nodes)

    def kernel(edge, three, one, down, up, down_out, up_out, three_out, one_out):
        lane = lax.broadcasted_iota(jnp.int32, (rows_c, half), 1)
        is_three = (lane < s.coarse_z).astype(f32)
        is_one = (lane >= s.coarse_z).astype(f32)[0:8]
        for y in range(ny):
            plane = edge[y]
            if y >= ny - 6:
                j = y - (ny - 6)
                plane = plane + down[0:8, lanes * j : lanes * (j + 1)]
            down_out[6 * y : 6 * y + 6, :] = plane[2:8]
        base = 6 * lanes
        first = 6 * ny
        down_out[first:, :] = jnp.zeros((down_out.shape[0] - first, lanes), f32)
        up_out[...] = jnp.zeros(up_out.shape, f32)

        def from_above(k, count):
            row, at = (rows_c * (k % 2), base + half * (k // 2))
            return down[row : row + count, at : at + half]

        for j in range(3 * ey):
            plane = three[3 + j]
            if j >= 3 * ey - 3:
                plane = plane + from_above(j - (3 * ey - 3), rows_c)
            if j == 0:
                plane = plane + up[0:rows_c, 0:half]
            plane = plane * is_three
            three_out[j] = plane
            row, at = coarse_place(s, 3 * j)
            down_out[first + row : first + row + 3, at : at + half] = plane[0:3]
            row, at = coarse_place(s, j)
            up_out[row : row + 1, at : at + half] = plane[s.coarse_x - 1 : s.coarse_x]
        for j in range(ey + 6):
            y = j - 3
            plane = None
            if -1 <= y <= ey:
                plane = one[y + 1]
            if y <= 0:
                k = y + 3
                part = up[0:8, half * k : half * (k + 1)]
                plane = part if plane is None else plane + part
            if y >= ey - 1:
                part = from_above(y - (ey - 1), 8)
                plane = part if plane is None else plane + part
            plane = plane * is_one
            one_out[j] = plane
            row, at = coarse_place(s, 4 * j)
            down_out[first + row : first + row + 4, at : at + half] += plane[0:4]
            up_out[row : row + 4, at : at + half] += plane[s.x_elems - 2 : s.x_elems + 2]

    return kernel


def shared_lanes(s, shape):
    lane = lax.broadcasted_iota(jnp.int32, shape, 1)
    return ((lane >= s.split) & (lane < s.split + 6)).astype(f32)


def base_kernel(s):
    lanes, nx, ny = (s.lanes, s.x_nodes, s.y_nodes)
    width = ny * s.z_nodes

    def kernel(guess, weight, own, down, out):
        gx = lax.axis_index("gx")
        gy = lax.axis_index("gy")
        shape = (nx, lanes)
        row = lax.broadcasted_iota(jnp.int32, shape, 0)
        live = (lane_mask(s, shape, 1) & ((row != 0) | (gx > 0))).astype(f32)
        live_y = (gy > 0).astype(f32)
        shared = shared_lanes(s, shape)
        for y in range(ny):
            plane = own[y, 0:nx, :]
            if y >= ny - 6:
                j = y - (ny - 6)
                plane = plane + down[8 : 8 + nx, lanes * j : lanes * (j + 1)]
            plane = plane + pltpu.roll(plane, lanes - (LANES - s.split), 1) * shared
            mask = live if y else live * live_y
            factor = weight[...] * (1.0 if y % 7 == 0 else 0.5)
            put_line(s, out, y, (get_line(s, guess, y, width) + factor * plane) * mask)

    return kernel


def finish_kernel(s, x_total, y_total):
    lanes, half, rows_c, nz = (s.lanes, s.coarse_lanes, s.coarse_rows, s.z_nodes)
    ex, ey, nx, ny = (s.x_elems, s.y_elems, s.x_nodes, s.y_nodes)
    one_rows = up_to(ex + 6, 8)
    split = s.split

    def kernel(
        base, weight, right, left, three, one,
        smooth_out, three_out, coarse_out, fine, level,
    ):
        gx = lax.axis_index("gx")
        gy = lax.axis_index("gy")
        live_y = (gy > 0).astype(f32)
        shared = shared_lanes(s, (6, lanes))
        smooth_out[...] = base[...]
        for y in range(ny):
            plane = right[6 * y : 6 * y + 6, :]
            plane = plane + pltpu.roll(plane, lanes - (LANES - split), 1) * shared
            plane = plane * weight[nx - 6 : nx, :] * (1.0 if y % 7 == 0 else 0.5)
            for t in range(2):
                at = nz * y + split * t
                lanes_at = LANES * t + 6
                smooth_out[nx - 6 : nx, at : at + split] += plane[:, lanes_at : lanes_at + split]
        first = 6 * ny
        nzc = s.coarse_z
        lane = lax.broadcasted_iota(jnp.int32, (3 * ex, nzc), 1)
        row = lax.broadcasted_iota(jnp.int32, (3 * ex, nzc), 0)
        live = ((lane >= 1) & ((row >= 1) | (gx > 0))).astype(f32)
        for j in range(3 * ey):
            fine[j] = three[j]
            at_row, at = coarse_place(s, 3 * j)
            at_row += first
            fine[j, 3 * ex : 3 * ex + 3, :] += right[at_row : at_row + 3, at : at + half]
            at_row, at = coarse_place(s, j)
            fine[j, 3:4, :] += left[at_row : at_row + 1, at : at + half]
            mask = live if j else live * live_y
            three_out[:, nzc * j : nzc * (j + 1)] = fine[j, 3 : 3 * ex + 3, 0:nzc] * mask
        level[...] = jnp.zeros((ey + 6, one_rows, LANES), f32)
        for j in range(ey + 6):
            level[j, 2 : ex + 4, :] = one[j, 0 : ex + 2, :]
            at_row, at = coarse_place(s, 4 * j)
            level[j, 0:4, :] += left[at_row : at_row + 4, at : at + half]
            at_row += first
            level[j, ex + 2 : ex + 6, :] += right[at_row : at_row + 4, at : at + half]
        shape = (one_rows, LANES)
        lane = lax.broadcasted_iota(jnp.int32, shape, 1)
        row = lax.broadcasted_iota(jnp.int32, shape, 0)
        global_x = gx * ex + row - 3
        plane_mask = (
            (lane > s.coarse_z) & (lane < s.coarse_z + s.z_elems) & (row < ex + 6)
            & (global_x >= 1) & (global_x < x_total)
        )
        masks = []
        for j in range(ey + 6):
            global_y = gy * ey + (j - 3)
            inside = (global_y >= 1) & (global_y < y_total)
            masks.append((plane_mask & inside).astype(f32))
        levels = [level[j] for j in range(ey + 6)]
        error = [damping / 12.0 * a * m for a, m in zip(levels, masks)]
        zero = jnp.zeros(shape, f32)
        for sweep in range(1, JAC):
            lower = [zero] + error[:-1]
            upper = error[1:] + [zero]
            fresh = []
            for j in range(ey + 6):
                here = error[j]
                neighbours = (
                    lower[j]
                    + upper[j]
                    + pltpu.roll(here, 1, 0)
                    + pltpu.roll(here, one_rows - 1, 0)
                    + pltpu.roll(here, 1, 1)
                    + pltpu.roll(here, LANES - 1, 1)
                )
                applied = 12.0 * here - 2.0 * neighbours
                fresh.append((here + damping / 12.0 * (levels[j] - applied)) * masks[j])
            error = fresh
        nze = s.z_elems
        for j in range(ey):
            coarse_out[:, nze * j : nze * (j + 1)] = error[3 + j][
                3 : 3 + ex, s.coarse_z : s.coarse_z + nze
            ]

    return kernel


def local(load_vector, initial_guess):
    z_nodes = 7 * EZ
    x_nodes = load_vector.shape[0]
    y_nodes = load_vector.shape[1] // z_nodes
    s = Sizes(x_nodes, y_nodes, z_nodes)
    rows, lanes, half = (s.rows, s.lanes, s.coarse_lanes)
    ny, ey = (s.y_nodes, s.y_elems)
    width = y_nodes * z_nodes
    shape = lambda *dims: jax.ShapeDtypeStruct(dims, f32)
    params = pltpu.CompilerParams(vmem_limit_bytes=36 * 2**20)
    vmem = lambda count: [pl.BlockSpec(memory_space=pltpu.VMEM)] * count

    def call(kernel, name, outputs, operands, scratch=(), spaces=None, semaphores=0):
        specs = vmem(len(operands))
        for index, space in (spaces or {}).items():
            specs[index] = pl.BlockSpec(memory_space=space)
        return pl.pallas_call(
            kernel,
            out_shape=tuple(shape(*dims) for dims in outputs),
            in_specs=specs,
            out_specs=tuple(vmem(len(outputs))),
            scratch_shapes=[pltpu.VMEM(d, f32) if isinstance(d, tuple) else d for d in scratch]
            + ([pltpu.SemaphoreType.DMA((semaphores,))] if semaphores else []),
            compiler_params=params,
            name=name,
        )(*operands)

    in_hbm = lambda values: [pltpu.with_memory_space_constraint(v, pltpu.HBM) for v in values]
    hbm = {index: pltpu.HBM for index in range(4)}
    low = (x_nodes - 7) // 8 * 8
    constants = residual_constants(s, low)
    up, u_first = call(
        send_kernel(s),
        "send",
        ((8, up_to((ny + 2) * z_nodes, LANES)), (up_to(ny, 8), lanes)),
        in_hbm([initial_guess, load_vector] + constants),
        [
            (ny + 1, s.own_rows - low, lanes),
            (ny + 1, s.own_rows - low, lanes),
            (x_nodes - low, width),
            (x_nodes - low, width),
            constants[0].shape,
            pltpu.VMEM(constants[1].shape, jnp.bfloat16),
            (8, width),
        ],
        spaces=hbm,
        semaphores=5,
    )
    below = shifted(up, "gx", 1)
    above = shifted(u_first, "gx", -1)
    constants = residual_constants(s, 0)
    r_own, edge = call(
        residual_kernel(s),
        "residual",
        ((ny + 1, s.own_rows, lanes), (s.own_rows, lanes)),
        in_hbm([initial_guess, load_vector] + constants),
        [
            (ny + 1, s.own_rows, lanes),
            initial_guess.shape,
            load_vector.shape,
            constants[0].shape,
            pltpu.VMEM(constants[1].shape, jnp.bfloat16),
        ],
        spaces=hbm,
        semaphores=4,
    )
    r_x, line, up = call(
        joined_x_kernel(s),
        "joined_x",
        (
            (ny + 1, rows, lanes),
            (rows, lanes),
            (rows, up_to(7 * z_nodes, LANES)),
        ),
        [r_own, edge, u_first, below, above]
        + [jnp.asarray(v, f32) for v in coupling_constants(s)],
    )
    below = shifted(up, "gy", 1)
    above = shifted(line, "gy", -1)
    edge, own, three, one, down, up = call(
        patch_kernel(s),
        "patches",
        (
            (ny, 8, lanes),
            (ny, rows - 8, lanes),
            (s.coarse_y, s.coarse_rows, half),
            (ey + 2, 8, LANES),
            (rows, 6 * lanes + 2 * half),
            (s.coarse_rows, 4 * half),
        ),
        [r_x, line, below, above] + patch_constants(s),
        [
            (ny + 6, rows, lanes),
            (13, ey, rows, lanes),
            (13, ey, rows, lanes),
            (ny + 6, rows, lanes),
            (ny + 6, rows, 2 * half),
            (ny, rows, half),
            (ny + 6, s.coarse_rows, half),
            (ny + 6, s.coarse_rows, half),
            (ny, s.coarse_rows, half),
            (2, s.modes_x, s.modes_z),
        ],
        spaces={4: pltpu.SMEM},
    )
    down = shifted(down, "gy", -1)
    up = shifted(up, "gy", 1)
    right, left, three, one = call(
        join_kernel(s),
        "join",
        (
            (6 * ny + coarse_height(s), lanes),
            (coarse_height(s), lanes),
            (3 * ey, s.coarse_rows, half),
            (ey + 6, 8, LANES),
        ),
        [edge, three, one, down, up],
    )
    right = shifted(right, "gx", -1)
    left = shifted(left, "gx", 1)
    weight_z = np.where(np.arange(z_nodes) % 7 == 0, 1.0, 0.5)
    weight = jnp.asarray(
        np.where(np.arange(x_nodes) % 7 == 0, 1.0, 0.5)[:, None]
        * rows_by_node(s, weight_z[:, None], True)[:, 0],
        f32,
    )
    (base,) = call(
        base_kernel(s), "base", ((x_nodes, width),), [initial_guess, weight, own, down]
    )
    return call(
        finish_kernel(s, s.x_elems * lax.axis_size("gx"), ey * lax.axis_size("gy")),
        "finish",
        (
            (x_nodes, width),
            (3 * s.x_elems, 3 * ey * s.coarse_z),
            (s.x_elems, ey * s.z_elems),
        ),
        [base, weight, right, left, three, one],
        [
            (3 * ey, s.coarse_rows, half),
            (ey + 6, up_to(s.x_elems + 6, 8), LANES),
        ],
    )


def solution(mesh):
    in_specs = (P("gx", "gy"), P("gx", "gy"))
    out_specs = (P("gx", "gy"), P("gx", "gy"), P("gx", "gy"))
    return jax.shard_map(local, mesh=mesh, in_specs=in_specs, out_specs=out_specs, check_vma=False)
```

```python
import math

import jax
import jax.numpy as jnp
import numpy as np
from jax import lax
from jax.experimental import pallas as pl
from jax.experimental.pallas import tpu as pltpu
from jax.sharding import PartitionSpec as P

EZ = 32
JAC = 4


points_seven = (
    -1.0,
    -0.8717401485096066,
    -0.5917001814331423,
    -0.2092992179024789,
    0.2092992179024789,
    0.5917001814331423,
    0.8717401485096066,
    1.0,
)
points_three = (-1.0, -0.4472135954999579, 0.4472135954999579, 1.0)
points_one = (-1.0, 1.0)
damping = 2.0 / 3.0


def shifted(array, axis, by):
    devices = lax.axis_size(axis)
    pairs = [(i, i + by) for i in range(devices) if 0 <= i + by < devices]
    return lax.ppermute(array, axis, pairs)


def legendre_at(degree, location):
    previous, current = (1.0, location)
    for level_idx in range(1, degree):
        previous, current = (
            current,
            ((2 * level_idx + 1) * location * current - level_idx * previous) / (level_idx + 1),
        )
    return current


def quadrature_weights():
    return np.array([2.0 / (56.0 * legendre_at(7, x) * legendre_at(7, x)) for x in points_seven])


def derivative_matrix():
    points = np.array(points_seven)
    products = np.array(
        [np.prod([points[i] - points[k] for k in range(8) if k != i]) for i in range(8)]
    )
    result = np.zeros((8, 8))
    for i in range(8):
        for j in range(8):
            if i != j:
                result[i, j] = products[i] / (products[j] * (points[i] - points[j]))
        result[i, i] = np.sum([1.0 / (points[i] - points[k]) for k in range(8) if k != i])
    return result


def element_stiffness():
    derivative = derivative_matrix()
    return derivative.T @ (quadrature_weights()[:, None] * derivative)


def assemble_line(elements):
    stiffness = element_stiffness()
    weights = quadrature_weights()
    extent = 7 * elements + 1
    global_stiff = np.zeros((extent, extent))
    lumped = np.zeros(extent)
    for m in range(elements):
        global_stiff[7 * m : 7 * m + 8, 7 * m : 7 * m + 8] += stiffness
        lumped[7 * m : 7 * m + 8] += weights
    return (global_stiff, lumped)


def jacobi_eigen(matrix):
    rotated_mat = matrix.copy()
    extent = matrix.shape[0]
    vectors = np.eye(extent)
    for sweep_idx in range(12):
        for p in range(extent - 1):
            for q in range(p + 1, extent):
                angle_rot = 0.5 * math.atan2(
                    2.0 * float(rotated_mat[p, q]), float(rotated_mat[q, q] - rotated_mat[p, p])
                )
                rotation = np.eye(extent)
                rotation[p, p] = math.cos(angle_rot)
                rotation[q, q] = math.cos(angle_rot)
                rotation[p, q] = math.sin(angle_rot)
                rotation[q, p] = -math.sin(angle_rot)
                rotated_mat = rotation.T @ rotated_mat @ rotation
                vectors = vectors @ rotation
    return (np.array([rotated_mat[i, i] for i in range(extent)]), vectors)


def patch_basis():
    global_stiff, lumped = assemble_line(2)
    inv_root = 1.0 / np.sqrt(lumped[1:14])
    eigvals, vectors = jacobi_eigen(
        inv_root[:, None] * global_stiff[1:14, 1:14] * inv_root[None, :]
    )
    return (eigvals, inv_root[:, None] * vectors)


def interp_matrix(coarse_pts):
    result = np.ones((8, len(coarse_pts)))
    for a in range(8):
        for c in range(len(coarse_pts)):
            for k in range(len(coarse_pts)):
                if k != c:
                    result[a, c] *= (points_seven[a] - coarse_pts[k]) / (
                        coarse_pts[c] - coarse_pts[k]
                    )
    return result


def restriction_rows(coarse_pts):
    shared = np.ones(8)
    shared[0] = 0.5
    shared[7] = 0.5
    return (interp_matrix(coarse_pts) * shared[:, None]).T


def restriction_line(elements, coarse_pts):
    degree = len(coarse_pts) - 1
    rows_mat = restriction_rows(coarse_pts)
    result = np.zeros((degree * elements + 1, 7 * elements + 1))
    for m in range(elements):
        result[degree * m : degree * m + degree + 1, 7 * m : 7 * m + 8] += rows_mat
    return result


def patch_matrix(eigbasis, vertices, extent):
    result = np.zeros((13 * vertices, extent))
    for b in range(13):
        for v in range(vertices):
            for a in range(13):
                node_idx = 7 * v + a
                result[b * vertices + v, node_idx] = eigbasis[a, b]
    return result


high = lax.Precision.HIGH
LANES = 128
GROUP = 13
f32 = jnp.float32


def up_to(length, multiple):
    return -(-length // multiple) * multiple


def placed(matrix, shape, row=0, col=0):
    result = np.zeros(shape, np.float32)
    result[row : row + matrix.shape[0], col : col + matrix.shape[1]] = matrix
    return result


def mm(left, right):
    return lax.dot_general(
        left, right, (((1,), (0,)), ((), ())), precision=high, preferred_element_type=f32
    )


class Sizes:
    def __init__(self, x_nodes, y_nodes, z_nodes):
        self.x_nodes, self.y_nodes, self.z_nodes = (x_nodes, y_nodes, z_nodes)
        self.x_elems, self.y_elems, self.z_elems = (x_nodes // 7, y_nodes // 7, z_nodes // 7)
        self.own_rows = up_to(x_nodes + 1, 8)
        self.rows = up_to(x_nodes + 8, 8)
        self.half_z = self.z_elems // 2
        self.lanes = 2 * LANES
        self.modes_x = up_to(13 * self.x_elems, 8)
        self.modes_z = up_to(13 * self.half_z, LANES)
        self.coarse_x = 3 * self.x_elems + 4
        self.coarse_y = 3 * self.y_elems + 4
        self.coarse_z = 3 * self.z_elems
        self.coarse_rows = up_to(self.coarse_x, 8)
        self.coarse_lanes = up_to(self.coarse_z, LANES)
        split = 7 * self.half_z
        self.split = split
        self.node_of_lane = np.full(self.lanes, -1)
        self.node_of_lane[6 : 6 + split] = np.arange(split)
        self.node_of_lane[LANES : LANES + split + 6] = np.arange(split - 6, 2 * split)
        self.first_copy = self.node_of_lane >= 0
        self.first_copy[LANES : LANES + 6] = False


def line_tables(elements):
    nodes = 7 * elements
    stiff, lumped = assemble_line(elements + 2)
    restrict = restriction_line(elements + 3, points_three)[3 : 3 * elements + 7, 7 : nodes + 15]
    columns = np.arange(-6, nodes)
    weight = np.where(columns % 7 == 0, 1.0, 0.5)
    mass_part = restrict[:, 1:-1] * (lumped[1 : nodes + 7] * weight)[None, :]
    stiff_part = restrict @ (stiff[: nodes + 8, 1 : nodes + 7] * weight[None, :])
    return dict(
        own_stiff=stiff[7 : nodes + 8, 7 : nodes + 7],
        mass=lumped[1 : nodes + 7],
        own=restrict[:, 7:-1],
        mass_part=mass_part,
        stiff_part=stiff_part,
    )


def rows_by_node(s, matrix, every_copy):
    used = s.node_of_lane >= 0 if every_copy else s.first_copy
    return np.where(used[:, None], matrix[np.maximum(s.node_of_lane, 0)], 0.0)


def two_parts(matrix):
    high_part = matrix.astype(np.float32).astype(jnp.bfloat16)
    low_part = (matrix - high_part.astype(np.float64)).astype(jnp.bfloat16)
    return high_part, low_part


def residual_constants(s, low):
    line_x = line_tables(s.x_elems)
    stiff_z, lumped_z = assemble_line(s.z_elems)
    stiff_z, lumped_z = (stiff_z[: s.z_nodes, : s.z_nodes], lumped_z[: s.z_nodes])
    rows = s.own_rows - low
    mass_x = np.zeros(s.own_rows)
    mass_x[: s.x_nodes] = line_x["mass"][6:]
    mass_x = mass_x[low:]
    mass_z = rows_by_node(s, lumped_z[:, None], True)[:, 0]
    spread = np.ones((rows, s.lanes))
    stiff = rows_by_node(s, stiff_z, False)
    stiff = rows_by_node(s, stiff.T, True).T
    own_x = placed(line_x["own_stiff"], (s.own_rows, s.own_rows)).astype(np.float64)
    high_x, low_x = two_parts(own_x[low:, low:])
    table = np.concatenate(
        [
            stiff,
            spread * mass_x[:, None],
            spread * mass_z[None, :],
            mass_x[:, None] * mass_z[None, :],
        ]
    )
    return [
        jnp.asarray(table, f32),
        jnp.asarray(np.concatenate([high_x, high_x, low_x], 1), jnp.bfloat16),
    ]


def coupling_constants(s):
    stiffness = element_stiffness()
    lumped_z = assemble_line(s.z_elems)[1][: s.z_nodes]
    mass_z = rows_by_node(s, lumped_z[:, None], True)[:, 0]
    below, above = (np.zeros(s.rows), np.zeros(s.rows))
    below[2:8] = stiffness[1:7, 7]
    above[8 + s.x_nodes - 7 : 8 + s.x_nodes] = stiffness[:7, 7]
    return [below[:, None] * mass_z[None, :], above[:, None] * mass_z[None, :]]


def patch_constants(s):
    line_x = line_tables(s.x_elems)
    stiff_z, lumped_z = assemble_line(s.z_elems)
    stiff_z, lumped_z = (stiff_z[: s.z_nodes, : s.z_nodes], lumped_z[: s.z_nodes])
    weight_z = np.where(np.arange(s.z_nodes) % 7 == 0, 1.0, 0.5)
    restrict_z = restriction_line(s.z_elems, points_three)[: s.coarse_z, : s.z_nodes]
    eigvals, eigbasis = patch_basis()
    mass_z = rows_by_node(s, lumped_z[:, None], True)[:, 0]
    mass_x = np.zeros(s.rows)
    mass_x[2 : s.x_nodes + 8] = line_x["mass"]
    fwd_x = placed(
        patch_matrix(eigbasis, s.x_elems, s.x_nodes + 6), (s.modes_x, s.rows), col=2
    )
    high_x, low_x = two_parts(fwd_x.astype(np.float64))
    fwd_z = np.zeros((LANES, s.modes_z))
    fwd_z[:, : 13 * s.half_z] = patch_matrix(eigbasis, s.half_z, LANES).T
    high_z, low_z = two_parts(fwd_z)
    sums = np.ones((s.modes_x, s.modes_z))
    sums[: 13 * s.x_elems, : 13 * s.half_z] = (
        np.repeat(eigvals, s.x_elems)[:, None] + np.repeat(eigvals, s.half_z)[None, :]
    )
    coarse_of_z = np.zeros((s.z_nodes, 2 * s.coarse_lanes))
    coarse_of_z[:, : s.coarse_z] = (restrict_z * (lumped_z * weight_z)[None, :]).T
    coarse_of_z[:, s.coarse_lanes : s.coarse_lanes + s.coarse_z] = (
        restrict_z @ (stiff_z * weight_z[None, :])
    ).T
    coarse_of_x = np.zeros((2 * s.coarse_rows, s.rows))
    coarse_of_x[: s.coarse_x, 2 : s.x_nodes + 8] = line_x["mass_part"]
    coarse_of_x[s.coarse_rows : s.coarse_rows + s.coarse_x, 2 : s.x_nodes + 8] = line_x[
        "stiff_part"
    ]
    own_z = np.zeros((s.z_nodes, s.coarse_lanes))
    own_z[:, : s.coarse_z] = restrict_z.T
    one_z = placed(
        linear_from_cubic(0, s.z_elems - 1, 0, s.coarse_z - 1).T,
        (s.coarse_lanes, LANES),
        col=s.coarse_z,
    )
    one_x = placed(linear_from_cubic(-1, s.x_elems, -3, 3 * s.x_elems), (8, s.coarse_rows))
    singles = [
        mass_x[:, None] * mass_z[None, :],
        rows_by_node(s, coarse_of_z, True),
        rows_by_node(s, own_z, False),
        one_z,
        one_x,
    ]
    own_x = placed(line_x["own"], (s.coarse_rows, s.rows), col=8).astype(np.float64)
    high_q, low_q = two_parts(coarse_of_x)
    high_r, low_r = two_parts(own_x)
    solve = [
        np.concatenate([high_x, high_x, low_x], 1),
        np.concatenate([high_x.T, high_x.T, low_x.T], 1),
        np.concatenate([high_z, high_z], 0),
        low_z,
        np.concatenate([high_z.T, low_z.T], 1),
        high_z.T,
    ]
    coarse = [
        np.concatenate([high_q, high_q, low_q], 1),
        np.concatenate([high_r, high_r, low_r], 1),
    ]
    return (
        [jnp.asarray(eigvals, f32), jnp.asarray(sums, f32)]
        + [jnp.asarray(value, jnp.bfloat16) for value in solve],
        [jnp.asarray(value, f32) for value in singles]
        + [jnp.asarray(value, jnp.bfloat16) for value in coarse],
    )


def halves_of(value):
    high_part = value.astype(jnp.bfloat16)
    return high_part, (value - high_part.astype(f32)).astype(jnp.bfloat16)


def stacked_rows(value):
    high_part = value.astype(jnp.bfloat16).astype(f32)
    return jnp.concatenate([high_part, value - high_part, high_part], 0).astype(jnp.bfloat16)


def dot(left, right):
    return lax.dot_general(left, right, (((1,), (0,)), ((), ())), preferred_element_type=f32)


def linear_from_cubic(first, last, first_three, last_three):
    result = np.zeros((last - first + 1, last_three - first_three + 1))
    for m in range(first, last + 1):
        for offset, factor in (
            (0, 1.0),
            (1, (1.0 - points_three[1]) / 2.0),
            (2, (1.0 - points_three[2]) / 2.0),
            (-2, (1.0 + points_three[1]) / 2.0),
            (-1, (1.0 + points_three[2]) / 2.0),
        ):
            node = 3 * m + offset - first_three
            if 0 <= node < result.shape[1]:
                result[m - first, node] = factor
    return result


def line_of_planes(coefficients, planes):
    total = None
    for coefficient, plane in zip(coefficients, planes):
        if coefficient != 0.0:
            part = plane() * float(coefficient)
            total = part if total is None else total + part
    return total


def symmetric(vector):
    return abs(vector[0] - vector[-1]) < abs(vector[0] + vector[-1])


def lane_window(ref, start, width):
    if start < 0:
        return pltpu.roll(ref[:, 0:LANES], -start, 1)
    if start + LANES > width:
        return pltpu.roll(ref[:, width - LANES : width], width - start, 1)
    return ref[:, start : start + LANES]


def lane_mask(s, shape, first):
    lane = lax.broadcasted_iota(jnp.int32, shape, 1)
    return ((lane >= 6 + first) & (lane < 6 + s.split)) | (
        (lane >= LANES) & (lane < LANES + s.split + 6)
    )


def put_line(s, ref, index, plane):
    at = s.z_nodes * index
    rows = plane.shape[0]
    ref[0:rows, at : at + s.split] = plane[:, 6 : 6 + s.split]
    ref[0:rows, at + s.split : at + 2 * s.split] = plane[:, LANES + 6 : LANES + 6 + s.split]


def get_line(s, ref, index, width):
    at = s.z_nodes * index
    return jnp.concatenate(
        [lane_window(ref, at - 6, width), lane_window(ref, at + s.split - 6, width)], 1
    )


def own_residual(s, low, first_copies, u, r, guess, load, table, k_x):
    lanes = s.lanes
    rows = s.own_rows - low
    ey, ny = (s.y_elems, s.y_nodes)
    nx = s.x_nodes - low
    width = ny * s.z_nodes
    mass_y = line_tables(ey)["mass"][6:]
    stiffness = element_stiffness()
    gx = lax.axis_index("gx")
    gy = lax.axis_index("gy")
    shape = (nx, lanes)
    row = lax.broadcasted_iota(jnp.int32, shape, 0) + low
    live = (lane_mask(s, shape, 1) & ((row != 0) | (gx > 0))).astype(f32)
    live_y = (gy > 0).astype(f32)
    inside = lane_mask(s, shape, 0).astype(f32)
    pad = jnp.zeros((rows - nx, lanes), f32)
    first_copies[0].wait()
    for y in range(ny):
        mask = live if y else live * live_y
        u[y, 0:nx] = get_line(s, guess, y, width) * mask
        u[y, nx:] = pad
    first_copies[1].wait()
    for y in range(ny):
        r[y, 0:nx] = get_line(s, load, y, width) * inside
        r[y, nx:] = pad
    u[ny] = jnp.zeros((rows, lanes), f32)
    r[ny] = jnp.zeros((rows, lanes), f32)
    for copy in first_copies[2:]:
        copy.wait()
    m_x, m_z, m_xz = [
        table.at[lanes + rows * i : lanes + rows * (i + 1)] for i in range(3)
    ]
    z_term = mm(u[0:ny].reshape(ny * rows, lanes), table[0:lanes]).reshape(ny, rows, lanes)
    for y in range(ny):
        x_term = dot(k_x[...], stacked_rows(u[y]))
        both = x_term * m_z[...] + z_term[y] * m_x[...]
        r[y] = r[y] - float(mass_y[y]) * both

    def along_y(tile, carry):
        at = pl.ds(pl.multiple_of(tile * 8, 8), 8)
        scale = m_xz[at, :]
        corner = None
        for e in range(ey):
            nodes = [u[7 * e + i, at, :] for i in range(8)]
            plus = [nodes[i] + nodes[7 - i] for i in range(4)]
            minus = [nodes[i] - nodes[7 - i] for i in range(4)]
            out = [None] * 8
            for i in range(4):
                even = sum(
                    plus[k] * float(0.5 * (stiffness[i, k] + stiffness[i, 7 - k]))
                    for k in range(4)
                )
                odd = sum(
                    minus[k] * float(0.5 * (stiffness[i, k] - stiffness[i, 7 - k]))
                    for k in range(4)
                )
                out[i], out[7 - i] = (even + odd, even - odd)
            if e:
                out[0] = out[0] + corner
            else:
                out[0] = out[0] + nodes[0] * float(stiffness[7, 7])
            corner = out[7]
            for i in range(8 if e == ey - 1 else 7):
                plane = 7 * e + i
                r[plane, at, :] = r[plane, at, :] - out[i] * scale
        return carry

    lax.fori_loop(0, rows // 8, along_y, 0)


def started(sources, targets, sems):
    copies = [
        pltpu.make_async_copy(source, target, sems.at[index])
        for index, (source, target) in enumerate(zip(sources, targets))
    ]
    for copy in copies:
        copy.start()
    return copies


def send_kernel(s):
    low = (s.x_nodes - 7) // 8 * 8
    lanes, nx, ny = (s.lanes, s.x_nodes, s.y_nodes)
    width = ny * s.z_nodes

    def kernel(
        guess_hbm, load_hbm, table_hbm, k_x_hbm,
        up_out, down_out,
        u, r, guess, load, table, k_x, top, sems,
    ):
        sources = [guess_hbm.at[low:nx], load_hbm.at[low:nx], table_hbm, k_x_hbm]
        sources += [guess_hbm.at[0:8]]
        copies = started(sources, [guess, load, table, k_x, top], sems)
        own_residual(s, low, copies[:4], u, r, guess, load, table, k_x)
        up_out[6:8, :] = jnp.zeros((2, up_out.shape[1]), f32)
        for y in range(ny + 1):
            put_line(s, up_out, y, r[y, nx - 6 - low : nx + 1 - low, :])
        put_line(s, up_out, ny + 1, u[0, nx - 6 - low : nx - low, :])
        copies[4].wait()
        gx = lax.axis_index("gx")
        gy = lax.axis_index("gy")
        live = lane_mask(s, (1, lanes), 1).astype(f32) * (gx > 0).astype(f32)
        live_y = (gy > 0).astype(f32)
        for y in range(ny):
            mask = live if y else live * live_y
            down_out[y : y + 1, :] = get_line(s, top, y, width)[0:1] * mask
        down_out[ny:, :] = jnp.zeros((down_out.shape[0] - ny, lanes), f32)

    return kernel


def residual_kernel(s):
    def kernel(
        guess_hbm, load_hbm, table_hbm, k_x_hbm,
        r, edge,
        u, guess, load, table, k_x, sems,
    ):
        sources = [guess_hbm, load_hbm, table_hbm, k_x_hbm]
        copies = started(sources, [guess, load, table, k_x], sems)
        own_residual(s, 0, copies, u, r, guess, load, table, k_x)
        edge[...] = u[0]

    return kernel


def joined_x_kernel(s):
    rows, lanes = (s.rows, s.lanes)
    nx, ny = (s.x_nodes, s.y_nodes)
    mass_y = line_tables(s.y_elems)["mass"][6:]

    def kernel(r_own, edge, u_first, below, above, c_below, c_above, r, line, up_out):
        width = below.shape[1]
        shape = (8, lanes)
        row = lax.broadcasted_iota(jnp.int32, shape, 0)
        inside = lane_mask(s, shape, 0)
        keep = (inside & (row < 6)).astype(f32)
        only = (inside & (row == 6)).astype(f32)
        zero = jnp.zeros((rows - 8 - nx, lanes), f32) if rows - 8 - nx else None
        for y in range(ny + 2):
            got = get_line(s, below, y, width)
            place = line if y == ny + 1 else r.at[y]
            own = edge[0:nx] if y == ny + 1 else r_own[y, 0:nx, :]
            place[0:2, :] = jnp.zeros((2, lanes), f32)
            place[2:8, :] = (got * keep)[0:6]
            place[8 : 8 + nx, :] = own
            if zero is not None:
                place[8 + nx :, :] = zero
            if y < ny:
                place[8:9, :] += (got * only)[6:7]
                both = (
                    c_below[...] * u_first[y : y + 1, :] + c_above[...] * above[y : y + 1, :]
                ) * float(mass_y[y])
                place[...] = place[...] - both
        for j in range(7):
            put_line(s, up_out, j, r[ny - 6 + j])
        up_out[:, 7 * s.z_nodes :] = jnp.zeros((rows, up_out.shape[1] - 7 * s.z_nodes), f32)

    return kernel


def patch_modes(s, vertices, plane_of, matrices, xf, xb, live):
    lam, sums, f_x, b_x, f_z, f_z_low, b_z, b_z_high = matrices
    rows = s.rows
    count = len(vertices)
    _, eigbasis = patch_basis()
    evens = [b for b in range(13) if symmetric(eigbasis[:, b])]
    gx = lax.axis_index("gx")
    gy = lax.axis_index("gy")
    shape = (s.modes_x, s.modes_z)
    mode = lax.broadcasted_iota(jnp.int32, shape, 0)
    vertex = lax.broadcasted_iota(jnp.int32, shape, 1) % s.half_z
    live_x = (mode % s.x_elems != 0) | (gx > 0)
    live[0] = (live_x & (vertex != 0)).astype(f32)
    live[1] = live_x.astype(f32)
    active = (gy > 0).astype(f32)

    def along_y(tile, carry):
        at = pl.ds(pl.multiple_of(tile * 8, 8), 8)
        for i, v in enumerate(vertices):
            first = [plane_of(7 * v + a - 6, at) for a in range(13)]
            if v == 0:
                first = [value * active for value in first]
            even = [first[6]] + [first[6 + a] + first[6 - a] for a in range(1, 7)]
            odd = [first[6 + a] - first[6 - a] for a in range(1, 7)]
            for b in range(13):
                if b in evens:
                    xf[b, i, at, :] = sum(even[a] * float(eigbasis[6 + a, b]) for a in range(7))
                else:
                    xf[b, i, at, :] = sum(odd[a] * float(eigbasis[7 + a, b]) for a in range(6))
        return carry

    lax.fori_loop(0, rows // 8, along_y, 0)

    def spectral(modes_of):
        pieces = []
        for b in modes_of:
            planes = [dot(f_x[...], stacked_rows(xf[b, v])) for v in range(count)]
            pieces += [plane[:, :LANES] for plane in planes]
            pieces += [plane[:, LANES:] for plane in planes]
        high_part, low_part = halves_of(jnp.concatenate(pieces, 0))
        modes = dot(jnp.concatenate([high_part, low_part], 1), f_z[...]) + dot(
            high_part, f_z_low[...]
        )
        modes = modes.reshape(len(modes_of), 2, count, s.modes_x, s.modes_z)
        pieces = []
        for i, b in enumerate(modes_of):
            factor = 1.0 / (sums[...] + lam[b])
            for t in range(2):
                scaled = modes[i, t] * (factor * live[t])[None]
                pieces.append(scaled.reshape(count * s.modes_x, s.modes_z))
        high_part, low_part = halves_of(jnp.concatenate(pieces, 0))
        both = dot(high_part, b_z[...])
        back = both[:, :LANES] + both[:, LANES:] + dot(low_part, b_z_high[...])
        back = back.reshape(len(modes_of), 2, count, s.modes_x, LANES)
        for i, b in enumerate(modes_of):
            for v in range(count):
                plane = jnp.concatenate([back[i, 0, v], back[i, 1, v]], 1)
                xb[b, v] = dot(b_x[...], stacked_rows(plane))

    for first in range(0, 13, GROUP):
        spectral(range(first, min(13, first + GROUP)))


def inner_kernel(s):
    def kernel(r_own, lam, sums, f_x, b_x, f_z, f_z_low, b_z, b_z_high, xb, xf, live):
        patch_modes(
            s,
            list(range(1, s.y_elems - 1)),
            lambda y, at: r_own[y, at, :],
            (lam, sums, f_x, b_x, f_z, f_z_low, b_z, b_z_high),
            xf,
            xb,
            live,
        )

    return kernel


def patch_kernel(s):
    rows, lanes = (s.rows, s.lanes)
    ey, ny = (s.y_elems, s.y_nodes)
    line_y = line_tables(ey)
    _, eigbasis = patch_basis()
    stiffness = element_stiffness()
    one_y = linear_from_cubic(-1, ey, -3, 3 * ey)
    evens = [b for b in range(13) if symmetric(eigbasis[:, b])]
    odds = [b for b in range(13) if b not in evens]

    def kernel(
        r_own, line, below, above, inner,
        lam, sums, f_x, b_x, f_z, f_z_low, b_z, b_z_high,
        m_xz, q_z, r_z, o_z, o_x, q_x, r_x,
        edge_out, own_out, three_out, one_out, down_out, up_out,
        r, xf, xb, c, cz, rz, hx, ex, rx, live,
    ):
        inside = lane_mask(s, (rows, lanes), 0).astype(f32)
        width = below.shape[1]
        lower = line[...] * m_xz[...]
        upper = above[...] * m_xz[...]
        for j in range(7):
            got = get_line(s, below, j, width) * inside
            if j < 6:
                r[j] = got - lower * float(stiffness[1 + j, 7])
            else:
                r[6] = r_own[0] + got
        for y in range(1, ny):
            plane = r_own[y]
            if y >= ny - 7:
                plane = plane - upper * float(stiffness[y - (ny - 7), 7])
            r[6 + y] = plane
        patch_modes(
            s,
            [0, ey - 1],
            lambda y, at: r[y + 6, at, :],
            (lam, sums, f_x, b_x, f_z, f_z_low, b_z, b_z_high),
            xf,
            xb,
            live,
        )

        def back_y(tile, carry):
            at = pl.ds(pl.multiple_of(tile * 8, 8), 8)
            tail = None
            for v in range(ey):
                if 0 < v < ey - 1:
                    modes = [inner[b, v - 1, at, :] for b in range(13)]
                else:
                    modes = [xb[b, min(v, 1), at, :] for b in range(13)]
                out = [None] * 13
                for a in range(7):
                    even = sum(modes[b] * float(eigbasis[6 + a, b]) for b in evens)
                    if a == 0:
                        out[6] = even
                        continue
                    odd = sum(modes[b] * float(eigbasis[6 + a, b]) for b in odds)
                    out[6 + a], out[6 - a] = (even + odd, even - odd)
                if v:
                    out[:6] = [value + other for value, other in zip(out[:6], tail)]
                tail = out[7:]
                for a in range(13 if v == ey - 1 else 7):
                    c[7 * v + a, at, :] = out[a]
            return carry

        lax.fori_loop(0, rows // 8, back_y, 0)

        for j in range(6):
            down_out[:, lanes * j : lanes * (j + 1)] = c[j]
        edge_out[...] = c[6:, 0:8, :]
        own_out[...] = c[6:, 8:, :]

        half = s.coarse_lanes
        rows_c = s.coarse_rows
        cz[...] = mm(c[...].reshape((ny + 6) * rows, lanes), q_z[...]).reshape(
            ny + 6, rows, 2 * half
        )
        rz[...] = mm(r[6 : ny + 6].reshape(ny * rows, lanes), r_z[...]).reshape(ny, rows, half)
        for y in range(ny + 6):
            plane = dot(q_x[...], stacked_rows(cz[y]))
            hx[y] = plane[:rows_c, :half]
            ex[y] = plane[rows_c:, :half] + plane[:rows_c, half:]
        for y in range(ny):
            rx[y] = dot(r_x[...], stacked_rows(rz[y]))
        for j in range(s.coarse_y):
            three_out[j] = line_of_planes(
                np.concatenate(
                    [line_y["own"][j], -line_y["stiff_part"][j], -line_y["mass_part"][j]]
                ),
                [lambda y=y: rx[y] for y in range(ny)]
                + [lambda y=y: hx[y] for y in range(ny + 6)]
                + [lambda y=y: ex[y] for y in range(ny + 6)],
            )
        one_all = mm(
            three_out[...].reshape(s.coarse_y * rows_c, half), o_z[...]
        ).reshape(s.coarse_y, rows_c, LANES)
        for m in range(ey + 2):
            mixed = line_of_planes(
                one_y[m], [lambda j=j: one_all[j] for j in range(s.coarse_y)]
            )
            one_out[m] = mm(o_x[...], mixed)
        base = 6 * lanes
        down_out[:, base:] = jnp.zeros((rows, 2 * half), f32)
        up_out[...] = jnp.zeros(up_out.shape, f32)
        up_out[:, 0:half] = three_out[s.coarse_y - 1]
        for j in range(4):
            first, at = (rows_c * (j % 2), base + half * (j // 2))
            if j < 3:
                down_out[first : first + rows_c, at : at + half] = three_out[j]
            down_out[first : first + 8, at : at + half] += one_out[j]
            up_out[0:8, half * j : half * (j + 1)] += one_out[ey - 2 + j]

    return kernel


def coarse_place(s, index):
    high_rows = coarse_height(s)
    return index % high_rows, LANES * (index // high_rows)


def coarse_height(s):
    return up_to(-(-max(9 * s.y_elems, 4 * s.y_elems + 24) // 2), 24)


def join_kernel(s):
    lanes, half, rows_c = (s.lanes, s.coarse_lanes, s.coarse_rows)
    ey, ny = (s.y_elems, s.y_nodes)

    def kernel(edge, three, one, down, up, down_out, up_out, three_out, one_out):
        lane = lax.broadcasted_iota(jnp.int32, (rows_c, half), 1)
        is_three = (lane < s.coarse_z).astype(f32)
        is_one = (lane >= s.coarse_z).astype(f32)[0:8]
        for y in range(ny):
            plane = edge[y]
            if y >= ny - 6:
                j = y - (ny - 6)
                plane = plane + down[0:8, lanes * j : lanes * (j + 1)]
            down_out[6 * y : 6 * y + 6, :] = plane[2:8]
        base = 6 * lanes
        first = 6 * ny
        down_out[first:, :] = jnp.zeros((down_out.shape[0] - first, lanes), f32)
        up_out[...] = jnp.zeros(up_out.shape, f32)

        def from_above(k, count):
            row, at = (rows_c * (k % 2), base + half * (k // 2))
            return down[row : row + count, at : at + half]

        for j in range(3 * ey):
            plane = three[3 + j]
            if j >= 3 * ey - 3:
                plane = plane + from_above(j - (3 * ey - 3), rows_c)
            if j == 0:
                plane = plane + up[0:rows_c, 0:half]
            plane = plane * is_three
            three_out[j] = plane
            row, at = coarse_place(s, 3 * j)
            down_out[first + row : first + row + 3, at : at + half] = plane[0:3]
            row, at = coarse_place(s, j)
            up_out[row : row + 1, at : at + half] = plane[s.coarse_x - 1 : s.coarse_x]
        for j in range(ey + 6):
            y = j - 3
            plane = None
            if -1 <= y <= ey:
                plane = one[y + 1]
            if y <= 0:
                k = y + 3
                part = up[0:8, half * k : half * (k + 1)]
                plane = part if plane is None else plane + part
            if y >= ey - 1:
                part = from_above(y - (ey - 1), 8)
                plane = part if plane is None else plane + part
            plane = plane * is_one
            one_out[j] = plane
            row, at = coarse_place(s, 4 * j)
            down_out[first + row : first + row + 4, at : at + half] += plane[0:4]
            up_out[row : row + 4, at : at + half] += plane[s.x_elems - 2 : s.x_elems + 2]

    return kernel


def shared_lanes(s, shape):
    lane = lax.broadcasted_iota(jnp.int32, shape, 1)
    return ((lane >= s.split) & (lane < s.split + 6)).astype(f32)


def base_kernel(s):
    lanes, nx, ny = (s.lanes, s.x_nodes, s.y_nodes)
    width = ny * s.z_nodes

    def kernel(guess, weight, own, down, out):
        gx = lax.axis_index("gx")
        gy = lax.axis_index("gy")
        shape = (nx, lanes)
        row = lax.broadcasted_iota(jnp.int32, shape, 0)
        live = (lane_mask(s, shape, 1) & ((row != 0) | (gx > 0))).astype(f32)
        live_y = (gy > 0).astype(f32)
        shared = shared_lanes(s, shape)
        for y in range(ny):
            plane = own[y, 0:nx, :]
            if y >= ny - 6:
                j = y - (ny - 6)
                plane = plane + down[8 : 8 + nx, lanes * j : lanes * (j + 1)]
            plane = plane + pltpu.roll(plane, lanes - (LANES - s.split), 1) * shared
            mask = live if y else live * live_y
            factor = weight[...] * (1.0 if y % 7 == 0 else 0.5)
            put_line(s, out, y, (get_line(s, guess, y, width) + factor * plane) * mask)

    return kernel


def finish_kernel(s, x_total, y_total):
    lanes, half, rows_c, nz = (s.lanes, s.coarse_lanes, s.coarse_rows, s.z_nodes)
    ex, ey, nx, ny = (s.x_elems, s.y_elems, s.x_nodes, s.y_nodes)
    one_rows = up_to(ex + 6, 8)
    split = s.split

    def kernel(
        base, weight, right, left, three, one,
        smooth_out, three_out, coarse_out, fine, level,
    ):
        gx = lax.axis_index("gx")
        gy = lax.axis_index("gy")
        live_y = (gy > 0).astype(f32)
        shared = shared_lanes(s, (6, lanes))
        smooth_out[...] = base[...]
        for y in range(ny):
            plane = right[6 * y : 6 * y + 6, :]
            plane = plane + pltpu.roll(plane, lanes - (LANES - split), 1) * shared
            plane = plane * weight[nx - 6 : nx, :] * (1.0 if y % 7 == 0 else 0.5)
            for t in range(2):
                at = nz * y + split * t
                lanes_at = LANES * t + 6
                smooth_out[nx - 6 : nx, at : at + split] += plane[:, lanes_at : lanes_at + split]
        first = 6 * ny
        nzc = s.coarse_z
        lane = lax.broadcasted_iota(jnp.int32, (3 * ex, nzc), 1)
        row = lax.broadcasted_iota(jnp.int32, (3 * ex, nzc), 0)
        live = ((lane >= 1) & ((row >= 1) | (gx > 0))).astype(f32)
        for j in range(3 * ey):
            fine[j] = three[j]
            at_row, at = coarse_place(s, 3 * j)
            at_row += first
            fine[j, 3 * ex : 3 * ex + 3, :] += right[at_row : at_row + 3, at : at + half]
            at_row, at = coarse_place(s, j)
            fine[j, 3:4, :] += left[at_row : at_row + 1, at : at + half]
            mask = live if j else live * live_y
            three_out[:, nzc * j : nzc * (j + 1)] = fine[j, 3 : 3 * ex + 3, 0:nzc] * mask
        level[...] = jnp.zeros((ey + 6, one_rows, LANES), f32)
        for j in range(ey + 6):
            level[j, 2 : ex + 4, :] = one[j, 0 : ex + 2, :]
            at_row, at = coarse_place(s, 4 * j)
            level[j, 0:4, :] += left[at_row : at_row + 4, at : at + half]
            at_row += first
            level[j, ex + 2 : ex + 6, :] += right[at_row : at_row + 4, at : at + half]
        shape = (one_rows, LANES)
        lane = lax.broadcasted_iota(jnp.int32, shape, 1)
        row = lax.broadcasted_iota(jnp.int32, shape, 0)
        global_x = gx * ex + row - 3
        plane_mask = (
            (lane > s.coarse_z) & (lane < s.coarse_z + s.z_elems) & (row < ex + 6)
            & (global_x >= 1) & (global_x < x_total)
        )
        masks = []
        for j in range(ey + 6):
            global_y = gy * ey + (j - 3)
            inside = (global_y >= 1) & (global_y < y_total)
            masks.append((plane_mask & inside).astype(f32))
        levels = [level[j] for j in range(ey + 6)]
        error = [damping / 12.0 * a * m for a, m in zip(levels, masks)]
        zero = jnp.zeros(shape, f32)
        for sweep in range(1, JAC):
            lower = [zero] + error[:-1]
            upper = error[1:] + [zero]
            fresh = []
            for j in range(ey + 6):
                here = error[j]
                neighbours = (
                    lower[j]
                    + upper[j]
                    + pltpu.roll(here, 1, 0)
                    + pltpu.roll(here, one_rows - 1, 0)
                    + pltpu.roll(here, 1, 1)
                    + pltpu.roll(here, LANES - 1, 1)
                )
                applied = 12.0 * here - 2.0 * neighbours
                fresh.append((here + damping / 12.0 * (levels[j] - applied)) * masks[j])
            error = fresh
        nze = s.z_elems
        for j in range(ey):
            coarse_out[:, nze * j : nze * (j + 1)] = error[3 + j][
                3 : 3 + ex, s.coarse_z : s.coarse_z + nze
            ]

    return kernel


def local(load_vector, initial_guess):
    z_nodes = 7 * EZ
    x_nodes = load_vector.shape[0]
    y_nodes = load_vector.shape[1] // z_nodes
    s = Sizes(x_nodes, y_nodes, z_nodes)
    rows, lanes, half = (s.rows, s.lanes, s.coarse_lanes)
    ny, ey = (s.y_nodes, s.y_elems)
    width = y_nodes * z_nodes
    shape = lambda *dims: jax.ShapeDtypeStruct(dims, f32)
    params = pltpu.CompilerParams(vmem_limit_bytes=36 * 2**20)
    vmem = lambda count: [pl.BlockSpec(memory_space=pltpu.VMEM)] * count

    def call(kernel, name, outputs, operands, scratch=(), spaces=None, semaphores=0):
        specs = vmem(len(operands))
        for index, space in (spaces or {}).items():
            specs[index] = pl.BlockSpec(memory_space=space)
        return pl.pallas_call(
            kernel,
            out_shape=tuple(shape(*dims) for dims in outputs),
            in_specs=specs,
            out_specs=tuple(vmem(len(outputs))),
            scratch_shapes=[pltpu.VMEM(d, f32) if isinstance(d, tuple) else d for d in scratch]
            + ([pltpu.SemaphoreType.DMA((semaphores,))] if semaphores else []),
            compiler_params=params,
            name=name,
        )(*operands)

    in_hbm = lambda values: [pltpu.with_memory_space_constraint(v, pltpu.HBM) for v in values]
    hbm = {index: pltpu.HBM for index in range(4)}
    low = (x_nodes - 7) // 8 * 8
    constants = residual_constants(s, low)
    up, u_first = call(
        send_kernel(s),
        "send",
        ((8, up_to((ny + 2) * z_nodes, LANES)), (up_to(ny, 8), lanes)),
        in_hbm([initial_guess, load_vector] + constants),
        [
            (ny + 1, s.own_rows - low, lanes),
            (ny + 1, s.own_rows - low, lanes),
            (x_nodes - low, width),
            (x_nodes - low, width),
            constants[0].shape,
            pltpu.VMEM(constants[1].shape, jnp.bfloat16),
            (8, width),
        ],
        spaces=hbm,
        semaphores=5,
    )
    below = shifted(up, "gx", 1)
    above = shifted(u_first, "gx", -1)
    constants = residual_constants(s, 0)
    r_own, edge = call(
        residual_kernel(s),
        "residual",
        ((ny + 1, s.own_rows, lanes), (s.own_rows, lanes)),
        in_hbm([initial_guess, load_vector] + constants),
        [
            (ny + 1, s.own_rows, lanes),
            initial_guess.shape,
            load_vector.shape,
            constants[0].shape,
            pltpu.VMEM(constants[1].shape, jnp.bfloat16),
        ],
        spaces=hbm,
        semaphores=4,
    )
    r_x, line, up = call(
        joined_x_kernel(s),
        "joined_x",
        (
            (ny + 1, rows, lanes),
            (rows, lanes),
            (rows, up_to(7 * z_nodes, LANES)),
        ),
        [r_own, edge, u_first, below, above]
        + [jnp.asarray(v, f32) for v in coupling_constants(s)],
    )
    below = shifted(up, "gy", 1)
    above = shifted(line, "gy", -1)
    solve, coarse = patch_constants(s)
    (inner,) = call(
        inner_kernel(s),
        "inner",
        ((13, ey - 2, rows, lanes),),
        [r_x] + solve,
        [(13, ey - 2, rows, lanes), (2, s.modes_x, s.modes_z)],
        spaces={1: pltpu.SMEM},
    )
    edge, own, three, one, down, up = call(
        patch_kernel(s),
        "patches",
        (
            (ny, 8, lanes),
            (ny, rows - 8, lanes),
            (s.coarse_y, s.coarse_rows, half),
            (ey + 2, 8, LANES),
            (rows, 6 * lanes + 2 * half),
            (s.coarse_rows, 4 * half),
        ),
        [r_x, line, below, above, inner] + solve + coarse,
        [
            (ny + 6, rows, lanes),
            (13, 2, rows, lanes),
            (13, 2, rows, lanes),
            (ny + 6, rows, lanes),
            (ny + 6, rows, 2 * half),
            (ny, rows, half),
            (ny + 6, s.coarse_rows, half),
            (ny + 6, s.coarse_rows, half),
            (ny, s.coarse_rows, half),
            (2, s.modes_x, s.modes_z),
        ],
        spaces={5: pltpu.SMEM},
    )
    down = shifted(down, "gy", -1)
    up = shifted(up, "gy", 1)
    right, left, three, one = call(
        join_kernel(s),
        "join",
        (
            (6 * ny + coarse_height(s), lanes),
            (coarse_height(s), lanes),
            (3 * ey, s.coarse_rows, half),
            (ey + 6, 8, LANES),
        ),
        [edge, three, one, down, up],
    )
    right = shifted(right, "gx", -1)
    left = shifted(left, "gx", 1)
    weight_z = np.where(np.arange(z_nodes) % 7 == 0, 1.0, 0.5)
    weight = jnp.asarray(
        np.where(np.arange(x_nodes) % 7 == 0, 1.0, 0.5)[:, None]
        * rows_by_node(s, weight_z[:, None], True)[:, 0],
        f32,
    )
    (base,) = call(
        base_kernel(s), "base", ((x_nodes, width),), [initial_guess, weight, own, down]
    )
    return call(
        finish_kernel(s, s.x_elems * lax.axis_size("gx"), ey * lax.axis_size("gy")),
        "finish",
        (
            (x_nodes, width),
            (3 * s.x_elems, 3 * ey * s.coarse_z),
            (s.x_elems, ey * s.z_elems),
        ),
        [base, weight, right, left, three, one],
        [
            (3 * ey, s.coarse_rows, half),
            (ey + 6, up_to(s.x_elems + 6, 8), LANES),
        ],
    )


def solution(mesh):
    in_specs = (P("gx", "gy"), P("gx", "gy"))
    out_specs = (P("gx", "gy"), P("gx", "gy"), P("gx", "gy"))
    return jax.shard_map(local, mesh=mesh, in_specs=in_specs, out_specs=out_specs, check_vma=False)
```

```python
import math

import jax
import jax.numpy as jnp
import numpy as np
from jax import lax
from jax.experimental import pallas as pl
from jax.experimental.pallas import tpu as pltpu
from jax.sharding import PartitionSpec as P

EZ = 32
JAC = 4


points_seven = (
    -1.0,
    -0.8717401485096066,
    -0.5917001814331423,
    -0.2092992179024789,
    0.2092992179024789,
    0.5917001814331423,
    0.8717401485096066,
    1.0,
)
points_three = (-1.0, -0.4472135954999579, 0.4472135954999579, 1.0)
points_one = (-1.0, 1.0)
damping = 2.0 / 3.0


def shifted(array, axis, by):
    devices = lax.axis_size(axis)
    pairs = [(i, i + by) for i in range(devices) if 0 <= i + by < devices]
    return lax.ppermute(array, axis, pairs)


def legendre_at(degree, location):
    previous, current = (1.0, location)
    for level_idx in range(1, degree):
        previous, current = (
            current,
            ((2 * level_idx + 1) * location * current - level_idx * previous) / (level_idx + 1),
        )
    return current


def quadrature_weights():
    return np.array([2.0 / (56.0 * legendre_at(7, x) * legendre_at(7, x)) for x in points_seven])


def derivative_matrix():
    points = np.array(points_seven)
    products = np.array(
        [np.prod([points[i] - points[k] for k in range(8) if k != i]) for i in range(8)]
    )
    result = np.zeros((8, 8))
    for i in range(8):
        for j in range(8):
            if i != j:
                result[i, j] = products[i] / (products[j] * (points[i] - points[j]))
        result[i, i] = np.sum([1.0 / (points[i] - points[k]) for k in range(8) if k != i])
    return result


def element_stiffness():
    derivative = derivative_matrix()
    return derivative.T @ (quadrature_weights()[:, None] * derivative)


def assemble_line(elements):
    stiffness = element_stiffness()
    weights = quadrature_weights()
    extent = 7 * elements + 1
    global_stiff = np.zeros((extent, extent))
    lumped = np.zeros(extent)
    for m in range(elements):
        global_stiff[7 * m : 7 * m + 8, 7 * m : 7 * m + 8] += stiffness
        lumped[7 * m : 7 * m + 8] += weights
    return (global_stiff, lumped)


def jacobi_eigen(matrix):
    rotated_mat = matrix.copy()
    extent = matrix.shape[0]
    vectors = np.eye(extent)
    for sweep_idx in range(12):
        for p in range(extent - 1):
            for q in range(p + 1, extent):
                angle_rot = 0.5 * math.atan2(
                    2.0 * float(rotated_mat[p, q]), float(rotated_mat[q, q] - rotated_mat[p, p])
                )
                rotation = np.eye(extent)
                rotation[p, p] = math.cos(angle_rot)
                rotation[q, q] = math.cos(angle_rot)
                rotation[p, q] = math.sin(angle_rot)
                rotation[q, p] = -math.sin(angle_rot)
                rotated_mat = rotation.T @ rotated_mat @ rotation
                vectors = vectors @ rotation
    return (np.array([rotated_mat[i, i] for i in range(extent)]), vectors)


def patch_basis():
    global_stiff, lumped = assemble_line(2)
    inv_root = 1.0 / np.sqrt(lumped[1:14])
    eigvals, vectors = jacobi_eigen(
        inv_root[:, None] * global_stiff[1:14, 1:14] * inv_root[None, :]
    )
    return (eigvals, inv_root[:, None] * vectors)


def interp_matrix(coarse_pts):
    result = np.ones((8, len(coarse_pts)))
    for a in range(8):
        for c in range(len(coarse_pts)):
            for k in range(len(coarse_pts)):
                if k != c:
                    result[a, c] *= (points_seven[a] - coarse_pts[k]) / (
                        coarse_pts[c] - coarse_pts[k]
                    )
    return result


def restriction_rows(coarse_pts):
    shared = np.ones(8)
    shared[0] = 0.5
    shared[7] = 0.5
    return (interp_matrix(coarse_pts) * shared[:, None]).T


def restriction_line(elements, coarse_pts):
    degree = len(coarse_pts) - 1
    rows_mat = restriction_rows(coarse_pts)
    result = np.zeros((degree * elements + 1, 7 * elements + 1))
    for m in range(elements):
        result[degree * m : degree * m + degree + 1, 7 * m : 7 * m + 8] += rows_mat
    return result


def patch_matrix(eigbasis, vertices, extent):
    result = np.zeros((13 * vertices, extent))
    for b in range(13):
        for v in range(vertices):
            for a in range(13):
                node_idx = 7 * v + a
                result[b * vertices + v, node_idx] = eigbasis[a, b]
    return result


high = lax.Precision.HIGH
highest = lax.Precision.HIGHEST
LANES = 128
GROUP = 13
f32 = jnp.float32


def up_to(length, multiple):
    return -(-length // multiple) * multiple


def placed(matrix, shape, row=0, col=0):
    result = np.zeros(shape, np.float32)
    result[row : row + matrix.shape[0], col : col + matrix.shape[1]] = matrix
    return result


def mm(left, right, precision=high):
    return lax.dot_general(
        left, right, (((1,), (0,)), ((), ())), precision=precision, preferred_element_type=f32
    )


class Sizes:
    def __init__(self, x_nodes, y_nodes, z_nodes):
        self.x_nodes, self.y_nodes, self.z_nodes = (x_nodes, y_nodes, z_nodes)
        self.x_elems, self.y_elems, self.z_elems = (x_nodes // 7, y_nodes // 7, z_nodes // 7)
        self.own_rows = up_to(x_nodes + 1, 8)
        self.rows = up_to(x_nodes + 8, 8)
        self.half_z = self.z_elems // 2
        self.lanes = 2 * LANES
        self.modes_x = up_to(13 * self.x_elems, 8)
        self.modes_z = up_to(13 * self.half_z, LANES)
        self.coarse_x = 3 * self.x_elems + 4
        self.coarse_y = 3 * self.y_elems + 4
        self.coarse_z = 3 * self.z_elems
        self.coarse_rows = up_to(self.coarse_x, 8)
        self.coarse_lanes = up_to(self.coarse_z, LANES)
        split = 7 * self.half_z
        self.split = split
        self.node_of_lane = np.full(self.lanes, -1)
        self.node_of_lane[6 : 6 + split] = np.arange(split)
        self.node_of_lane[LANES : LANES + split + 6] = np.arange(split - 6, 2 * split)
        self.first_copy = self.node_of_lane >= 0
        self.first_copy[LANES : LANES + 6] = False


def line_tables(elements):
    nodes = 7 * elements
    stiff, lumped = assemble_line(elements + 2)
    restrict = restriction_line(elements + 3, points_three)[3 : 3 * elements + 7, 7 : nodes + 15]
    columns = np.arange(-6, nodes)
    weight = np.where(columns % 7 == 0, 1.0, 0.5)
    mass_part = restrict[:, 1:-1] * (lumped[1 : nodes + 7] * weight)[None, :]
    stiff_part = restrict @ (stiff[: nodes + 8, 1 : nodes + 7] * weight[None, :])
    return dict(
        own_stiff=stiff[7 : nodes + 8, 7 : nodes + 7],
        mass=lumped[1 : nodes + 7],
        own=restrict[:, 7:-1],
        mass_part=mass_part,
        stiff_part=stiff_part,
    )


def rows_by_node(s, matrix, every_copy):
    used = s.node_of_lane >= 0 if every_copy else s.first_copy
    return np.where(used[:, None], matrix[np.maximum(s.node_of_lane, 0)], 0.0)


def two_parts(matrix, low_type=jnp.bfloat16):
    high_part = matrix.astype(np.float32).astype(jnp.bfloat16)
    low_part = (matrix - high_part.astype(np.float64)).astype(low_type)
    return high_part, low_part


def residual_constants(s, low):
    line_x = line_tables(s.x_elems)
    stiff_z, lumped_z = assemble_line(s.z_elems)
    stiff_z, lumped_z = (stiff_z[: s.z_nodes, : s.z_nodes], lumped_z[: s.z_nodes])
    rows = s.own_rows - low
    mass_x = np.zeros(s.own_rows)
    mass_x[: s.x_nodes] = line_x["mass"][6:]
    mass_x = mass_x[low:]
    mass_z = rows_by_node(s, lumped_z[:, None], True)[:, 0]
    spread = np.ones((rows, s.lanes))
    stiff = rows_by_node(s, stiff_z, False)
    stiff = rows_by_node(s, stiff.T, True).T
    own_x = placed(line_x["own_stiff"], (s.own_rows, s.own_rows)).astype(np.float64)
    high_x, rest = two_parts(own_x[low:, low:], np.float64)
    mid_x, low_x = two_parts(rest)
    table = np.concatenate(
        [
            stiff,
            spread * mass_x[:, None],
            spread * mass_z[None, :],
            mass_x[:, None] * mass_z[None, :],
        ]
    )
    return [
        jnp.asarray(table, f32),
        jnp.asarray(
            np.concatenate([high_x, high_x, high_x, mid_x, mid_x, low_x], 1), jnp.bfloat16
        ),
    ]


def coupling_constants(s):
    stiffness = element_stiffness()
    lumped_z = assemble_line(s.z_elems)[1][: s.z_nodes]
    mass_z = rows_by_node(s, lumped_z[:, None], True)[:, 0]
    below, above = (np.zeros(s.rows), np.zeros(s.rows))
    below[2:8] = stiffness[1:7, 7]
    above[8 + s.x_nodes - 7 : 8 + s.x_nodes] = stiffness[:7, 7]
    return [below[:, None] * mass_z[None, :], above[:, None] * mass_z[None, :]]


def patch_constants(s):
    line_x = line_tables(s.x_elems)
    stiff_z, lumped_z = assemble_line(s.z_elems)
    stiff_z, lumped_z = (stiff_z[: s.z_nodes, : s.z_nodes], lumped_z[: s.z_nodes])
    weight_z = np.where(np.arange(s.z_nodes) % 7 == 0, 1.0, 0.5)
    restrict_z = restriction_line(s.z_elems, points_three)[: s.coarse_z, : s.z_nodes]
    eigvals, eigbasis = patch_basis()
    mass_z = rows_by_node(s, lumped_z[:, None], True)[:, 0]
    mass_x = np.zeros(s.rows)
    mass_x[2 : s.x_nodes + 8] = line_x["mass"]
    fwd_x = placed(
        patch_matrix(eigbasis, s.x_elems, s.x_nodes + 6), (s.modes_x, s.rows), col=2
    )
    high_x, low_x = two_parts(fwd_x.astype(np.float64))
    fwd_z = np.zeros((LANES, s.modes_z))
    fwd_z[:, : 13 * s.half_z] = patch_matrix(eigbasis, s.half_z, LANES).T
    high_z, low_z = two_parts(fwd_z)
    sums = np.ones((s.modes_x, s.modes_z))
    sums[: 13 * s.x_elems, : 13 * s.half_z] = (
        np.repeat(eigvals, s.x_elems)[:, None] + np.repeat(eigvals, s.half_z)[None, :]
    )
    coarse_of_z = np.zeros((s.z_nodes, 2 * s.coarse_lanes))
    coarse_of_z[:, : s.coarse_z] = (restrict_z * (lumped_z * weight_z)[None, :]).T
    coarse_of_z[:, s.coarse_lanes : s.coarse_lanes + s.coarse_z] = (
        restrict_z @ (stiff_z * weight_z[None, :])
    ).T
    coarse_of_x = np.zeros((2 * s.coarse_rows, s.rows))
    coarse_of_x[: s.coarse_x, 2 : s.x_nodes + 8] = line_x["mass_part"]
    coarse_of_x[s.coarse_rows : s.coarse_rows + s.coarse_x, 2 : s.x_nodes + 8] = line_x[
        "stiff_part"
    ]
    own_z = np.zeros((s.z_nodes, s.coarse_lanes))
    own_z[:, : s.coarse_z] = restrict_z.T
    one_z = placed(
        linear_from_cubic(0, s.z_elems - 1, 0, s.coarse_z - 1).T,
        (s.coarse_lanes, LANES),
        col=s.coarse_z,
    )
    one_x = placed(linear_from_cubic(-1, s.x_elems, -3, 3 * s.x_elems), (8, s.coarse_rows))
    singles = [
        mass_x[:, None] * mass_z[None, :],
        rows_by_node(s, coarse_of_z, True),
        rows_by_node(s, own_z, False),
        one_z,
        one_x,
    ]
    own_x = placed(line_x["own"], (s.coarse_rows, s.rows), col=8).astype(np.float64)
    high_q, low_q = two_parts(coarse_of_x)
    high_r, low_r = two_parts(own_x)
    solve = [
        np.concatenate([high_x, high_x, low_x], 1),
        np.concatenate([high_x.T, high_x.T, low_x.T], 1),
        np.concatenate([high_z, high_z], 0),
        low_z,
        np.concatenate([high_z.T, low_z.T], 1),
        high_z.T,
    ]
    coarse = [
        np.concatenate([high_q, high_q, low_q], 1),
        np.concatenate([high_r, high_r, low_r], 1),
    ]
    return (
        [jnp.asarray(eigvals, f32), jnp.asarray(sums, f32)]
        + [jnp.asarray(value, jnp.bfloat16) for value in solve],
        [jnp.asarray(value, f32) for value in singles]
        + [jnp.asarray(value, jnp.bfloat16) for value in coarse],
    )


def halves_of(value):
    high_part = value.astype(jnp.bfloat16)
    return high_part, (value - high_part.astype(f32)).astype(jnp.bfloat16)


def stacked_whole(value):
    high_part = value.astype(jnp.bfloat16).astype(f32)
    rest = value - high_part
    mid_part = rest.astype(jnp.bfloat16).astype(f32)
    return jnp.concatenate(
        [high_part, mid_part, rest - mid_part, high_part, mid_part, high_part], 0
    ).astype(jnp.bfloat16)


def stacked_rows(value):
    high_part = value.astype(jnp.bfloat16).astype(f32)
    return jnp.concatenate([high_part, value - high_part, high_part], 0).astype(jnp.bfloat16)


def dot(left, right):
    return lax.dot_general(left, right, (((1,), (0,)), ((), ())), preferred_element_type=f32)


def linear_from_cubic(first, last, first_three, last_three):
    result = np.zeros((last - first + 1, last_three - first_three + 1))
    for m in range(first, last + 1):
        for offset, factor in (
            (0, 1.0),
            (1, (1.0 - points_three[1]) / 2.0),
            (2, (1.0 - points_three[2]) / 2.0),
            (-2, (1.0 + points_three[1]) / 2.0),
            (-1, (1.0 + points_three[2]) / 2.0),
        ):
            node = 3 * m + offset - first_three
            if 0 <= node < result.shape[1]:
                result[m - first, node] = factor
    return result


def line_of_planes(coefficients, planes):
    total = None
    for coefficient, plane in zip(coefficients, planes):
        if coefficient != 0.0:
            part = plane() * float(coefficient)
            total = part if total is None else total + part
    return total


def symmetric(vector):
    return abs(vector[0] - vector[-1]) < abs(vector[0] + vector[-1])


def lane_window(ref, start, width):
    if start < 0:
        return pltpu.roll(ref[:, 0:LANES], -start, 1)
    if start + LANES > width:
        return pltpu.roll(ref[:, width - LANES : width], width - start, 1)
    return ref[:, start : start + LANES]


def lane_mask(s, shape, first):
    lane = lax.broadcasted_iota(jnp.int32, shape, 1)
    return ((lane >= 6 + first) & (lane < 6 + s.split)) | (
        (lane >= LANES) & (lane < LANES + s.split + 6)
    )


def put_line(s, ref, index, plane):
    at = s.z_nodes * index
    rows = plane.shape[0]
    ref[0:rows, at : at + s.split] = plane[:, 6 : 6 + s.split]
    ref[0:rows, at + s.split : at + 2 * s.split] = plane[:, LANES + 6 : LANES + 6 + s.split]


def get_line(s, ref, index, width):
    at = s.z_nodes * index
    return jnp.concatenate(
        [lane_window(ref, at - 6, width), lane_window(ref, at + s.split - 6, width)], 1
    )


def own_residual(s, low, first_copies, u, r, guess, load, table, k_x):
    lanes = s.lanes
    rows = s.own_rows - low
    ey, ny = (s.y_elems, s.y_nodes)
    nx = s.x_nodes - low
    width = ny * s.z_nodes
    mass_y = line_tables(ey)["mass"][6:]
    stiffness = element_stiffness()
    gx = lax.axis_index("gx")
    gy = lax.axis_index("gy")
    shape = (nx, lanes)
    row = lax.broadcasted_iota(jnp.int32, shape, 0) + low
    live = (lane_mask(s, shape, 1) & ((row != 0) | (gx > 0))).astype(f32)
    live_y = (gy > 0).astype(f32)
    inside = lane_mask(s, shape, 0).astype(f32)
    pad = jnp.zeros((rows - nx, lanes), f32)
    first_copies[0].wait()
    for y in range(ny):
        mask = live if y else live * live_y
        u[y, 0:nx] = get_line(s, guess, y, width) * mask
        u[y, nx:] = pad
    first_copies[1].wait()
    for y in range(ny):
        r[y, 0:nx] = get_line(s, load, y, width) * inside
        r[y, nx:] = pad
    u[ny] = jnp.zeros((rows, lanes), f32)
    r[ny] = jnp.zeros((rows, lanes), f32)
    for copy in first_copies[2:]:
        copy.wait()
    m_x, m_z, m_xz = [
        table.at[lanes + rows * i : lanes + rows * (i + 1)] for i in range(3)
    ]
    planes = u[0:ny].reshape(ny * rows, lanes)
    z_term = mm(planes, table[0:lanes], highest).reshape(ny, rows, lanes)
    for y in range(ny):
        x_term = dot(k_x[...], stacked_whole(u[y]))
        both = x_term * m_z[...] + z_term[y] * m_x[...]
        r[y] = r[y] - float(mass_y[y]) * both

    def along_y(tile, carry):
        at = pl.ds(pl.multiple_of(tile * 8, 8), 8)
        scale = m_xz[at, :]
        corner = None
        for e in range(ey):
            nodes = [u[7 * e + i, at, :] for i in range(8)]
            plus = [nodes[i] + nodes[7 - i] for i in range(4)]
            minus = [nodes[i] - nodes[7 - i] for i in range(4)]
            out = [None] * 8
            for i in range(4):
                even = sum(
                    plus[k] * float(0.5 * (stiffness[i, k] + stiffness[i, 7 - k]))
                    for k in range(4)
                )
                odd = sum(
                    minus[k] * float(0.5 * (stiffness[i, k] - stiffness[i, 7 - k]))
                    for k in range(4)
                )
                out[i], out[7 - i] = (even + odd, even - odd)
            if e:
                out[0] = out[0] + corner
            else:
                out[0] = out[0] + nodes[0] * float(stiffness[7, 7])
            corner = out[7]
            for i in range(8 if e == ey - 1 else 7):
                plane = 7 * e + i
                r[plane, at, :] = r[plane, at, :] - out[i] * scale
        return carry

    lax.fori_loop(0, rows // 8, along_y, 0)


def started(sources, targets, sems):
    copies = [
        pltpu.make_async_copy(source, target, sems.at[index])
        for index, (source, target) in enumerate(zip(sources, targets))
    ]
    for copy in copies:
        copy.start()
    return copies


def send_kernel(s):
    low = (s.x_nodes - 7) // 8 * 8
    lanes, nx, ny = (s.lanes, s.x_nodes, s.y_nodes)
    width = ny * s.z_nodes

    def kernel(
        guess_hbm, load_hbm, table_hbm, k_x_hbm,
        up_out, down_out,
        u, r, guess, load, table, k_x, top, sems,
    ):
        sources = [guess_hbm.at[low:nx], load_hbm.at[low:nx], table_hbm, k_x_hbm]
        sources += [guess_hbm.at[0:8]]
        copies = started(sources, [guess, load, table, k_x, top], sems)
        own_residual(s, low, copies[:4], u, r, guess, load, table, k_x)
        up_out[6:8, :] = jnp.zeros((2, up_out.shape[1]), f32)
        for y in range(ny + 1):
            put_line(s, up_out, y, r[y, nx - 6 - low : nx + 1 - low, :])
        put_line(s, up_out, ny + 1, u[0, nx - 6 - low : nx - low, :])
        copies[4].wait()
        gx = lax.axis_index("gx")
        gy = lax.axis_index("gy")
        live = lane_mask(s, (1, lanes), 1).astype(f32) * (gx > 0).astype(f32)
        live_y = (gy > 0).astype(f32)
        for y in range(ny):
            mask = live if y else live * live_y
            down_out[y : y + 1, :] = get_line(s, top, y, width)[0:1] * mask
        down_out[ny:, :] = jnp.zeros((down_out.shape[0] - ny, lanes), f32)

    return kernel


def residual_kernel(s):
    def kernel(
        guess_hbm, load_hbm, table_hbm, k_x_hbm,
        r, edge,
        u, guess, load, table, k_x, sems,
    ):
        sources = [guess_hbm, load_hbm, table_hbm, k_x_hbm]
        copies = started(sources, [guess, load, table, k_x], sems)
        own_residual(s, 0, copies, u, r, guess, load, table, k_x)
        edge[...] = u[0]

    return kernel


def joined_x_kernel(s):
    rows, lanes = (s.rows, s.lanes)
    nx, ny = (s.x_nodes, s.y_nodes)
    mass_y = line_tables(s.y_elems)["mass"][6:]

    def kernel(r_own, edge, u_first, below, above, c_below, c_above, r, line, up_out):
        width = below.shape[1]
        shape = (8, lanes)
        row = lax.broadcasted_iota(jnp.int32, shape, 0)
        inside = lane_mask(s, shape, 0)
        keep = (inside & (row < 6)).astype(f32)
        only = (inside & (row == 6)).astype(f32)
        zero = jnp.zeros((rows - 8 - nx, lanes), f32) if rows - 8 - nx else None
        for y in range(ny + 2):
            got = get_line(s, below, y, width)
            place = line if y == ny + 1 else r.at[y]
            own = edge[0:nx] if y == ny + 1 else r_own[y, 0:nx, :]
            place[0:2, :] = jnp.zeros((2, lanes), f32)
            place[2:8, :] = (got * keep)[0:6]
            place[8 : 8 + nx, :] = own
            if zero is not None:
                place[8 + nx :, :] = zero
            if y < ny:
                place[8:9, :] += (got * only)[6:7]
                both = (
                    c_below[...] * u_first[y : y + 1, :] + c_above[...] * above[y : y + 1, :]
                ) * float(mass_y[y])
                place[...] = place[...] - both
        for j in range(7):
            put_line(s, up_out, j, r[ny - 6 + j])
        up_out[:, 7 * s.z_nodes :] = jnp.zeros((rows, up_out.shape[1] - 7 * s.z_nodes), f32)

    return kernel


def patch_modes(s, vertices, plane_of, matrices, xf, xb, live):
    lam, sums, f_x, b_x, f_z, f_z_low, b_z, b_z_high = matrices
    rows = s.rows
    count = len(vertices)
    _, eigbasis = patch_basis()
    evens = [b for b in range(13) if symmetric(eigbasis[:, b])]
    gx = lax.axis_index("gx")
    gy = lax.axis_index("gy")
    shape = (s.modes_x, s.modes_z)
    mode = lax.broadcasted_iota(jnp.int32, shape, 0)
    vertex = lax.broadcasted_iota(jnp.int32, shape, 1) % s.half_z
    live_x = (mode % s.x_elems != 0) | (gx > 0)
    live[0] = (live_x & (vertex != 0)).astype(f32)
    live[1] = live_x.astype(f32)
    active = (gy > 0).astype(f32)

    def along_y(tile, carry):
        at = pl.ds(pl.multiple_of(tile * 8, 8), 8)
        for i, v in enumerate(vertices):
            first = [plane_of(7 * v + a - 6, at) for a in range(13)]
            if v == 0:
                first = [value * active for value in first]
            even = [first[6]] + [first[6 + a] + first[6 - a] for a in range(1, 7)]
            odd = [first[6 + a] - first[6 - a] for a in range(1, 7)]
            for b in range(13):
                if b in evens:
                    xf[b, i, at, :] = sum(even[a] * float(eigbasis[6 + a, b]) for a in range(7))
                else:
                    xf[b, i, at, :] = sum(odd[a] * float(eigbasis[7 + a, b]) for a in range(6))
        return carry

    lax.fori_loop(0, rows // 8, along_y, 0)

    def spectral(modes_of):
        pieces = []
        for b in modes_of:
            planes = [dot(f_x[...], stacked_rows(xf[b, v])) for v in range(count)]
            pieces += [plane[:, :LANES] for plane in planes]
            pieces += [plane[:, LANES:] for plane in planes]
        high_part, low_part = halves_of(jnp.concatenate(pieces, 0))
        modes = dot(jnp.concatenate([high_part, low_part], 1), f_z[...]) + dot(
            high_part, f_z_low[...]
        )
        modes = modes.reshape(len(modes_of), 2, count, s.modes_x, s.modes_z)
        pieces = []
        for i, b in enumerate(modes_of):
            factor = 1.0 / (sums[...] + lam[b])
            for t in range(2):
                scaled = modes[i, t] * (factor * live[t])[None]
                pieces.append(scaled.reshape(count * s.modes_x, s.modes_z))
        high_part, low_part = halves_of(jnp.concatenate(pieces, 0))
        both = dot(high_part, b_z[...])
        back = both[:, :LANES] + both[:, LANES:] + dot(low_part, b_z_high[...])
        back = back.reshape(len(modes_of), 2, count, s.modes_x, LANES)
        for i, b in enumerate(modes_of):
            for v in range(count):
                plane = jnp.concatenate([back[i, 0, v], back[i, 1, v]], 1)
                xb[b, v] = dot(b_x[...], stacked_rows(plane))

    for first in range(0, 13, GROUP):
        spectral(range(first, min(13, first + GROUP)))


def inner_kernel(s):
    def kernel(r_own, lam, sums, f_x, b_x, f_z, f_z_low, b_z, b_z_high, xb, xf, live):
        patch_modes(
            s,
            list(range(1, s.y_elems - 1)),
            lambda y, at: r_own[y, at, :],
            (lam, sums, f_x, b_x, f_z, f_z_low, b_z, b_z_high),
            xf,
            xb,
            live,
        )

    return kernel


def patch_kernel(s):
    rows, lanes = (s.rows, s.lanes)
    ey, ny = (s.y_elems, s.y_nodes)
    line_y = line_tables(ey)
    _, eigbasis = patch_basis()
    stiffness = element_stiffness()
    one_y = linear_from_cubic(-1, ey, -3, 3 * ey)
    evens = [b for b in range(13) if symmetric(eigbasis[:, b])]
    odds = [b for b in range(13) if b not in evens]

    def kernel(
        r_own, line, below, above, inner,
        lam, sums, f_x, b_x, f_z, f_z_low, b_z, b_z_high,
        m_xz, q_z, r_z, o_z, o_x, q_x, r_x,
        edge_out, own_out, three_out, one_out, down_out, up_out,
        r, xf, xb, c, cz, rz, hx, ex, rx, live,
    ):
        inside = lane_mask(s, (rows, lanes), 0).astype(f32)
        width = below.shape[1]
        lower = line[...] * m_xz[...]
        upper = above[...] * m_xz[...]
        for j in range(7):
            got = get_line(s, below, j, width) * inside
            if j < 6:
                r[j] = got - lower * float(stiffness[1 + j, 7])
            else:
                r[6] = r_own[0] + got
        for y in range(1, ny):
            plane = r_own[y]
            if y >= ny - 7:
                plane = plane - upper * float(stiffness[y - (ny - 7), 7])
            r[6 + y] = plane
        patch_modes(
            s,
            [0, ey - 1],
            lambda y, at: r[y + 6, at, :],
            (lam, sums, f_x, b_x, f_z, f_z_low, b_z, b_z_high),
            xf,
            xb,
            live,
        )

        def back_y(tile, carry):
            at = pl.ds(pl.multiple_of(tile * 8, 8), 8)
            tail = None
            for v in range(ey):
                if 0 < v < ey - 1:
                    modes = [inner[b, v - 1, at, :] for b in range(13)]
                else:
                    modes = [xb[b, min(v, 1), at, :] for b in range(13)]
                out = [None] * 13
                for a in range(7):
                    even = sum(modes[b] * float(eigbasis[6 + a, b]) for b in evens)
                    if a == 0:
                        out[6] = even
                        continue
                    odd = sum(modes[b] * float(eigbasis[6 + a, b]) for b in odds)
                    out[6 + a], out[6 - a] = (even + odd, even - odd)
                if v:
                    out[:6] = [value + other for value, other in zip(out[:6], tail)]
                tail = out[7:]
                for a in range(13 if v == ey - 1 else 7):
                    c[7 * v + a, at, :] = out[a]
            return carry

        lax.fori_loop(0, rows // 8, back_y, 0)

        for j in range(6):
            down_out[:, lanes * j : lanes * (j + 1)] = c[j]
        edge_out[...] = c[6:, 0:8, :]
        own_out[...] = c[6:, 8:, :]

        half = s.coarse_lanes
        rows_c = s.coarse_rows
        cz[...] = mm(c[...].reshape((ny + 6) * rows, lanes), q_z[...]).reshape(
            ny + 6, rows, 2 * half
        )
        rz[...] = mm(r[6 : ny + 6].reshape(ny * rows, lanes), r_z[...]).reshape(ny, rows, half)
        for y in range(ny + 6):
            plane = dot(q_x[...], stacked_rows(cz[y]))
            hx[y] = plane[:rows_c, :half]
            ex[y] = plane[rows_c:, :half] + plane[:rows_c, half:]
        for y in range(0, ny - 1, 2):
            pair = jnp.concatenate([rz[y], rz[y + 1]], 1)
            pair = dot(r_x[...], stacked_rows(pair))
            rx[y], rx[y + 1] = (pair[:, :half], pair[:, half:])
        if ny % 2:
            rx[ny - 1] = dot(r_x[...], stacked_rows(rz[ny - 1]))
        for j in range(s.coarse_y):
            three_out[j] = line_of_planes(
                np.concatenate(
                    [line_y["own"][j], -line_y["stiff_part"][j], -line_y["mass_part"][j]]
                ),
                [lambda y=y: rx[y] for y in range(ny)]
                + [lambda y=y: hx[y] for y in range(ny + 6)]
                + [lambda y=y: ex[y] for y in range(ny + 6)],
            )
        one_all = mm(
            three_out[...].reshape(s.coarse_y * rows_c, half), o_z[...]
        ).reshape(s.coarse_y, rows_c, LANES)
        for m in range(ey + 2):
            mixed = line_of_planes(
                one_y[m], [lambda j=j: one_all[j] for j in range(s.coarse_y)]
            )
            one_out[m] = mm(o_x[...], mixed)
        base = 6 * lanes
        down_out[:, base:] = jnp.zeros((rows, 2 * half), f32)
        up_out[...] = jnp.zeros(up_out.shape, f32)
        up_out[:, 0:half] = three_out[s.coarse_y - 1]
        for j in range(4):
            first, at = (rows_c * (j % 2), base + half * (j // 2))
            if j < 3:
                down_out[first : first + rows_c, at : at + half] = three_out[j]
            down_out[first : first + 8, at : at + half] += one_out[j]
            up_out[0:8, half * j : half * (j + 1)] += one_out[ey - 2 + j]

    return kernel


def coarse_place(s, index):
    high_rows = coarse_height(s)
    return index % high_rows, LANES * (index // high_rows)


def coarse_height(s):
    return up_to(-(-max(9 * s.y_elems, 4 * s.y_elems + 24) // 2), 24)


def join_kernel(s):
    lanes, half, rows_c = (s.lanes, s.coarse_lanes, s.coarse_rows)
    ey, ny = (s.y_elems, s.y_nodes)

    def kernel(edge, three, one, down, up, down_out, up_out, three_out, one_out):
        lane = lax.broadcasted_iota(jnp.int32, (rows_c, half), 1)
        is_three = (lane < s.coarse_z).astype(f32)
        is_one = (lane >= s.coarse_z).astype(f32)[0:8]
        for y in range(ny):
            plane = edge[y]
            if y >= ny - 6:
                j = y - (ny - 6)
                plane = plane + down[0:8, lanes * j : lanes * (j + 1)]
            down_out[6 * y : 6 * y + 6, :] = plane[2:8]
        base = 6 * lanes
        first = 6 * ny
        down_out[first:, :] = jnp.zeros((down_out.shape[0] - first, lanes), f32)
        up_out[...] = jnp.zeros(up_out.shape, f32)

        def from_above(k, count):
            row, at = (rows_c * (k % 2), base + half * (k // 2))
            return down[row : row + count, at : at + half]

        for j in range(3 * ey):
            plane = three[3 + j]
            if j >= 3 * ey - 3:
                plane = plane + from_above(j - (3 * ey - 3), rows_c)
            if j == 0:
                plane = plane + up[0:rows_c, 0:half]
            plane = plane * is_three
            three_out[j] = plane
            row, at = coarse_place(s, 3 * j)
            down_out[first + row : first + row + 3, at : at + half] = plane[0:3]
            row, at = coarse_place(s, j)
            up_out[row : row + 1, at : at + half] = plane[s.coarse_x - 1 : s.coarse_x]
        for j in range(ey + 6):
            y = j - 3
            plane = None
            if -1 <= y <= ey:
                plane = one[y + 1]
            if y <= 0:
                k = y + 3
                part = up[0:8, half * k : half * (k + 1)]
                plane = part if plane is None else plane + part
            if y >= ey - 1:
                part = from_above(y - (ey - 1), 8)
                plane = part if plane is None else plane + part
            plane = plane * is_one
            one_out[j] = plane
            row, at = coarse_place(s, 4 * j)
            down_out[first + row : first + row + 4, at : at + half] += plane[0:4]
            up_out[row : row + 4, at : at + half] += plane[s.x_elems - 2 : s.x_elems + 2]

    return kernel


def shared_lanes(s, shape):
    lane = lax.broadcasted_iota(jnp.int32, shape, 1)
    return ((lane >= s.split) & (lane < s.split + 6)).astype(f32)


def base_kernel(s):
    lanes, nx, ny = (s.lanes, s.x_nodes, s.y_nodes)
    width = ny * s.z_nodes

    def kernel(guess, weight, own, down, out):
        gx = lax.axis_index("gx")
        gy = lax.axis_index("gy")
        shape = (nx, lanes)
        row = lax.broadcasted_iota(jnp.int32, shape, 0)
        live = (lane_mask(s, shape, 1) & ((row != 0) | (gx > 0))).astype(f32)
        live_y = (gy > 0).astype(f32)
        shared = shared_lanes(s, shape)
        for y in range(ny):
            plane = own[y, 0:nx, :]
            if y >= ny - 6:
                j = y - (ny - 6)
                plane = plane + down[8 : 8 + nx, lanes * j : lanes * (j + 1)]
            plane = plane + pltpu.roll(plane, lanes - (LANES - s.split), 1) * shared
            mask = live if y else live * live_y
            factor = weight[...] * (1.0 if y % 7 == 0 else 0.5)
            put_line(s, out, y, (get_line(s, guess, y, width) + factor * plane) * mask)

    return kernel


def finish_kernel(s, x_total, y_total):
    lanes, half, rows_c, nz = (s.lanes, s.coarse_lanes, s.coarse_rows, s.z_nodes)
    ex, ey, nx, ny = (s.x_elems, s.y_elems, s.x_nodes, s.y_nodes)
    one_rows = up_to(ex + 6, 8)
    split = s.split

    def kernel(
        base, weight, right, left, three, one,
        smooth_out, three_out, coarse_out, fine, level,
    ):
        gx = lax.axis_index("gx")
        gy = lax.axis_index("gy")
        live_y = (gy > 0).astype(f32)
        shared = shared_lanes(s, (6, lanes))
        smooth_out[...] = base[...]
        for y in range(ny):
            plane = right[6 * y : 6 * y + 6, :]
            plane = plane + pltpu.roll(plane, lanes - (LANES - split), 1) * shared
            plane = plane * weight[nx - 6 : nx, :] * (1.0 if y % 7 == 0 else 0.5)
            for t in range(2):
                at = nz * y + split * t
                lanes_at = LANES * t + 6
                smooth_out[nx - 6 : nx, at : at + split] += plane[:, lanes_at : lanes_at + split]
        first = 6 * ny
        nzc = s.coarse_z
        lane = lax.broadcasted_iota(jnp.int32, (3 * ex, nzc), 1)
        row = lax.broadcasted_iota(jnp.int32, (3 * ex, nzc), 0)
        live = ((lane >= 1) & ((row >= 1) | (gx > 0))).astype(f32)
        for j in range(3 * ey):
            fine[j] = three[j]
            at_row, at = coarse_place(s, 3 * j)
            at_row += first
            fine[j, 3 * ex : 3 * ex + 3, :] += right[at_row : at_row + 3, at : at + half]
            at_row, at = coarse_place(s, j)
            fine[j, 3:4, :] += left[at_row : at_row + 1, at : at + half]
            mask = live if j else live * live_y
            three_out[:, nzc * j : nzc * (j + 1)] = fine[j, 3 : 3 * ex + 3, 0:nzc] * mask
        level[...] = jnp.zeros((ey + 6, one_rows, LANES), f32)
        for j in range(ey + 6):
            level[j, 2 : ex + 4, :] = one[j, 0 : ex + 2, :]
            at_row, at = coarse_place(s, 4 * j)
            level[j, 0:4, :] += left[at_row : at_row + 4, at : at + half]
            at_row += first
            level[j, ex + 2 : ex + 6, :] += right[at_row : at_row + 4, at : at + half]
        shape = (one_rows, LANES)
        lane = lax.broadcasted_iota(jnp.int32, shape, 1)
        row = lax.broadcasted_iota(jnp.int32, shape, 0)
        global_x = gx * ex + row - 3
        plane_mask = (
            (lane > s.coarse_z) & (lane < s.coarse_z + s.z_elems) & (row < ex + 6)
            & (global_x >= 1) & (global_x < x_total)
        )
        masks = []
        for j in range(ey + 6):
            global_y = gy * ey + (j - 3)
            inside = (global_y >= 1) & (global_y < y_total)
            masks.append((plane_mask & inside).astype(f32))
        levels = [level[j] for j in range(ey + 6)]
        error = [damping / 12.0 * a * m for a, m in zip(levels, masks)]
        zero = jnp.zeros(shape, f32)
        for sweep in range(1, JAC):
            lower = [zero] + error[:-1]
            upper = error[1:] + [zero]
            fresh = []
            for j in range(ey + 6):
                here = error[j]
                neighbours = (
                    lower[j]
                    + upper[j]
                    + pltpu.roll(here, 1, 0)
                    + pltpu.roll(here, one_rows - 1, 0)
                    + pltpu.roll(here, 1, 1)
                    + pltpu.roll(here, LANES - 1, 1)
                )
                applied = 12.0 * here - 2.0 * neighbours
                fresh.append((here + damping / 12.0 * (levels[j] - applied)) * masks[j])
            error = fresh
        nze = s.z_elems
        for j in range(ey):
            coarse_out[:, nze * j : nze * (j + 1)] = error[3 + j][
                3 : 3 + ex, s.coarse_z : s.coarse_z + nze
            ]

    return kernel


def local(load_vector, initial_guess):
    z_nodes = 7 * EZ
    x_nodes = load_vector.shape[0]
    y_nodes = load_vector.shape[1] // z_nodes
    s = Sizes(x_nodes, y_nodes, z_nodes)
    rows, lanes, half = (s.rows, s.lanes, s.coarse_lanes)
    ny, ey = (s.y_nodes, s.y_elems)
    width = y_nodes * z_nodes
    shape = lambda *dims: jax.ShapeDtypeStruct(dims, f32)
    params = pltpu.CompilerParams(vmem_limit_bytes=36 * 2**20)
    vmem = lambda count: [pl.BlockSpec(memory_space=pltpu.VMEM)] * count

    def call(kernel, name, outputs, operands, scratch=(), spaces=None, semaphores=0):
        specs = vmem(len(operands))
        for index, space in (spaces or {}).items():
            specs[index] = pl.BlockSpec(memory_space=space)
        return pl.pallas_call(
            kernel,
            out_shape=tuple(shape(*dims) for dims in outputs),
            in_specs=specs,
            out_specs=tuple(vmem(len(outputs))),
            scratch_shapes=[pltpu.VMEM(d, f32) if isinstance(d, tuple) else d for d in scratch]
            + ([pltpu.SemaphoreType.DMA((semaphores,))] if semaphores else []),
            compiler_params=params,
            name=name,
        )(*operands)

    in_hbm = lambda values: [pltpu.with_memory_space_constraint(v, pltpu.HBM) for v in values]
    hbm = {index: pltpu.HBM for index in range(4)}
    low = (x_nodes - 7) // 8 * 8
    constants = residual_constants(s, low)
    up, u_first = call(
        send_kernel(s),
        "send",
        ((8, up_to((ny + 2) * z_nodes, LANES)), (up_to(ny, 8), lanes)),
        in_hbm([initial_guess, load_vector] + constants),
        [
            (ny + 1, s.own_rows - low, lanes),
            (ny + 1, s.own_rows - low, lanes),
            (x_nodes - low, width),
            (x_nodes - low, width),
            constants[0].shape,
            pltpu.VMEM(constants[1].shape, jnp.bfloat16),
            (8, width),
        ],
        spaces=hbm,
        semaphores=5,
    )
    below = shifted(up, "gx", 1)
    above = shifted(u_first, "gx", -1)
    constants = residual_constants(s, 0)
    r_own, edge = call(
        residual_kernel(s),
        "residual",
        ((ny + 1, s.own_rows, lanes), (s.own_rows, lanes)),
        in_hbm([initial_guess, load_vector] + constants),
        [
            (ny + 1, s.own_rows, lanes),
            initial_guess.shape,
            load_vector.shape,
            constants[0].shape,
            pltpu.VMEM(constants[1].shape, jnp.bfloat16),
        ],
        spaces=hbm,
        semaphores=4,
    )
    r_x, line, up = call(
        joined_x_kernel(s),
        "joined_x",
        (
            (ny + 1, rows, lanes),
            (rows, lanes),
            (rows, up_to(7 * z_nodes, LANES)),
        ),
        [r_own, edge, u_first, below, above]
        + [jnp.asarray(v, f32) for v in coupling_constants(s)],
    )
    below = shifted(up, "gy", 1)
    above = shifted(line, "gy", -1)
    solve, coarse = patch_constants(s)
    (inner,) = call(
        inner_kernel(s),
        "inner",
        ((13, ey - 2, rows, lanes),),
        [r_x] + solve,
        [(13, ey - 2, rows, lanes), (2, s.modes_x, s.modes_z)],
        spaces={1: pltpu.SMEM},
    )
    edge, own, three, one, down, up = call(
        patch_kernel(s),
        "patches",
        (
            (ny, 8, lanes),
            (ny, rows - 8, lanes),
            (s.coarse_y, s.coarse_rows, half),
            (ey + 2, 8, LANES),
            (rows, 6 * lanes + 2 * half),
            (s.coarse_rows, 4 * half),
        ),
        [r_x, line, below, above, inner] + solve + coarse,
        [
            (ny + 6, rows, lanes),
            (13, 2, rows, lanes),
            (13, 2, rows, lanes),
            (ny + 6, rows, lanes),
            (ny + 6, rows, 2 * half),
            (ny, rows, half),
            (ny + 6, s.coarse_rows, half),
            (ny + 6, s.coarse_rows, half),
            (ny, s.coarse_rows, half),
            (2, s.modes_x, s.modes_z),
        ],
        spaces={5: pltpu.SMEM},
    )
    down = shifted(down, "gy", -1)
    up = shifted(up, "gy", 1)
    right, left, three, one = call(
        join_kernel(s),
        "join",
        (
            (6 * ny + coarse_height(s), lanes),
            (coarse_height(s), lanes),
            (3 * ey, s.coarse_rows, half),
            (ey + 6, 8, LANES),
        ),
        [edge, three, one, down, up],
    )
    right = shifted(right, "gx", -1)
    left = shifted(left, "gx", 1)
    weight_z = np.where(np.arange(z_nodes) % 7 == 0, 1.0, 0.5)
    weight = jnp.asarray(
        np.where(np.arange(x_nodes) % 7 == 0, 1.0, 0.5)[:, None]
        * rows_by_node(s, weight_z[:, None], True)[:, 0],
        f32,
    )
    (base,) = call(
        base_kernel(s), "base", ((x_nodes, width),), [initial_guess, weight, own, down]
    )
    return call(
        finish_kernel(s, s.x_elems * lax.axis_size("gx"), ey * lax.axis_size("gy")),
        "finish",
        (
            (x_nodes, width),
            (3 * s.x_elems, 3 * ey * s.coarse_z),
            (s.x_elems, ey * s.z_elems),
        ),
        [base, weight, right, left, three, one],
        [
            (3 * ey, s.coarse_rows, half),
            (ey + 6, up_to(s.x_elems + 6, 8), LANES),
        ],
    )


def solution(mesh):
    in_specs = (P("gx", "gy"), P("gx", "gy"))
    out_specs = (P("gx", "gy"), P("gx", "gy"), P("gx", "gy"))
    return jax.shard_map(local, mesh=mesh, in_specs=in_specs, out_specs=out_specs, check_vma=False)
```

```python
import math

import jax
import jax.numpy as jnp
import numpy as np
from jax import lax
from jax.experimental import pallas as pl
from jax.experimental.pallas import tpu as pltpu
from jax.sharding import PartitionSpec as P

EZ = 32
JAC = 4


points_seven = (
    -1.0,
    -0.8717401485096066,
    -0.5917001814331423,
    -0.2092992179024789,
    0.2092992179024789,
    0.5917001814331423,
    0.8717401485096066,
    1.0,
)
points_three = (-1.0, -0.4472135954999579, 0.4472135954999579, 1.0)
points_one = (-1.0, 1.0)
damping = 2.0 / 3.0


def shifted(array, axis, by):
    devices = lax.axis_size(axis)
    pairs = [(i, i + by) for i in range(devices) if 0 <= i + by < devices]
    return lax.ppermute(array, axis, pairs)


def legendre_at(degree, location):
    previous, current = (1.0, location)
    for level_idx in range(1, degree):
        previous, current = (
            current,
            ((2 * level_idx + 1) * location * current - level_idx * previous) / (level_idx + 1),
        )
    return current


def quadrature_weights():
    return np.array([2.0 / (56.0 * legendre_at(7, x) * legendre_at(7, x)) for x in points_seven])


def derivative_matrix():
    points = np.array(points_seven)
    products = np.array(
        [np.prod([points[i] - points[k] for k in range(8) if k != i]) for i in range(8)]
    )
    result = np.zeros((8, 8))
    for i in range(8):
        for j in range(8):
            if i != j:
                result[i, j] = products[i] / (products[j] * (points[i] - points[j]))
        result[i, i] = np.sum([1.0 / (points[i] - points[k]) for k in range(8) if k != i])
    return result


def element_stiffness():
    derivative = derivative_matrix()
    return derivative.T @ (quadrature_weights()[:, None] * derivative)


def assemble_line(elements):
    stiffness = element_stiffness()
    weights = quadrature_weights()
    extent = 7 * elements + 1
    global_stiff = np.zeros((extent, extent))
    lumped = np.zeros(extent)
    for m in range(elements):
        global_stiff[7 * m : 7 * m + 8, 7 * m : 7 * m + 8] += stiffness
        lumped[7 * m : 7 * m + 8] += weights
    return (global_stiff, lumped)


def jacobi_eigen(matrix):
    rotated_mat = matrix.copy()
    extent = matrix.shape[0]
    vectors = np.eye(extent)
    for sweep_idx in range(12):
        for p in range(extent - 1):
            for q in range(p + 1, extent):
                angle_rot = 0.5 * math.atan2(
                    2.0 * float(rotated_mat[p, q]), float(rotated_mat[q, q] - rotated_mat[p, p])
                )
                rotation = np.eye(extent)
                rotation[p, p] = math.cos(angle_rot)
                rotation[q, q] = math.cos(angle_rot)
                rotation[p, q] = math.sin(angle_rot)
                rotation[q, p] = -math.sin(angle_rot)
                rotated_mat = rotation.T @ rotated_mat @ rotation
                vectors = vectors @ rotation
    return (np.array([rotated_mat[i, i] for i in range(extent)]), vectors)


def patch_basis():
    global_stiff, lumped = assemble_line(2)
    inv_root = 1.0 / np.sqrt(lumped[1:14])
    eigvals, vectors = jacobi_eigen(
        inv_root[:, None] * global_stiff[1:14, 1:14] * inv_root[None, :]
    )
    return (eigvals, inv_root[:, None] * vectors)


def interp_matrix(coarse_pts):
    result = np.ones((8, len(coarse_pts)))
    for a in range(8):
        for c in range(len(coarse_pts)):
            for k in range(len(coarse_pts)):
                if k != c:
                    result[a, c] *= (points_seven[a] - coarse_pts[k]) / (
                        coarse_pts[c] - coarse_pts[k]
                    )
    return result


def restriction_rows(coarse_pts):
    shared = np.ones(8)
    shared[0] = 0.5
    shared[7] = 0.5
    return (interp_matrix(coarse_pts) * shared[:, None]).T


def restriction_line(elements, coarse_pts):
    degree = len(coarse_pts) - 1
    rows_mat = restriction_rows(coarse_pts)
    result = np.zeros((degree * elements + 1, 7 * elements + 1))
    for m in range(elements):
        result[degree * m : degree * m + degree + 1, 7 * m : 7 * m + 8] += rows_mat
    return result


def patch_matrix(eigbasis, vertices, extent):
    result = np.zeros((13 * vertices, extent))
    for b in range(13):
        for v in range(vertices):
            for a in range(13):
                node_idx = 7 * v + a
                result[b * vertices + v, node_idx] = eigbasis[a, b]
    return result


high = lax.Precision.HIGH
highest = lax.Precision.HIGHEST
LANES = 128
GROUP = 13
f32 = jnp.float32


def up_to(length, multiple):
    return -(-length // multiple) * multiple


def placed(matrix, shape, row=0, col=0):
    result = np.zeros(shape, np.float32)
    result[row : row + matrix.shape[0], col : col + matrix.shape[1]] = matrix
    return result


def mm(left, right, precision=high):
    return lax.dot_general(
        left, right, (((1,), (0,)), ((), ())), precision=precision, preferred_element_type=f32
    )


class Sizes:
    def __init__(self, x_nodes, y_nodes, z_nodes):
        self.x_nodes, self.y_nodes, self.z_nodes = (x_nodes, y_nodes, z_nodes)
        self.x_elems, self.y_elems, self.z_elems = (x_nodes // 7, y_nodes // 7, z_nodes // 7)
        self.own_rows = up_to(x_nodes + 1, 8)
        self.rows = up_to(x_nodes + 8, 8)
        self.half_z = self.z_elems // 2
        self.lanes = 2 * LANES
        self.modes_x = up_to(13 * self.x_elems, 8)
        self.modes_z = up_to(13 * self.half_z, LANES)
        self.coarse_x = 3 * self.x_elems + 4
        self.coarse_y = 3 * self.y_elems + 4
        self.coarse_z = 3 * self.z_elems
        self.coarse_rows = up_to(self.coarse_x, 8)
        self.coarse_lanes = up_to(self.coarse_z, LANES)
        split = 7 * self.half_z
        self.split = split
        self.node_of_lane = np.full(self.lanes, -1)
        self.node_of_lane[6 : 6 + split] = np.arange(split)
        self.node_of_lane[LANES : LANES + split + 6] = np.arange(split - 6, 2 * split)
        self.first_copy = self.node_of_lane >= 0
        self.first_copy[LANES : LANES + 6] = False


def line_tables(elements):
    nodes = 7 * elements
    stiff, lumped = assemble_line(elements + 2)
    restrict = restriction_line(elements + 3, points_three)[3 : 3 * elements + 7, 7 : nodes + 15]
    columns = np.arange(-6, nodes)
    weight = np.where(columns % 7 == 0, 1.0, 0.5)
    mass_part = restrict[:, 1:-1] * (lumped[1 : nodes + 7] * weight)[None, :]
    stiff_part = restrict @ (stiff[: nodes + 8, 1 : nodes + 7] * weight[None, :])
    return dict(
        own_stiff=stiff[7 : nodes + 8, 7 : nodes + 7],
        mass=lumped[1 : nodes + 7],
        own=restrict[:, 7:-1],
        mass_part=mass_part,
        stiff_part=stiff_part,
    )


def rows_by_node(s, matrix, every_copy):
    used = s.node_of_lane >= 0 if every_copy else s.first_copy
    return np.where(used[:, None], matrix[np.maximum(s.node_of_lane, 0)], 0.0)


def two_parts(matrix, low_type=jnp.bfloat16):
    high_part = matrix.astype(np.float32).astype(jnp.bfloat16)
    low_part = (matrix - high_part.astype(np.float64)).astype(low_type)
    return high_part, low_part


def residual_constants(s, low):
    line_x = line_tables(s.x_elems)
    stiff_z, lumped_z = assemble_line(s.z_elems)
    stiff_z, lumped_z = (stiff_z[: s.z_nodes, : s.z_nodes], lumped_z[: s.z_nodes])
    rows = up_to(s.x_nodes + 1 - low, 8)
    mass_x = np.zeros(low + rows)
    mass_x[: s.x_nodes] = line_x["mass"][6:]
    mass_x = mass_x[low:]
    mass_z = rows_by_node(s, lumped_z[:, None], True)[:, 0]
    spread = np.ones((rows, s.lanes))
    stiff = rows_by_node(s, stiff_z, False)
    stiff = rows_by_node(s, stiff.T, True).T
    own_x = placed(line_x["own_stiff"], (low + rows, low + rows)).astype(np.float64)
    high_x, rest = two_parts(own_x[low:, low:], np.float64)
    mid_x, low_x = two_parts(rest)
    table = np.concatenate(
        [
            stiff,
            spread * mass_x[:, None],
            spread * mass_z[None, :],
            mass_x[:, None] * mass_z[None, :],
        ]
    )
    return [
        jnp.asarray(table, f32),
        jnp.asarray(
            np.concatenate([high_x, high_x, high_x, mid_x, mid_x, low_x], 1), jnp.bfloat16
        ),
    ]


def coupling_constants(s):
    stiffness = element_stiffness()
    lumped_z = assemble_line(s.z_elems)[1][: s.z_nodes]
    mass_z = rows_by_node(s, lumped_z[:, None], True)[:, 0]
    below, above = (np.zeros(s.rows), np.zeros(s.rows))
    below[2:8] = stiffness[1:7, 7]
    above[8 + s.x_nodes - 7 : 8 + s.x_nodes] = stiffness[:7, 7]
    return [below[:, None] * mass_z[None, :], above[:, None] * mass_z[None, :]]


def patch_constants(s):
    line_x = line_tables(s.x_elems)
    stiff_z, lumped_z = assemble_line(s.z_elems)
    stiff_z, lumped_z = (stiff_z[: s.z_nodes, : s.z_nodes], lumped_z[: s.z_nodes])
    weight_z = np.where(np.arange(s.z_nodes) % 7 == 0, 1.0, 0.5)
    restrict_z = restriction_line(s.z_elems, points_three)[: s.coarse_z, : s.z_nodes]
    eigvals, eigbasis = patch_basis()
    mass_z = rows_by_node(s, lumped_z[:, None], True)[:, 0]
    mass_x = np.zeros(s.rows)
    mass_x[2 : s.x_nodes + 8] = line_x["mass"]
    fwd_x = placed(
        patch_matrix(eigbasis, s.x_elems, s.x_nodes + 6), (s.modes_x, s.rows), col=2
    )
    high_x, low_x = two_parts(fwd_x.astype(np.float64))
    fwd_z = np.zeros((LANES, s.modes_z))
    fwd_z[:, : 13 * s.half_z] = patch_matrix(eigbasis, s.half_z, LANES).T
    high_z, low_z = two_parts(fwd_z)
    sums = np.ones((s.modes_x, s.modes_z))
    sums[: 13 * s.x_elems, : 13 * s.half_z] = (
        np.repeat(eigvals, s.x_elems)[:, None] + np.repeat(eigvals, s.half_z)[None, :]
    )
    coarse_of_z = np.zeros((s.z_nodes, 2 * s.coarse_lanes))
    coarse_of_z[:, : s.coarse_z] = (restrict_z * (lumped_z * weight_z)[None, :]).T
    coarse_of_z[:, s.coarse_lanes : s.coarse_lanes + s.coarse_z] = (
        restrict_z @ (stiff_z * weight_z[None, :])
    ).T
    coarse_of_x = np.zeros((2 * s.coarse_rows, s.rows))
    coarse_of_x[: s.coarse_x, 2 : s.x_nodes + 8] = line_x["mass_part"]
    coarse_of_x[s.coarse_rows : s.coarse_rows + s.coarse_x, 2 : s.x_nodes + 8] = line_x[
        "stiff_part"
    ]
    own_z = np.zeros((s.z_nodes, s.coarse_lanes))
    own_z[:, : s.coarse_z] = restrict_z.T
    one_z = placed(
        linear_from_cubic(0, s.z_elems - 1, 0, s.coarse_z - 1).T,
        (s.coarse_lanes, LANES),
        col=s.coarse_z,
    )
    one_x = placed(linear_from_cubic(-1, s.x_elems, -3, 3 * s.x_elems), (8, s.coarse_rows))
    singles = [
        mass_x[:, None] * mass_z[None, :],
        rows_by_node(s, coarse_of_z, True),
        rows_by_node(s, own_z, False),
        one_z,
        one_x,
    ]
    own_x = placed(line_x["own"], (s.coarse_rows, s.rows), col=8).astype(np.float64)
    high_q, low_q = two_parts(coarse_of_x)
    high_r, low_r = two_parts(own_x)
    solve = [
        np.concatenate([high_x, high_x, low_x], 1),
        np.concatenate([high_x.T, high_x.T, low_x.T], 1),
        np.concatenate([high_z, high_z], 0),
        low_z,
        np.concatenate([high_z.T, low_z.T], 1),
        high_z.T,
    ]
    coarse = [
        np.concatenate([high_q, high_q, low_q], 1),
        np.concatenate([high_r, high_r, low_r], 1),
    ]
    return (
        [jnp.asarray(eigvals, f32), jnp.asarray(sums, f32)]
        + [jnp.asarray(value, jnp.bfloat16) for value in solve],
        [jnp.asarray(value, f32) for value in singles]
        + [jnp.asarray(value, jnp.bfloat16) for value in coarse],
    )


def halves_of(value):
    high_part = value.astype(jnp.bfloat16)
    return high_part, (value - high_part.astype(f32)).astype(jnp.bfloat16)


def stacked_whole(value):
    high_part = value.astype(jnp.bfloat16).astype(f32)
    rest = value - high_part
    mid_part = rest.astype(jnp.bfloat16).astype(f32)
    return jnp.concatenate(
        [high_part, mid_part, rest - mid_part, high_part, mid_part, high_part], 0
    ).astype(jnp.bfloat16)


def stacked_rows(value):
    high_part = value.astype(jnp.bfloat16).astype(f32)
    return jnp.concatenate([high_part, value - high_part, high_part], 0).astype(jnp.bfloat16)


def dot(left, right):
    return lax.dot_general(left, right, (((1,), (0,)), ((), ())), preferred_element_type=f32)


def linear_from_cubic(first, last, first_three, last_three):
    result = np.zeros((last - first + 1, last_three - first_three + 1))
    for m in range(first, last + 1):
        for offset, factor in (
            (0, 1.0),
            (1, (1.0 - points_three[1]) / 2.0),
            (2, (1.0 - points_three[2]) / 2.0),
            (-2, (1.0 + points_three[1]) / 2.0),
            (-1, (1.0 + points_three[2]) / 2.0),
        ):
            node = 3 * m + offset - first_three
            if 0 <= node < result.shape[1]:
                result[m - first, node] = factor
    return result


def line_of_planes(coefficients, planes):
    total = None
    for coefficient, plane in zip(coefficients, planes):
        if coefficient != 0.0:
            part = plane() * float(coefficient)
            total = part if total is None else total + part
    return total


def symmetric(vector):
    return abs(vector[0] - vector[-1]) < abs(vector[0] + vector[-1])


def lane_window(ref, start, width):
    if start < 0:
        return pltpu.roll(ref[:, 0:LANES], -start, 1)
    if start + LANES > width:
        return pltpu.roll(ref[:, width - LANES : width], width - start, 1)
    return ref[:, start : start + LANES]


def lane_mask(s, shape, first):
    lane = lax.broadcasted_iota(jnp.int32, shape, 1)
    return ((lane >= 6 + first) & (lane < 6 + s.split)) | (
        (lane >= LANES) & (lane < LANES + s.split + 6)
    )


def put_line(s, ref, index, plane):
    at = s.z_nodes * index
    rows = plane.shape[0]
    ref[0:rows, at : at + s.split] = plane[:, 6 : 6 + s.split]
    ref[0:rows, at + s.split : at + 2 * s.split] = plane[:, LANES + 6 : LANES + 6 + s.split]


def get_line(s, ref, index, width):
    at = s.z_nodes * index
    return jnp.concatenate(
        [lane_window(ref, at - 6, width), lane_window(ref, at + s.split - 6, width)], 1
    )


def own_residual(s, low, first_copies, u, r, guess, load, table, k_x, skip=0):
    lanes = s.lanes
    rows = up_to(s.x_nodes + 1 - low, 8)
    ey, ny = (s.y_elems, s.y_nodes)
    nx = s.x_nodes - low
    width = ny * s.z_nodes
    mass_y = line_tables(ey)["mass"][6:]
    stiffness = element_stiffness()
    gx = lax.axis_index("gx")
    gy = lax.axis_index("gy")
    shape = (nx, lanes)
    row = lax.broadcasted_iota(jnp.int32, shape, 0) + low
    live = (lane_mask(s, shape, 1) & ((row != 0) | (gx > 0))).astype(f32)
    live_y = (gy > 0).astype(f32)
    inside = lane_mask(s, shape, 0).astype(f32)
    pad = jnp.zeros((rows - nx, lanes), f32)
    first_copies[0].wait()
    for y in range(ny):
        mask = live if y else live * live_y
        u[y, 0:nx] = get_line(s, guess, y, width)[skip:] * mask
        u[y, nx:] = pad
    first_copies[1].wait()
    for y in range(ny):
        r[y, 0:nx] = get_line(s, load, y, width)[skip:] * inside
        r[y, nx:] = pad
    u[ny] = jnp.zeros((rows, lanes), f32)
    r[ny] = jnp.zeros((rows, lanes), f32)
    for copy in first_copies[2:]:
        copy.wait()
    m_x, m_z, m_xz = [
        table.at[lanes + rows * i : lanes + rows * (i + 1)] for i in range(3)
    ]
    planes = u[0:ny].reshape(ny * rows, lanes)
    z_term = mm(planes, table[0:lanes], highest).reshape(ny, rows, lanes)
    for y in range(ny):
        x_term = dot(k_x[...], stacked_whole(u[y]))
        both = x_term * m_z[...] + z_term[y] * m_x[...]
        r[y] = r[y] - float(mass_y[y]) * both

    def along_y(tile, carry):
        at = pl.ds(pl.multiple_of(tile * 8, 8), 8)
        scale = m_xz[at, :]
        corner = None
        for e in range(ey):
            nodes = [u[7 * e + i, at, :] for i in range(8)]
            plus = [nodes[i] + nodes[7 - i] for i in range(4)]
            minus = [nodes[i] - nodes[7 - i] for i in range(4)]
            out = [None] * 8
            for i in range(4):
                even = sum(
                    plus[k] * float(0.5 * (stiffness[i, k] + stiffness[i, 7 - k]))
                    for k in range(4)
                )
                odd = sum(
                    minus[k] * float(0.5 * (stiffness[i, k] - stiffness[i, 7 - k]))
                    for k in range(4)
                )
                out[i], out[7 - i] = (even + odd, even - odd)
            if e:
                out[0] = out[0] + corner
            else:
                out[0] = out[0] + nodes[0] * float(stiffness[7, 7])
            corner = out[7]
            for i in range(8 if e == ey - 1 else 7):
                plane = 7 * e + i
                r[plane, at, :] = r[plane, at, :] - out[i] * scale
        return carry

    lax.fori_loop(0, rows // 8, along_y, 0)


def started(sources, targets, sems):
    copies = [
        pltpu.make_async_copy(source, target, sems.at[index])
        for index, (source, target) in enumerate(zip(sources, targets))
    ]
    for copy in copies:
        copy.start()
    return copies


def send_kernel(s):
    low = s.x_nodes - 7
    tile_low = low // 8 * 8
    lanes, nx, ny = (s.lanes, s.x_nodes, s.y_nodes)
    width = ny * s.z_nodes

    def kernel(
        guess_hbm, load_hbm, table_hbm, k_x_hbm,
        up_out, down_out,
        u, r, guess, load, table, k_x, top, sems,
    ):
        sources = [guess_hbm.at[tile_low:nx], load_hbm.at[tile_low:nx], table_hbm, k_x_hbm]
        sources += [guess_hbm.at[0:8]]
        copies = started(sources, [guess, load, table, k_x, top], sems)
        skip = low - tile_low
        own_residual(s, low, copies[:4], u, r, guess, load, table, k_x, skip)
        up_out[6:8, :] = jnp.zeros((2, up_out.shape[1]), f32)
        for y in range(ny + 1):
            put_line(s, up_out, y, r[y, nx - 6 - low : nx + 1 - low, :])
        put_line(s, up_out, ny + 1, u[0, nx - 6 - low : nx - low, :])
        copies[4].wait()
        gx = lax.axis_index("gx")
        gy = lax.axis_index("gy")
        live = lane_mask(s, (1, lanes), 1).astype(f32) * (gx > 0).astype(f32)
        live_y = (gy > 0).astype(f32)
        for y in range(ny):
            mask = live if y else live * live_y
            down_out[y : y + 1, :] = get_line(s, top, y, width)[0:1] * mask
        down_out[ny:, :] = jnp.zeros((down_out.shape[0] - ny, lanes), f32)

    return kernel


def residual_kernel(s):
    def kernel(
        guess_hbm, load_hbm, table_hbm, k_x_hbm,
        r, edge,
        u, guess, load, table, k_x, sems,
    ):
        sources = [guess_hbm, load_hbm, table_hbm, k_x_hbm]
        copies = started(sources, [guess, load, table, k_x], sems)
        own_residual(s, 0, copies, u, r, guess, load, table, k_x)
        edge[...] = u[0]

    return kernel


def joined_x_kernel(s):
    rows, lanes = (s.rows, s.lanes)
    nx, ny = (s.x_nodes, s.y_nodes)
    mass_y = line_tables(s.y_elems)["mass"][6:]

    def kernel(r_own, edge, u_first, below, above, c_below, c_above, r, line, up_out):
        width = below.shape[1]
        shape = (8, lanes)
        row = lax.broadcasted_iota(jnp.int32, shape, 0)
        inside = lane_mask(s, shape, 0)
        keep = (inside & (row < 6)).astype(f32)
        only = (inside & (row == 6)).astype(f32)
        zero = jnp.zeros((rows - 8 - nx, lanes), f32) if rows - 8 - nx else None
        for y in range(ny + 2):
            got = get_line(s, below, y, width)
            place = line if y == ny + 1 else r.at[y]
            own = edge[0:nx] if y == ny + 1 else r_own[y, 0:nx, :]
            place[0:2, :] = jnp.zeros((2, lanes), f32)
            place[2:8, :] = (got * keep)[0:6]
            place[8 : 8 + nx, :] = own
            if zero is not None:
                place[8 + nx :, :] = zero
            if y < ny:
                place[8:9, :] += (got * only)[6:7]
                both = (
                    c_below[...] * u_first[y : y + 1, :] + c_above[...] * above[y : y + 1, :]
                ) * float(mass_y[y])
                place[...] = place[...] - both
        for j in range(7):
            put_line(s, up_out, j, r[ny - 6 + j])
        up_out[:, 7 * s.z_nodes :] = jnp.zeros((rows, up_out.shape[1] - 7 * s.z_nodes), f32)

    return kernel


def patch_modes(s, vertices, plane_of, matrices, xf, xb, live):
    lam, sums, f_x, b_x, f_z, f_z_low, b_z, b_z_high = matrices
    rows = s.rows
    count = len(vertices)
    _, eigbasis = patch_basis()
    evens = [b for b in range(13) if symmetric(eigbasis[:, b])]
    gx = lax.axis_index("gx")
    gy = lax.axis_index("gy")
    shape = (s.modes_x, s.modes_z)
    mode = lax.broadcasted_iota(jnp.int32, shape, 0)
    vertex = lax.broadcasted_iota(jnp.int32, shape, 1) % s.half_z
    live_x = (mode % s.x_elems != 0) | (gx > 0)
    live[0] = (live_x & (vertex != 0)).astype(f32)
    live[1] = live_x.astype(f32)
    active = (gy > 0).astype(f32)

    def along_y(tile, carry):
        at = pl.ds(pl.multiple_of(tile * 8, 8), 8)
        for i, v in enumerate(vertices):
            first = [plane_of(7 * v + a - 6, at) for a in range(13)]
            if v == 0:
                first = [value * active for value in first]
            even = [first[6]] + [first[6 + a] + first[6 - a] for a in range(1, 7)]
            odd = [first[6 + a] - first[6 - a] for a in range(1, 7)]
            for b in range(13):
                if b in evens:
                    xf[b, i, at, :] = sum(even[a] * float(eigbasis[6 + a, b]) for a in range(7))
                else:
                    xf[b, i, at, :] = sum(odd[a] * float(eigbasis[7 + a, b]) for a in range(6))
        return carry

    lax.fori_loop(0, rows // 8, along_y, 0)

    def spectral(modes_of):
        pieces = []
        for b in modes_of:
            planes = [dot(f_x[...], stacked_rows(xf[b, v])) for v in range(count)]
            pieces += [plane[:, :LANES] for plane in planes]
            pieces += [plane[:, LANES:] for plane in planes]
        high_part, low_part = halves_of(jnp.concatenate(pieces, 0))
        modes = dot(jnp.concatenate([high_part, low_part], 1), f_z[...]) + dot(
            high_part, f_z_low[...]
        )
        modes = modes.reshape(len(modes_of), 2, count, s.modes_x, s.modes_z)
        pieces = []
        for i, b in enumerate(modes_of):
            factor = 1.0 / (sums[...] + lam[b])
            for t in range(2):
                scaled = modes[i, t] * (factor * live[t])[None]
                pieces.append(scaled.reshape(count * s.modes_x, s.modes_z))
        high_part, low_part = halves_of(jnp.concatenate(pieces, 0))
        both = dot(high_part, b_z[...])
        back = both[:, :LANES] + both[:, LANES:] + dot(low_part, b_z_high[...])
        back = back.reshape(len(modes_of), 2, count, s.modes_x, LANES)
        for i, b in enumerate(modes_of):
            for v in range(count):
                plane = jnp.concatenate([back[i, 0, v], back[i, 1, v]], 1)
                xb[b, v] = dot(b_x[...], stacked_rows(plane))

    for first in range(0, 13, GROUP):
        spectral(range(first, min(13, first + GROUP)))


def inner_kernel(s):
    def kernel(r_own, lam, sums, f_x, b_x, f_z, f_z_low, b_z, b_z_high, xb, xf, live):
        patch_modes(
            s,
            list(range(1, s.y_elems - 1)),
            lambda y, at: r_own[y, at, :],
            (lam, sums, f_x, b_x, f_z, f_z_low, b_z, b_z_high),
            xf,
            xb,
            live,
        )

    return kernel


def patch_kernel(s):
    rows, lanes = (s.rows, s.lanes)
    ey, ny = (s.y_elems, s.y_nodes)
    line_y = line_tables(ey)
    _, eigbasis = patch_basis()
    stiffness = element_stiffness()
    one_y = linear_from_cubic(-1, ey, -3, 3 * ey)
    evens = [b for b in range(13) if symmetric(eigbasis[:, b])]
    odds = [b for b in range(13) if b not in evens]

    def kernel(
        r_own, line, below, above, inner,
        lam, sums, f_x, b_x, f_z, f_z_low, b_z, b_z_high,
        m_xz, q_z, r_z, o_z, o_x, q_x, r_x,
        edge_out, own_out, three_out, one_out, down_out, up_out,
        r, xf, xb, c, cz, rz, hx, ex, rx, live,
    ):
        inside = lane_mask(s, (rows, lanes), 0).astype(f32)
        width = below.shape[1]
        lower = line[...] * m_xz[...]
        upper = above[...] * m_xz[...]
        for j in range(7):
            got = get_line(s, below, j, width) * inside
            if j < 6:
                r[j] = got - lower * float(stiffness[1 + j, 7])
            else:
                r[6] = r_own[0] + got
        for y in range(1, ny):
            plane = r_own[y]
            if y >= ny - 7:
                plane = plane - upper * float(stiffness[y - (ny - 7), 7])
            r[6 + y] = plane
        patch_modes(
            s,
            [0, ey - 1],
            lambda y, at: r[y + 6, at, :],
            (lam, sums, f_x, b_x, f_z, f_z_low, b_z, b_z_high),
            xf,
            xb,
            live,
        )

        def back_y(tile, carry):
            at = pl.ds(pl.multiple_of(tile * 8, 8), 8)
            tail = None
            for v in range(ey):
                if 0 < v < ey - 1:
                    modes = [inner[b, v - 1, at, :] for b in range(13)]
                else:
                    modes = [xb[b, min(v, 1), at, :] for b in range(13)]
                out = [None] * 13
                for a in range(7):
                    even = sum(modes[b] * float(eigbasis[6 + a, b]) for b in evens)
                    if a == 0:
                        out[6] = even
                        continue
                    odd = sum(modes[b] * float(eigbasis[6 + a, b]) for b in odds)
                    out[6 + a], out[6 - a] = (even + odd, even - odd)
                if v:
                    out[:6] = [value + other for value, other in zip(out[:6], tail)]
                tail = out[7:]
                for a in range(13 if v == ey - 1 else 7):
                    c[7 * v + a, at, :] = out[a]
            return carry

        lax.fori_loop(0, rows // 8, back_y, 0)

        for j in range(6):
            down_out[:, lanes * j : lanes * (j + 1)] = c[j]
        edge_out[...] = c[6:, 0:8, :]
        own_out[...] = c[6:, 8:, :]

        half = s.coarse_lanes
        rows_c = s.coarse_rows
        cz[...] = mm(c[...].reshape((ny + 6) * rows, lanes), q_z[...]).reshape(
            ny + 6, rows, 2 * half
        )
        rz[...] = mm(r[6 : ny + 6].reshape(ny * rows, lanes), r_z[...]).reshape(ny, rows, half)
        for y in range(ny + 6):
            plane = dot(q_x[...], stacked_rows(cz[y]))
            hx[y] = plane[:rows_c, :half]
            ex[y] = plane[rows_c:, :half] + plane[:rows_c, half:]
        for y in range(0, ny - 1, 2):
            pair = jnp.concatenate([rz[y], rz[y + 1]], 1)
            pair = dot(r_x[...], stacked_rows(pair))
            rx[y], rx[y + 1] = (pair[:, :half], pair[:, half:])
        if ny % 2:
            rx[ny - 1] = dot(r_x[...], stacked_rows(rz[ny - 1]))
        for j in range(s.coarse_y):
            three_out[j] = line_of_planes(
                np.concatenate(
                    [line_y["own"][j], -line_y["stiff_part"][j], -line_y["mass_part"][j]]
                ),
                [lambda y=y: rx[y] for y in range(ny)]
                + [lambda y=y: hx[y] for y in range(ny + 6)]
                + [lambda y=y: ex[y] for y in range(ny + 6)],
            )
        one_all = mm(
            three_out[...].reshape(s.coarse_y * rows_c, half), o_z[...]
        ).reshape(s.coarse_y, rows_c, LANES)
        for m in range(ey + 2):
            mixed = line_of_planes(
                one_y[m], [lambda j=j: one_all[j] for j in range(s.coarse_y)]
            )
            one_out[m] = mm(o_x[...], mixed)
        base = 6 * lanes
        down_out[:, base:] = jnp.zeros((rows, 2 * half), f32)
        up_out[...] = jnp.zeros(up_out.shape, f32)
        up_out[:, 0:half] = three_out[s.coarse_y - 1]
        for j in range(4):
            first, at = (rows_c * (j % 2), base + half * (j // 2))
            if j < 3:
                down_out[first : first + rows_c, at : at + half] = three_out[j]
            down_out[first : first + 8, at : at + half] += one_out[j]
            up_out[0:8, half * j : half * (j + 1)] += one_out[ey - 2 + j]

    return kernel


def coarse_place(s, index):
    high_rows = coarse_height(s)
    return index % high_rows, LANES * (index // high_rows)


def coarse_height(s):
    return up_to(-(-max(9 * s.y_elems, 4 * s.y_elems + 24) // 2), 24)


def join_kernel(s):
    lanes, half, rows_c = (s.lanes, s.coarse_lanes, s.coarse_rows)
    ey, ny = (s.y_elems, s.y_nodes)

    def kernel(edge, three, one, down, up, down_out, up_out, three_out, one_out):
        lane = lax.broadcasted_iota(jnp.int32, (rows_c, half), 1)
        is_three = (lane < s.coarse_z).astype(f32)
        is_one = (lane >= s.coarse_z).astype(f32)[0:8]
        for y in range(ny):
            plane = edge[y]
            if y >= ny - 6:
                j = y - (ny - 6)
                plane = plane + down[0:8, lanes * j : lanes * (j + 1)]
            down_out[6 * y : 6 * y + 6, :] = plane[2:8]
        base = 6 * lanes
        first = 6 * ny
        down_out[first:, :] = jnp.zeros((down_out.shape[0] - first, lanes), f32)
        up_out[...] = jnp.zeros(up_out.shape, f32)

        def from_above(k, count):
            row, at = (rows_c * (k % 2), base + half * (k // 2))
            return down[row : row + count, at : at + half]

        for j in range(3 * ey):
            plane = three[3 + j]
            if j >= 3 * ey - 3:
                plane = plane + from_above(j - (3 * ey - 3), rows_c)
            if j == 0:
                plane = plane + up[0:rows_c, 0:half]
            plane = plane * is_three
            three_out[j] = plane
            row, at = coarse_place(s, 3 * j)
            down_out[first + row : first + row + 3, at : at + half] = plane[0:3]
            row, at = coarse_place(s, j)
            up_out[row : row + 1, at : at + half] = plane[s.coarse_x - 1 : s.coarse_x]
        for j in range(ey + 6):
            y = j - 3
            plane = None
            if -1 <= y <= ey:
                plane = one[y + 1]
            if y <= 0:
                k = y + 3
                part = up[0:8, half * k : half * (k + 1)]
                plane = part if plane is None else plane + part
            if y >= ey - 1:
                part = from_above(y - (ey - 1), 8)
                plane = part if plane is None else plane + part
            plane = plane * is_one
            one_out[j] = plane
            row, at = coarse_place(s, 4 * j)
            down_out[first + row : first + row + 4, at : at + half] += plane[0:4]
            up_out[row : row + 4, at : at + half] += plane[s.x_elems - 2 : s.x_elems + 2]

    return kernel


def shared_lanes(s, shape):
    lane = lax.broadcasted_iota(jnp.int32, shape, 1)
    return ((lane >= s.split) & (lane < s.split + 6)).astype(f32)


def base_kernel(s):
    lanes, nx, ny = (s.lanes, s.x_nodes, s.y_nodes)
    width = ny * s.z_nodes

    def kernel(guess, weight, own, down, out):
        gx = lax.axis_index("gx")
        gy = lax.axis_index("gy")
        shape = (nx, lanes)
        row = lax.broadcasted_iota(jnp.int32, shape, 0)
        live = (lane_mask(s, shape, 1) & ((row != 0) | (gx > 0))).astype(f32)
        live_y = (gy > 0).astype(f32)
        shared = shared_lanes(s, shape)
        for y in range(ny):
            plane = own[y, 0:nx, :]
            if y >= ny - 6:
                j = y - (ny - 6)
                plane = plane + down[8 : 8 + nx, lanes * j : lanes * (j + 1)]
            plane = plane + pltpu.roll(plane, lanes - (LANES - s.split), 1) * shared
            mask = live if y else live * live_y
            factor = weight[...] * (1.0 if y % 7 == 0 else 0.5)
            put_line(s, out, y, (get_line(s, guess, y, width) + factor * plane) * mask)

    return kernel


def finish_kernel(s, x_total, y_total):
    lanes, half, rows_c, nz = (s.lanes, s.coarse_lanes, s.coarse_rows, s.z_nodes)
    ex, ey, nx, ny = (s.x_elems, s.y_elems, s.x_nodes, s.y_nodes)
    one_rows = up_to(ex + 6, 8)
    split = s.split

    def kernel(
        base, weight, right, left, three, one,
        smooth_out, three_out, coarse_out, fine, level,
    ):
        gx = lax.axis_index("gx")
        gy = lax.axis_index("gy")
        live_y = (gy > 0).astype(f32)
        shared = shared_lanes(s, (6, lanes))
        smooth_out[...] = base[...]
        for y in range(ny):
            plane = right[6 * y : 6 * y + 6, :]
            plane = plane + pltpu.roll(plane, lanes - (LANES - split), 1) * shared
            plane = plane * weight[nx - 6 : nx, :] * (1.0 if y % 7 == 0 else 0.5)
            for t in range(2):
                at = nz * y + split * t
                lanes_at = LANES * t + 6
                smooth_out[nx - 6 : nx, at : at + split] += plane[:, lanes_at : lanes_at + split]
        first = 6 * ny
        nzc = s.coarse_z
        lane = lax.broadcasted_iota(jnp.int32, (3 * ex, nzc), 1)
        row = lax.broadcasted_iota(jnp.int32, (3 * ex, nzc), 0)
        live = ((lane >= 1) & ((row >= 1) | (gx > 0))).astype(f32)
        for j in range(3 * ey):
            fine[j] = three[j]
            at_row, at = coarse_place(s, 3 * j)
            at_row += first
            fine[j, 3 * ex : 3 * ex + 3, :] += right[at_row : at_row + 3, at : at + half]
            at_row, at = coarse_place(s, j)
            fine[j, 3:4, :] += left[at_row : at_row + 1, at : at + half]
            mask = live if j else live * live_y
            three_out[:, nzc * j : nzc * (j + 1)] = fine[j, 3 : 3 * ex + 3, 0:nzc] * mask
        level[...] = jnp.zeros((ey + 6, one_rows, LANES), f32)
        for j in range(ey + 6):
            level[j, 2 : ex + 4, :] = one[j, 0 : ex + 2, :]
            at_row, at = coarse_place(s, 4 * j)
            level[j, 0:4, :] += left[at_row : at_row + 4, at : at + half]
            at_row += first
            level[j, ex + 2 : ex + 6, :] += right[at_row : at_row + 4, at : at + half]
        shape = (one_rows, LANES)
        lane = lax.broadcasted_iota(jnp.int32, shape, 1)
        row = lax.broadcasted_iota(jnp.int32, shape, 0)
        global_x = gx * ex + row - 3
        plane_mask = (
            (lane > s.coarse_z) & (lane < s.coarse_z + s.z_elems) & (row < ex + 6)
            & (global_x >= 1) & (global_x < x_total)
        )
        masks = []
        for j in range(ey + 6):
            global_y = gy * ey + (j - 3)
            inside = (global_y >= 1) & (global_y < y_total)
            masks.append((plane_mask & inside).astype(f32))
        levels = [level[j] for j in range(ey + 6)]
        error = [damping / 12.0 * a * m for a, m in zip(levels, masks)]
        zero = jnp.zeros(shape, f32)
        for sweep in range(1, JAC):
            lower = [zero] + error[:-1]
            upper = error[1:] + [zero]
            fresh = []
            for j in range(ey + 6):
                here = error[j]
                neighbours = (
                    lower[j]
                    + upper[j]
                    + pltpu.roll(here, 1, 0)
                    + pltpu.roll(here, one_rows - 1, 0)
                    + pltpu.roll(here, 1, 1)
                    + pltpu.roll(here, LANES - 1, 1)
                )
                applied = 12.0 * here - 2.0 * neighbours
                fresh.append((here + damping / 12.0 * (levels[j] - applied)) * masks[j])
            error = fresh
        nze = s.z_elems
        for j in range(ey):
            coarse_out[:, nze * j : nze * (j + 1)] = error[3 + j][
                3 : 3 + ex, s.coarse_z : s.coarse_z + nze
            ]

    return kernel


def local(load_vector, initial_guess):
    z_nodes = 7 * EZ
    x_nodes = load_vector.shape[0]
    y_nodes = load_vector.shape[1] // z_nodes
    s = Sizes(x_nodes, y_nodes, z_nodes)
    rows, lanes, half = (s.rows, s.lanes, s.coarse_lanes)
    ny, ey = (s.y_nodes, s.y_elems)
    width = y_nodes * z_nodes
    shape = lambda *dims: jax.ShapeDtypeStruct(dims, f32)
    params = pltpu.CompilerParams(vmem_limit_bytes=36 * 2**20)
    vmem = lambda count: [pl.BlockSpec(memory_space=pltpu.VMEM)] * count

    def call(kernel, name, outputs, operands, scratch=(), spaces=None, semaphores=0):
        specs = vmem(len(operands))
        for index, space in (spaces or {}).items():
            specs[index] = pl.BlockSpec(memory_space=space)
        return pl.pallas_call(
            kernel,
            out_shape=tuple(shape(*dims) for dims in outputs),
            in_specs=specs,
            out_specs=tuple(vmem(len(outputs))),
            scratch_shapes=[pltpu.VMEM(d, f32) if isinstance(d, tuple) else d for d in scratch]
            + ([pltpu.SemaphoreType.DMA((semaphores,))] if semaphores else []),
            compiler_params=params,
            name=name,
        )(*operands)

    in_hbm = lambda values: [pltpu.with_memory_space_constraint(v, pltpu.HBM) for v in values]
    hbm = {index: pltpu.HBM for index in range(4)}
    low = x_nodes - 7
    taken = x_nodes - low // 8 * 8
    constants = residual_constants(s, low)
    up, u_first = call(
        send_kernel(s),
        "send",
        ((8, up_to((ny + 2) * z_nodes, LANES)), (up_to(ny, 8), lanes)),
        in_hbm([initial_guess, load_vector] + constants),
        [
            (ny + 1, 8, lanes),
            (ny + 1, 8, lanes),
            (taken, width),
            (taken, width),
            constants[0].shape,
            pltpu.VMEM(constants[1].shape, jnp.bfloat16),
            (8, width),
        ],
        spaces=hbm,
        semaphores=5,
    )
    below = shifted(up, "gx", 1)
    above = shifted(u_first, "gx", -1)
    constants = residual_constants(s, 0)
    r_own, edge = call(
        residual_kernel(s),
        "residual",
        ((ny + 1, s.own_rows, lanes), (s.own_rows, lanes)),
        in_hbm([initial_guess, load_vector] + constants),
        [
            (ny + 1, s.own_rows, lanes),
            initial_guess.shape,
            load_vector.shape,
            constants[0].shape,
            pltpu.VMEM(constants[1].shape, jnp.bfloat16),
        ],
        spaces=hbm,
        semaphores=4,
    )
    r_x, line, up = call(
        joined_x_kernel(s),
        "joined_x",
        (
            (ny + 1, rows, lanes),
            (rows, lanes),
            (rows, up_to(7 * z_nodes, LANES)),
        ),
        [r_own, edge, u_first, below, above]
        + [jnp.asarray(v, f32) for v in coupling_constants(s)],
    )
    below = shifted(up, "gy", 1)
    above = shifted(line, "gy", -1)
    solve, coarse = patch_constants(s)
    (inner,) = call(
        inner_kernel(s),
        "inner",
        ((13, ey - 2, rows, lanes),),
        [r_x] + solve,
        [(13, ey - 2, rows, lanes), (2, s.modes_x, s.modes_z)],
        spaces={1: pltpu.SMEM},
    )
    edge, own, three, one, down, up = call(
        patch_kernel(s),
        "patches",
        (
            (ny, 8, lanes),
            (ny, rows - 8, lanes),
            (s.coarse_y, s.coarse_rows, half),
            (ey + 2, 8, LANES),
            (rows, 6 * lanes + 2 * half),
            (s.coarse_rows, 4 * half),
        ),
        [r_x, line, below, above, inner] + solve + coarse,
        [
            (ny + 6, rows, lanes),
            (13, 2, rows, lanes),
            (13, 2, rows, lanes),
            (ny + 6, rows, lanes),
            (ny + 6, rows, 2 * half),
            (ny, rows, half),
            (ny + 6, s.coarse_rows, half),
            (ny + 6, s.coarse_rows, half),
            (ny, s.coarse_rows, half),
            (2, s.modes_x, s.modes_z),
        ],
        spaces={5: pltpu.SMEM},
    )
    down = shifted(down, "gy", -1)
    up = shifted(up, "gy", 1)
    right, left, three, one = call(
        join_kernel(s),
        "join",
        (
            (6 * ny + coarse_height(s), lanes),
            (coarse_height(s), lanes),
            (3 * ey, s.coarse_rows, half),
            (ey + 6, 8, LANES),
        ),
        [edge, three, one, down, up],
    )
    right = shifted(right, "gx", -1)
    left = shifted(left, "gx", 1)
    weight_z = np.where(np.arange(z_nodes) % 7 == 0, 1.0, 0.5)
    weight = jnp.asarray(
        np.where(np.arange(x_nodes) % 7 == 0, 1.0, 0.5)[:, None]
        * rows_by_node(s, weight_z[:, None], True)[:, 0],
        f32,
    )
    (base,) = call(
        base_kernel(s), "base", ((x_nodes, width),), [initial_guess, weight, own, down]
    )
    return call(
        finish_kernel(s, s.x_elems * lax.axis_size("gx"), ey * lax.axis_size("gy")),
        "finish",
        (
            (x_nodes, width),
            (3 * s.x_elems, 3 * ey * s.coarse_z),
            (s.x_elems, ey * s.z_elems),
        ),
        [base, weight, right, left, three, one],
        [
            (3 * ey, s.coarse_rows, half),
            (ey + 6, up_to(s.x_elems + 6, 8), LANES),
        ],
    )


def solution(mesh):
    in_specs = (P("gx", "gy"), P("gx", "gy"))
    out_specs = (P("gx", "gy"), P("gx", "gy"), P("gx", "gy"))
    return jax.shard_map(local, mesh=mesh, in_specs=in_specs, out_specs=out_specs, check_vma=False)
```

```python
import math

import jax
import jax.numpy as jnp
import numpy as np
from jax import lax
from jax.experimental import pallas as pl
from jax.experimental.pallas import tpu as pltpu
from jax.sharding import PartitionSpec as P

EZ = 32
JAC = 4


points_seven = (
    -1.0,
    -0.8717401485096066,
    -0.5917001814331423,
    -0.2092992179024789,
    0.2092992179024789,
    0.5917001814331423,
    0.8717401485096066,
    1.0,
)
points_three = (-1.0, -0.4472135954999579, 0.4472135954999579, 1.0)
points_one = (-1.0, 1.0)
damping = 2.0 / 3.0


def shifted(array, axis, by):
    devices = lax.axis_size(axis)
    pairs = [(i, i + by) for i in range(devices) if 0 <= i + by < devices]
    return lax.ppermute(array, axis, pairs)


def legendre_at(degree, location):
    previous, current = (1.0, location)
    for level_idx in range(1, degree):
        previous, current = (
            current,
            ((2 * level_idx + 1) * location * current - level_idx * previous) / (level_idx + 1),
        )
    return current


def quadrature_weights():
    return np.array([2.0 / (56.0 * legendre_at(7, x) * legendre_at(7, x)) for x in points_seven])


def derivative_matrix():
    points = np.array(points_seven)
    products = np.array(
        [np.prod([points[i] - points[k] for k in range(8) if k != i]) for i in range(8)]
    )
    result = np.zeros((8, 8))
    for i in range(8):
        for j in range(8):
            if i != j:
                result[i, j] = products[i] / (products[j] * (points[i] - points[j]))
        result[i, i] = np.sum([1.0 / (points[i] - points[k]) for k in range(8) if k != i])
    return result


def element_stiffness():
    derivative = derivative_matrix()
    return derivative.T @ (quadrature_weights()[:, None] * derivative)


def assemble_line(elements):
    stiffness = element_stiffness()
    weights = quadrature_weights()
    extent = 7 * elements + 1
    global_stiff = np.zeros((extent, extent))
    lumped = np.zeros(extent)
    for m in range(elements):
        global_stiff[7 * m : 7 * m + 8, 7 * m : 7 * m + 8] += stiffness
        lumped[7 * m : 7 * m + 8] += weights
    return (global_stiff, lumped)


def jacobi_eigen(matrix):
    rotated_mat = matrix.copy()
    extent = matrix.shape[0]
    vectors = np.eye(extent)
    for sweep_idx in range(12):
        for p in range(extent - 1):
            for q in range(p + 1, extent):
                angle_rot = 0.5 * math.atan2(
                    2.0 * float(rotated_mat[p, q]), float(rotated_mat[q, q] - rotated_mat[p, p])
                )
                rotation = np.eye(extent)
                rotation[p, p] = math.cos(angle_rot)
                rotation[q, q] = math.cos(angle_rot)
                rotation[p, q] = math.sin(angle_rot)
                rotation[q, p] = -math.sin(angle_rot)
                rotated_mat = rotation.T @ rotated_mat @ rotation
                vectors = vectors @ rotation
    return (np.array([rotated_mat[i, i] for i in range(extent)]), vectors)


def patch_basis():
    global_stiff, lumped = assemble_line(2)
    inv_root = 1.0 / np.sqrt(lumped[1:14])
    eigvals, vectors = jacobi_eigen(
        inv_root[:, None] * global_stiff[1:14, 1:14] * inv_root[None, :]
    )
    return (eigvals, inv_root[:, None] * vectors)


def interp_matrix(coarse_pts):
    result = np.ones((8, len(coarse_pts)))
    for a in range(8):
        for c in range(len(coarse_pts)):
            for k in range(len(coarse_pts)):
                if k != c:
                    result[a, c] *= (points_seven[a] - coarse_pts[k]) / (
                        coarse_pts[c] - coarse_pts[k]
                    )
    return result


def restriction_rows(coarse_pts):
    shared = np.ones(8)
    shared[0] = 0.5
    shared[7] = 0.5
    return (interp_matrix(coarse_pts) * shared[:, None]).T


def restriction_line(elements, coarse_pts):
    degree = len(coarse_pts) - 1
    rows_mat = restriction_rows(coarse_pts)
    result = np.zeros((degree * elements + 1, 7 * elements + 1))
    for m in range(elements):
        result[degree * m : degree * m + degree + 1, 7 * m : 7 * m + 8] += rows_mat
    return result


def patch_matrix(eigbasis, vertices, extent):
    result = np.zeros((13 * vertices, extent))
    for b in range(13):
        for v in range(vertices):
            for a in range(13):
                node_idx = 7 * v + a
                result[b * vertices + v, node_idx] = eigbasis[a, b]
    return result


high = lax.Precision.HIGH
highest = lax.Precision.HIGHEST
LANES = 128
GROUP = 13
f32 = jnp.float32


def up_to(length, multiple):
    return -(-length // multiple) * multiple


def placed(matrix, shape, row=0, col=0):
    result = np.zeros(shape, np.float32)
    result[row : row + matrix.shape[0], col : col + matrix.shape[1]] = matrix
    return result


def mm(left, right, precision=high):
    return lax.dot_general(
        left, right, (((1,), (0,)), ((), ())), precision=precision, preferred_element_type=f32
    )


class Sizes:
    def __init__(self, x_nodes, y_nodes, z_nodes):
        self.x_nodes, self.y_nodes, self.z_nodes = (x_nodes, y_nodes, z_nodes)
        self.x_elems, self.y_elems, self.z_elems = (x_nodes // 7, y_nodes // 7, z_nodes // 7)
        self.own_rows = up_to(x_nodes + 1, 8)
        self.rows = up_to(x_nodes + 8, 8)
        self.half_z = self.z_elems // 2
        self.lanes = 2 * LANES
        self.modes_x = up_to(13 * self.x_elems, 8)
        self.modes_z = up_to(13 * self.half_z, LANES)
        self.coarse_x = 3 * self.x_elems + 4
        self.coarse_y = 3 * self.y_elems + 4
        self.coarse_z = 3 * self.z_elems
        self.coarse_rows = up_to(self.coarse_x, 8)
        self.coarse_lanes = up_to(self.coarse_z, LANES)
        split = 7 * self.half_z
        self.split = split
        self.node_of_lane = np.full(self.lanes, -1)
        self.node_of_lane[6 : 6 + split] = np.arange(split)
        self.node_of_lane[LANES : LANES + split + 6] = np.arange(split - 6, 2 * split)
        self.first_copy = self.node_of_lane >= 0
        self.first_copy[LANES : LANES + 6] = False


def line_tables(elements):
    nodes = 7 * elements
    stiff, lumped = assemble_line(elements + 2)
    restrict = restriction_line(elements + 3, points_three)[3 : 3 * elements + 7, 7 : nodes + 15]
    columns = np.arange(-6, nodes)
    weight = np.where(columns % 7 == 0, 1.0, 0.5)
    mass_part = restrict[:, 1:-1] * (lumped[1 : nodes + 7] * weight)[None, :]
    stiff_part = restrict @ (stiff[: nodes + 8, 1 : nodes + 7] * weight[None, :])
    return dict(
        own_stiff=stiff[7 : nodes + 8, 7 : nodes + 7],
        mass=lumped[1 : nodes + 7],
        own=restrict[:, 7:-1],
        mass_part=mass_part,
        stiff_part=stiff_part,
    )


def rows_by_node(s, matrix, every_copy):
    used = s.node_of_lane >= 0 if every_copy else s.first_copy
    return np.where(used[:, None], matrix[np.maximum(s.node_of_lane, 0)], 0.0)


def two_parts(matrix, low_type=jnp.bfloat16):
    high_part = matrix.astype(np.float32).astype(jnp.bfloat16)
    low_part = (matrix - high_part.astype(np.float64)).astype(low_type)
    return high_part, low_part


def residual_constants(s, low):
    line_x = line_tables(s.x_elems)
    stiff_z, lumped_z = assemble_line(s.z_elems)
    stiff_z, lumped_z = (stiff_z[: s.z_nodes, : s.z_nodes], lumped_z[: s.z_nodes])
    rows = up_to(s.x_nodes + 1 - low, 8)
    mass_x = np.zeros(low + rows)
    mass_x[: s.x_nodes] = line_x["mass"][6:]
    mass_x = mass_x[low:]
    mass_z = rows_by_node(s, lumped_z[:, None], True)[:, 0]
    spread = np.ones((rows, s.lanes))
    stiff = rows_by_node(s, stiff_z, False)
    stiff = rows_by_node(s, stiff.T, True).T
    own_x = placed(line_x["own_stiff"], (low + rows, low + rows)).astype(np.float64)
    high_x, rest = two_parts(own_x[low:, low:], np.float64)
    mid_x, low_x = two_parts(rest)
    table = np.concatenate(
        [
            stiff,
            spread * mass_x[:, None],
            spread * mass_z[None, :],
            mass_x[:, None] * mass_z[None, :],
        ]
    )
    return [
        jnp.asarray(table, f32),
        jnp.asarray(
            np.concatenate([high_x, high_x, high_x, mid_x, mid_x, low_x], 1), jnp.bfloat16
        ),
    ]


def coupling_constants(s):
    stiffness = element_stiffness()
    lumped_z = assemble_line(s.z_elems)[1][: s.z_nodes]
    mass_z = rows_by_node(s, lumped_z[:, None], True)[:, 0]
    below, above = (np.zeros(s.rows), np.zeros(s.rows))
    below[2:8] = stiffness[1:7, 7]
    above[8 + s.x_nodes - 7 : 8 + s.x_nodes] = stiffness[:7, 7]
    return [below[:, None] * mass_z[None, :], above[:, None] * mass_z[None, :]]


def patch_constants(s):
    line_x = line_tables(s.x_elems)
    stiff_z, lumped_z = assemble_line(s.z_elems)
    stiff_z, lumped_z = (stiff_z[: s.z_nodes, : s.z_nodes], lumped_z[: s.z_nodes])
    weight_z = np.where(np.arange(s.z_nodes) % 7 == 0, 1.0, 0.5)
    restrict_z = restriction_line(s.z_elems, points_three)[: s.coarse_z, : s.z_nodes]
    eigvals, eigbasis = patch_basis()
    mass_z = rows_by_node(s, lumped_z[:, None], True)[:, 0]
    mass_x = np.zeros(s.rows)
    mass_x[2 : s.x_nodes + 8] = line_x["mass"]
    fwd_x = placed(
        patch_matrix(eigbasis, s.x_elems, s.x_nodes + 6), (s.modes_x, s.rows), col=2
    )
    high_x, low_x = two_parts(fwd_x.astype(np.float64))
    fwd_z = np.zeros((LANES, s.modes_z))
    fwd_z[:, : 13 * s.half_z] = patch_matrix(eigbasis, s.half_z, LANES).T
    high_z, low_z = two_parts(fwd_z)
    sums = np.ones((s.modes_x, s.modes_z))
    sums[: 13 * s.x_elems, : 13 * s.half_z] = (
        np.repeat(eigvals, s.x_elems)[:, None] + np.repeat(eigvals, s.half_z)[None, :]
    )
    coarse_of_z = np.zeros((s.z_nodes, 2 * s.coarse_lanes))
    coarse_of_z[:, : s.coarse_z] = (restrict_z * (lumped_z * weight_z)[None, :]).T
    coarse_of_z[:, s.coarse_lanes : s.coarse_lanes + s.coarse_z] = (
        restrict_z @ (stiff_z * weight_z[None, :])
    ).T
    coarse_of_x = np.zeros((2 * s.coarse_rows, s.rows))
    coarse_of_x[: s.coarse_x, 2 : s.x_nodes + 8] = line_x["mass_part"]
    coarse_of_x[s.coarse_rows : s.coarse_rows + s.coarse_x, 2 : s.x_nodes + 8] = line_x[
        "stiff_part"
    ]
    own_z = np.zeros((s.z_nodes, s.coarse_lanes))
    own_z[:, : s.coarse_z] = restrict_z.T
    one_z = placed(
        linear_from_cubic(0, s.z_elems - 1, 0, s.coarse_z - 1).T,
        (s.coarse_lanes, LANES),
        col=s.coarse_z,
    )
    one_x = placed(linear_from_cubic(-1, s.x_elems, -3, 3 * s.x_elems), (8, s.coarse_rows))
    singles = [
        mass_x[:, None] * mass_z[None, :],
        rows_by_node(s, coarse_of_z, True),
        rows_by_node(s, own_z, False),
        one_z,
        one_x,
    ]
    own_x = placed(line_x["own"], (s.coarse_rows, s.rows), col=8).astype(np.float64)
    high_q, low_q = two_parts(coarse_of_x)
    high_r, low_r = two_parts(own_x)
    solve = [
        np.concatenate([high_x, high_x, low_x], 1),
        np.concatenate([high_x.T, high_x.T, low_x.T], 1),
        np.concatenate([high_z, high_z], 0),
        low_z,
        np.concatenate([high_z.T, low_z.T], 1),
        high_z.T,
    ]
    coarse = [
        np.concatenate([high_q, high_q, low_q], 1),
        np.concatenate([high_r, high_r, low_r], 1),
    ]
    return (
        [jnp.asarray(eigvals, f32), jnp.asarray(sums, f32)]
        + [jnp.asarray(value, jnp.bfloat16) for value in solve],
        [jnp.asarray(value, f32) for value in singles]
        + [jnp.asarray(value, jnp.bfloat16) for value in coarse],
    )


def halves_of(value):
    high_part = value.astype(jnp.bfloat16)
    return high_part, (value - high_part.astype(f32)).astype(jnp.bfloat16)


def stacked_whole(value):
    high_part = value.astype(jnp.bfloat16).astype(f32)
    rest = value - high_part
    mid_part = rest.astype(jnp.bfloat16).astype(f32)
    return jnp.concatenate(
        [high_part, mid_part, rest - mid_part, high_part, mid_part, high_part], 0
    ).astype(jnp.bfloat16)


def stacked_rows(value):
    high_part = value.astype(jnp.bfloat16).astype(f32)
    return jnp.concatenate([high_part, value - high_part, high_part], 0).astype(jnp.bfloat16)


def dot(left, right):
    return lax.dot_general(left, right, (((1,), (0,)), ((), ())), preferred_element_type=f32)


def linear_from_cubic(first, last, first_three, last_three):
    result = np.zeros((last - first + 1, last_three - first_three + 1))
    for m in range(first, last + 1):
        for offset, factor in (
            (0, 1.0),
            (1, (1.0 - points_three[1]) / 2.0),
            (2, (1.0 - points_three[2]) / 2.0),
            (-2, (1.0 + points_three[1]) / 2.0),
            (-1, (1.0 + points_three[2]) / 2.0),
        ):
            node = 3 * m + offset - first_three
            if 0 <= node < result.shape[1]:
                result[m - first, node] = factor
    return result


def line_of_planes(coefficients, planes):
    total = None
    for coefficient, plane in zip(coefficients, planes):
        if coefficient != 0.0:
            part = plane() * float(coefficient)
            total = part if total is None else total + part
    return total


def symmetric(vector):
    return abs(vector[0] - vector[-1]) < abs(vector[0] + vector[-1])


def lane_window(ref, start, width):
    if start < 0:
        return pltpu.roll(ref[:, 0:LANES], -start, 1)
    if start + LANES > width:
        return pltpu.roll(ref[:, width - LANES : width], width - start, 1)
    return ref[:, start : start + LANES]


def lane_mask(s, shape, first):
    lane = lax.broadcasted_iota(jnp.int32, shape, 1)
    return ((lane >= 6 + first) & (lane < 6 + s.split)) | (
        (lane >= LANES) & (lane < LANES + s.split + 6)
    )


def put_line(s, ref, index, plane):
    at = s.z_nodes * index
    rows = plane.shape[0]
    ref[0:rows, at : at + s.split] = plane[:, 6 : 6 + s.split]
    ref[0:rows, at + s.split : at + 2 * s.split] = plane[:, LANES + 6 : LANES + 6 + s.split]


def get_line(s, ref, index, width):
    at = s.z_nodes * index
    return jnp.concatenate(
        [lane_window(ref, at - 6, width), lane_window(ref, at + s.split - 6, width)], 1
    )


def own_residual(s, low, first_copies, u, r, guess, load, table, k_x, skip=0):
    lanes = s.lanes
    rows = up_to(s.x_nodes + 1 - low, 8)
    ey, ny = (s.y_elems, s.y_nodes)
    nx = s.x_nodes - low
    width = ny * s.z_nodes
    mass_y = line_tables(ey)["mass"][6:]
    stiffness = element_stiffness()
    gx = lax.axis_index("gx")
    gy = lax.axis_index("gy")
    shape = (nx, lanes)
    row = lax.broadcasted_iota(jnp.int32, shape, 0) + low
    live = (lane_mask(s, shape, 1) & ((row != 0) | (gx > 0))).astype(f32)
    live_y = (gy > 0).astype(f32)
    inside = lane_mask(s, shape, 0).astype(f32)
    pad = jnp.zeros((rows - nx, lanes), f32)
    first_copies[0].wait()
    for y in range(ny):
        mask = live if y else live * live_y
        u[y, 0:nx] = get_line(s, guess, y, width)[skip:] * mask
        u[y, nx:] = pad
    first_copies[1].wait()
    for y in range(ny):
        r[y, 0:nx] = get_line(s, load, y, width)[skip:] * inside
        r[y, nx:] = pad
    u[ny] = jnp.zeros((rows, lanes), f32)
    r[ny] = jnp.zeros((rows, lanes), f32)
    for copy in first_copies[2:]:
        copy.wait()
    m_x, m_z, m_xz = [
        table.at[lanes + rows * i : lanes + rows * (i + 1)] for i in range(3)
    ]
    planes = u[0:ny].reshape(ny * rows, lanes)
    z_term = mm(planes, table[0:lanes], highest).reshape(ny, rows, lanes)
    for y in range(ny):
        x_term = dot(k_x[...], stacked_whole(u[y]))
        both = x_term * m_z[...] + z_term[y] * m_x[...]
        r[y] = r[y] - float(mass_y[y]) * both

    def along_y(tile, carry):
        at = pl.ds(pl.multiple_of(tile * 8, 8), 8)
        scale = m_xz[at, :]
        corner = None
        for e in range(ey):
            nodes = [u[7 * e + i, at, :] for i in range(8)]
            plus = [nodes[i] + nodes[7 - i] for i in range(4)]
            minus = [nodes[i] - nodes[7 - i] for i in range(4)]
            out = [None] * 8
            for i in range(4):
                even = sum(
                    plus[k] * float(0.5 * (stiffness[i, k] + stiffness[i, 7 - k]))
                    for k in range(4)
                )
                odd = sum(
                    minus[k] * float(0.5 * (stiffness[i, k] - stiffness[i, 7 - k]))
                    for k in range(4)
                )
                out[i], out[7 - i] = (even + odd, even - odd)
            if e:
                out[0] = out[0] + corner
            else:
                out[0] = out[0] + nodes[0] * float(stiffness[7, 7])
            corner = out[7]
            for i in range(8 if e == ey - 1 else 7):
                plane = 7 * e + i
                r[plane, at, :] = r[plane, at, :] - out[i] * scale
        return carry

    lax.fori_loop(0, rows // 8, along_y, 0)


def started(sources, targets, sems):
    copies = [
        pltpu.make_async_copy(source, target, sems.at[index])
        for index, (source, target) in enumerate(zip(sources, targets))
    ]
    for copy in copies:
        copy.start()
    return copies


def send_kernel(s):
    low = s.x_nodes - 7
    tile_low = low // 8 * 8
    lanes, nx, ny = (s.lanes, s.x_nodes, s.y_nodes)
    width = ny * s.z_nodes

    def kernel(
        guess_hbm, load_hbm, table_hbm, k_x_hbm,
        up_out, down_out,
        u, r, guess, load, table, k_x, top, sems,
    ):
        sources = [guess_hbm.at[tile_low:nx], load_hbm.at[tile_low:nx], table_hbm, k_x_hbm]
        sources += [guess_hbm.at[0:8]]
        copies = started(sources, [guess, load, table, k_x, top], sems)
        skip = low - tile_low
        own_residual(s, low, copies[:4], u, r, guess, load, table, k_x, skip)
        up_out[6:8, :] = jnp.zeros((2, up_out.shape[1]), f32)
        for y in range(ny + 1):
            put_line(s, up_out, y, r[y, nx - 6 - low : nx + 1 - low, :])
        put_line(s, up_out, ny + 1, u[0, nx - 6 - low : nx - low, :])
        copies[4].wait()
        gx = lax.axis_index("gx")
        gy = lax.axis_index("gy")
        live = lane_mask(s, (1, lanes), 1).astype(f32) * (gx > 0).astype(f32)
        live_y = (gy > 0).astype(f32)
        for y in range(ny):
            mask = live if y else live * live_y
            down_out[y : y + 1, :] = get_line(s, top, y, width)[0:1] * mask
        down_out[ny:, :] = jnp.zeros((down_out.shape[0] - ny, lanes), f32)

    return kernel


def residual_kernel(s):
    def kernel(
        guess_hbm, load_hbm, table_hbm, k_x_hbm,
        r, edge,
        u, guess, load, table, k_x, sems,
    ):
        sources = [guess_hbm, load_hbm, table_hbm, k_x_hbm]
        copies = started(sources, [guess, load, table, k_x], sems)
        own_residual(s, 0, copies, u, r, guess, load, table, k_x)
        edge[...] = u[0]

    return kernel


def joined_x_kernel(s):
    rows, lanes = (s.rows, s.lanes)
    nx, ny = (s.x_nodes, s.y_nodes)
    mass_y = line_tables(s.y_elems)["mass"][6:]

    def kernel(r_own, edge, u_first, below, above, c_below, c_above, r, line, up_out):
        width = below.shape[1]
        shape = (8, lanes)
        row = lax.broadcasted_iota(jnp.int32, shape, 0)
        inside = lane_mask(s, shape, 0)
        keep = (inside & (row < 6)).astype(f32)
        only = (inside & (row == 6)).astype(f32)
        zero = jnp.zeros((rows - 8 - nx, lanes), f32) if rows - 8 - nx else None
        for y in range(ny + 2):
            got = get_line(s, below, y, width)
            place = line if y == ny + 1 else r.at[y]
            own = edge[0:nx] if y == ny + 1 else r_own[y, 0:nx, :]
            place[0:2, :] = jnp.zeros((2, lanes), f32)
            place[2:8, :] = (got * keep)[0:6]
            place[8 : 8 + nx, :] = own
            if zero is not None:
                place[8 + nx :, :] = zero
            if y < ny:
                place[8:9, :] += (got * only)[6:7]
                both = (
                    c_below[...] * u_first[y : y + 1, :] + c_above[...] * above[y : y + 1, :]
                ) * float(mass_y[y])
                place[...] = place[...] - both
        for j in range(7):
            put_line(s, up_out, j, r[ny - 6 + j])
        up_out[:, 7 * s.z_nodes :] = jnp.zeros((rows, up_out.shape[1] - 7 * s.z_nodes), f32)

    return kernel


def patch_modes(s, vertices, plane_of, matrices, xf, xb, live):
    lam, sums, f_x, b_x, f_z, f_z_low, b_z, b_z_high = matrices
    rows = s.rows
    count = len(vertices)
    _, eigbasis = patch_basis()
    evens = [b for b in range(13) if symmetric(eigbasis[:, b])]
    gx = lax.axis_index("gx")
    gy = lax.axis_index("gy")
    shape = (s.modes_x, s.modes_z)
    mode = lax.broadcasted_iota(jnp.int32, shape, 0)
    vertex = lax.broadcasted_iota(jnp.int32, shape, 1) % s.half_z
    live_x = (mode % s.x_elems != 0) | (gx > 0)
    live[0] = (live_x & (vertex != 0)).astype(f32)
    live[1] = live_x.astype(f32)
    active = (gy > 0).astype(f32)

    def along_y(tile, carry):
        at = pl.ds(pl.multiple_of(tile * 8, 8), 8)
        for i, v in enumerate(vertices):
            first = [plane_of(7 * v + a - 6, at) for a in range(13)]
            if v == 0:
                first = [value * active for value in first]
            even = [first[6]] + [first[6 + a] + first[6 - a] for a in range(1, 7)]
            odd = [first[6 + a] - first[6 - a] for a in range(1, 7)]
            for b in range(13):
                if b in evens:
                    xf[b, i, at, :] = sum(even[a] * float(eigbasis[6 + a, b]) for a in range(7))
                else:
                    xf[b, i, at, :] = sum(odd[a] * float(eigbasis[7 + a, b]) for a in range(6))
        return carry

    lax.fori_loop(0, rows // 8, along_y, 0)

    def spectral(modes_of):
        pieces = []
        for b in modes_of:
            planes = [dot(f_x[...], stacked_rows(xf[b, v])) for v in range(count)]
            pieces += [plane[:, :LANES] for plane in planes]
            pieces += [plane[:, LANES:] for plane in planes]
        high_part, low_part = halves_of(jnp.concatenate(pieces, 0))
        modes = dot(jnp.concatenate([high_part, low_part], 1), f_z[...]) + dot(
            high_part, f_z_low[...]
        )
        modes = modes.reshape(len(modes_of), 2, count, s.modes_x, s.modes_z)
        pieces = []
        for i, b in enumerate(modes_of):
            factor = 1.0 / (sums[...] + lam[b])
            for t in range(2):
                scaled = modes[i, t] * (factor * live[t])[None]
                pieces.append(scaled.reshape(count * s.modes_x, s.modes_z))
        high_part, low_part = halves_of(jnp.concatenate(pieces, 0))
        both = dot(high_part, b_z[...])
        back = both[:, :LANES] + both[:, LANES:] + dot(low_part, b_z_high[...])
        back = back.reshape(len(modes_of), 2, count, s.modes_x, LANES)
        for i, b in enumerate(modes_of):
            for v in range(count):
                plane = jnp.concatenate([back[i, 0, v], back[i, 1, v]], 1)
                xb[b, v] = dot(b_x[...], stacked_rows(plane))

    for first in range(0, 13, GROUP):
        spectral(range(first, min(13, first + GROUP)))


def inner_kernel(s):
    def kernel(r_own, lam, sums, f_x, b_x, f_z, f_z_low, b_z, b_z_high, xb, xf, live):
        patch_modes(
            s,
            list(range(1, s.y_elems - 1)),
            lambda y, at: r_own[y, at, :],
            (lam, sums, f_x, b_x, f_z, f_z_low, b_z, b_z_high),
            xf,
            xb,
            live,
        )

    return kernel


def patch_kernel(s):
    rows, lanes = (s.rows, s.lanes)
    ey, ny = (s.y_elems, s.y_nodes)
    line_y = line_tables(ey)
    _, eigbasis = patch_basis()
    stiffness = element_stiffness()
    one_y = linear_from_cubic(-1, ey, -3, 3 * ey)
    evens = [b for b in range(13) if symmetric(eigbasis[:, b])]
    odds = [b for b in range(13) if b not in evens]

    def kernel(
        r_own, line, below, above, inner,
        lam, sums, f_x, b_x, f_z, f_z_low, b_z, b_z_high,
        m_xz, q_z, r_z, o_z, o_x, q_x, r_x,
        edge_out, own_out, three_out, one_out, down_out, up_out,
        r, xf, xb, c, cz, rz, hx, ex, rx, live,
    ):
        inside = lane_mask(s, (rows, lanes), 0).astype(f32)
        width = below.shape[1]
        lower = line[...] * m_xz[...]
        upper = above[...] * m_xz[...]
        for j in range(7):
            got = get_line(s, below, j, width) * inside
            if j < 6:
                r[j] = got - lower * float(stiffness[1 + j, 7])
            else:
                r[6] = r_own[0] + got
        for y in range(1, ny):
            plane = r_own[y]
            if y >= ny - 7:
                plane = plane - upper * float(stiffness[y - (ny - 7), 7])
            r[6 + y] = plane
        patch_modes(
            s,
            [0, ey - 1],
            lambda y, at: r[y + 6, at, :],
            (lam, sums, f_x, b_x, f_z, f_z_low, b_z, b_z_high),
            xf,
            xb,
            live,
        )

        def back_y(tile, carry):
            at = pl.ds(pl.multiple_of(tile * 8, 8), 8)
            tail = None
            for v in range(ey):
                if 0 < v < ey - 1:
                    modes = [inner[b, v - 1, at, :] for b in range(13)]
                else:
                    modes = [xb[b, min(v, 1), at, :] for b in range(13)]
                out = [None] * 13
                for a in range(7):
                    even = sum(modes[b] * float(eigbasis[6 + a, b]) for b in evens)
                    if a == 0:
                        out[6] = even
                        continue
                    odd = sum(modes[b] * float(eigbasis[6 + a, b]) for b in odds)
                    out[6 + a], out[6 - a] = (even + odd, even - odd)
                if v:
                    out[:6] = [value + other for value, other in zip(out[:6], tail)]
                tail = out[7:]
                for a in range(13 if v == ey - 1 else 7):
                    c[7 * v + a, at, :] = out[a]
            return carry

        lax.fori_loop(0, rows // 8, back_y, 0)

        for j in range(6):
            down_out[:, lanes * j : lanes * (j + 1)] = c[j]
        edge_out[...] = c[6:, 0:8, :]
        own_out[...] = c[6:, 8:, :]

        half = s.coarse_lanes
        rows_c = s.coarse_rows
        cz[...] = mm(c[...].reshape((ny + 6) * rows, lanes), q_z[...]).reshape(
            ny + 6, rows, 2 * half
        )
        rz[...] = mm(r[6 : ny + 6].reshape(ny * rows, lanes), r_z[...]).reshape(ny, rows, half)
        for y in range(ny + 6):
            plane = dot(q_x[...], stacked_rows(cz[y]))
            hx[y] = plane[:rows_c, :half]
            ex[y] = plane[rows_c:, :half] + plane[:rows_c, half:]
        for y in range(0, ny - 1, 2):
            pair = jnp.concatenate([rz[y], rz[y + 1]], 1)
            pair = dot(r_x[...], stacked_rows(pair))
            rx[y], rx[y + 1] = (pair[:, :half], pair[:, half:])
        if ny % 2:
            rx[ny - 1] = dot(r_x[...], stacked_rows(rz[ny - 1]))
        for j in range(s.coarse_y):
            three_out[j] = line_of_planes(
                np.concatenate(
                    [line_y["own"][j], -line_y["stiff_part"][j], -line_y["mass_part"][j]]
                ),
                [lambda y=y: rx[y] for y in range(ny)]
                + [lambda y=y: hx[y] for y in range(ny + 6)]
                + [lambda y=y: ex[y] for y in range(ny + 6)],
            )
        one_all = mm(
            three_out[...].reshape(s.coarse_y * rows_c, half), o_z[...]
        ).reshape(s.coarse_y, rows_c, LANES)
        for m in range(ey + 2):
            mixed = line_of_planes(
                one_y[m], [lambda j=j: one_all[j] for j in range(s.coarse_y)]
            )
            one_out[m] = mm(o_x[...], mixed)
        base = 6 * lanes
        down_out[:, base:] = jnp.zeros((rows, 2 * half), f32)
        up_out[...] = jnp.zeros(up_out.shape, f32)
        up_out[:, 0:half] = three_out[s.coarse_y - 1]
        for j in range(4):
            first, at = (rows_c * (j % 2), base + half * (j // 2))
            if j < 3:
                down_out[first : first + rows_c, at : at + half] = three_out[j]
            down_out[first : first + 8, at : at + half] += one_out[j]
            up_out[0:8, half * j : half * (j + 1)] += one_out[ey - 2 + j]

    return kernel


def coarse_place(s, index):
    high_rows = coarse_height(s)
    return index % high_rows, LANES * (index // high_rows)


def line_lanes(s):
    return up_to(-(-s.y_nodes // 4) * s.z_nodes, LANES)


def coarse_height(s):
    return up_to(-(-max(9 * s.y_elems, 4 * s.y_elems + 24) // 2), 24)


def join_kernel(s):
    lanes, half, rows_c = (s.lanes, s.coarse_lanes, s.coarse_rows)
    ey, ny = (s.y_elems, s.y_nodes)

    def kernel(edge, three, one, down, up, down_out, up_out, three_out, one_out):
        lane = lax.broadcasted_iota(jnp.int32, (rows_c, half), 1)
        is_three = (lane < s.coarse_z).astype(f32)
        is_one = (lane >= s.coarse_z).astype(f32)[0:8]
        down_out[...] = jnp.zeros(down_out.shape, f32)
        shared = shared_lanes(s, (8, lanes))
        for y in range(ny):
            plane = edge[y]
            if y >= ny - 6:
                j = y - (ny - 6)
                plane = plane + down[0:8, lanes * j : lanes * (j + 1)]
            plane = plane + pltpu.roll(plane, lanes - (LANES - s.split), 1) * shared
            here = pl.ds(6 * (y % 4), 6)
            at = s.z_nodes * (y // 4)
            for t in range(2):
                first = LANES * t + 6
                down_out[here, at + s.split * t : at + s.split * (t + 1)] = plane[
                    2:8, first : first + s.split
                ]
        base = 6 * lanes
        tiles = line_lanes(s)
        up_out[...] = jnp.zeros(up_out.shape, f32)

        def from_above(k, count):
            row, at = (rows_c * (k % 2), base + half * (k // 2))
            return down[row : row + count, at : at + half]

        for j in range(3 * ey):
            plane = three[3 + j]
            if j >= 3 * ey - 3:
                plane = plane + from_above(j - (3 * ey - 3), rows_c)
            if j == 0:
                plane = plane + up[0:rows_c, 0:half]
            plane = plane * is_three
            three_out[j] = plane
            row, at = coarse_place(s, 3 * j)
            down_out[row : row + 3, tiles + at : tiles + at + half] = plane[0:3]
            row, at = coarse_place(s, j)
            up_out[row : row + 1, at : at + half] = plane[s.coarse_x - 1 : s.coarse_x]
        for j in range(ey + 6):
            y = j - 3
            plane = None
            if -1 <= y <= ey:
                plane = one[y + 1]
            if y <= 0:
                k = y + 3
                part = up[0:8, half * k : half * (k + 1)]
                plane = part if plane is None else plane + part
            if y >= ey - 1:
                part = from_above(y - (ey - 1), 8)
                plane = part if plane is None else plane + part
            plane = plane * is_one
            one_out[j] = plane
            row, at = coarse_place(s, 4 * j)
            down_out[row : row + 4, tiles + at : tiles + at + half] += plane[0:4]
            up_out[row : row + 4, at : at + half] += plane[s.x_elems - 2 : s.x_elems + 2]

    return kernel


def shared_lanes(s, shape):
    lane = lax.broadcasted_iota(jnp.int32, shape, 1)
    return ((lane >= s.split) & (lane < s.split + 6)).astype(f32)


def base_kernel(s):
    lanes, nx, ny = (s.lanes, s.x_nodes, s.y_nodes)
    width = ny * s.z_nodes

    def kernel(guess, weight, own, down, out):
        gx = lax.axis_index("gx")
        gy = lax.axis_index("gy")
        shape = (nx, lanes)
        row = lax.broadcasted_iota(jnp.int32, shape, 0)
        live = (lane_mask(s, shape, 1) & ((row != 0) | (gx > 0))).astype(f32)
        live_y = (gy > 0).astype(f32)
        shared = shared_lanes(s, shape)
        for y in range(ny):
            plane = own[y, 0:nx, :]
            if y >= ny - 6:
                j = y - (ny - 6)
                plane = plane + down[8 : 8 + nx, lanes * j : lanes * (j + 1)]
            plane = plane + pltpu.roll(plane, lanes - (LANES - s.split), 1) * shared
            mask = live if y else live * live_y
            factor = weight[...] * (1.0 if y % 7 == 0 else 0.5)
            put_line(s, out, y, (get_line(s, guess, y, width) + factor * plane) * mask)

    return kernel


def finish_kernel(s, x_total, y_total):
    lanes, half, rows_c, nz = (s.lanes, s.coarse_lanes, s.coarse_rows, s.z_nodes)
    ex, ey, nx, ny = (s.x_elems, s.y_elems, s.x_nodes, s.y_nodes)
    one_rows = up_to(ex + 6, 8)
    split = s.split

    def kernel(
        base, weight, right, left, three, one,
        smooth_out, three_out, coarse_out, fine, level,
    ):
        gx = lax.axis_index("gx")
        gy = lax.axis_index("gy")
        live_y = (gy > 0).astype(f32)
        smooth_out[...] = base[...]
        for y in range(ny):
            at = nz * (y // 4)
            piece = right[6 * (y % 4) : 6 * (y % 4) + 6, at : at + nz] * weight[...]
            smooth_out[nx - 6 : nx, nz * y : nz * (y + 1)] += piece * (1.0 if y % 7 == 0 else 0.5)
        tiles = line_lanes(s)
        nzc = s.coarse_z
        lane = lax.broadcasted_iota(jnp.int32, (3 * ex, nzc), 1)
        row = lax.broadcasted_iota(jnp.int32, (3 * ex, nzc), 0)
        live = ((lane >= 1) & ((row >= 1) | (gx > 0))).astype(f32)
        for j in range(3 * ey):
            fine[j] = three[j]
            at_row, at = coarse_place(s, 3 * j)
            at += tiles
            fine[j, 3 * ex : 3 * ex + 3, :] += right[at_row : at_row + 3, at : at + half]
            at_row, at = coarse_place(s, j)
            fine[j, 3:4, :] += left[at_row : at_row + 1, at : at + half]
            mask = live if j else live * live_y
            three_out[:, nzc * j : nzc * (j + 1)] = fine[j, 3 : 3 * ex + 3, 0:nzc] * mask
        level[...] = jnp.zeros((ey + 6, one_rows, LANES), f32)
        for j in range(ey + 6):
            level[j, 2 : ex + 4, :] = one[j, 0 : ex + 2, :]
            at_row, at = coarse_place(s, 4 * j)
            level[j, 0:4, :] += left[at_row : at_row + 4, at : at + half]
            at += tiles
            level[j, ex + 2 : ex + 6, :] += right[at_row : at_row + 4, at : at + half]
        shape = (one_rows, LANES)
        lane = lax.broadcasted_iota(jnp.int32, shape, 1)
        row = lax.broadcasted_iota(jnp.int32, shape, 0)
        global_x = gx * ex + row - 3
        plane_mask = (
            (lane > s.coarse_z) & (lane < s.coarse_z + s.z_elems) & (row < ex + 6)
            & (global_x >= 1) & (global_x < x_total)
        )
        masks = []
        for j in range(ey + 6):
            global_y = gy * ey + (j - 3)
            inside = (global_y >= 1) & (global_y < y_total)
            masks.append((plane_mask & inside).astype(f32))
        levels = [level[j] for j in range(ey + 6)]
        error = [damping / 12.0 * a * m for a, m in zip(levels, masks)]
        zero = jnp.zeros(shape, f32)
        for sweep in range(1, JAC):
            lower = [zero] + error[:-1]
            upper = error[1:] + [zero]
            fresh = []
            for j in range(ey + 6):
                here = error[j]
                neighbours = (
                    lower[j]
                    + upper[j]
                    + pltpu.roll(here, 1, 0)
                    + pltpu.roll(here, one_rows - 1, 0)
                    + pltpu.roll(here, 1, 1)
                    + pltpu.roll(here, LANES - 1, 1)
                )
                applied = 12.0 * here - 2.0 * neighbours
                fresh.append((here + damping / 12.0 * (levels[j] - applied)) * masks[j])
            error = fresh
        nze = s.z_elems
        for j in range(ey):
            coarse_out[:, nze * j : nze * (j + 1)] = error[3 + j][
                3 : 3 + ex, s.coarse_z : s.coarse_z + nze
            ]

    return kernel


def local(load_vector, initial_guess):
    z_nodes = 7 * EZ
    x_nodes = load_vector.shape[0]
    y_nodes = load_vector.shape[1] // z_nodes
    s = Sizes(x_nodes, y_nodes, z_nodes)
    rows, lanes, half = (s.rows, s.lanes, s.coarse_lanes)
    ny, ey = (s.y_nodes, s.y_elems)
    width = y_nodes * z_nodes
    shape = lambda *dims: jax.ShapeDtypeStruct(dims, f32)
    params = pltpu.CompilerParams(vmem_limit_bytes=36 * 2**20)
    vmem = lambda count: [pl.BlockSpec(memory_space=pltpu.VMEM)] * count

    def call(kernel, name, outputs, operands, scratch=(), spaces=None, semaphores=0):
        specs = vmem(len(operands))
        for index, space in (spaces or {}).items():
            specs[index] = pl.BlockSpec(memory_space=space)
        return pl.pallas_call(
            kernel,
            out_shape=tuple(shape(*dims) for dims in outputs),
            in_specs=specs,
            out_specs=tuple(vmem(len(outputs))),
            scratch_shapes=[pltpu.VMEM(d, f32) if isinstance(d, tuple) else d for d in scratch]
            + ([pltpu.SemaphoreType.DMA((semaphores,))] if semaphores else []),
            compiler_params=params,
            name=name,
        )(*operands)

    in_hbm = lambda values: [pltpu.with_memory_space_constraint(v, pltpu.HBM) for v in values]
    hbm = {index: pltpu.HBM for index in range(4)}
    low = x_nodes - 7
    taken = x_nodes - low // 8 * 8
    constants = residual_constants(s, low)
    up, u_first = call(
        send_kernel(s),
        "send",
        ((8, up_to((ny + 2) * z_nodes, LANES)), (up_to(ny, 8), lanes)),
        in_hbm([initial_guess, load_vector] + constants),
        [
            (ny + 1, 8, lanes),
            (ny + 1, 8, lanes),
            (taken, width),
            (taken, width),
            constants[0].shape,
            pltpu.VMEM(constants[1].shape, jnp.bfloat16),
            (8, width),
        ],
        spaces=hbm,
        semaphores=5,
    )
    below = shifted(up, "gx", 1)
    above = shifted(u_first, "gx", -1)
    constants = residual_constants(s, 0)
    r_own, edge = call(
        residual_kernel(s),
        "residual",
        ((ny + 1, s.own_rows, lanes), (s.own_rows, lanes)),
        in_hbm([initial_guess, load_vector] + constants),
        [
            (ny + 1, s.own_rows, lanes),
            initial_guess.shape,
            load_vector.shape,
            constants[0].shape,
            pltpu.VMEM(constants[1].shape, jnp.bfloat16),
        ],
        spaces=hbm,
        semaphores=4,
    )
    r_x, line, up = call(
        joined_x_kernel(s),
        "joined_x",
        (
            (ny + 1, rows, lanes),
            (rows, lanes),
            (rows, up_to(7 * z_nodes, LANES)),
        ),
        [r_own, edge, u_first, below, above]
        + [jnp.asarray(v, f32) for v in coupling_constants(s)],
    )
    below = shifted(up, "gy", 1)
    above = shifted(line, "gy", -1)
    solve, coarse = patch_constants(s)
    (inner,) = call(
        inner_kernel(s),
        "inner",
        ((13, ey - 2, rows, lanes),),
        [r_x] + solve,
        [(13, ey - 2, rows, lanes), (2, s.modes_x, s.modes_z)],
        spaces={1: pltpu.SMEM},
    )
    edge, own, three, one, down, up = call(
        patch_kernel(s),
        "patches",
        (
            (ny, 8, lanes),
            (ny, rows - 8, lanes),
            (s.coarse_y, s.coarse_rows, half),
            (ey + 2, 8, LANES),
            (rows, 6 * lanes + 2 * half),
            (s.coarse_rows, 4 * half),
        ),
        [r_x, line, below, above, inner] + solve + coarse,
        [
            (ny + 6, rows, lanes),
            (13, 2, rows, lanes),
            (13, 2, rows, lanes),
            (ny + 6, rows, lanes),
            (ny + 6, rows, 2 * half),
            (ny, rows, half),
            (ny + 6, s.coarse_rows, half),
            (ny + 6, s.coarse_rows, half),
            (ny, s.coarse_rows, half),
            (2, s.modes_x, s.modes_z),
        ],
        spaces={5: pltpu.SMEM},
    )
    down = shifted(down, "gy", -1)
    up = shifted(up, "gy", 1)
    right, left, three, one = call(
        join_kernel(s),
        "join",
        (
            (coarse_height(s), line_lanes(s) + 2 * half),
            (coarse_height(s), lanes),
            (3 * ey, s.coarse_rows, half),
            (ey + 6, 8, LANES),
        ),
        [edge, three, one, down, up],
    )
    right = shifted(right, "gx", -1)
    left = shifted(left, "gx", 1)
    weight_z = np.where(np.arange(z_nodes) % 7 == 0, 1.0, 0.5)
    weight = jnp.asarray(
        np.where(np.arange(x_nodes) % 7 == 0, 1.0, 0.5)[:, None]
        * rows_by_node(s, weight_z[:, None], True)[:, 0],
        f32,
    )
    weight_x = np.where(np.arange(x_nodes) % 7 == 0, 1.0, 0.5)[-6:]
    edge_weight = jnp.asarray(weight_x[:, None] * weight_z[None, :], f32)
    (base,) = call(
        base_kernel(s), "base", ((x_nodes, width),), [initial_guess, weight, own, down]
    )
    return call(
        finish_kernel(s, s.x_elems * lax.axis_size("gx"), ey * lax.axis_size("gy")),
        "finish",
        (
            (x_nodes, width),
            (3 * s.x_elems, 3 * ey * s.coarse_z),
            (s.x_elems, ey * s.z_elems),
        ),
        [base, edge_weight, right, left, three, one],
        [
            (3 * ey, s.coarse_rows, half),
            (ey + 6, up_to(s.x_elems + 6, 8), LANES),
        ],
    )


def solution(mesh):
    in_specs = (P("gx", "gy"), P("gx", "gy"))
    out_specs = (P("gx", "gy"), P("gx", "gy"), P("gx", "gy"))
    return jax.shard_map(local, mesh=mesh, in_specs=in_specs, out_specs=out_specs, check_vma=False)
```

```python
import math

import jax
import jax.numpy as jnp
import numpy as np
from jax import lax
from jax.experimental import pallas as pl
from jax.experimental.pallas import tpu as pltpu
from jax.sharding import PartitionSpec as P

EZ = 32
JAC = 4


points_seven = (
    -1.0,
    -0.8717401485096066,
    -0.5917001814331423,
    -0.2092992179024789,
    0.2092992179024789,
    0.5917001814331423,
    0.8717401485096066,
    1.0,
)
points_three = (-1.0, -0.4472135954999579, 0.4472135954999579, 1.0)
points_one = (-1.0, 1.0)
damping = 2.0 / 3.0


def shifted(array, axis, by):
    devices = lax.axis_size(axis)
    pairs = [(i, i + by) for i in range(devices) if 0 <= i + by < devices]
    return lax.ppermute(array, axis, pairs)


def legendre_at(degree, location):
    previous, current = (1.0, location)
    for level_idx in range(1, degree):
        previous, current = (
            current,
            ((2 * level_idx + 1) * location * current - level_idx * previous) / (level_idx + 1),
        )
    return current


def quadrature_weights():
    return np.array([2.0 / (56.0 * legendre_at(7, x) * legendre_at(7, x)) for x in points_seven])


def derivative_matrix():
    points = np.array(points_seven)
    products = np.array(
        [np.prod([points[i] - points[k] for k in range(8) if k != i]) for i in range(8)]
    )
    result = np.zeros((8, 8))
    for i in range(8):
        for j in range(8):
            if i != j:
                result[i, j] = products[i] / (products[j] * (points[i] - points[j]))
        result[i, i] = np.sum([1.0 / (points[i] - points[k]) for k in range(8) if k != i])
    return result


def element_stiffness():
    derivative = derivative_matrix()
    return derivative.T @ (quadrature_weights()[:, None] * derivative)


def assemble_line(elements):
    stiffness = element_stiffness()
    weights = quadrature_weights()
    extent = 7 * elements + 1
    global_stiff = np.zeros((extent, extent))
    lumped = np.zeros(extent)
    for m in range(elements):
        global_stiff[7 * m : 7 * m + 8, 7 * m : 7 * m + 8] += stiffness
        lumped[7 * m : 7 * m + 8] += weights
    return (global_stiff, lumped)


def jacobi_eigen(matrix):
    rotated_mat = matrix.copy()
    extent = matrix.shape[0]
    vectors = np.eye(extent)
    for sweep_idx in range(12):
        for p in range(extent - 1):
            for q in range(p + 1, extent):
                angle_rot = 0.5 * math.atan2(
                    2.0 * float(rotated_mat[p, q]), float(rotated_mat[q, q] - rotated_mat[p, p])
                )
                rotation = np.eye(extent)
                rotation[p, p] = math.cos(angle_rot)
                rotation[q, q] = math.cos(angle_rot)
                rotation[p, q] = math.sin(angle_rot)
                rotation[q, p] = -math.sin(angle_rot)
                rotated_mat = rotation.T @ rotated_mat @ rotation
                vectors = vectors @ rotation
    return (np.array([rotated_mat[i, i] for i in range(extent)]), vectors)


def patch_basis():
    global_stiff, lumped = assemble_line(2)
    inv_root = 1.0 / np.sqrt(lumped[1:14])
    eigvals, vectors = jacobi_eigen(
        inv_root[:, None] * global_stiff[1:14, 1:14] * inv_root[None, :]
    )
    return (eigvals, inv_root[:, None] * vectors)


def interp_matrix(coarse_pts):
    result = np.ones((8, len(coarse_pts)))
    for a in range(8):
        for c in range(len(coarse_pts)):
            for k in range(len(coarse_pts)):
                if k != c:
                    result[a, c] *= (points_seven[a] - coarse_pts[k]) / (
                        coarse_pts[c] - coarse_pts[k]
                    )
    return result


def restriction_rows(coarse_pts):
    shared = np.ones(8)
    shared[0] = 0.5
    shared[7] = 0.5
    return (interp_matrix(coarse_pts) * shared[:, None]).T


def restriction_line(elements, coarse_pts):
    degree = len(coarse_pts) - 1
    rows_mat = restriction_rows(coarse_pts)
    result = np.zeros((degree * elements + 1, 7 * elements + 1))
    for m in range(elements):
        result[degree * m : degree * m + degree + 1, 7 * m : 7 * m + 8] += rows_mat
    return result


def patch_matrix(eigbasis, vertices, extent):
    result = np.zeros((13 * vertices, extent))
    for b in range(13):
        for v in range(vertices):
            for a in range(13):
                node_idx = 7 * v + a
                result[b * vertices + v, node_idx] = eigbasis[a, b]
    return result


high = lax.Precision.HIGH
highest = lax.Precision.HIGHEST
LANES = 128
GROUP = 13
f32 = jnp.float32


def up_to(length, multiple):
    return -(-length // multiple) * multiple


def placed(matrix, shape, row=0, col=0):
    result = np.zeros(shape, np.float32)
    result[row : row + matrix.shape[0], col : col + matrix.shape[1]] = matrix
    return result


def mm(left, right, precision=high):
    return lax.dot_general(
        left, right, (((1,), (0,)), ((), ())), precision=precision, preferred_element_type=f32
    )


class Sizes:
    def __init__(self, x_nodes, y_nodes, z_nodes):
        self.x_nodes, self.y_nodes, self.z_nodes = (x_nodes, y_nodes, z_nodes)
        self.x_elems, self.y_elems, self.z_elems = (x_nodes // 7, y_nodes // 7, z_nodes // 7)
        self.own_rows = up_to(x_nodes + 1, 8)
        self.rows = up_to(x_nodes + 8, 8)
        self.half_z = self.z_elems // 2
        self.lanes = 2 * LANES
        self.modes_x = up_to(13 * self.x_elems, 8)
        self.modes_z = up_to(13 * self.half_z, LANES)
        self.coarse_x = 3 * self.x_elems + 4
        self.coarse_y = 3 * self.y_elems + 4
        self.coarse_z = 3 * self.z_elems
        self.coarse_rows = up_to(self.coarse_x, 8)
        self.coarse_lanes = up_to(self.coarse_z, LANES)
        split = 7 * self.half_z
        self.split = split
        self.node_of_lane = np.full(self.lanes, -1)
        self.node_of_lane[6 : 6 + split] = np.arange(split)
        self.node_of_lane[LANES : LANES + split + 6] = np.arange(split - 6, 2 * split)
        self.first_copy = self.node_of_lane >= 0
        self.first_copy[LANES : LANES + 6] = False


def line_tables(elements):
    nodes = 7 * elements
    stiff, lumped = assemble_line(elements + 2)
    restrict = restriction_line(elements + 3, points_three)[3 : 3 * elements + 7, 7 : nodes + 15]
    columns = np.arange(-6, nodes)
    weight = np.where(columns % 7 == 0, 1.0, 0.5)
    mass_part = restrict[:, 1:-1] * (lumped[1 : nodes + 7] * weight)[None, :]
    stiff_part = restrict @ (stiff[: nodes + 8, 1 : nodes + 7] * weight[None, :])
    return dict(
        own_stiff=stiff[7 : nodes + 8, 7 : nodes + 7],
        mass=lumped[1 : nodes + 7],
        own=restrict[:, 7:-1],
        mass_part=mass_part,
        stiff_part=stiff_part,
    )


def rows_by_node(s, matrix, every_copy):
    used = s.node_of_lane >= 0 if every_copy else s.first_copy
    return np.where(used[:, None], matrix[np.maximum(s.node_of_lane, 0)], 0.0)


def two_parts(matrix, low_type=jnp.bfloat16):
    high_part = matrix.astype(np.float32).astype(jnp.bfloat16)
    low_part = (matrix - high_part.astype(np.float64)).astype(low_type)
    return high_part, low_part


def residual_constants(s, low):
    line_x = line_tables(s.x_elems)
    stiff_z, lumped_z = assemble_line(s.z_elems)
    stiff_z, lumped_z = (stiff_z[: s.z_nodes, : s.z_nodes], lumped_z[: s.z_nodes])
    rows = up_to(s.x_nodes + 1 - low, 8)
    mass_x = np.zeros(low + rows)
    mass_x[: s.x_nodes] = line_x["mass"][6:]
    mass_x = mass_x[low:]
    mass_z = rows_by_node(s, lumped_z[:, None], True)[:, 0]
    spread = np.ones((rows, s.lanes))
    stiff = rows_by_node(s, stiff_z, False)
    stiff = rows_by_node(s, stiff.T, True).T
    own_x = placed(line_x["own_stiff"], (low + rows, low + rows)).astype(np.float64)
    high_x, rest = two_parts(own_x[low:, low:], np.float64)
    mid_x, low_x = two_parts(rest)
    table = np.concatenate(
        [
            stiff,
            spread * mass_x[:, None],
            spread * mass_z[None, :],
            mass_x[:, None] * mass_z[None, :],
        ]
    )
    return [
        jnp.asarray(table, f32),
        jnp.asarray(
            np.concatenate([high_x, high_x, high_x, mid_x, mid_x, low_x], 1), jnp.bfloat16
        ),
    ]


def coupling_constants(s):
    stiffness = element_stiffness()
    lumped_z = assemble_line(s.z_elems)[1][: s.z_nodes]
    mass_z = rows_by_node(s, lumped_z[:, None], True)[:, 0]
    below, above = (np.zeros(s.rows), np.zeros(s.rows))
    below[2:8] = stiffness[1:7, 7]
    above[8 + s.x_nodes - 7 : 8 + s.x_nodes] = stiffness[:7, 7]
    return [below[:, None] * mass_z[None, :], above[:, None] * mass_z[None, :]]


def patch_constants(s):
    line_x = line_tables(s.x_elems)
    stiff_z, lumped_z = assemble_line(s.z_elems)
    stiff_z, lumped_z = (stiff_z[: s.z_nodes, : s.z_nodes], lumped_z[: s.z_nodes])
    weight_z = np.where(np.arange(s.z_nodes) % 7 == 0, 1.0, 0.5)
    restrict_z = restriction_line(s.z_elems, points_three)[: s.coarse_z, : s.z_nodes]
    eigvals, eigbasis = patch_basis()
    mass_z = rows_by_node(s, lumped_z[:, None], True)[:, 0]
    mass_x = np.zeros(s.rows)
    mass_x[2 : s.x_nodes + 8] = line_x["mass"]
    fwd_x = placed(
        patch_matrix(eigbasis, s.x_elems, s.x_nodes + 6), (s.modes_x, s.rows), col=2
    )
    high_x, low_x = two_parts(fwd_x.astype(np.float64))
    fwd_z = np.zeros((LANES, s.modes_z))
    fwd_z[:, : 13 * s.half_z] = patch_matrix(eigbasis, s.half_z, LANES).T
    high_z, low_z = two_parts(fwd_z)
    sums = np.ones((s.modes_x, s.modes_z))
    sums[: 13 * s.x_elems, : 13 * s.half_z] = (
        np.repeat(eigvals, s.x_elems)[:, None] + np.repeat(eigvals, s.half_z)[None, :]
    )
    coarse_of_z = np.zeros((s.z_nodes, 2 * s.coarse_lanes))
    coarse_of_z[:, : s.coarse_z] = (restrict_z * (lumped_z * weight_z)[None, :]).T
    coarse_of_z[:, s.coarse_lanes : s.coarse_lanes + s.coarse_z] = (
        restrict_z @ (stiff_z * weight_z[None, :])
    ).T
    coarse_of_x = np.zeros((2 * s.coarse_rows, s.rows))
    coarse_of_x[: s.coarse_x, 2 : s.x_nodes + 8] = line_x["mass_part"]
    coarse_of_x[s.coarse_rows : s.coarse_rows + s.coarse_x, 2 : s.x_nodes + 8] = line_x[
        "stiff_part"
    ]
    own_z = np.zeros((s.z_nodes, s.coarse_lanes))
    own_z[:, : s.coarse_z] = restrict_z.T
    one_z = placed(
        linear_from_cubic(0, s.z_elems - 1, 0, s.coarse_z - 1).T,
        (s.coarse_lanes, LANES),
        col=s.coarse_z,
    )
    one_x = placed(linear_from_cubic(-1, s.x_elems, -3, 3 * s.x_elems), (8, s.coarse_rows))
    singles = [
        mass_x[:, None] * mass_z[None, :],
        rows_by_node(s, coarse_of_z, True),
        rows_by_node(s, own_z, False),
        one_z,
        one_x,
    ]
    own_x = placed(line_x["own"], (s.coarse_rows, s.rows - 8)).astype(np.float64)
    high_q, low_q = two_parts(coarse_of_x)
    high_r, low_r = two_parts(own_x)
    solve = [
        np.concatenate([high_x, high_x, low_x], 1),
        np.concatenate([high_x.T, high_x.T, low_x.T], 1),
        np.concatenate([high_z, high_z], 0),
        low_z,
        np.concatenate([high_z.T, low_z.T], 1),
        high_z.T,
    ]
    coarse = [
        np.concatenate([high_q, high_q, low_q], 1),
        np.concatenate([high_r, high_r, low_r], 1),
    ]
    return (
        [jnp.asarray(eigvals, f32), jnp.asarray(sums, f32)]
        + [jnp.asarray(value, jnp.bfloat16) for value in solve],
        [jnp.asarray(value, f32) for value in singles]
        + [jnp.asarray(value, jnp.bfloat16) for value in coarse],
    )


def halves_of(value):
    high_part = value.astype(jnp.bfloat16)
    return high_part, (value - high_part.astype(f32)).astype(jnp.bfloat16)


def stacked_whole(value):
    high_part = value.astype(jnp.bfloat16).astype(f32)
    rest = value - high_part
    mid_part = rest.astype(jnp.bfloat16).astype(f32)
    return jnp.concatenate(
        [high_part, mid_part, rest - mid_part, high_part, mid_part, high_part], 0
    ).astype(jnp.bfloat16)


def stacked_rows(value):
    high_part = value.astype(jnp.bfloat16).astype(f32)
    return jnp.concatenate([high_part, value - high_part, high_part], 0).astype(jnp.bfloat16)


def dot(left, right):
    return lax.dot_general(left, right, (((1,), (0,)), ((), ())), preferred_element_type=f32)


def linear_from_cubic(first, last, first_three, last_three):
    result = np.zeros((last - first + 1, last_three - first_three + 1))
    for m in range(first, last + 1):
        for offset, factor in (
            (0, 1.0),
            (1, (1.0 - points_three[1]) / 2.0),
            (2, (1.0 - points_three[2]) / 2.0),
            (-2, (1.0 + points_three[1]) / 2.0),
            (-1, (1.0 + points_three[2]) / 2.0),
        ):
            node = 3 * m + offset - first_three
            if 0 <= node < result.shape[1]:
                result[m - first, node] = factor
    return result


def line_of_planes(coefficients, planes):
    total = None
    for coefficient, plane in zip(coefficients, planes):
        if coefficient != 0.0:
            part = plane() * float(coefficient)
            total = part if total is None else total + part
    return total


def symmetric(vector):
    return abs(vector[0] - vector[-1]) < abs(vector[0] + vector[-1])


def lane_window(ref, start, width):
    if start < 0:
        return pltpu.roll(ref[:, 0:LANES], -start, 1)
    if start + LANES > width:
        return pltpu.roll(ref[:, width - LANES : width], width - start, 1)
    return ref[:, start : start + LANES]


def lane_mask(s, shape, first):
    lane = lax.broadcasted_iota(jnp.int32, shape, 1)
    return ((lane >= 6 + first) & (lane < 6 + s.split)) | (
        (lane >= LANES) & (lane < LANES + s.split + 6)
    )


def put_line(s, ref, index, plane):
    at = s.z_nodes * index
    rows = plane.shape[0]
    ref[0:rows, at : at + s.split] = plane[:, 6 : 6 + s.split]
    ref[0:rows, at + s.split : at + 2 * s.split] = plane[:, LANES + 6 : LANES + 6 + s.split]


def get_line(s, ref, index, width):
    at = s.z_nodes * index
    return jnp.concatenate(
        [lane_window(ref, at - 6, width), lane_window(ref, at + s.split - 6, width)], 1
    )


def own_residual(s, low, first_copies, u, r, guess, load, table, k_x, skip=0):
    lanes = s.lanes
    rows = up_to(s.x_nodes + 1 - low, 8)
    ey, ny = (s.y_elems, s.y_nodes)
    nx = s.x_nodes - low
    width = ny * s.z_nodes
    mass_y = line_tables(ey)["mass"][6:]
    stiffness = element_stiffness()
    gx = lax.axis_index("gx")
    gy = lax.axis_index("gy")
    shape = (nx, lanes)
    row = lax.broadcasted_iota(jnp.int32, shape, 0) + low
    live = (lane_mask(s, shape, 1) & ((row != 0) | (gx > 0))).astype(f32)
    live_y = (gy > 0).astype(f32)
    inside = lane_mask(s, shape, 0).astype(f32)
    pad = jnp.zeros((rows - nx, lanes), f32)
    first_copies[0].wait()
    for y in range(ny):
        mask = live if y else live * live_y
        u[y, 0:nx] = get_line(s, guess, y, width)[skip:] * mask
        u[y, nx:] = pad
    first_copies[1].wait()
    for y in range(ny):
        r[y, 0:nx] = get_line(s, load, y, width)[skip:] * inside
        r[y, nx:] = pad
    u[ny] = jnp.zeros((rows, lanes), f32)
    r[ny] = jnp.zeros((rows, lanes), f32)
    for copy in first_copies[2:]:
        copy.wait()
    m_x, m_z, m_xz = [
        table.at[lanes + rows * i : lanes + rows * (i + 1)] for i in range(3)
    ]
    planes = u[0:ny].reshape(ny * rows, lanes)
    z_term = mm(planes, table[0:lanes], highest).reshape(ny, rows, lanes)
    for y in range(ny):
        x_term = dot(k_x[...], stacked_whole(u[y]))
        both = x_term * m_z[...] + z_term[y] * m_x[...]
        r[y] = r[y] - float(mass_y[y]) * both

    def along_y(tile, carry):
        at = pl.ds(pl.multiple_of(tile * 8, 8), 8)
        scale = m_xz[at, :]
        corner = None
        for e in range(ey):
            nodes = [u[7 * e + i, at, :] for i in range(8)]
            plus = [nodes[i] + nodes[7 - i] for i in range(4)]
            minus = [nodes[i] - nodes[7 - i] for i in range(4)]
            out = [None] * 8
            for i in range(4):
                even = sum(
                    plus[k] * float(0.5 * (stiffness[i, k] + stiffness[i, 7 - k]))
                    for k in range(4)
                )
                odd = sum(
                    minus[k] * float(0.5 * (stiffness[i, k] - stiffness[i, 7 - k]))
                    for k in range(4)
                )
                out[i], out[7 - i] = (even + odd, even - odd)
            if e:
                out[0] = out[0] + corner
            else:
                out[0] = out[0] + nodes[0] * float(stiffness[7, 7])
            corner = out[7]
            for i in range(8 if e == ey - 1 else 7):
                plane = 7 * e + i
                r[plane, at, :] = r[plane, at, :] - out[i] * scale
        return carry

    lax.fori_loop(0, rows // 8, along_y, 0, unroll=True)


def started(sources, targets, sems):
    copies = [
        pltpu.make_async_copy(source, target, sems.at[index])
        for index, (source, target) in enumerate(zip(sources, targets))
    ]
    for copy in copies:
        copy.start()
    return copies


def send_kernel(s):
    low = s.x_nodes - 7
    tile_low = low // 8 * 8
    lanes, nx, ny = (s.lanes, s.x_nodes, s.y_nodes)
    width = ny * s.z_nodes

    def kernel(
        guess_hbm, load_hbm, table_hbm, k_x_hbm,
        up_out, down_out,
        u, r, guess, load, table, k_x, top, sems,
    ):
        sources = [guess_hbm.at[tile_low:nx], load_hbm.at[tile_low:nx], table_hbm, k_x_hbm]
        sources += [guess_hbm.at[0:8]]
        copies = started(sources, [guess, load, table, k_x, top], sems)
        skip = low - tile_low
        own_residual(s, low, copies[:4], u, r, guess, load, table, k_x, skip)
        up_out[6:8, :] = jnp.zeros((2, up_out.shape[1]), f32)
        for y in range(ny + 1):
            put_line(s, up_out, y, r[y, nx - 6 - low : nx + 1 - low, :])
        put_line(s, up_out, ny + 1, u[0, nx - 6 - low : nx - low, :])
        copies[4].wait()
        gx = lax.axis_index("gx")
        gy = lax.axis_index("gy")
        live = lane_mask(s, (1, lanes), 1).astype(f32) * (gx > 0).astype(f32)
        live_y = (gy > 0).astype(f32)
        for y in range(ny):
            mask = live if y else live * live_y
            down_out[y : y + 1, :] = get_line(s, top, y, width)[0:1] * mask
        down_out[ny:, :] = jnp.zeros((down_out.shape[0] - ny, lanes), f32)

    return kernel


def residual_kernel(s):
    def kernel(
        guess_hbm, load_hbm, table_hbm, k_x_hbm,
        r, edge,
        u, guess, load, table, k_x, sems,
    ):
        sources = [guess_hbm, load_hbm, table_hbm, k_x_hbm]
        copies = started(sources, [guess, load, table, k_x], sems)
        own_residual(s, 0, copies, u, r, guess, load, table, k_x)
        edge[...] = u[0]

    return kernel


def joined_x_kernel(s):
    rows, lanes = (s.rows, s.lanes)
    nx, ny = (s.x_nodes, s.y_nodes)
    mass_y = line_tables(s.y_elems)["mass"][6:]

    def kernel(r_own, edge, u_first, below, above, c_below, c_above, r, line, up_out):
        width = below.shape[1]
        shape = (8, lanes)
        row = lax.broadcasted_iota(jnp.int32, shape, 0)
        inside = lane_mask(s, shape, 0)
        keep = (inside & (row < 6)).astype(f32)
        only = (inside & (row == 6)).astype(f32)
        zero = jnp.zeros((rows - 8 - nx, lanes), f32) if rows - 8 - nx else None
        for y in range(ny + 2):
            got = get_line(s, below, y, width)
            place = line if y == ny + 1 else r.at[y]
            own = edge[0:nx] if y == ny + 1 else r_own[y, 0:nx, :]
            place[0:2, :] = jnp.zeros((2, lanes), f32)
            place[2:8, :] = (got * keep)[0:6]
            place[8 : 8 + nx, :] = own
            if zero is not None:
                place[8 + nx :, :] = zero
            if y < ny:
                place[8:9, :] += (got * only)[6:7]
                both = (
                    c_below[...] * u_first[y : y + 1, :] + c_above[...] * above[y : y + 1, :]
                ) * float(mass_y[y])
                place[...] = place[...] - both
        for j in range(7):
            put_line(s, up_out, j, r[ny - 6 + j])
        up_out[:, 7 * s.z_nodes :] = jnp.zeros((rows, up_out.shape[1] - 7 * s.z_nodes), f32)

    return kernel


def patch_modes(s, vertices, plane_of, matrices, xf, xb, live):
    lam, sums, f_x, b_x, f_z, f_z_low, b_z, b_z_high = matrices
    rows = s.rows
    count = len(vertices)
    _, eigbasis = patch_basis()
    evens = [b for b in range(13) if symmetric(eigbasis[:, b])]
    gx = lax.axis_index("gx")
    gy = lax.axis_index("gy")
    shape = (s.modes_x, s.modes_z)
    mode = lax.broadcasted_iota(jnp.int32, shape, 0)
    vertex = lax.broadcasted_iota(jnp.int32, shape, 1) % s.half_z
    live_x = (mode % s.x_elems != 0) | (gx > 0)
    live[0] = (live_x & (vertex != 0)).astype(f32)
    live[1] = live_x.astype(f32)
    active = (gy > 0).astype(f32)

    def along_y(tile, carry):
        at = pl.ds(pl.multiple_of(tile * 8, 8), 8)
        for i, v in enumerate(vertices):
            first = [plane_of(7 * v + a - 6, at) for a in range(13)]
            if v == 0:
                first = [value * active for value in first]
            even = [first[6]] + [first[6 + a] + first[6 - a] for a in range(1, 7)]
            odd = [first[6 + a] - first[6 - a] for a in range(1, 7)]
            for b in range(13):
                if b in evens:
                    xf[b, i, at, :] = sum(even[a] * float(eigbasis[6 + a, b]) for a in range(7))
                else:
                    xf[b, i, at, :] = sum(odd[a] * float(eigbasis[7 + a, b]) for a in range(6))
        return carry

    lax.fori_loop(0, rows // 8, along_y, 0, unroll=True)

    def spectral(modes_of):
        pieces = []
        for b in modes_of:
            planes = [dot(f_x[...], stacked_rows(xf[b, v])) for v in range(count)]
            pieces += [plane[:, :LANES] for plane in planes]
            pieces += [plane[:, LANES:] for plane in planes]
        high_part, low_part = halves_of(jnp.concatenate(pieces, 0))
        modes = dot(jnp.concatenate([high_part, low_part], 1), f_z[...]) + dot(
            high_part, f_z_low[...]
        )
        modes = modes.reshape(len(modes_of), 2, count, s.modes_x, s.modes_z)
        pieces = []
        for i, b in enumerate(modes_of):
            factor = 1.0 / (sums[...] + lam[b])
            for t in range(2):
                scaled = modes[i, t] * (factor * live[t])[None]
                pieces.append(scaled.reshape(count * s.modes_x, s.modes_z))
        high_part, low_part = halves_of(jnp.concatenate(pieces, 0))
        both = dot(high_part, b_z[...])
        back = both[:, :LANES] + both[:, LANES:] + dot(low_part, b_z_high[...])
        back = back.reshape(len(modes_of), 2, count, s.modes_x, LANES)
        for i, b in enumerate(modes_of):
            for v in range(count):
                plane = jnp.concatenate([back[i, 0, v], back[i, 1, v]], 1)
                xb[b, v] = dot(b_x[...], stacked_rows(plane))

    for first in range(0, 13, GROUP):
        spectral(range(first, min(13, first + GROUP)))


def inner_kernel(s):
    def kernel(r_own, lam, sums, f_x, b_x, f_z, f_z_low, b_z, b_z_high, xb, xf, live):
        patch_modes(
            s,
            list(range(1, s.y_elems - 1)),
            lambda y, at: r_own[y, at, :],
            (lam, sums, f_x, b_x, f_z, f_z_low, b_z, b_z_high),
            xf,
            xb,
            live,
        )

    return kernel


def patch_kernel(s):
    rows, lanes = (s.rows, s.lanes)
    ey, ny = (s.y_elems, s.y_nodes)
    line_y = line_tables(ey)
    _, eigbasis = patch_basis()
    stiffness = element_stiffness()
    one_y = linear_from_cubic(-1, ey, -3, 3 * ey)
    evens = [b for b in range(13) if symmetric(eigbasis[:, b])]
    odds = [b for b in range(13) if b not in evens]

    def kernel(
        r_own, line, below, above, inner,
        lam, sums, f_x, b_x, f_z, f_z_low, b_z, b_z_high,
        m_xz, q_z, r_z, o_z, o_x, q_x, r_x,
        edge_out, own_out, three_out, one_out, down_out, up_out,
        r, xf, xb, c, cz, rz, hx, ex, rx, live,
    ):
        inside = lane_mask(s, (rows, lanes), 0).astype(f32)
        width = below.shape[1]
        lower = line[...] * m_xz[...]
        upper = above[...] * m_xz[...]
        for j in range(7):
            got = get_line(s, below, j, width) * inside
            if j < 6:
                r[j] = got - lower * float(stiffness[1 + j, 7])
            else:
                r[6] = r_own[0] + got
        for y in range(1, ny):
            plane = r_own[y]
            if y >= ny - 7:
                plane = plane - upper * float(stiffness[y - (ny - 7), 7])
            r[6 + y] = plane
        patch_modes(
            s,
            [0, ey - 1],
            lambda y, at: r[y + 6, at, :],
            (lam, sums, f_x, b_x, f_z, f_z_low, b_z, b_z_high),
            xf,
            xb,
            live,
        )

        def back_y(tile, carry):
            at = pl.ds(pl.multiple_of(tile * 8, 8), 8)
            tail = None
            for v in range(ey):
                if 0 < v < ey - 1:
                    modes = [inner[b, v - 1, at, :] for b in range(13)]
                else:
                    modes = [xb[b, min(v, 1), at, :] for b in range(13)]
                out = [None] * 13
                for a in range(7):
                    even = sum(modes[b] * float(eigbasis[6 + a, b]) for b in evens)
                    if a == 0:
                        out[6] = even
                        continue
                    odd = sum(modes[b] * float(eigbasis[6 + a, b]) for b in odds)
                    out[6 + a], out[6 - a] = (even + odd, even - odd)
                if v:
                    out[:6] = [value + other for value, other in zip(out[:6], tail)]
                tail = out[7:]
                for a in range(13 if v == ey - 1 else 7):
                    c[7 * v + a, at, :] = out[a]
            return carry

        lax.fori_loop(0, rows // 8, back_y, 0, unroll=True)

        for j in range(6):
            down_out[:, lanes * j : lanes * (j + 1)] = c[j]
        edge_out[...] = c[6:, 0:8, :]
        own_out[...] = c[6:, 8:, :]

        half = s.coarse_lanes
        rows_c = s.coarse_rows
        cz[...] = mm(c[...].reshape((ny + 6) * rows, lanes), q_z[...]).reshape(
            ny + 6, rows, 2 * half
        )
        own_rows = r[6 : ny + 6, 8:, :].reshape(ny * (rows - 8), lanes)
        rz[...] = mm(own_rows, r_z[...]).reshape(ny, rows - 8, half)
        for y in range(ny + 6):
            plane = dot(q_x[...], stacked_rows(cz[y]))
            hx[y] = plane[:rows_c, :half]
            ex[y] = plane[rows_c:, :half] + plane[:rows_c, half:]
        for y in range(0, ny - 1, 2):
            pair = jnp.concatenate([rz[y], rz[y + 1]], 1)
            pair = dot(r_x[...], stacked_rows(pair))
            rx[y], rx[y + 1] = (pair[:, :half], pair[:, half:])
        if ny % 2:
            rx[ny - 1] = dot(r_x[...], stacked_rows(rz[ny - 1]))
        for j in range(s.coarse_y):
            three_out[j] = line_of_planes(
                np.concatenate(
                    [line_y["own"][j], -line_y["stiff_part"][j], -line_y["mass_part"][j]]
                ),
                [lambda y=y: rx[y] for y in range(ny)]
                + [lambda y=y: hx[y] for y in range(ny + 6)]
                + [lambda y=y: ex[y] for y in range(ny + 6)],
            )
        one_all = mm(
            three_out[...].reshape(s.coarse_y * rows_c, half), o_z[...]
        ).reshape(s.coarse_y, rows_c, LANES)
        for m in range(ey + 2):
            mixed = line_of_planes(
                one_y[m], [lambda j=j: one_all[j] for j in range(s.coarse_y)]
            )
            one_out[m] = mm(o_x[...], mixed)
        base = 6 * lanes
        down_out[:, base:] = jnp.zeros((rows, 2 * half), f32)
        up_out[...] = jnp.zeros(up_out.shape, f32)
        up_out[:, 0:half] = three_out[s.coarse_y - 1]
        for j in range(4):
            first, at = (rows_c * (j % 2), base + half * (j // 2))
            if j < 3:
                down_out[first : first + rows_c, at : at + half] = three_out[j]
            down_out[first : first + 8, at : at + half] += one_out[j]
            up_out[0:8, half * j : half * (j + 1)] += one_out[ey - 2 + j]

    return kernel


def coarse_place(s, index):
    high_rows = coarse_height(s)
    return index % high_rows, LANES * (index // high_rows)


def line_lanes(s):
    return up_to(-(-s.y_nodes // 4) * s.z_nodes, LANES)


def coarse_height(s):
    return up_to(-(-max(9 * s.y_elems, 4 * s.y_elems + 24) // 2), 24)


def join_kernel(s):
    lanes, half, rows_c = (s.lanes, s.coarse_lanes, s.coarse_rows)
    ey, ny = (s.y_elems, s.y_nodes)

    def kernel(edge, three, one, down, up, down_out, up_out, three_out, one_out):
        lane = lax.broadcasted_iota(jnp.int32, (rows_c, half), 1)
        is_three = (lane < s.coarse_z).astype(f32)
        is_one = (lane >= s.coarse_z).astype(f32)[0:8]
        down_out[...] = jnp.zeros(down_out.shape, f32)
        shared = shared_lanes(s, (8, lanes))
        for y in range(ny):
            plane = edge[y]
            if y >= ny - 6:
                j = y - (ny - 6)
                plane = plane + down[0:8, lanes * j : lanes * (j + 1)]
            plane = plane + pltpu.roll(plane, lanes - (LANES - s.split), 1) * shared
            here = pl.ds(6 * (y % 4), 6)
            at = s.z_nodes * (y // 4)
            for t in range(2):
                first = LANES * t + 6
                down_out[here, at + s.split * t : at + s.split * (t + 1)] = plane[
                    2:8, first : first + s.split
                ]
        base = 6 * lanes
        tiles = line_lanes(s)
        up_out[...] = jnp.zeros(up_out.shape, f32)

        def from_above(k, count):
            row, at = (rows_c * (k % 2), base + half * (k // 2))
            return down[row : row + count, at : at + half]

        for j in range(3 * ey):
            plane = three[3 + j]
            if j >= 3 * ey - 3:
                plane = plane + from_above(j - (3 * ey - 3), rows_c)
            if j == 0:
                plane = plane + up[0:rows_c, 0:half]
            plane = plane * is_three
            three_out[j] = plane
            row, at = coarse_place(s, 3 * j)
            down_out[row : row + 3, tiles + at : tiles + at + half] = plane[0:3]
            row, at = coarse_place(s, j)
            up_out[row : row + 1, at : at + half] = plane[s.coarse_x - 1 : s.coarse_x]
        for j in range(ey + 6):
            y = j - 3
            plane = None
            if -1 <= y <= ey:
                plane = one[y + 1]
            if y <= 0:
                k = y + 3
                part = up[0:8, half * k : half * (k + 1)]
                plane = part if plane is None else plane + part
            if y >= ey - 1:
                part = from_above(y - (ey - 1), 8)
                plane = part if plane is None else plane + part
            plane = plane * is_one
            one_out[j] = plane
            row, at = coarse_place(s, 4 * j)
            down_out[row : row + 4, tiles + at : tiles + at + half] += plane[0:4]
            up_out[row : row + 4, at : at + half] += plane[s.x_elems - 2 : s.x_elems + 2]

    return kernel


def shared_lanes(s, shape):
    lane = lax.broadcasted_iota(jnp.int32, shape, 1)
    return ((lane >= s.split) & (lane < s.split + 6)).astype(f32)


def base_kernel(s):
    lanes, nx, ny = (s.lanes, s.x_nodes, s.y_nodes)
    width = ny * s.z_nodes

    def kernel(guess, weight, own, down, out):
        gx = lax.axis_index("gx")
        gy = lax.axis_index("gy")
        shape = (nx, lanes)
        row = lax.broadcasted_iota(jnp.int32, shape, 0)
        live = (lane_mask(s, shape, 1) & ((row != 0) | (gx > 0))).astype(f32)
        live_y = (gy > 0).astype(f32)
        shared = shared_lanes(s, shape)
        for y in range(ny):
            plane = own[y, 0:nx, :]
            if y >= ny - 6:
                j = y - (ny - 6)
                plane = plane + down[8 : 8 + nx, lanes * j : lanes * (j + 1)]
            plane = plane + pltpu.roll(plane, lanes - (LANES - s.split), 1) * shared
            mask = live if y else live * live_y
            factor = weight[...] * (1.0 if y % 7 == 0 else 0.5)
            put_line(s, out, y, (get_line(s, guess, y, width) + factor * plane) * mask)

    return kernel


def finish_kernel(s, x_total, y_total):
    lanes, half, rows_c, nz = (s.lanes, s.coarse_lanes, s.coarse_rows, s.z_nodes)
    ex, ey, nx, ny = (s.x_elems, s.y_elems, s.x_nodes, s.y_nodes)
    one_rows = up_to(ex + 6, 8)
    split = s.split

    def kernel(
        base, weight, right, left, three, one,
        smooth_out, three_out, coarse_out, fine, level,
    ):
        gx = lax.axis_index("gx")
        gy = lax.axis_index("gy")
        live_y = (gy > 0).astype(f32)
        smooth_out[...] = base[...]
        for y in range(ny):
            at = nz * (y // 4)
            piece = right[6 * (y % 4) : 6 * (y % 4) + 6, at : at + nz] * weight[...]
            smooth_out[nx - 6 : nx, nz * y : nz * (y + 1)] += piece * (1.0 if y % 7 == 0 else 0.5)
        tiles = line_lanes(s)
        nzc = s.coarse_z
        lane = lax.broadcasted_iota(jnp.int32, (3 * ex, nzc), 1)
        row = lax.broadcasted_iota(jnp.int32, (3 * ex, nzc), 0)
        live = ((lane >= 1) & ((row >= 1) | (gx > 0))).astype(f32)
        for j in range(3 * ey):
            fine[j] = three[j]
            at_row, at = coarse_place(s, 3 * j)
            at += tiles
            fine[j, 3 * ex : 3 * ex + 3, :] += right[at_row : at_row + 3, at : at + half]
            at_row, at = coarse_place(s, j)
            fine[j, 3:4, :] += left[at_row : at_row + 1, at : at + half]
            mask = live if j else live * live_y
            three_out[:, nzc * j : nzc * (j + 1)] = fine[j, 3 : 3 * ex + 3, 0:nzc] * mask
        level[...] = jnp.zeros((ey + 6, one_rows, LANES), f32)
        for j in range(ey + 6):
            level[j, 2 : ex + 4, :] = one[j, 0 : ex + 2, :]
            at_row, at = coarse_place(s, 4 * j)
            level[j, 0:4, :] += left[at_row : at_row + 4, at : at + half]
            at += tiles
            level[j, ex + 2 : ex + 6, :] += right[at_row : at_row + 4, at : at + half]
        shape = (one_rows, LANES)
        lane = lax.broadcasted_iota(jnp.int32, shape, 1)
        row = lax.broadcasted_iota(jnp.int32, shape, 0)
        global_x = gx * ex + row - 3
        plane_mask = (
            (lane > s.coarse_z) & (lane < s.coarse_z + s.z_elems) & (row < ex + 6)
            & (global_x >= 1) & (global_x < x_total)
        )
        masks = []
        for j in range(ey + 6):
            global_y = gy * ey + (j - 3)
            inside = (global_y >= 1) & (global_y < y_total)
            masks.append((plane_mask & inside).astype(f32))
        levels = [level[j] for j in range(ey + 6)]
        error = [damping / 12.0 * a * m for a, m in zip(levels, masks)]
        zero = jnp.zeros(shape, f32)
        for sweep in range(1, JAC):
            lower = [zero] + error[:-1]
            upper = error[1:] + [zero]
            fresh = []
            for j in range(ey + 6):
                here = error[j]
                neighbours = (
                    lower[j]
                    + upper[j]
                    + pltpu.roll(here, 1, 0)
                    + pltpu.roll(here, one_rows - 1, 0)
                    + pltpu.roll(here, 1, 1)
                    + pltpu.roll(here, LANES - 1, 1)
                )
                applied = 12.0 * here - 2.0 * neighbours
                fresh.append((here + damping / 12.0 * (levels[j] - applied)) * masks[j])
            error = fresh
        nze = s.z_elems
        for j in range(ey):
            coarse_out[:, nze * j : nze * (j + 1)] = error[3 + j][
                3 : 3 + ex, s.coarse_z : s.coarse_z + nze
            ]

    return kernel


def local(load_vector, initial_guess):
    z_nodes = 7 * EZ
    x_nodes = load_vector.shape[0]
    y_nodes = load_vector.shape[1] // z_nodes
    s = Sizes(x_nodes, y_nodes, z_nodes)
    rows, lanes, half = (s.rows, s.lanes, s.coarse_lanes)
    ny, ey = (s.y_nodes, s.y_elems)
    width = y_nodes * z_nodes
    shape = lambda *dims: jax.ShapeDtypeStruct(dims, f32)
    params = pltpu.CompilerParams(vmem_limit_bytes=36 * 2**20)
    vmem = lambda count: [pl.BlockSpec(memory_space=pltpu.VMEM)] * count

    def call(kernel, name, outputs, operands, scratch=(), spaces=None, semaphores=0):
        specs = vmem(len(operands))
        for index, space in (spaces or {}).items():
            specs[index] = pl.BlockSpec(memory_space=space)
        return pl.pallas_call(
            kernel,
            out_shape=tuple(shape(*dims) for dims in outputs),
            in_specs=specs,
            out_specs=tuple(vmem(len(outputs))),
            scratch_shapes=[pltpu.VMEM(d, f32) if isinstance(d, tuple) else d for d in scratch]
            + ([pltpu.SemaphoreType.DMA((semaphores,))] if semaphores else []),
            compiler_params=params,
            name=name,
        )(*operands)

    in_hbm = lambda values: [pltpu.with_memory_space_constraint(v, pltpu.HBM) for v in values]
    hbm = {index: pltpu.HBM for index in range(4)}
    low = x_nodes - 7
    taken = x_nodes - low // 8 * 8
    constants = residual_constants(s, low)
    up, u_first = call(
        send_kernel(s),
        "send",
        ((8, up_to((ny + 2) * z_nodes, LANES)), (up_to(ny, 8), lanes)),
        in_hbm([initial_guess, load_vector] + constants),
        [
            (ny + 1, 8, lanes),
            (ny + 1, 8, lanes),
            (taken, width),
            (taken, width),
            constants[0].shape,
            pltpu.VMEM(constants[1].shape, jnp.bfloat16),
            (8, width),
        ],
        spaces=hbm,
        semaphores=5,
    )
    below = shifted(up, "gx", 1)
    above = shifted(u_first, "gx", -1)
    constants = residual_constants(s, 0)
    r_own, edge = call(
        residual_kernel(s),
        "residual",
        ((ny + 1, s.own_rows, lanes), (s.own_rows, lanes)),
        in_hbm([initial_guess, load_vector] + constants),
        [
            (ny + 1, s.own_rows, lanes),
            initial_guess.shape,
            load_vector.shape,
            constants[0].shape,
            pltpu.VMEM(constants[1].shape, jnp.bfloat16),
        ],
        spaces=hbm,
        semaphores=4,
    )
    r_x, line, up = call(
        joined_x_kernel(s),
        "joined_x",
        (
            (ny + 1, rows, lanes),
            (rows, lanes),
            (rows, up_to(7 * z_nodes, LANES)),
        ),
        [r_own, edge, u_first, below, above]
        + [jnp.asarray(v, f32) for v in coupling_constants(s)],
    )
    below = shifted(up, "gy", 1)
    above = shifted(line, "gy", -1)
    solve, coarse = patch_constants(s)
    (inner,) = call(
        inner_kernel(s),
        "inner",
        ((13, ey - 2, rows, lanes),),
        [r_x] + solve,
        [(13, ey - 2, rows, lanes), (2, s.modes_x, s.modes_z)],
        spaces={1: pltpu.SMEM},
    )
    edge, own, three, one, down, up = call(
        patch_kernel(s),
        "patches",
        (
            (ny, 8, lanes),
            (ny, rows - 8, lanes),
            (s.coarse_y, s.coarse_rows, half),
            (ey + 2, 8, LANES),
            (rows, 6 * lanes + 2 * half),
            (s.coarse_rows, 4 * half),
        ),
        [r_x, line, below, above, inner] + solve + coarse,
        [
            (ny + 6, rows, lanes),
            (13, 2, rows, lanes),
            (13, 2, rows, lanes),
            (ny + 6, rows, lanes),
            (ny + 6, rows, 2 * half),
            (ny, rows - 8, half),
            (ny + 6, s.coarse_rows, half),
            (ny + 6, s.coarse_rows, half),
            (ny, s.coarse_rows, half),
            (2, s.modes_x, s.modes_z),
        ],
        spaces={5: pltpu.SMEM},
    )
    down = shifted(down, "gy", -1)
    up = shifted(up, "gy", 1)
    right, left, three, one = call(
        join_kernel(s),
        "join",
        (
            (coarse_height(s), line_lanes(s) + 2 * half),
            (coarse_height(s), lanes),
            (3 * ey, s.coarse_rows, half),
            (ey + 6, 8, LANES),
        ),
        [edge, three, one, down, up],
    )
    right = shifted(right, "gx", -1)
    left = shifted(left, "gx", 1)
    weight_z = np.where(np.arange(z_nodes) % 7 == 0, 1.0, 0.5)
    weight = jnp.asarray(
        np.where(np.arange(x_nodes) % 7 == 0, 1.0, 0.5)[:, None]
        * rows_by_node(s, weight_z[:, None], True)[:, 0],
        f32,
    )
    weight_x = np.where(np.arange(x_nodes) % 7 == 0, 1.0, 0.5)[-6:]
    edge_weight = jnp.asarray(weight_x[:, None] * weight_z[None, :], f32)
    (base,) = call(
        base_kernel(s), "base", ((x_nodes, width),), [initial_guess, weight, own, down]
    )
    return call(
        finish_kernel(s, s.x_elems * lax.axis_size("gx"), ey * lax.axis_size("gy")),
        "finish",
        (
            (x_nodes, width),
            (3 * s.x_elems, 3 * ey * s.coarse_z),
            (s.x_elems, ey * s.z_elems),
        ),
        [base, edge_weight, right, left, three, one],
        [
            (3 * ey, s.coarse_rows, half),
            (ey + 6, up_to(s.x_elems + 6, 8), LANES),
        ],
    )


def solution(mesh):
    in_specs = (P("gx", "gy"), P("gx", "gy"))
    out_specs = (P("gx", "gy"), P("gx", "gy"), P("gx", "gy"))
    return jax.shard_map(local, mesh=mesh, in_specs=in_specs, out_specs=out_specs, check_vma=False)
```
